32 devices in a mesh: shard: 2 (over x), ctx: 8 (over z, core), tp: 2 (over y).
Axes of the slice: x: 2, y: 2, z: 4, core: 2. Of those that a mesh axis runs over, the one named last changes fastest.
Arguments:
- tokens: bfloat16 [4, 4096, 768], P('shard', 'ctx'), may hold values from -6 to 6
- cotangent: bfloat16 [4, 4096, 768], P('shard', 'ctx'), may hold values from -6 to 6
- segment_ids: int32 [4, 4096], P('shard'), may hold values from 0 to 3, never falling along the last dimension, each value on 1 to 1920 neighbouring positions
- w_qkv: float32 [3, 768, 768], P(None, 'shard', 'tp'), may hold values from -0.21875 to 0.21875
- w_out: float32 [768, 768], P('tp', 'shard'), may hold values from -0.21875 to 0.21875
- w_fc1: float32 [768, 3072], P('shard', 'tp'), may hold values from -0.21875 to 0.21875
- w_fc2: float32 [3072, 768], P('tp', 'shard'), may hold values from -0.109375 to 0.109375
- norm_gain: float32 [2, 768], P(None, 'shard'), may hold values from 0.1 to 1.9
- norm_bias: float32 [4, 768], P(None, 'shard'), may hold values from -3 to 3
- head_gain: float32 [768], P('tp'), may hold values from 0.1 to 1.9
- head_bias: float32 [3, 768], P(None, 'tp'), may hold values from -3 to 3
- ffn_gain: float32 [3072], P('tp'), may hold values from 0.1 to 1.9
- ffn_bias: float32 [2, 3072], P(None, 'tp'), may hold values from -3 to 3
Outputs:
- out: bfloat16 [4, 4096, 768], P('shard', 'ctx')
- grad_tokens: bfloat16 [4, 4096, 768], P('shard', 'ctx')
- grad_w_qkv: float32 [3, 768, 768], P(None, ('shard', 'ctx'), 'tp')
- grad_w_out: float32 [768, 768], P('tp', ('shard', 'ctx'))
- grad_w_fc1: float32 [768, 3072], P(('shard', 'ctx'), 'tp')
- grad_w_fc2: float32 [3072, 768], P('tp', ('shard', 'ctx'))
- grad_norm_gain: float32 [2, 768], P(None, ('shard', 'ctx'))
- grad_norm_bias: float32 [4, 768], P(None, ('shard', 'ctx'))
- grad_head_gain: float32 [768], P('tp')
- grad_head_bias: float32 [3, 768], P(None, 'tp')
- grad_ffn_gain: float32 [3072], P('tp')
- grad_ffn_bias: float32 [2, 3072], P(None, 'tp')
The draws below stay inside these ranges and needn't reach their ends.
Inputs may be any that keep to these rules, and one draw needn't show every extreme that they name: `segment_ids`: along each sequence the document number never falls; every document holds 1 to 1920 tokens and some document holds exactly 1920.
All inputs are finite; a program needn't handle non-finite values.
Results may differ from the reference program's by a relative error of at most 0.014.
Values may be sent and summed in bfloat16 or wider, within the bound.
A program may use at most 192 MiB of HBM per device.

```python
import math
import jax
import jax.numpy as jnp
import numpy as np
from jax import lax

D = 768
HEADS = 12
HEAD_DIM = 64
FF = 3072
SEQ = 4096
DOCS = 4
MAXDOC = 1920
SEQS = 4


def shard_levels(stream_key, extent, pieces, smallest, largest):
    factor_of = 1.0
    for position, shards_of in pieces:
        heights = jax.random.uniform(jax.random.fold_in(jax.random.fold_in(stream_key, 6), position), (shards_of,), jnp.float32, smallest / len(pieces), largest / len(pieces))
        factor_of = factor_of * jnp.repeat(jnp.exp(heights), extent[position] // shards_of).reshape((-1,) + (1,) * (len(extent) - 1 - position))
    return factor_of


def profile(number_of, total, reach, skew):
    loads = [(1 << 20) // math.isqrt(standing ** skew) + 1 for standing in range(2, number_of + 1)]
    surplus, holding = total - reach - (number_of - 1), [1] * (number_of - 1)
    while surplus > 0:
        movable = [i for i in range(number_of - 1) if holding[i] < reach]
        pool, budget = sum([loads[i] for i in movable]), surplus
        for i in movable:
            extra = min(reach - holding[i], max(1, budget * loads[i] // pool), surplus)
            holding[i] = holding[i] + extra
            surplus = surplus - extra
    return np.array([reach] + holding)


def ragged(stream_key, number_of, total, bound, slope):
    if number_of == 2:
        one = jax.random.randint(stream_key, (), max(1, total - bound), min(bound, total - 1) + 1)
        return jnp.stack([one, total - one])
    tallies = jnp.asarray(profile(number_of, total, bound, slope), jnp.int32)
    twos = (number_of - 1) // 2
    donor, sink = tallies[1:1 + 2 * twos:2], tallies[2:2 + 2 * twos:2]
    room = jnp.minimum(donor - 1, bound - sink)
    moved = jax.random.randint(jax.random.fold_in(stream_key, 1), (twos,), 0, 1 << 20) % (room + 1)
    tallies = tallies.at[1:1 + 2 * twos:2].set(donor - moved).at[2:2 + 2 * twos:2].set(sink + moved)
    return tallies[jax.random.permutation(jax.random.fold_in(stream_key, 2), number_of)]


def noise(key, shape, width, limit, split=(), held_as=jnp.bfloat16):
    values = jax.random.normal(key, shape, jnp.float32) * width
    if len(split) > 0:
        values = shard_levels(key, shape, split, -0.22, 0.18) * values
    return jnp.clip(values, min=-limit, max=limit).astype(held_as)


def setup_inputs(seed: int = 0) -> dict:
    seeds = jax.random.split(jax.random.key(seed), 14)
    tokens = noise(seeds[0], (SEQS, SEQ, D), 1.0, 6.0, ((0, 2), (1, 8)))
    cotangent = noise(seeds[1], (SEQS, SEQ, D), 1.0, 6.0, ((0, 2), (1, 8)))
    segment_ids = jax.vmap(lambda own: jnp.searchsorted(jnp.cumsum(ragged(own, DOCS, SEQ, MAXDOC, 1)), jnp.arange(SEQ), side="right"))(jax.random.split(seeds[2], SEQS)).reshape((SEQS, SEQ)).astype(jnp.int32)
    w_qkv = noise(seeds[3], (3, D, D), D ** -0.5, 0.21875, ((1, 2), (2, 2)), jnp.float32)
    w_out = noise(seeds[4], (D, D), D ** -0.5, 0.21875, ((0, 2), (1, 2)), jnp.float32)
    w_fc1 = noise(seeds[5], (D, FF), D ** -0.5, 0.21875, ((0, 2), (1, 2)), jnp.float32)
    w_fc2 = noise(seeds[6], (FF, D), FF ** -0.5, 0.109375, ((0, 2), (1, 2)), jnp.float32)
    norm_gain = jnp.clip(1.0 + 0.18 * jax.random.normal(seeds[7], (2, D), jnp.float32), 0.1, 1.9)
    norm_bias = noise(seeds[8], (4, D), 0.5, 3.0, ((1, 2),), jnp.float32)
    head_gain = jnp.clip(1.0 + 0.18 * jax.random.normal(seeds[9], (D,), jnp.float32), 0.1, 1.9)
    head_bias = noise(seeds[10], (3, D), 0.5, 3.0, ((1, 2),), jnp.float32)
    ffn_gain = jnp.clip(1.0 + 0.18 * jax.random.normal(seeds[11], (FF,), jnp.float32), 0.1, 1.9)
    ffn_bias = noise(seeds[12], (2, FF), 0.5, 3.0, ((1, 2),), jnp.float32)
    return dict(tokens=tokens, cotangent=cotangent, segment_ids=segment_ids, w_qkv=w_qkv, w_out=w_out, w_fc1=w_fc1, w_fc2=w_fc2, norm_gain=norm_gain, norm_bias=norm_bias, head_gain=head_gain, head_bias=head_bias, ffn_gain=ffn_gain, ffn_bias=ffn_bias)


EPS = 1e-05
NEGATIVE = -1e+30
HIGH = lax.Precision.HIGHEST

@jax.custom_vjp
def low(v):
    return lax.optimization_barrier(v.astype(jnp.bfloat16)).astype(jnp.float32)

@jax.custom_vjp
def low_back(v):
    return v

def low_keep(v):
    return (low(v), None)

def low_pass(kept, grad):
    return (grad,)

def back_keep(v):
    return (v, None)

def back_low(kept, grad):
    return (low(grad),)
low.defvjp(low_keep, low_pass)
low_back.defvjp(back_keep, back_low)

def layer_norm(values, gain, shift):
    row_mean = lax.optimization_barrier(jnp.mean(values, -1, keepdims=True))
    centred = values - row_mean
    variance = lax.optimization_barrier(jnp.mean(centred * centred, -1, keepdims=True))
    return centred * lax.rsqrt(variance + EPS) * gain + shift

def matmul(left, right):
    return jnp.dot(left, right, precision=HIGH)

def attend(query, keys, values, segment):
    length = query.shape[0]
    positions = jnp.arange(length)

    @jax.checkpoint
    def one_head(block):
        query_head, key_head, value_head = block
        allowed = (segment[:, None] == segment[None, :]) & (positions[None, :] <= positions[:, None])
        raw = low_back(matmul(query_head, key_head.T) * 0.125)
        masked = jnp.where(allowed, raw, NEGATIVE)
        peak = lax.optimization_barrier(jnp.max(masked, -1, keepdims=True))
        expo = jnp.exp(masked - peak)
        probs = expo / lax.optimization_barrier(jnp.sum(expo, -1, keepdims=True))
        return matmul(low(probs), value_head)

    def split_heads(array):
        return array.reshape(length, HEADS, HEAD_DIM).transpose(1, 0, 2)
    mixed = lax.map(one_head, (split_heads(query), split_heads(keys), split_heads(values)))
    return mixed.transpose(1, 0, 2).reshape(length, HEADS * HEAD_DIM)

def layer(params, inputs, segment):
    w_qkv, w_out, w_fc1, w_fc2, norm_gain, norm_bias, head_gain, head_bias, ffn_gain, ffn_bias = params
    qkv_low = low(w_qkv)
    out_low = low(w_out)
    up_low = low(w_fc1)
    down_low = low(w_fc2)
    gains = low(norm_gain)
    biases = low(norm_bias)
    normed = low(layer_norm(inputs, gains[0], biases[0]))
    query = low(low_back(matmul(normed, qkv_low[0]) + head_bias[0]))
    keys = low(low_back(matmul(normed, qkv_low[1])))
    values = low(low_back(matmul(normed, qkv_low[2]) + head_bias[1]))
    attended = low_back(attend(query, keys, values, segment))
    sub_out = low(layer_norm(attended, head_gain, head_bias[2]))
    residual = inputs + low_back(matmul(sub_out, out_low) + biases[2])
    ffn_in = low(layer_norm(residual, gains[1], biases[1]))
    hidden = low_back(matmul(ffn_in, up_low) + ffn_bias[0])
    inner = low(layer_norm(jax.nn.gelu(hidden), ffn_gain, ffn_bias[1]))
    return residual + low_back(matmul(inner, down_low) + biases[3])

def reference(tokens, cotangent, segment_ids, w_qkv, w_out, w_fc1, w_fc2, norm_gain, norm_bias, head_gain, head_bias, ffn_gain, ffn_bias):
    params = (w_qkv, w_out, w_fc1, w_fc2, norm_gain, norm_bias, head_gain, head_bias, ffn_gain, ffn_bias)

    def per_sequence(carried, block):
        seq_tokens, seq_grad, segment = block
        inputs = seq_tokens.astype(jnp.float32)
        result, pull = jax.vjp(lambda weights, values: layer(weights, values, segment), params, inputs)
        weight_grads, input_grad = pull(seq_grad.astype(jnp.float32))
        carried = jax.tree.map(jnp.add, carried, weight_grads)
        return (carried, (result.astype(jnp.bfloat16), input_grad.astype(jnp.bfloat16)))
    zeros = jax.tree.map(jnp.zeros_like, params)
    totals, (outputs, grad_tokens) = lax.scan(per_sequence, zeros, (tokens, cotangent, segment_ids))
    return (outputs, grad_tokens, totals[0], totals[1], totals[2], totals[3], totals[4], totals[5], totals[6], totals[7], totals[8], totals[9])
```

```python
import functools
import jax
import jax.numpy as jnp
from jax import lax
from jax.experimental import pallas as pl
from jax.experimental.pallas import tpu as pltpu
from jax.sharding import PartitionSpec as P
HD=64
NEG=-1e30
VL=48*1024*1024

def fwd_kernel(diag,first,last,heads,L,BQ,BK, lo_sm, qT_ref,kv_ref,lo_ref,*rest):
    n=heads*HD
    if first:
        ins=(); rest=rest
    else:
        m_in,l_in,a_in=rest[:3]; rest=rest[3:]
    if last:
        c_ref,oT_ref,lse_ref,mean_ref=rest[:4]; rest=rest[4:]
    else:
        m_out,l_out,a_out=rest[:3]; rest=rest[3:]
    m_s,l_s,acc,qm,vT=rest
    if first:
        m_s[...]=jnp.full_like(m_s,NEG); l_s[...]=jnp.zeros_like(l_s); acc[...]=jnp.zeros_like(acc)
    else:
        m_s[...]=m_in[...]; l_s[...]=l_in[...]; acc[...]=a_in[...]
    nq,nk=L//BQ,L//BK
    rowi=lax.broadcasted_iota(jnp.int32,(2*HD,L),0)
    for p in range(heads//2):
        blk=qT_ref[p*128:(p+1)*128,:]
        qm[2*p]=jnp.where(rowi<HD,blk,jnp.zeros_like(blk))
        qm[2*p+1]=jnp.where(rowi>=HD,blk,jnp.zeros_like(blk))
        vT[p*128:(p+1)*128,:]=kv_ref[:,n+p*128:n+(p+1)*128].T
    def block(qb,kb,masked):
        qs=slice(qb*BQ,(qb+1)*BQ); ks=slice(kb*BK,(kb+1)*BK)
        if masked:
            kk=lax.broadcasted_iota(jnp.int32,(BK,BQ),0)+kb*BK
            valid=kk>=lo_ref[:,qs]
            if diag and (kb+1)*BK>qb*BQ+1:
                valid=valid&(kk<=lax.broadcasted_iota(jnp.int32,(BK,BQ),1)+qb*BQ)
        for h in range(heads):
            p=h//2
            s=jnp.dot(kv_ref[ks,p*128:(p+1)*128],qm[h,:,qs],preferred_element_type=jnp.float32)
            if masked: s=jnp.where(valid,s,NEG)
            mo=m_s[h:h+1,qs]
            mn=jnp.maximum(mo,jnp.max(s,0,keepdims=True))
            e=jnp.exp(s-mn); al=jnp.exp(mo-mn)
            m_s[h:h+1,qs]=mn
            l_s[h:h+1,qs]=l_s[h:h+1,qs]*al+jnp.sum(e,0,keepdims=True)
            hs=slice(h*HD,(h+1)*HD)
            acc[hs,qs]=acc[hs,qs]*al+jnp.dot(vT[hs,ks],e.astype(jnp.bfloat16),preferred_element_type=jnp.float32)
    for qb in range(nq):
        for kb in range(nk):
            if diag and kb*BK>qb*BQ+BQ-1: continue
            vis=lo_sm[qb]<=kb*BK+BK-1
            if diag and (kb+1)*BK>qb*BQ+1:
                pl.when(vis)(functools.partial(block,qb,kb,True))
            else:
                full=lo_sm[nq+qb]<=kb*BK
                pl.when(full)(functools.partial(block,qb,kb,False))
                pl.when(jnp.logical_and(vis,jnp.logical_not(full)))(functools.partial(block,qb,kb,True))
    if last:
        tot=jnp.zeros((1,L),jnp.float32)
        for h in range(heads):
            hs=slice(h*HD,(h+1)*HD)
            o=acc[hs,:]/l_s[h:h+1,:]
            oT_ref[hs,:]=o
            tot=tot+jnp.sum(o,0,keepdims=True)
        mean=tot/n
        mean_ref[...]=mean
        lse_ref[...]=m_s[...]+jnp.log(l_s[...])
        for p in range(heads//2):
            c_ref[:,p*128:(p+1)*128]=(oT_ref[p*128:(p+1)*128,:]-mean).T.astype(jnp.bfloat16)
    else:
        m_out[...]=m_s[...]; l_out[...]=l_s[...]; a_out[...]=acc[...]

def fwd_step(w,nw,lo_sm,qT,kv,lo,state):
    n,L=qT.shape; heads=n//HD
    BQ=min(256,L); BK=min(256,L)
    first=w==0; last=w==nw
    V=pl.BlockSpec(memory_space=pltpu.VMEM)
    st=(jax.ShapeDtypeStruct((8,L),jnp.float32),jax.ShapeDtypeStruct((8,L),jnp.float32),jax.ShapeDtypeStruct((n,L),jnp.float32))
    outs=st if not last else (jax.ShapeDtypeStruct((L,n),jnp.bfloat16),st[2],st[0],jax.ShapeDtypeStruct((1,L),jnp.float32))
    args=(lo_sm,qT,kv,lo)+(() if first else tuple(state))
    return pl.pallas_call(
        functools.partial(fwd_kernel,w==0,first,last,heads,L,BQ,BK),
        out_shape=outs,
        in_specs=[pl.BlockSpec(memory_space=pltpu.SMEM)]+[V]*(len(args)-1),
        out_specs=tuple([V]*len(outs)),
        scratch_shapes=[pltpu.VMEM((8,L),jnp.float32),pltpu.VMEM((8,L),jnp.float32),pltpu.VMEM((n,L),jnp.float32),
            pltpu.VMEM((heads,128,L),jnp.bfloat16),pltpu.VMEM((n,L),jnp.bfloat16)],
        compiler_params=pltpu.CompilerParams(vmem_limit_bytes=VL),
        cost_estimate=pl.CostEstimate(flops=4*L*L*n,bytes_accessed=4*L*n*4,transcendentals=heads*L*L),
        name="attn_fwd",
    )(*args)

def bwd_kernel(NT,diag,first,last,heads,L,BQ,BK,lo_sm,qT_ref,q_ref,doT_ref,do_ref,kv_ref,lse_ref,dd_ref,lo_ref,*rest):
    n=heads*HD
    if first:
        pass
    else:
        dq_in,dkv_in=rest[:2]; rest=rest[2:]
    dq_out,dkv_out=rest[:2]; rest=rest[2:]
    qm,dm,kT,dk,dv=rest
    if first: dq_out[...]=jnp.zeros_like(dq_out)
    else: dq_out[...]=dq_in[...]
    dk[...]=jnp.zeros_like(dk); dv[...]=jnp.zeros_like(dv)
    nq,nk=L//BQ,L//BK
    rowi=lax.broadcasted_iota(jnp.int32,(2*HD,L),0)
    for p in range(heads//2):
        ps=slice(p*128,(p+1)*128)
        for ref,dst in ((qT_ref,qm),(doT_ref,dm)):
            blk=ref[ps,:]
            dst[2*p]=jnp.where(rowi<HD,blk,jnp.zeros_like(blk))
            dst[2*p+1]=jnp.where(rowi>=HD,blk,jnp.zeros_like(blk))
        kT[ps,:]=kv_ref[:,ps].T
    lane=lax.broadcasted_iota(jnp.int32,(BK,128),1)
    def block(qb,kb,masked):
        qs=slice(qb*BQ,(qb+1)*BQ); ks=slice(kb*BK,(kb+1)*BK)
        if masked:
            kk=lax.broadcasted_iota(jnp.int32,(BK,BQ),0)+kb*BK
            valid=kk>=lo_ref[:,qs]
            if diag and (kb+1)*BK>qb*BQ+1:
                valid=valid&(kk<=lax.broadcasted_iota(jnp.int32,(BK,BQ),1)+qb*BQ)
        for p in range(heads//2):
            ps=slice(p*128,(p+1)*128)
            pv=slice(n+p*128,n+(p+1)*128)
            parts=[]
            for h in (2*p,2*p+1):
                hs=slice(h*HD,(h+1)*HD)
                s=jnp.dot(kv_ref[ks,ps],qm[h,:,qs],preferred_element_type=jnp.float32)
                dp=jnp.dot(kv_ref[ks,pv],dm[h,:,qs],preferred_element_type=jnp.float32)
                if masked: s=jnp.where(valid,s,NEG)
                e=jnp.exp(s-lse_ref[h:h+1,qs])
                ds=(e*(dp-dd_ref[h:h+1,qs])).astype(jnp.bfloat16)
                eb=e.astype(jnp.bfloat16)
                if NT:
                    nt=(((1,),(1,)),((),()))
                    dv[hs,ks]+=lax.dot_general(doT_ref[hs,qs],eb,nt,preferred_element_type=jnp.float32)
                    dk[hs,ks]+=lax.dot_general(qT_ref[hs,qs],ds,nt,preferred_element_type=jnp.float32)
                else:
                    parts.append((jnp.dot(eb,do_ref[qs,ps],preferred_element_type=jnp.float32),
                              jnp.dot(ds,q_ref[qs,ps],preferred_element_type=jnp.float32)))
                dq_out[hs,qs]+=jnp.dot(kT[hs,ks],ds,preferred_element_type=jnp.float32)
            if not NT:
                dv[ks,ps]+=jnp.where(lane<HD,parts[0][0],parts[1][0])
                dk[ks,ps]+=jnp.where(lane<HD,parts[0][1],parts[1][1])
    for qb in range(nq):
        for kb in range(nk):
            if diag and kb*BK>qb*BQ+BQ-1: continue
            vis=lo_sm[qb]<=kb*BK+BK-1
            if diag and (kb+1)*BK>qb*BQ+1:
                pl.when(vis)(functools.partial(block,qb,kb,True))
            else:
                full=lo_sm[nq+qb]<=kb*BK
                pl.when(full)(functools.partial(block,qb,kb,False))
                pl.when(jnp.logical_and(vis,jnp.logical_not(full)))(functools.partial(block,qb,kb,True))
    for p in range(heads//2):
        ps=slice(p*128,(p+1)*128)
        pv=slice(n+p*128,n+(p+1)*128)
        a,b=(dk[ps,:].T,dv[ps,:].T) if NT else (dk[:,ps],dv[:,ps])
        if first:
            dkv_out[:,ps]=a.astype(jnp.bfloat16); dkv_out[:,pv]=b.astype(jnp.bfloat16)
        else:
            dkv_out[:,ps]=(a+dkv_in[:,ps].astype(jnp.float32)).astype(jnp.bfloat16)
            dkv_out[:,pv]=(b+dkv_in[:,pv].astype(jnp.float32)).astype(jnp.bfloat16)

def bwd_step(w,nw,lo_sm,qT,q,doT,do,kv,lse,dd,lo,dq,dkv,NT=False):
    n,L=qT.shape; heads=n//HD
    BQ=min(256,L); BK=min(256,L)
    first=w==nw
    V=pl.BlockSpec(memory_space=pltpu.VMEM)
    outs=(jax.ShapeDtypeStruct((n,L),jnp.float32),jax.ShapeDtypeStruct((L,2*n),jnp.bfloat16))
    args=(lo_sm,qT,q,doT,do,kv,lse,dd,lo)+(() if first else (dq,dkv))
    return pl.pallas_call(
        functools.partial(bwd_kernel,NT,w==0,first,w==0,heads,L,BQ,BK),
        out_shape=outs,
        in_specs=[pl.BlockSpec(memory_space=pltpu.SMEM)]+[V]*(len(args)-1),
        out_specs=(V,V),
        scratch_shapes=[pltpu.VMEM((heads,128,L),jnp.bfloat16),pltpu.VMEM((heads,128,L),jnp.bfloat16),pltpu.VMEM((n,L),jnp.bfloat16)]
            +[pltpu.VMEM((n,L) if NT else (L,n),jnp.float32)]*2,
        compiler_params=pltpu.CompilerParams(vmem_limit_bytes=VL),
        cost_estimate=pl.CostEstimate(flops=10*L*L*n,bytes_accessed=8*L*n*4,transcendentals=heads*L*L),
        name="attn_bwd",
    )(*args)


EPS = 1e-05
MAXDOC = 1920
BF = jnp.bfloat16
F32 = jnp.float32
NT_DIMS = (((1,), (1,)), ((), ()))
VMEM_SPEC = pl.BlockSpec(memory_space=pltpu.VMEM)
ANY_SPEC = pl.BlockSpec(memory_space=pl.ANY)
GELU_C = 0.7978845608028654
GELU_A = 0.044715


def dot(left, right):
    return jnp.dot(left, right, preferred_element_type=F32)


def dot_nt(left, right):
    return lax.dot_general(left, right, NT_DIMS, preferred_element_type=F32)


def row_mean(values):
    return jnp.mean(values, -1, keepdims=True)


def col_sum(values):
    return jnp.sum(values, 0, keepdims=True)


def qkv_kernel(x_ref, w_ref, gain_ref, shift_ref, qb_ref, vb_ref, a_ref, q_ref, qT_ref, kv_ref):
    n = qb_ref.shape[1]
    x = x_ref[...].astype(F32)
    cen = x - row_mean(x)
    a = cen * lax.rsqrt(row_mean(cen * cen) + EPS) * gain_ref[...] + shift_ref[...]
    a = a.astype(BF)
    a_ref[...] = a
    q = (dot(a, w_ref[0]) + qb_ref[...]).astype(BF).astype(F32) * 0.125
    q = q.astype(BF)
    q_ref[...] = q
    for p in range(n // 128):
        ps = slice(p * 128, (p + 1) * 128)
        qT_ref[ps, :] = q[:, ps].T
    kv_ref[:, :n] = dot(a, w_ref[1]).astype(BF)
    kv_ref[:, n:] = (dot(a, w_ref[2]) + vb_ref[...]).astype(BF)


def qkv_call(x, w, gain, shift, qb, vb):
    rows, width = x.shape
    n = qb.shape[1]
    return pl.pallas_call(
        qkv_kernel,
        out_shape=(
            jax.ShapeDtypeStruct((rows, width), BF),
            jax.ShapeDtypeStruct((rows, n), BF),
            jax.ShapeDtypeStruct((n, rows), BF),
            jax.ShapeDtypeStruct((rows, 2 * n), BF),
        ),
        in_specs=[VMEM_SPEC] * 6,
        out_specs=(VMEM_SPEC,) * 4,
        compiler_params=pltpu.CompilerParams(vmem_limit_bytes=VL),
        cost_estimate=pl.CostEstimate(
            flops=6 * rows * width * n, bytes_accessed=rows * width * 8 + 6 * width * n, transcendentals=rows
        ),
        name="qkv",
    )(x, w, gain, shift, qb, vb)


def gelu_pair(h):
    inner = GELU_C * (h + GELU_A * h * h * h)
    t = jnp.tanh(inner)
    half = 0.5 * (1.0 + t)
    slope = half + 0.5 * h * (1.0 - t * t) * (GELU_C * (1.0 + (3.0 * GELU_A) * h * h))
    return h * half, slope


def ffn_kernel(
    step,
    c0_ref, c1_ref, delta_ref, x_ref, g_ref, fw_ref, hg_ref, hb_ref, vec_ref, fvec_ref,
    out_ref, g1_ref, dat_ref, o_ref, f_ref, z_ref, dh_ref, hsum_ref, dsum_ref, fsum_ref,
    fw, u_s, gp_s, e_s, sems,
):
    ff2 = z_ref.shape[1] // 2
    n = c0_ref.shape[1]
    copies = []
    for i, (lo, hi) in enumerate(((2 * ff2, 2 * ff2 + n), (0, ff2), (ff2, 2 * ff2))):
        cp = pltpu.make_async_copy(fw_ref.at[:, :, lo:hi], fw.at[:, :, lo:hi], sems.at[i])
        cp.start()
        copies.append(cp)
    ocols = slice(2 * ff2, 2 * ff2 + n)

    n0 = c0_ref[...].astype(F32) + delta_ref[...]
    n1 = c1_ref[...].astype(F32) - delta_ref[...]
    var = (jnp.sum(n0 * n0, -1, keepdims=True) + jnp.sum(n1 * n1, -1, keepdims=True)) / (2 * n)
    rs = lax.rsqrt(var + EPS)
    nh = (n0 * rs, n1 * rs)
    os = []
    for p in range(2):
        cs = slice(p * n, (p + 1) * n)
        o = (nh[p] * hg_ref[:, cs] + hb_ref[:, cs]).astype(BF)
        o_ref[:, cs] = o
        os.append(o)
    copies[0].wait()
    y1 = x_ref[...].astype(F32) + vec_ref[2:3, :]
    for p in range(2):
        y1 = y1 + dot_nt(os[p], fw[p, :, ocols])
    cen = y1 - row_mean(y1)
    r2 = lax.rsqrt(row_mean(cen * cen) + EPS)
    yh = cen * r2
    f = (yh * vec_ref[0:1, :] + vec_ref[1:2, :]).astype(BF)
    f_ref[...] = f
    copies[1].wait()
    usum = 0.0
    chunks = [(p, j) for p in range(2) for j in range(0, ff2, step)]
    for p, j in chunks:
        cs = slice(p * ff2 + j, p * ff2 + j + step)
        h = dot(f, fw[p, :, j : j + step]) + fvec_ref[0:1, cs]
        u, slope = gelu_pair(h)
        u_s[:, cs] = u
        gp_s[:, cs] = slope
        usum = usum + jnp.sum(u, -1, keepdims=True)
    mu = usum / (2 * ff2)
    ssum = 0.0
    for p, j in chunks:
        cs = slice(p * ff2 + j, p * ff2 + j + step)
        d = u_s[:, cs] - mu
        ssum = ssum + jnp.sum(d * d, -1, keepdims=True)
    ru = lax.rsqrt(ssum / (2 * ff2) + EPS)
    copies[2].wait()
    g2 = g_ref[...]
    y2 = y1 + vec_ref[3:4, :]
    esum = 0.0
    ezsum = 0.0
    for p, j in chunks:
        cs = slice(p * ff2 + j, p * ff2 + j + step)
        w2 = fw[p, :, ff2 + j : ff2 + j + step]
        zh = (u_s[:, cs] - mu) * ru
        u_s[:, cs] = zh
        z = (zh * fvec_ref[1:2, cs] + fvec_ref[2:3, cs]).astype(BF)
        z_ref[:, cs] = z
        y2 = y2 + dot_nt(z, w2)
        dz = dot(g2, w2)
        fsum_ref[1:2, cs] = col_sum(dz * zh)
        fsum_ref[2:3, cs] = col_sum(dz)
        e = dz * fvec_ref[1:2, cs]
        e_s[:, cs] = e
        esum = esum + jnp.sum(e, -1, keepdims=True)
        ezsum = ezsum + jnp.sum(e * zh, -1, keepdims=True)
    out_ref[...] = y2.astype(BF)
    em = esum / (2 * ff2)
    ezm = ezsum / (2 * ff2)
    df = jnp.zeros_like(y1)
    for p, j in chunks:
        cs = slice(p * ff2 + j, p * ff2 + j + step)
        du = ru * (e_s[:, cs] - em - u_s[:, cs] * ezm)
        dh = (du * gp_s[:, cs]).astype(BF)
        dh_ref[:, cs] = dh
        fsum_ref[0:1, cs] = col_sum(dh.astype(F32))
        df = df + dot_nt(dh, fw[p, :, j : j + step])
    dsum_ref[0:1, :] = col_sum(df * yh)
    dsum_ref[1:2, :] = col_sum(df)
    e2 = df * vec_ref[0:1, :]
    g = g2.astype(F32)
    dy1 = g + r2 * (e2 - row_mean(e2) - yh * row_mean(e2 * yh))
    g1 = dy1.astype(BF)
    g1_ref[...] = g1
    dsum_ref[2:3, :] = col_sum(g1.astype(F32))
    dsum_ref[3:4, :] = col_sum(g)
    es = []
    for p in range(2):
        cs = slice(p * n, (p + 1) * n)
        dsub = dot(g1, fw[p, :, ocols])
        hsum_ref[0:1, cs] = col_sum(dsub * nh[p])
        hsum_ref[1:2, cs] = col_sum(dsub)
        es.append(dsub * hg_ref[:, cs])
    em = sum(jnp.sum(e, -1, keepdims=True) for e in es) / (2 * n)
    ezm = sum(jnp.sum(e * h, -1, keepdims=True) for e, h in zip(es, nh)) / (2 * n)
    for p in range(2):
        cs = slice(p * n, (p + 1) * n)
        dat_ref[:, cs] = (rs * (es[p] - em - nh[p] * ezm)).astype(BF)


def ffn_call(c0, c1, delta, x, g, fw, hg, hb, vec, fvec):
    rows, n = c0.shape
    width = x.shape[1]
    ff = fvec.shape[1]
    step = 512
    sds = jax.ShapeDtypeStruct
    return pl.pallas_call(
        functools.partial(ffn_kernel, step),
        out_shape=(
            sds((rows, width), BF),
            sds((rows, width), BF),
            sds((rows, 2 * n), BF),
            sds((rows, 2 * n), BF),
            sds((rows, width), BF),
            sds((rows, ff), BF),
            sds((rows, ff), BF),
            sds((2, 2 * n), F32),
            sds((4, width), F32),
            sds((3, ff), F32),
        ),
        in_specs=[VMEM_SPEC] * 5 + [ANY_SPEC] + [VMEM_SPEC] * 4,
        out_specs=(VMEM_SPEC,) * 10,
        scratch_shapes=[
            pltpu.VMEM(fw.shape, BF),
            pltpu.VMEM((rows, ff), F32),
            pltpu.VMEM((rows, ff), F32),
            pltpu.VMEM((rows, ff), F32),
            pltpu.SemaphoreType.DMA((3,)),
        ],
        compiler_params=pltpu.CompilerParams(vmem_limit_bytes=VL),
        cost_estimate=pl.CostEstimate(
            flops=2 * rows * fw.size * 2, bytes_accessed=2 * fw.size, transcendentals=rows * ff
        ),
        name="ffn",
    )(c0, c1, delta, x, g, fw, hg, hb, vec, fvec)


def tail_kernel(own_ref, peer_ref, x_ref, g1_ref, gain_ref, out_ref, sum_ref):
    da = own_ref[...].astype(F32) + peer_ref[...].astype(F32)
    x = x_ref[...].astype(F32)
    cen = x - row_mean(x)
    r = lax.rsqrt(row_mean(cen * cen) + EPS)
    xh = cen * r
    sum_ref[0:1, :] = col_sum(da * xh)
    sum_ref[1:2, :] = col_sum(da)
    e = da * gain_ref[...]
    dx = r * (e - row_mean(e) - xh * row_mean(e * xh))
    out_ref[...] = (g1_ref[...].astype(F32) + dx).astype(BF)


def tail_call(own, peer, x, g1, gain):
    rows, width = x.shape
    return pl.pallas_call(
        tail_kernel,
        out_shape=(jax.ShapeDtypeStruct((rows, width), BF), jax.ShapeDtypeStruct((2, width), F32)),
        in_specs=[VMEM_SPEC] * 5,
        out_specs=(VMEM_SPEC, VMEM_SPEC),
        compiler_params=pltpu.CompilerParams(vmem_limit_bytes=VL),
        cost_estimate=pl.CostEstimate(
            flops=20 * rows * width, bytes_accessed=10 * rows * width, transcendentals=rows
        ),
        name="tail",
    )(own, peer, x, g1, gain)


def swap(value, axis):
    return lax.ppermute(value, axis, [(0, 1), (1, 0)])


def hop(value, bit):
    size = lax.axis_size("ctx")
    return lax.ppermute(value, "ctx", [(i, i ^ bit) for i in range(size)])


def shift(value, by):
    size = lax.axis_size("ctx")
    return lax.ppermute(value, "ctx", [(i, i + by) for i in range(size) if 0 <= i + by < size])


def ordered(own, peer, index, axis):
    first = jnp.where(index == 0, own, peer)
    second = jnp.where(index == 0, peer, own)
    return jnp.concatenate([first, second], axis)


def put(whole, piece, *start):
    return lax.dynamic_update_slice(whole, piece, start)


def gather_qkv(w, fast, s, c):
    if not fast:
        return lax.all_gather(w, "shard", axis=1, tiled=True)
    k, rows, cols = w.shape
    half = rows // 2
    mine = lax.dynamic_slice_in_dim(w, c * half, half, 1)
    far = swap(mine, "shard")
    rest = hop(far, 1)
    full = jnp.zeros((k, 2 * rows, cols), w.dtype)
    full = put(full, w, 0, s * rows, 0)
    full = put(full, far, 0, (1 - s) * rows + c * half, 0)
    return put(full, rest, 0, (1 - s) * rows + (1 - c) * half, 0)


def gather_ffn(w, fast, s, c, t):
    if not fast:
        w = lax.all_gather(w, "shard", axis=0, tiled=True)
        return lax.all_gather(w, "tp", axis=0)
    rows, cols = w.shape
    half = rows // 2
    mine = lax.dynamic_slice_in_dim(w, c * half, half, 0)
    near = swap(mine, "tp")
    far = swap(mine, "shard")
    both = swap(far, "tp")
    full = jnp.zeros((2, 2 * rows, cols), w.dtype)
    full = put(full, w[None], t, s * rows, 0)
    for piece, ti, si in ((far, t, 1 - s), (near, 1 - t, s), (both, 1 - t, 1 - s)):
        full = put(full, piece[None], ti, si * rows + c * half, 0)
        full = put(full, hop(piece, 1)[None], ti, si * rows + (1 - c) * half, 0)
    return full


def take(value, index, axis):
    return lax.dynamic_index_in_dim(value, index, axis, keepdims=False)


def scatter_rows(grad, fast, s, z, c, t=None):
    width, cols = grad.shape
    if not fast:
        if t is not None:
            grad = lax.psum_scatter(grad.reshape(width, 2, cols // 2), "tp", scatter_dimension=1, tiled=False)
        return lax.psum_scatter(grad.astype(F32), ("shard", "ctx"), scatter_dimension=0, tiled=True)
    nz = lax.axis_size("ctx") // 2
    part = grad.astype(BF).reshape(2, nz, 2, width // (4 * nz), cols)

    def fold(value, index, axis, send):
        got = send(take(value, 1 - index, axis))
        return (take(value, index, axis).astype(F32) + got.astype(F32)).astype(BF)

    part = fold(part, c, 2, lambda v: hop(v, 1))
    if t is not None:
        part = part.reshape(part.shape[:-1] + (2, cols // 2))
        part = fold(part, t, part.ndim - 2, lambda v: swap(v, "tp"))
    part = fold(part, s, 0, lambda v: swap(v, "shard"))
    bit = nz // 2
    while bit:
        part = part.reshape((2, bit) + part.shape[-2:])
        part = fold(part, (z // bit) % 2, 0, lambda v, b=2 * bit: hop(v, b))
        bit //= 2
    return part.reshape(part.shape[-2:]).astype(F32)


def per_device(
    tokens,
    cotangent,
    segment_ids,
    w_qkv,
    w_out,
    w_fc1,
    w_fc2,
    norm_gain,
    norm_bias,
    head_gain,
    head_bias,
    ffn_gain,
    ffn_bias,
):
    seqs, length, width = tokens.shape
    n = w_qkv.shape[2]
    heads = n // HD
    ff2 = w_fc1.shape[1]
    half = length // 2
    s, r, t = lax.axis_index("shard"), lax.axis_index("ctx"), lax.axis_index("tp")
    c, z = r % 2, r // 2
    fast = lax.axis_size("shard") == 2
    nw = min(-(-(MAXDOC - 1) // length), lax.axis_size("ctx") - 1)

    wqkv = gather_qkv(w_qkv.astype(BF), fast, s, c)
    small = jnp.concatenate([norm_gain, norm_bias]).astype(BF)
    if fast:
        small = ordered(small, swap(small, "shard"), s, 1)
    else:
        small = lax.all_gather(small, "shard", axis=1, tiled=True)
    small = small.astype(F32)
    gains, biases = small[:2], small[2:]
    vectors = jnp.concatenate([ffn_bias[0], ffn_gain, ffn_bias[1], head_gain, head_bias[2]])
    far = swap(vectors, "tp")
    v0, v1 = jnp.where(t == 0, vectors, far), jnp.where(t == 0, far, vectors)
    fvec = jnp.concatenate([v0[: 3 * ff2].reshape(3, ff2), v1[: 3 * ff2].reshape(3, ff2)], 1)
    hvec = jnp.concatenate([v0[3 * ff2 :].reshape(2, n), v1[3 * ff2 :].reshape(2, n)], 1)
    hg, hb = hvec[:1], hvec[1:]
    pack = jnp.concatenate([w_fc1.astype(BF), w_fc2.astype(BF).T, w_out.astype(BF).T], 1)
    fw = gather_ffn(pack, fast, s, c, t)
    vec = jnp.stack([gains[1], biases[1], biases[2], biases[3]])

    below = jnp.sum(segment_ids[:, None, :] < jnp.arange(1, 4, dtype=jnp.int32)[None, :, None], -1, dtype=jnp.int32)
    seg_q = lax.dynamic_slice_in_dim(segment_ids, r * length, length, 1)
    start = jnp.zeros_like(seg_q)
    for v in range(1, 4):
        start = jnp.where(seg_q == v, below[:, v - 1 : v], start)
    block = min(256, length)

    def bounds(b, w):
        lo = start[b] + (w - r) * length
        return jnp.concatenate([lo[::block], lo[block - 1 :: block]]), lo[None]

    acts, qs, qTs, rings, states = [], [], [], [], []
    for b in range(seqs):
        a, q, qT, kv = qkv_call(tokens[b], wqkv, gains[:1], biases[:1], head_bias[:1], head_bias[1:2])
        acts.append(a)
        qs.append(q)
        qTs.append(qT)
        rings.append([kv])
        states.append(None)
    for w in range(nw):
        for b in range(seqs):
            rings[b].append(shift(rings[b][w], 1))
    for w in range(nw + 1):
        for b in range(seqs):
            sm, lo = bounds(b, w)
            states[b] = fwd_step(w, nw, sm, qTs[b], rings[b][w], lo, states[b])

    def own_rows(value, index):
        return lax.dynamic_slice_in_dim(value, index * half, half, 0)

    outs, g1s, dos, mids = [], [], [], []
    for b in range(seqs):
        cen, oT, lse, mean = states[b]
        own, peer = own_rows(cen, t), swap(own_rows(cen, 1 - t), "tp")
        mrow = mean.reshape(length, 1)
        mown, mpeer = own_rows(mrow, t), swap(own_rows(mean[0], 1 - t), "tp").reshape(half, 1)
        first = t == 0
        c0, c1 = jnp.where(first, own, peer), jnp.where(first, peer, own)
        delta = jnp.where(first, mown - mpeer, mpeer - mown) * 0.5
        x, g = own_rows(tokens[b], t), own_rows(cotangent[b], t)
        mid = ffn_call(c0, c1, delta, x, g, fw, hg, hb, vec, fvec)
        out, g1, dat = mid[:3]
        mids.append(mid[3:] + (g, g1))
        mine = lax.dynamic_slice_in_dim(dat, t * n, n, 1)
        theirs = lax.dynamic_slice_in_dim(dat, (1 - t) * n, n, 1)
        dos.append(ordered(mine, swap(theirs, "tp"), t, 0))
        outs.append(ordered(out, swap(out, "tp"), t, 0))
        g1s.append(ordered(g1, swap(g1, "tp"), t, 0))

    prep, dqs, dkvs = [], [None] * seqs, [None] * seqs
    for b in range(seqs):
        cen, oT, lse, mean = states[b]
        doT = dos[b].T
        dd = jnp.sum(doT.reshape(heads, HD, length).astype(F32) * oT.reshape(heads, HD, length), 1)
        dd = jnp.concatenate([dd, jnp.zeros((8 - heads, length), F32)])
        prep.append((doT, dd))
    for w in range(nw, -1, -1):
        for b in range(seqs):
            sm, lo = bounds(b, w)
            doT, dd = prep[b]
            dqs[b], dkvs[b] = bwd_step(
                w, nw, sm, qTs[b], qs[b], doT, dos[b], rings[b][w], states[b][2], dd, lo, dqs[b], dkvs[b]
            )
            if w:
                dkvs[b] = shift(dkvs[b], -1)

    def rows_of(i):
        return jnp.concatenate([mids[b][i] for b in range(seqs)])

    def outer(left, right):
        return lax.dot_general(left, right, (((0,), (0,)), ((), ())), preferred_element_type=F32).astype(BF)

    o_all, f_all, z_all, dh_all, g_all, g1_all = (rows_of(i) for i in (0, 1, 2, 3, 7, 8))
    grad_down = scatter_rows(outer(g_all, z_all), fast, s, z, c, t).T
    grad_up = scatter_rows(outer(f_all, dh_all), fast, s, z, c, t)
    grad_out = scatter_rows(outer(g1_all, o_all), fast, s, z, c, t).T
    hsum, dsum, fsum = (sum(mids[b][i] for b in range(seqs)) for i in (4, 5, 6))
    mid_sums = lax.psum(
        jnp.concatenate([hsum.reshape(-1), dsum.reshape(-1), fsum.reshape(-1)]), ("shard", "ctx", "tp")
    )
    hsum = mid_sums[: hsum.size].reshape(hsum.shape)
    fsum = mid_sums[hsum.size + dsum.size :].reshape(fsum.shape)
    dsum = mid_sums[hsum.size : hsum.size + dsum.size].reshape(dsum.shape)

    grad_tokens, in_sums, projs = [], 0.0, []
    for b in range(seqs):
        dq = (dqs[b].T * 0.125).astype(BF)
        proj = jnp.concatenate([dq, dkvs[b]], 1)
        projs.append(proj)
        da = sum(dot_nt(proj[:, i * n : (i + 1) * n], wqkv[i]) for i in range(3)).astype(BF)
        gt, sums = tail_call(da, swap(da, "tp"), tokens[b], g1s[b], gains[:1])
        grad_tokens.append(gt)
        in_sums = in_sums + sums
    proj = jnp.concatenate(projs)
    grad_qkv = scatter_rows(outer(jnp.concatenate(acts), proj), fast, s, z, c)
    grad_qkv = grad_qkv.reshape(-1, 3, n).transpose(1, 0, 2)
    bias_sums = jnp.sum(proj.astype(F32), 0)
    tail_sums = lax.psum(jnp.concatenate([in_sums.reshape(-1), bias_sums]), ("shard", "ctx"))
    in_sums = tail_sums[: 2 * width].reshape(2, width)
    bias_sums = tail_sums[2 * width :]

    piece = width // (lax.axis_size("shard") * lax.axis_size("ctx"))
    mine = (s * lax.axis_size("ctx") + r) * piece
    grad_gain = lax.dynamic_slice_in_dim(jnp.stack([in_sums[0], dsum[0]]), mine, piece, 1)
    grad_bias = lax.dynamic_slice_in_dim(jnp.stack([in_sums[1], dsum[1], dsum[2], dsum[3]]), mine, piece, 1)
    hsum = lax.dynamic_slice_in_dim(hsum, t * n, n, 1)
    fsum = lax.dynamic_slice_in_dim(fsum, t * ff2, ff2, 1)
    return (
        jnp.stack(outs),
        jnp.stack(grad_tokens),
        grad_qkv,
        grad_out,
        grad_up,
        grad_down,
        grad_gain,
        grad_bias,
        hsum[0],
        jnp.stack([bias_sums[:n], bias_sums[2 * n :], hsum[1]]),
        fsum[1],
        jnp.stack([fsum[0], fsum[2]]),
    )


def solution(mesh):
    in_specs = (
        P("shard", "ctx", None),
        P("shard", "ctx", None),
        P("shard", None),
        P(None, "shard", "tp"),
        P("tp", "shard"),
        P("shard", "tp"),
        P("tp", "shard"),
        P(None, "shard"),
        P(None, "shard"),
        P("tp"),
        P(None, "tp"),
        P("tp"),
        P(None, "tp"),
    )
    out_specs = (
        P("shard", "ctx", None),
        P("shard", "ctx", None),
        P(None, ("shard", "ctx"), "tp"),
        P("tp", ("shard", "ctx")),
        P(("shard", "ctx"), "tp"),
        P("tp", ("shard", "ctx")),
        P(None, ("shard", "ctx")),
        P(None, ("shard", "ctx")),
        P("tp"),
        P(None, "tp"),
        P("tp"),
        P(None, "tp"),
    )
    return jax.shard_map(
        per_device, mesh=mesh, in_specs=in_specs, out_specs=out_specs, check_vma=False
    )
```

```python
import functools
import jax
import jax.numpy as jnp
from jax import lax
from jax.experimental import pallas as pl
from jax.experimental.pallas import tpu as pltpu
from jax.sharding import PartitionSpec as P
HD=64
NEG=-1e30
VL=48*1024*1024

def fwd_kernel(diag,first,last,heads,L,BQ,BK, lo_sm, qT_ref,kv_ref,lo_ref,*rest):
    n=heads*HD
    if first:
        ins=(); rest=rest
    else:
        m_in,l_in,a_in=rest[:3]; rest=rest[3:]
    if last:
        c_ref,oT_ref,lse_ref,mean_ref=rest[:4]; rest=rest[4:]
    else:
        m_out,l_out,a_out=rest[:3]; rest=rest[3:]
    m_s,l_s,acc,qm,vT=rest
    if first:
        m_s[...]=jnp.full_like(m_s,NEG); l_s[...]=jnp.zeros_like(l_s); acc[...]=jnp.zeros_like(acc)
    else:
        m_s[...]=m_in[...]; l_s[...]=l_in[...]; acc[...]=a_in[...]
    nq,nk=L//BQ,L//BK
    rowi=lax.broadcasted_iota(jnp.int32,(2*HD,L),0)
    for p in range(heads//2):
        blk=qT_ref[p*128:(p+1)*128,:]
        qm[2*p]=jnp.where(rowi<HD,blk,jnp.zeros_like(blk))
        qm[2*p+1]=jnp.where(rowi>=HD,blk,jnp.zeros_like(blk))
        vT[p*128:(p+1)*128,:]=kv_ref[:,n+p*128:n+(p+1)*128].T
    def block(qb,kb,masked):
        qs=slice(qb*BQ,(qb+1)*BQ); ks=slice(kb*BK,(kb+1)*BK)
        if masked:
            kk=lax.broadcasted_iota(jnp.int32,(BK,BQ),0)+kb*BK
            valid=kk>=lo_ref[:,qs]
            if diag and (kb+1)*BK>qb*BQ+1:
                valid=valid&(kk<=lax.broadcasted_iota(jnp.int32,(BK,BQ),1)+qb*BQ)
        for h in range(heads):
            p=h//2
            s=jnp.dot(kv_ref[ks,p*128:(p+1)*128],qm[h,:,qs],preferred_element_type=jnp.float32)
            if masked: s=jnp.where(valid,s,NEG)
            mo=m_s[h:h+1,qs]
            mn=jnp.maximum(mo,jnp.max(s,0,keepdims=True))
            e=jnp.exp(s-mn); al=jnp.exp(mo-mn)
            m_s[h:h+1,qs]=mn
            l_s[h:h+1,qs]=l_s[h:h+1,qs]*al+jnp.sum(e,0,keepdims=True)
            hs=slice(h*HD,(h+1)*HD)
            acc[hs,qs]=acc[hs,qs]*al+jnp.dot(vT[hs,ks],e.astype(jnp.bfloat16),preferred_element_type=jnp.float32)
    for qb in range(nq):
        for kb in range(nk):
            if diag and kb*BK>qb*BQ+BQ-1: continue
            vis=lo_sm[qb]<=kb*BK+BK-1
            if diag and (kb+1)*BK>qb*BQ+1:
                pl.when(vis)(functools.partial(block,qb,kb,True))
            else:
                full=lo_sm[nq+qb]<=kb*BK
                pl.when(full)(functools.partial(block,qb,kb,False))
                pl.when(jnp.logical_and(vis,jnp.logical_not(full)))(functools.partial(block,qb,kb,True))
    if last:
        tot=jnp.zeros((1,L),jnp.float32)
        for h in range(heads):
            hs=slice(h*HD,(h+1)*HD)
            o=acc[hs,:]/l_s[h:h+1,:]
            oT_ref[hs,:]=o
            tot=tot+jnp.sum(o,0,keepdims=True)
        mean=tot/n
        mean_ref[...]=mean
        lse_ref[...]=m_s[...]+jnp.log(l_s[...])
        for p in range(heads//2):
            c_ref[:,p*128:(p+1)*128]=(oT_ref[p*128:(p+1)*128,:]-mean).T.astype(jnp.bfloat16)
    else:
        m_out[...]=m_s[...]; l_out[...]=l_s[...]; a_out[...]=acc[...]

def fwd_step(w,nw,lo_sm,qT,kv,lo,state):
    n,L=qT.shape; heads=n//HD
    BQ=min(256,L); BK=min(256,L)
    first=w==0; last=w==nw
    V=pl.BlockSpec(memory_space=pltpu.VMEM)
    st=(jax.ShapeDtypeStruct((8,L),jnp.float32),jax.ShapeDtypeStruct((8,L),jnp.float32),jax.ShapeDtypeStruct((n,L),jnp.float32))
    outs=st if not last else (jax.ShapeDtypeStruct((L,n),jnp.bfloat16),st[2],st[0],jax.ShapeDtypeStruct((1,L),jnp.float32))
    args=(lo_sm,qT,kv,lo)+(() if first else tuple(state))
    return pl.pallas_call(
        functools.partial(fwd_kernel,w==0,first,last,heads,L,BQ,BK),
        out_shape=outs,
        in_specs=[pl.BlockSpec(memory_space=pltpu.SMEM)]+[V]*(len(args)-1),
        out_specs=tuple([V]*len(outs)),
        scratch_shapes=[pltpu.VMEM((8,L),jnp.float32),pltpu.VMEM((8,L),jnp.float32),pltpu.VMEM((n,L),jnp.float32),
            pltpu.VMEM((heads,128,L),jnp.bfloat16),pltpu.VMEM((n,L),jnp.bfloat16)],
        compiler_params=pltpu.CompilerParams(vmem_limit_bytes=VL),
        cost_estimate=pl.CostEstimate(flops=4*L*L*n,bytes_accessed=4*L*n*4,transcendentals=heads*L*L),
        name="attn_fwd",
    )(*args)

def bwd_kernel(NT,diag,first,last,heads,L,BQ,BK,lo_sm,qT_ref,q_ref,doT_ref,do_ref,kv_ref,lse_ref,dd_ref,lo_ref,*rest):
    n=heads*HD
    if first:
        pass
    else:
        dq_in,dkv_in=rest[:2]; rest=rest[2:]
    dq_out,dkv_out=rest[:2]; rest=rest[2:]
    qm,dm,kT,dk,dv=rest
    if first: dq_out[...]=jnp.zeros_like(dq_out)
    else: dq_out[...]=dq_in[...]
    dk[...]=jnp.zeros_like(dk); dv[...]=jnp.zeros_like(dv)
    nq,nk=L//BQ,L//BK
    rowi=lax.broadcasted_iota(jnp.int32,(2*HD,L),0)
    for p in range(heads//2):
        ps=slice(p*128,(p+1)*128)
        for ref,dst in ((qT_ref,qm),(doT_ref,dm)):
            blk=ref[ps,:]
            dst[2*p]=jnp.where(rowi<HD,blk,jnp.zeros_like(blk))
            dst[2*p+1]=jnp.where(rowi>=HD,blk,jnp.zeros_like(blk))
        kT[ps,:]=kv_ref[:,ps].T
    lane=lax.broadcasted_iota(jnp.int32,(BK,128),1)
    def block(qb,kb,masked):
        qs=slice(qb*BQ,(qb+1)*BQ); ks=slice(kb*BK,(kb+1)*BK)
        if masked:
            kk=lax.broadcasted_iota(jnp.int32,(BK,BQ),0)+kb*BK
            valid=kk>=lo_ref[:,qs]
            if diag and (kb+1)*BK>qb*BQ+1:
                valid=valid&(kk<=lax.broadcasted_iota(jnp.int32,(BK,BQ),1)+qb*BQ)
        for p in range(heads//2):
            ps=slice(p*128,(p+1)*128)
            pv=slice(n+p*128,n+(p+1)*128)
            parts=[]
            for h in (2*p,2*p+1):
                hs=slice(h*HD,(h+1)*HD)
                s=jnp.dot(kv_ref[ks,ps],qm[h,:,qs],preferred_element_type=jnp.float32)
                dp=jnp.dot(kv_ref[ks,pv],dm[h,:,qs],preferred_element_type=jnp.float32)
                if masked: s=jnp.where(valid,s,NEG)
                e=jnp.exp(s-lse_ref[h:h+1,qs])
                ds=(e*(dp-dd_ref[h:h+1,qs])).astype(jnp.bfloat16)
                eb=e.astype(jnp.bfloat16)
                if NT:
                    nt=(((1,),(1,)),((),()))
                    dv[hs,ks]+=lax.dot_general(doT_ref[hs,qs],eb,nt,preferred_element_type=jnp.float32)
                    dk[hs,ks]+=lax.dot_general(qT_ref[hs,qs],ds,nt,preferred_element_type=jnp.float32)
                else:
                    parts.append((jnp.dot(eb,do_ref[qs,ps],preferred_element_type=jnp.float32),
                              jnp.dot(ds,q_ref[qs,ps],preferred_element_type=jnp.float32)))
                dq_out[hs,qs]+=jnp.dot(kT[hs,ks],ds,preferred_element_type=jnp.float32)
            if not NT:
                dv[ks,ps]+=jnp.where(lane<HD,parts[0][0],parts[1][0])
                dk[ks,ps]+=jnp.where(lane<HD,parts[0][1],parts[1][1])
    for qb in range(nq):
        for kb in range(nk):
            if diag and kb*BK>qb*BQ+BQ-1: continue
            vis=lo_sm[qb]<=kb*BK+BK-1
            if diag and (kb+1)*BK>qb*BQ+1:
                pl.when(vis)(functools.partial(block,qb,kb,True))
            else:
                full=lo_sm[nq+qb]<=kb*BK
                pl.when(full)(functools.partial(block,qb,kb,False))
                pl.when(jnp.logical_and(vis,jnp.logical_not(full)))(functools.partial(block,qb,kb,True))
    for p in range(heads//2):
        ps=slice(p*128,(p+1)*128)
        pv=slice(n+p*128,n+(p+1)*128)
        a,b=(dk[ps,:].T,dv[ps,:].T) if NT else (dk[:,ps],dv[:,ps])
        if first:
            dkv_out[:,ps]=a.astype(jnp.bfloat16); dkv_out[:,pv]=b.astype(jnp.bfloat16)
        else:
            dkv_out[:,ps]=(a+dkv_in[:,ps].astype(jnp.float32)).astype(jnp.bfloat16)
            dkv_out[:,pv]=(b+dkv_in[:,pv].astype(jnp.float32)).astype(jnp.bfloat16)

def bwd_step(w,nw,lo_sm,qT,q,doT,do,kv,lse,dd,lo,dq,dkv,NT=False):
    n,L=qT.shape; heads=n//HD
    BQ=min(256,L); BK=min(256,L)
    first=w==nw
    V=pl.BlockSpec(memory_space=pltpu.VMEM)
    outs=(jax.ShapeDtypeStruct((n,L),jnp.float32),jax.ShapeDtypeStruct((L,2*n),jnp.bfloat16))
    args=(lo_sm,qT,q,doT,do,kv,lse,dd,lo)+(() if first else (dq,dkv))
    return pl.pallas_call(
        functools.partial(bwd_kernel,NT,w==0,first,w==0,heads,L,BQ,BK),
        out_shape=outs,
        in_specs=[pl.BlockSpec(memory_space=pltpu.SMEM)]+[V]*(len(args)-1),
        out_specs=(V,V),
        scratch_shapes=[pltpu.VMEM((heads,128,L),jnp.bfloat16),pltpu.VMEM((heads,128,L),jnp.bfloat16),pltpu.VMEM((n,L),jnp.bfloat16)]
            +[pltpu.VMEM((n,L) if NT else (L,n),jnp.float32)]*2,
        compiler_params=pltpu.CompilerParams(vmem_limit_bytes=VL),
        cost_estimate=pl.CostEstimate(flops=10*L*L*n,bytes_accessed=8*L*n*4,transcendentals=heads*L*L),
        name="attn_bwd",
    )(*args)


EPS = 1e-05
MAXDOC = 1920
BF = jnp.bfloat16
F32 = jnp.float32
NT_DIMS = (((1,), (1,)), ((), ()))
VMEM_SPEC = pl.BlockSpec(memory_space=pltpu.VMEM)
ANY_SPEC = pl.BlockSpec(memory_space=pl.ANY)
GELU_C = 0.7978845608028654
GELU_A = 0.044715


def dot(left, right):
    return jnp.dot(left, right, preferred_element_type=F32)


def dot_nt(left, right):
    return lax.dot_general(left, right, NT_DIMS, preferred_element_type=F32)


def row_mean(values):
    return jnp.mean(values, -1, keepdims=True)


def col_sum(values):
    return jnp.sum(values, 0, keepdims=True)


def qkv_kernel(x_ref, w_ref, gain_ref, shift_ref, qb_ref, vb_ref, a_ref, q_ref, qT_ref, kv_ref):
    n = qb_ref.shape[1]
    x = x_ref[...].astype(F32)
    cen = x - row_mean(x)
    a = cen * lax.rsqrt(row_mean(cen * cen) + EPS) * gain_ref[...] + shift_ref[...]
    a = a.astype(BF)
    a_ref[...] = a
    q = (dot(a, w_ref[0]) + qb_ref[...]).astype(BF).astype(F32) * 0.125
    q = q.astype(BF)
    q_ref[...] = q
    for p in range(n // 128):
        ps = slice(p * 128, (p + 1) * 128)
        qT_ref[ps, :] = q[:, ps].T
    kv_ref[:, :n] = dot(a, w_ref[1]).astype(BF)
    kv_ref[:, n:] = (dot(a, w_ref[2]) + vb_ref[...]).astype(BF)


def qkv_call(x, w, gain, shift, qb, vb):
    rows, width = x.shape
    n = qb.shape[1]
    return pl.pallas_call(
        qkv_kernel,
        out_shape=(
            jax.ShapeDtypeStruct((rows, width), BF),
            jax.ShapeDtypeStruct((rows, n), BF),
            jax.ShapeDtypeStruct((n, rows), BF),
            jax.ShapeDtypeStruct((rows, 2 * n), BF),
        ),
        in_specs=[VMEM_SPEC] * 6,
        out_specs=(VMEM_SPEC,) * 4,
        compiler_params=pltpu.CompilerParams(vmem_limit_bytes=VL),
        cost_estimate=pl.CostEstimate(
            flops=6 * rows * width * n, bytes_accessed=rows * width * 8 + 6 * width * n, transcendentals=rows
        ),
        name="qkv",
    )(x, w, gain, shift, qb, vb)


def gelu_pair(h):
    inner = GELU_C * (h + GELU_A * h * h * h)
    t = jnp.tanh(inner)
    half = 0.5 * (1.0 + t)
    slope = half + 0.5 * h * (1.0 - t * t) * (GELU_C * (1.0 + (3.0 * GELU_A) * h * h))
    return h * half, slope


def ffn_kernel(
    step,
    c0_ref, c1_ref, delta_ref, x_ref, g_ref, fw_ref, hg_ref, hb_ref, vec_ref, fvec_ref,
    out_ref, g1_ref, dat_ref, o_ref, f_ref, z_ref, dh_ref, hsum_ref, dsum_ref, fsum_ref,
    fw, u_s, gp_s, e_s, sems,
):
    ff2 = z_ref.shape[1] // 2
    n = c0_ref.shape[1]
    copies = []
    for i, (lo, hi) in enumerate(((2 * ff2, 2 * ff2 + n), (0, ff2), (ff2, 2 * ff2))):
        cp = pltpu.make_async_copy(fw_ref.at[:, :, lo:hi], fw.at[:, :, lo:hi], sems.at[i])
        cp.start()
        copies.append(cp)
    ocols = slice(2 * ff2, 2 * ff2 + n)

    n0 = c0_ref[...].astype(F32) + delta_ref[...]
    n1 = c1_ref[...].astype(F32) - delta_ref[...]
    var = (jnp.sum(n0 * n0, -1, keepdims=True) + jnp.sum(n1 * n1, -1, keepdims=True)) / (2 * n)
    rs = lax.rsqrt(var + EPS)
    nh = (n0 * rs, n1 * rs)
    os = []
    for p in range(2):
        cs = slice(p * n, (p + 1) * n)
        o = (nh[p] * hg_ref[:, cs] + hb_ref[:, cs]).astype(BF)
        o_ref[:, cs] = o
        os.append(o)
    copies[0].wait()
    y1 = x_ref[...].astype(F32) + vec_ref[2:3, :]
    for p in range(2):
        y1 = y1 + dot_nt(os[p], fw[p, :, ocols])
    cen = y1 - row_mean(y1)
    r2 = lax.rsqrt(row_mean(cen * cen) + EPS)
    yh = cen * r2
    f = (yh * vec_ref[0:1, :] + vec_ref[1:2, :]).astype(BF)
    f_ref[...] = f
    copies[1].wait()
    usum = 0.0
    chunks = [(p, j) for p in range(2) for j in range(0, ff2, step)]
    for p, j in chunks:
        cs = slice(p * ff2 + j, p * ff2 + j + step)
        h = dot(f, fw[p, :, j : j + step]) + fvec_ref[0:1, cs]
        u, slope = gelu_pair(h)
        u_s[:, cs] = u
        gp_s[:, cs] = slope
        usum = usum + jnp.sum(u, -1, keepdims=True)
    mu = usum / (2 * ff2)
    ssum = 0.0
    for p, j in chunks:
        cs = slice(p * ff2 + j, p * ff2 + j + step)
        d = u_s[:, cs] - mu
        ssum = ssum + jnp.sum(d * d, -1, keepdims=True)
    ru = lax.rsqrt(ssum / (2 * ff2) + EPS)
    copies[2].wait()
    g2 = g_ref[...]
    y2 = y1 + vec_ref[3:4, :]
    esum = 0.0
    ezsum = 0.0
    for p, j in chunks:
        cs = slice(p * ff2 + j, p * ff2 + j + step)
        w2 = fw[p, :, ff2 + j : ff2 + j + step]
        zh = (u_s[:, cs] - mu) * ru
        u_s[:, cs] = zh
        z = (zh * fvec_ref[1:2, cs] + fvec_ref[2:3, cs]).astype(BF)
        z_ref[:, cs] = z
        y2 = y2 + dot_nt(z, w2)
        dz = dot(g2, w2)
        fsum_ref[1:2, cs] = col_sum(dz * zh)
        fsum_ref[2:3, cs] = col_sum(dz)
        e = dz * fvec_ref[1:2, cs]
        e_s[:, cs] = e
        esum = esum + jnp.sum(e, -1, keepdims=True)
        ezsum = ezsum + jnp.sum(e * zh, -1, keepdims=True)
    out_ref[...] = y2.astype(BF)
    em = esum / (2 * ff2)
    ezm = ezsum / (2 * ff2)
    df = jnp.zeros_like(y1)
    for p, j in chunks:
        cs = slice(p * ff2 + j, p * ff2 + j + step)
        du = ru * (e_s[:, cs] - em - u_s[:, cs] * ezm)
        dh = (du * gp_s[:, cs]).astype(BF)
        dh_ref[:, cs] = dh
        fsum_ref[0:1, cs] = col_sum(dh.astype(F32))
        df = df + dot_nt(dh, fw[p, :, j : j + step])
    dsum_ref[0:1, :] = col_sum(df * yh)
    dsum_ref[1:2, :] = col_sum(df)
    e2 = df * vec_ref[0:1, :]
    g = g2.astype(F32)
    dy1 = g + r2 * (e2 - row_mean(e2) - yh * row_mean(e2 * yh))
    g1 = dy1.astype(BF)
    g1_ref[...] = g1
    dsum_ref[2:3, :] = col_sum(g1.astype(F32))
    dsum_ref[3:4, :] = col_sum(g)
    es = []
    for p in range(2):
        cs = slice(p * n, (p + 1) * n)
        dsub = dot(g1, fw[p, :, ocols])
        hsum_ref[0:1, cs] = col_sum(dsub * nh[p])
        hsum_ref[1:2, cs] = col_sum(dsub)
        es.append(dsub * hg_ref[:, cs])
    em = sum(jnp.sum(e, -1, keepdims=True) for e in es) / (2 * n)
    ezm = sum(jnp.sum(e * h, -1, keepdims=True) for e, h in zip(es, nh)) / (2 * n)
    for p in range(2):
        cs = slice(p * n, (p + 1) * n)
        dat_ref[:, cs] = (rs * (es[p] - em - nh[p] * ezm)).astype(BF)


def ffn_call(c0, c1, delta, x, g, fw, hg, hb, vec, fvec):
    rows, n = c0.shape
    width = x.shape[1]
    ff = fvec.shape[1]
    step = 512
    sds = jax.ShapeDtypeStruct
    return pl.pallas_call(
        functools.partial(ffn_kernel, step),
        out_shape=(
            sds((rows, width), BF),
            sds((rows, width), BF),
            sds((rows, 2 * n), BF),
            sds((rows, 2 * n), BF),
            sds((rows, width), BF),
            sds((rows, ff), BF),
            sds((rows, ff), BF),
            sds((2, 2 * n), F32),
            sds((4, width), F32),
            sds((3, ff), F32),
        ),
        in_specs=[VMEM_SPEC] * 5 + [ANY_SPEC] + [VMEM_SPEC] * 4,
        out_specs=(VMEM_SPEC,) * 10,
        scratch_shapes=[
            pltpu.VMEM(fw.shape, BF),
            pltpu.VMEM((rows, ff), F32),
            pltpu.VMEM((rows, ff), F32),
            pltpu.VMEM((rows, ff), F32),
            pltpu.SemaphoreType.DMA((3,)),
        ],
        compiler_params=pltpu.CompilerParams(vmem_limit_bytes=VL),
        cost_estimate=pl.CostEstimate(
            flops=2 * rows * fw.size * 2, bytes_accessed=2 * fw.size, transcendentals=rows * ff
        ),
        name="ffn",
    )(c0, c1, delta, x, g, fw, hg, hb, vec, fvec)


def tail_kernel(own_ref, peer_ref, x_ref, g1_ref, gain_ref, out_ref, sum_ref):
    da = own_ref[...].astype(F32) + peer_ref[...].astype(F32)
    x = x_ref[...].astype(F32)
    cen = x - row_mean(x)
    r = lax.rsqrt(row_mean(cen * cen) + EPS)
    xh = cen * r
    sum_ref[0:1, :] = col_sum(da * xh)
    sum_ref[1:2, :] = col_sum(da)
    e = da * gain_ref[...]
    dx = r * (e - row_mean(e) - xh * row_mean(e * xh))
    out_ref[...] = (g1_ref[...].astype(F32) + dx).astype(BF)


def tail_call(own, peer, x, g1, gain):
    rows, width = x.shape
    return pl.pallas_call(
        tail_kernel,
        out_shape=(jax.ShapeDtypeStruct((rows, width), BF), jax.ShapeDtypeStruct((2, width), F32)),
        in_specs=[VMEM_SPEC] * 5,
        out_specs=(VMEM_SPEC, VMEM_SPEC),
        compiler_params=pltpu.CompilerParams(vmem_limit_bytes=VL),
        cost_estimate=pl.CostEstimate(
            flops=20 * rows * width, bytes_accessed=10 * rows * width, transcendentals=rows
        ),
        name="tail",
    )(own, peer, x, g1, gain)


def swap(value, axis):
    return lax.ppermute(value, axis, [(0, 1), (1, 0)])


def hop(value, bit):
    size = lax.axis_size("ctx")
    return lax.ppermute(value, "ctx", [(i, i ^ bit) for i in range(size)])


def shift(value, by):
    size = lax.axis_size("ctx")
    return lax.ppermute(value, "ctx", [(i, i + by) for i in range(size) if 0 <= i + by < size])


def ordered(own, peer, index, axis):
    first = jnp.where(index == 0, own, peer)
    second = jnp.where(index == 0, peer, own)
    return jnp.concatenate([first, second], axis)


def put(whole, piece, *start):
    return lax.dynamic_update_slice(whole, piece, start)


def gather_qkv(w, fast, s, c):
    if not fast:
        return lax.all_gather(w, "shard", axis=1, tiled=True)
    k, rows, cols = w.shape
    half = rows // 2
    mine = lax.dynamic_slice_in_dim(w, c * half, half, 1)
    far = swap(mine, "shard")
    rest = hop(far, 1)
    full = jnp.zeros((k, 2 * rows, cols), w.dtype)
    full = put(full, w, 0, s * rows, 0)
    full = put(full, far, 0, (1 - s) * rows + c * half, 0)
    return put(full, rest, 0, (1 - s) * rows + (1 - c) * half, 0)


def gather_ffn(w, fast, s, c, t):
    if not fast:
        w = lax.all_gather(w, "shard", axis=0, tiled=True)
        return lax.all_gather(w, "tp", axis=0)
    rows, cols = w.shape
    half = rows // 2
    mine = lax.dynamic_slice_in_dim(w, c * half, half, 0)
    near = swap(mine, "tp")
    far = swap(mine, "shard")
    both = swap(far, "tp")
    full = jnp.zeros((2, 2 * rows, cols), w.dtype)
    full = put(full, w[None], t, s * rows, 0)
    for piece, ti, si in ((far, t, 1 - s), (near, 1 - t, s), (both, 1 - t, 1 - s)):
        full = put(full, piece[None], ti, si * rows + c * half, 0)
        full = put(full, hop(piece, 1)[None], ti, si * rows + (1 - c) * half, 0)
    return full


def take(value, index, axis):
    return lax.dynamic_index_in_dim(value, index, axis, keepdims=False)


def scatter_rows(grad, fast, s, z, c, t=None):
    width, cols = grad.shape
    if not fast:
        if t is not None:
            grad = lax.psum_scatter(grad.reshape(width, 2, cols // 2), "tp", scatter_dimension=1, tiled=False)
        return lax.psum_scatter(grad.astype(F32), ("shard", "ctx"), scatter_dimension=0, tiled=True)
    nz = lax.axis_size("ctx") // 2
    part = grad.astype(BF).reshape(2, nz, 2, width // (4 * nz), cols)

    def fold(value, index, axis, send):
        got = send(take(value, 1 - index, axis))
        return (take(value, index, axis).astype(F32) + got.astype(F32)).astype(BF)

    part = fold(part, c, 2, lambda v: hop(v, 1))
    if t is not None:
        part = part.reshape(part.shape[:-1] + (2, cols // 2))
        part = fold(part, t, part.ndim - 2, lambda v: swap(v, "tp"))
    part = fold(part, s, 0, lambda v: swap(v, "shard"))
    bit = nz // 2
    while bit:
        part = part.reshape((2, bit) + part.shape[-2:])
        part = fold(part, (z // bit) % 2, 0, lambda v, b=2 * bit: hop(v, b))
        bit //= 2
    return part.reshape(part.shape[-2:]).astype(F32)


def total(value, fast, over_tp):
    if not fast:
        return lax.psum(value, ("shard", "ctx", "tp") if over_tp else ("shard", "ctx"))
    if over_tp:
        value = value + swap(value, "tp")
    value = value + swap(value, "shard")
    bit = 1
    while bit < lax.axis_size("ctx"):
        value = value + hop(value, bit)
        bit *= 2
    return value


def per_device(
    tokens,
    cotangent,
    segment_ids,
    w_qkv,
    w_out,
    w_fc1,
    w_fc2,
    norm_gain,
    norm_bias,
    head_gain,
    head_bias,
    ffn_gain,
    ffn_bias,
):
    seqs, length, width = tokens.shape
    n = w_qkv.shape[2]
    heads = n // HD
    ff2 = w_fc1.shape[1]
    half = length // 2
    s, r, t = lax.axis_index("shard"), lax.axis_index("ctx"), lax.axis_index("tp")
    c, z = r % 2, r // 2
    fast = lax.axis_size("shard") == 2
    nw = min(-(-(MAXDOC - 1) // length), lax.axis_size("ctx") - 1)

    wqkv = gather_qkv(w_qkv.astype(BF), fast, s, c)
    small = jnp.concatenate([norm_gain, norm_bias]).astype(BF)
    if fast:
        small = ordered(small, swap(small, "shard"), s, 1)
    else:
        small = lax.all_gather(small, "shard", axis=1, tiled=True)
    small = small.astype(F32)
    gains, biases = small[:2], small[2:]
    vectors = jnp.concatenate([ffn_bias[0], ffn_gain, ffn_bias[1], head_gain, head_bias[2]])
    far = swap(vectors, "tp")
    v0, v1 = jnp.where(t == 0, vectors, far), jnp.where(t == 0, far, vectors)
    fvec = jnp.concatenate([v0[: 3 * ff2].reshape(3, ff2), v1[: 3 * ff2].reshape(3, ff2)], 1)
    hvec = jnp.concatenate([v0[3 * ff2 :].reshape(2, n), v1[3 * ff2 :].reshape(2, n)], 1)
    hg, hb = hvec[:1], hvec[1:]
    pack = jnp.concatenate([w_fc1.astype(BF), w_fc2.astype(BF).T, w_out.astype(BF).T], 1)
    fw = gather_ffn(pack, fast, s, c, t)
    vec = jnp.stack([gains[1], biases[1], biases[2], biases[3]])

    below = jnp.sum(segment_ids[:, None, :] < jnp.arange(1, 4, dtype=jnp.int32)[None, :, None], -1, dtype=jnp.int32)
    seg_q = lax.dynamic_slice_in_dim(segment_ids, r * length, length, 1)
    start = jnp.zeros_like(seg_q)
    for v in range(1, 4):
        start = jnp.where(seg_q == v, below[:, v - 1 : v], start)
    block = min(256, length)

    def bounds(b, w):
        lo = start[b] + (w - r) * length
        return jnp.concatenate([lo[::block], lo[block - 1 :: block]]), lo[None]

    acts, qs, qTs, rings, states = [], [], [], [], []
    for b in range(seqs):
        a, q, qT, kv = qkv_call(tokens[b], wqkv, gains[:1], biases[:1], head_bias[:1], head_bias[1:2])
        acts.append(a)
        qs.append(q)
        qTs.append(qT)
        rings.append([kv])
        states.append(None)
    for w in range(nw):
        for b in range(seqs):
            rings[b].append(shift(rings[b][w], 1))
    for w in range(nw + 1):
        for b in range(seqs):
            sm, lo = bounds(b, w)
            states[b] = fwd_step(w, nw, sm, qTs[b], rings[b][w], lo, states[b])

    def own_rows(value, index):
        return lax.dynamic_slice_in_dim(value, index * half, half, 0)

    outs, g1s, dos, mids = [], [], [], []
    for b in range(seqs):
        cen, oT, lse, mean = states[b]
        own, peer = own_rows(cen, t), swap(own_rows(cen, 1 - t), "tp")
        mrow = mean.reshape(length, 1)
        mown, mpeer = own_rows(mrow, t), swap(own_rows(mean[0], 1 - t), "tp").reshape(half, 1)
        first = t == 0
        c0, c1 = jnp.where(first, own, peer), jnp.where(first, peer, own)
        delta = jnp.where(first, mown - mpeer, mpeer - mown) * 0.5
        x, g = own_rows(tokens[b], t), own_rows(cotangent[b], t)
        mid = ffn_call(c0, c1, delta, x, g, fw, hg, hb, vec, fvec)
        out, g1, dat = mid[:3]
        mids.append(mid[3:] + (g, g1))
        mine = lax.dynamic_slice_in_dim(dat, t * n, n, 1)
        theirs = lax.dynamic_slice_in_dim(dat, (1 - t) * n, n, 1)
        dos.append(ordered(mine, swap(theirs, "tp"), t, 0))
        outs.append(ordered(out, swap(out, "tp"), t, 0))
        g1s.append(ordered(g1, swap(g1, "tp"), t, 0))

    prep, dqs, dkvs = [], [None] * seqs, [None] * seqs
    for b in range(seqs):
        cen, oT, lse, mean = states[b]
        doT = dos[b].T
        dd = jnp.sum(doT.reshape(heads, HD, length).astype(F32) * oT.reshape(heads, HD, length), 1)
        dd = jnp.concatenate([dd, jnp.zeros((8 - heads, length), F32)])
        prep.append((doT, dd))
    for w in range(nw, -1, -1):
        for b in range(seqs):
            sm, lo = bounds(b, w)
            doT, dd = prep[b]
            dqs[b], dkvs[b] = bwd_step(
                w, nw, sm, qTs[b], qs[b], doT, dos[b], rings[b][w], states[b][2], dd, lo, dqs[b], dkvs[b]
            )
            if w:
                dkvs[b] = shift(dkvs[b], -1)

    def rows_of(i):
        return jnp.concatenate([mids[b][i] for b in range(seqs)])

    def outer(left, right):
        return lax.dot_general(left, right, (((0,), (0,)), ((), ())), preferred_element_type=F32).astype(BF)

    o_all, f_all, z_all, dh_all, g_all, g1_all = (rows_of(i) for i in (0, 1, 2, 3, 7, 8))
    grad_down = scatter_rows(outer(g_all, z_all), fast, s, z, c, t).T
    grad_up = scatter_rows(outer(f_all, dh_all), fast, s, z, c, t)
    grad_out = scatter_rows(outer(g1_all, o_all), fast, s, z, c, t).T
    hsum, dsum, fsum = (sum(mids[b][i] for b in range(seqs)) for i in (4, 5, 6))
    mid_sums = total(jnp.concatenate([hsum.reshape(-1), dsum.reshape(-1), fsum.reshape(-1)]), fast, True)
    hsum = mid_sums[: hsum.size].reshape(hsum.shape)
    fsum = mid_sums[hsum.size + dsum.size :].reshape(fsum.shape)
    dsum = mid_sums[hsum.size : hsum.size + dsum.size].reshape(dsum.shape)

    grad_tokens, in_sums, projs = [], 0.0, []
    for b in range(seqs):
        dq = (dqs[b].T * 0.125).astype(BF)
        proj = jnp.concatenate([dq, dkvs[b]], 1)
        projs.append(proj)
        da = sum(dot_nt(proj[:, i * n : (i + 1) * n], wqkv[i]) for i in range(3)).astype(BF)
        gt, sums = tail_call(da, swap(da, "tp"), tokens[b], g1s[b], gains[:1])
        grad_tokens.append(gt)
        in_sums = in_sums + sums
    proj = jnp.concatenate(projs)
    grad_qkv = scatter_rows(outer(jnp.concatenate(acts), proj), fast, s, z, c)
    grad_qkv = grad_qkv.reshape(-1, 3, n).transpose(1, 0, 2)
    bias_sums = jnp.sum(proj.astype(F32), 0)
    tail_sums = total(jnp.concatenate([in_sums.reshape(-1), bias_sums]), fast, False)
    in_sums = tail_sums[: 2 * width].reshape(2, width)
    bias_sums = tail_sums[2 * width :]

    piece = width // (lax.axis_size("shard") * lax.axis_size("ctx"))
    mine = (s * lax.axis_size("ctx") + r) * piece
    grad_gain = lax.dynamic_slice_in_dim(jnp.stack([in_sums[0], dsum[0]]), mine, piece, 1)
    grad_bias = lax.dynamic_slice_in_dim(jnp.stack([in_sums[1], dsum[1], dsum[2], dsum[3]]), mine, piece, 1)
    hsum = lax.dynamic_slice_in_dim(hsum, t * n, n, 1)
    fsum = lax.dynamic_slice_in_dim(fsum, t * ff2, ff2, 1)
    return (
        jnp.stack(outs),
        jnp.stack(grad_tokens),
        grad_qkv,
        grad_out,
        grad_up,
        grad_down,
        grad_gain,
        grad_bias,
        hsum[0],
        jnp.stack([bias_sums[:n], bias_sums[2 * n :], hsum[1]]),
        fsum[1],
        jnp.stack([fsum[0], fsum[2]]),
    )


def solution(mesh):
    in_specs = (
        P("shard", "ctx", None),
        P("shard", "ctx", None),
        P("shard", None),
        P(None, "shard", "tp"),
        P("tp", "shard"),
        P("shard", "tp"),
        P("tp", "shard"),
        P(None, "shard"),
        P(None, "shard"),
        P("tp"),
        P(None, "tp"),
        P("tp"),
        P(None, "tp"),
    )
    out_specs = (
        P("shard", "ctx", None),
        P("shard", "ctx", None),
        P(None, ("shard", "ctx"), "tp"),
        P("tp", ("shard", "ctx")),
        P(("shard", "ctx"), "tp"),
        P("tp", ("shard", "ctx")),
        P(None, ("shard", "ctx")),
        P(None, ("shard", "ctx")),
        P("tp"),
        P(None, "tp"),
        P("tp"),
        P(None, "tp"),
    )
    return jax.shard_map(
        per_device, mesh=mesh, in_specs=in_specs, out_specs=out_specs, check_vma=False
    )
```

```python
import functools
import jax
import jax.numpy as jnp
from jax import lax
from jax.experimental import pallas as pl
from jax.experimental.pallas import tpu as pltpu
from jax.sharding import PartitionSpec as P
HD=64
NEG=-1e30
VL=48*1024*1024

def fwd_kernel(diag,first,last,heads,L,BQ,BK, lo_sm, qT_ref,kv_ref,lo_ref,*rest):
    n=heads*HD
    if first:
        ins=(); rest=rest
    else:
        m_in,l_in,a_in=rest[:3]; rest=rest[3:]
    if last:
        c_ref,oT_ref,lse_ref,mean_ref=rest[:4]; rest=rest[4:]
    else:
        m_out,l_out,a_out=rest[:3]; rest=rest[3:]
    m_s,l_s,acc,qm,vT=rest
    if first:
        m_s[...]=jnp.full_like(m_s,NEG); l_s[...]=jnp.zeros_like(l_s); acc[...]=jnp.zeros_like(acc)
    else:
        m_s[...]=m_in[...]; l_s[...]=l_in[...]; acc[...]=a_in[...]
    nq,nk=L//BQ,L//BK
    rowi=lax.broadcasted_iota(jnp.int32,(2*HD,L),0)
    for p in range(heads//2):
        blk=qT_ref[p*128:(p+1)*128,:]
        qm[2*p]=jnp.where(rowi<HD,blk,jnp.zeros_like(blk))
        qm[2*p+1]=jnp.where(rowi>=HD,blk,jnp.zeros_like(blk))
        vT[p*128:(p+1)*128,:]=kv_ref[:,n+p*128:n+(p+1)*128].T
    def block(qb,kb,masked):
        qs=slice(qb*BQ,(qb+1)*BQ); ks=slice(kb*BK,(kb+1)*BK)
        if masked:
            kk=lax.broadcasted_iota(jnp.int32,(BK,BQ),0)+kb*BK
            valid=kk>=lo_ref[:,qs]
            if diag and (kb+1)*BK>qb*BQ+1:
                valid=valid&(kk<=lax.broadcasted_iota(jnp.int32,(BK,BQ),1)+qb*BQ)
        for h in range(heads):
            p=h//2
            s=jnp.dot(kv_ref[ks,p*128:(p+1)*128],qm[h,:,qs],preferred_element_type=jnp.float32)
            if masked: s=jnp.where(valid,s,NEG)
            mo=m_s[h:h+1,qs]
            mn=jnp.maximum(mo,jnp.max(s,0,keepdims=True))
            e=jnp.exp(s-mn); al=jnp.exp(mo-mn)
            m_s[h:h+1,qs]=mn
            l_s[h:h+1,qs]=l_s[h:h+1,qs]*al+jnp.sum(e,0,keepdims=True)
            hs=slice(h*HD,(h+1)*HD)
            acc[hs,qs]=acc[hs,qs]*al+jnp.dot(vT[hs,ks],e.astype(jnp.bfloat16),preferred_element_type=jnp.float32)
    for qb in range(nq):
        for kb in range(nk):
            if diag and kb*BK>qb*BQ+BQ-1: continue
            vis=lo_sm[qb]<=kb*BK+BK-1
            if diag and (kb+1)*BK>qb*BQ+1:
                pl.when(vis)(functools.partial(block,qb,kb,True))
            else:
                full=lo_sm[nq+qb]<=kb*BK
                pl.when(full)(functools.partial(block,qb,kb,False))
                pl.when(jnp.logical_and(vis,jnp.logical_not(full)))(functools.partial(block,qb,kb,True))
    if last:
        tot=jnp.zeros((1,L),jnp.float32)
        for h in range(heads):
            hs=slice(h*HD,(h+1)*HD)
            o=acc[hs,:]/l_s[h:h+1,:]
            oT_ref[hs,:]=o
            tot=tot+jnp.sum(o,0,keepdims=True)
        mean=tot/n
        mean_ref[...]=mean
        lse_ref[...]=m_s[...]+jnp.log(l_s[...])
        for p in range(heads//2):
            c_ref[:,p*128:(p+1)*128]=(oT_ref[p*128:(p+1)*128,:]-mean).T.astype(jnp.bfloat16)
    else:
        m_out[...]=m_s[...]; l_out[...]=l_s[...]; a_out[...]=acc[...]

def fwd_step(w,nw,lo_sm,qT,kv,lo,state):
    n,L=qT.shape; heads=n//HD
    BQ=min(256,L); BK=min(256,L)
    first=w==0; last=w==nw
    V=pl.BlockSpec(memory_space=pltpu.VMEM)
    st=(jax.ShapeDtypeStruct((8,L),jnp.float32),jax.ShapeDtypeStruct((8,L),jnp.float32),jax.ShapeDtypeStruct((n,L),jnp.float32))
    outs=st if not last else (jax.ShapeDtypeStruct((L,n),jnp.bfloat16),st[2],st[0],jax.ShapeDtypeStruct((1,L),jnp.float32))
    args=(lo_sm,qT,kv,lo)+(() if first else tuple(state))
    return pl.pallas_call(
        functools.partial(fwd_kernel,w==0,first,last,heads,L,BQ,BK),
        out_shape=outs,
        in_specs=[pl.BlockSpec(memory_space=pltpu.SMEM)]+[V]*(len(args)-1),
        out_specs=tuple([V]*len(outs)),
        scratch_shapes=[pltpu.VMEM((8,L),jnp.float32),pltpu.VMEM((8,L),jnp.float32),pltpu.VMEM((n,L),jnp.float32),
            pltpu.VMEM((heads,128,L),jnp.bfloat16),pltpu.VMEM((n,L),jnp.bfloat16)],
        compiler_params=pltpu.CompilerParams(vmem_limit_bytes=VL),
        cost_estimate=pl.CostEstimate(flops=4*L*L*n,bytes_accessed=4*L*n*4,transcendentals=heads*L*L),
        name="attn_fwd",
    )(*args)


EPS = 1e-05
MAXDOC = 1920
BF = jnp.bfloat16
F32 = jnp.float32
NT_DIMS = (((1,), (1,)), ((), ()))
VMEM_SPEC = pl.BlockSpec(memory_space=pltpu.VMEM)
ANY_SPEC = pl.BlockSpec(memory_space=pl.ANY)
GELU_C = 0.7978845608028654
GELU_A = 0.044715


def dot(left, right):
    return jnp.dot(left, right, preferred_element_type=F32)


def dot_nt(left, right):
    return lax.dot_general(left, right, NT_DIMS, preferred_element_type=F32)


def row_mean(values):
    return jnp.mean(values, -1, keepdims=True)


def col_sum(values):
    return jnp.sum(values, 0, keepdims=True)


def put_transposed(value, dst, tmp):
    width = value.shape[1]
    for k in range(width // 128):
        tmp[k * 128 : (k + 1) * 128, :] = value[:, k * 128 : (k + 1) * 128].T
    piece = width // 16
    for shard in range(2):
        for z in range(4):
            for core in range(2):
                to = core * (width // 2) + shard * (width // 4) + z * piece
                at = shard * (width // 2) + (z * 2 + core) * piece
                dst[to : to + piece, :] = tmp[at : at + piece, :]


def qkv_kernel(fast, x_ref, w_ref, gain_ref, shift_ref, qb_ref, vb_ref, a_ref, qT_ref, kv_ref, tmp):
    n = qb_ref.shape[1]
    x = x_ref[...].astype(F32)
    cen = x - row_mean(x)
    a = cen * lax.rsqrt(row_mean(cen * cen) + EPS) * gain_ref[...] + shift_ref[...]
    a = a.astype(BF)
    if fast:
        put_transposed(a, a_ref, tmp)
    else:
        a_ref[...] = a
    q = (dot(a, w_ref[0]) + qb_ref[...]).astype(BF).astype(F32) * 0.125
    q = q.astype(BF)
    for p in range(n // 128):
        ps = slice(p * 128, (p + 1) * 128)
        qT_ref[ps, :] = q[:, ps].T
    kv_ref[:, :n] = dot(a, w_ref[1]).astype(BF)
    kv_ref[:, n:] = (dot(a, w_ref[2]) + vb_ref[...]).astype(BF)


def qkv_call(fast, x, w, gain, shift, qb, vb):
    rows, width = x.shape
    n = qb.shape[1]
    return pl.pallas_call(
        functools.partial(qkv_kernel, fast),
        out_shape=(
            jax.ShapeDtypeStruct((width, rows) if fast else (rows, width), BF),
            jax.ShapeDtypeStruct((n, rows), BF),
            jax.ShapeDtypeStruct((rows, 2 * n), BF),
        ),
        in_specs=[VMEM_SPEC] * 6,
        out_specs=(VMEM_SPEC,) * 3,
        scratch_shapes=[pltpu.VMEM((width, rows), BF)],
        compiler_params=pltpu.CompilerParams(vmem_limit_bytes=VL),
        cost_estimate=pl.CostEstimate(
            flops=6 * rows * width * n, bytes_accessed=rows * width * 8 + 6 * width * n, transcendentals=rows
        ),
        name="qkv",
    )(x, w, gain, shift, qb, vb)


def gelu_pair(h):
    inner = GELU_C * (h + GELU_A * h * h * h)
    t = jnp.tanh(inner)
    half = 0.5 * (1.0 + t)
    slope = half + 0.5 * h * (1.0 - t * t) * (GELU_C * (1.0 + (3.0 * GELU_A) * h * h))
    return h * half, slope


def ffn_kernel(
    fast, step,
    c0_ref, c1_ref, delta_ref, x_ref, g_ref, fw_ref, hg_ref, hb_ref, vec_ref, fvec_ref,
    out_ref, g1_ref, dat_ref, o_ref, f_ref, z_ref, dh_ref, hsum_ref, dsum_ref, fsum_ref,
    fw, u_s, gp_s, e_s, tmp, sems,
):
    ff2 = z_ref.shape[1] // 2
    n = c0_ref.shape[1]
    copies = []
    for i, (lo, hi) in enumerate(((2 * ff2, 2 * ff2 + n), (0, ff2), (ff2, 2 * ff2))):
        cp = pltpu.make_async_copy(fw_ref.at[:, :, lo:hi], fw.at[:, :, lo:hi], sems.at[i])
        cp.start()
        copies.append(cp)
    ocols = slice(2 * ff2, 2 * ff2 + n)

    n0 = c0_ref[...].astype(F32) + delta_ref[...]
    n1 = c1_ref[...].astype(F32) - delta_ref[...]
    var = (jnp.sum(n0 * n0, -1, keepdims=True) + jnp.sum(n1 * n1, -1, keepdims=True)) / (2 * n)
    rs = lax.rsqrt(var + EPS)
    nh = (n0 * rs, n1 * rs)
    os = []
    for p in range(2):
        cs = slice(p * n, (p + 1) * n)
        o = (nh[p] * hg_ref[:, cs] + hb_ref[:, cs]).astype(BF)
        o_ref[:, cs] = o
        os.append(o)
    copies[0].wait()
    y1 = x_ref[...].astype(F32) + vec_ref[2:3, :]
    for p in range(2):
        y1 = y1 + dot_nt(os[p], fw[p, :, ocols])
    cen = y1 - row_mean(y1)
    r2 = lax.rsqrt(row_mean(cen * cen) + EPS)
    yh = cen * r2
    f = (yh * vec_ref[0:1, :] + vec_ref[1:2, :]).astype(BF)
    if fast:
        put_transposed(g_ref[...], f_ref.at[0], tmp)
        put_transposed(f, f_ref.at[1], tmp)
    else:
        f_ref[...] = f
    copies[1].wait()
    usum = 0.0
    chunks = [(p, j) for p in range(2) for j in range(0, ff2, step)]
    for p, j in chunks:
        cs = slice(p * ff2 + j, p * ff2 + j + step)
        h = dot(f, fw[p, :, j : j + step]) + fvec_ref[0:1, cs]
        u, slope = gelu_pair(h)
        u_s[:, cs] = u
        gp_s[:, cs] = slope
        usum = usum + jnp.sum(u, -1, keepdims=True)
    mu = usum / (2 * ff2)
    ssum = 0.0
    for p, j in chunks:
        cs = slice(p * ff2 + j, p * ff2 + j + step)
        d = u_s[:, cs] - mu
        ssum = ssum + jnp.sum(d * d, -1, keepdims=True)
    ru = lax.rsqrt(ssum / (2 * ff2) + EPS)
    copies[2].wait()
    g2 = g_ref[...]
    y2 = y1 + vec_ref[3:4, :]
    esum = 0.0
    ezsum = 0.0
    for p, j in chunks:
        cs = slice(p * ff2 + j, p * ff2 + j + step)
        w2 = fw[p, :, ff2 + j : ff2 + j + step]
        zh = (u_s[:, cs] - mu) * ru
        u_s[:, cs] = zh
        z = (zh * fvec_ref[1:2, cs] + fvec_ref[2:3, cs]).astype(BF)
        z_ref[:, cs] = z
        y2 = y2 + dot_nt(z, w2)
        dz = dot(g2, w2)
        fsum_ref[1:2, cs] = col_sum(dz * zh)
        fsum_ref[2:3, cs] = col_sum(dz)
        e = dz * fvec_ref[1:2, cs]
        e_s[:, cs] = e
        esum = esum + jnp.sum(e, -1, keepdims=True)
        ezsum = ezsum + jnp.sum(e * zh, -1, keepdims=True)
    out_ref[...] = y2.astype(BF)
    em = esum / (2 * ff2)
    ezm = ezsum / (2 * ff2)
    df = jnp.zeros_like(y1)
    for p, j in chunks:
        cs = slice(p * ff2 + j, p * ff2 + j + step)
        du = ru * (e_s[:, cs] - em - u_s[:, cs] * ezm)
        dh = (du * gp_s[:, cs]).astype(BF)
        dh_ref[:, cs] = dh
        fsum_ref[0:1, cs] = col_sum(dh.astype(F32))
        df = df + dot_nt(dh, fw[p, :, j : j + step])
    dsum_ref[0:1, :] = col_sum(df * yh)
    dsum_ref[1:2, :] = col_sum(df)
    e2 = df * vec_ref[0:1, :]
    g = g2.astype(F32)
    dy1 = g + r2 * (e2 - row_mean(e2) - yh * row_mean(e2 * yh))
    g1 = dy1.astype(BF)
    g1_ref[...] = g1
    if fast:
        put_transposed(g1, f_ref.at[2], tmp)
    dsum_ref[2:3, :] = col_sum(g1.astype(F32))
    dsum_ref[3:4, :] = col_sum(g)
    es = []
    for p in range(2):
        cs = slice(p * n, (p + 1) * n)
        dsub = dot(g1, fw[p, :, ocols])
        hsum_ref[0:1, cs] = col_sum(dsub * nh[p])
        hsum_ref[1:2, cs] = col_sum(dsub)
        es.append(dsub * hg_ref[:, cs])
    em = sum(jnp.sum(e, -1, keepdims=True) for e in es) / (2 * n)
    ezm = sum(jnp.sum(e * h, -1, keepdims=True) for e, h in zip(es, nh)) / (2 * n)
    for p in range(2):
        cs = slice(p * n, (p + 1) * n)
        dat_ref[:, cs] = (rs * (es[p] - em - nh[p] * ezm)).astype(BF)


def ffn_call(fast, c0, c1, delta, x, g, fw, hg, hb, vec, fvec):
    rows, n = c0.shape
    width = x.shape[1]
    ff = fvec.shape[1]
    step = 512
    sds = jax.ShapeDtypeStruct
    return pl.pallas_call(
        functools.partial(ffn_kernel, fast, step),
        out_shape=(
            sds((rows, width), BF),
            sds((rows, width), BF),
            sds((rows, 2 * n), BF),
            sds((rows, 2 * n), BF),
            sds((3, width, rows) if fast else (rows, width), BF),
            sds((rows, ff), BF),
            sds((rows, ff), BF),
            sds((2, 2 * n), F32),
            sds((4, width), F32),
            sds((3, ff), F32),
        ),
        in_specs=[VMEM_SPEC] * 5 + [ANY_SPEC] + [VMEM_SPEC] * 4,
        out_specs=(VMEM_SPEC,) * 10,
        scratch_shapes=[
            pltpu.VMEM(fw.shape, BF),
            pltpu.VMEM((rows, ff), F32),
            pltpu.VMEM((rows, ff), F32),
            pltpu.VMEM((rows, ff), F32),
            pltpu.VMEM((width, rows), BF),
            pltpu.SemaphoreType.DMA((3,)),
        ],
        compiler_params=pltpu.CompilerParams(vmem_limit_bytes=VL),
        cost_estimate=pl.CostEstimate(
            flops=2 * rows * fw.size * 2, bytes_accessed=2 * fw.size, transcendentals=rows * ff
        ),
        name="ffn",
    )(c0, c1, delta, x, g, fw, hg, hb, vec, fvec)


def tail_kernel(own_ref, peer_ref, x_ref, g1_ref, gain_ref, out_ref, sum_ref):
    da = own_ref[...].astype(F32) + peer_ref[...].astype(F32)
    x = x_ref[...].astype(F32)
    cen = x - row_mean(x)
    r = lax.rsqrt(row_mean(cen * cen) + EPS)
    xh = cen * r
    sum_ref[0:1, :] = col_sum(da * xh)
    sum_ref[1:2, :] = col_sum(da)
    e = da * gain_ref[...]
    dx = r * (e - row_mean(e) - xh * row_mean(e * xh))
    out_ref[...] = (g1_ref[...].astype(F32) + dx).astype(BF)


def tail_call(own, peer, x, g1, gain):
    rows, width = x.shape
    return pl.pallas_call(
        tail_kernel,
        out_shape=(jax.ShapeDtypeStruct((rows, width), BF), jax.ShapeDtypeStruct((2, width), F32)),
        in_specs=[VMEM_SPEC] * 5,
        out_specs=(VMEM_SPEC, VMEM_SPEC),
        compiler_params=pltpu.CompilerParams(vmem_limit_bytes=VL),
        cost_estimate=pl.CostEstimate(
            flops=20 * rows * width, bytes_accessed=10 * rows * width, transcendentals=rows
        ),
        name="tail",
    )(own, peer, x, g1, gain)


MESH_ID = pl.DeviceIdType.MESH


def remote(src, dst, send, recv, device):
    return pltpu.make_async_remote_copy(
        src_ref=src, dst_ref=dst, send_sem=send, recv_sem=recv, device_id=device, device_id_type=MESH_ID
    )


def greet(devices):
    sem = pltpu.get_barrier_semaphore()
    count = 0
    for device, cond in devices:
        def signal(device=device):
            pl.semaphore_signal(sem, inc=1, device_id=device, device_id_type=MESH_ID)
        if cond is None:
            signal()
            count = count + 1
        else:
            pl.when(cond)(signal)
            count = count + cond.astype(jnp.int32)
    pl.semaphore_wait(sem, count)


def chunk_blocks(w, length, bq, bk):
    found = []
    for kb in range(length // bk):
        for qb in range(length // bq):
            if w == 0 and kb * bk > qb * bq + bq - 1:
                continue
            if qb * bq + w * length - (MAXDOC - 1) > kb * bk + bk - 1:
                continue
            found.append((qb, kb))
    return found


def block_bias(w, lo, qb, kb, bq, bk):
    key = lax.broadcasted_iota(jnp.int32, (bk, bq), 0) + kb * bk
    seen = key >= lo[:, qb * bq : (qb + 1) * bq]
    if w == 0 and (kb + 1) * bk > qb * bq + 1:
        seen = seen & (key <= lax.broadcasted_iota(jnp.int32, (bk, bq), 1) + qb * bq)
    return jnp.where(seen, 0.0, NEG)


def split_pairs(src, dst, heads):
    row = lax.broadcasted_iota(jnp.int32, (2 * HD, src.shape[1]), 0)
    for p in range(heads // 2):
        block = src[p * 128 : (p + 1) * 128, :]
        dst[2 * p] = jnp.where(row < HD, block, jnp.zeros_like(block))
        dst[2 * p + 1] = jnp.where(row >= HD, block, jnp.zeros_like(block))


def back_item(w, heads, length, bq, bk, kv, qT, doT, qm, dm, kT, lse, dd, lo, bias, dq, dk, dv):
    n = heads * HD
    for p in range(heads // 2):
        ps = slice(p * 128, (p + 1) * 128)
        kT[ps, :] = kv[:, ps].T
    blocks = chunk_blocks(w, length, bq, bk)
    for kb in range(length // bk):
        ks = slice(kb * bk, (kb + 1) * bk)
        mine = [qb for qb, other in blocks if other == kb]
        if not mine:
            dk[:, ks] = jnp.zeros((n, bk), F32)
            dv[:, ks] = jnp.zeros((n, bk), F32)
        for turn, qb in enumerate(mine):
            qs = slice(qb * bq, (qb + 1) * bq)
            bias[...] = block_bias(w, lo, qb, kb, bq, bk)

            def scores(h):
                ps = slice((h // 2) * 128, (h // 2 + 1) * 128)
                pv = slice(n + (h // 2) * 128, n + (h // 2 + 1) * 128)
                return dot(kv[ks, ps], qm[h, :, qs]) + bias[...], dot(kv[ks, pv], dm[h, :, qs])

            ahead = scores(0)
            for h in range(heads):
                hs = slice(h * HD, (h + 1) * HD)
                s, dp = ahead
                ahead = scores(h + 1) if h + 1 < heads else None
                e = jnp.exp(s - lse[h : h + 1, qs])
                ds = (e * (dp - dd[h : h + 1, qs])).astype(BF)
                new_v = dot_nt(doT[hs, qs], e.astype(BF))
                new_k = dot_nt(qT[hs, qs], ds)
                if turn:
                    dv[hs, ks] += new_v
                    dk[hs, ks] += new_k
                else:
                    dv[hs, ks] = new_v
                    dk[hs, ks] = new_k
                dq[hs, qs] += dot(kT[hs, ks], ds)


def back_kernel(
    fast, nw, nctx, heads, length,
    qT_ref, doT_ref, oT_ref, lse_ref, lo_ref, kv_hbm, lt_ref, z_ref, dh_ref, o_ref, out_own, g1_own, sum_ref,
    dq_ref, dkv_ref, part2_ref, part1_ref, parto_ref, total_ref, out_ref, g1_ref,
    slots, kvbuf, qm, dm, kT, bias, dk, dv, dd,
    ring_send, ring_recv, kv_sem, *rs,
):
    n = heads * HD
    bq = bk = min(256, length)
    s, r, t = lax.axis_index("shard"), lax.axis_index("ctx"), lax.axis_index("tp")
    c = lax.rem(r, 2)
    sib = {"ctx": r + 1 - 2 * c}
    left, right = {"ctx": r - 1}, {"ctx": r + 1}
    has_left, has_right = r > 0, r < nctx - 1
    half = length // 2
    people = [(left, has_left), (right, has_right), ({"tp": 1 - t}, None)]
    if fast:
        ypeer, xpeer = {"tp": 1 - t}, {"shard": 1 - s}
        z2 = lax.rem(r // 2, 2)
        people += [(xpeer, None)]
        people += [({"ctx": r + 2 - 4 * z2}, None)]
        hop4 = lax.rem(r // 4, 2)
        people += [({"ctx": r + 4 - 8 * hop4}, None)]
    greet(people)

    seqs = qT_ref.shape[0]
    items = [(w, b) for w in range(nw, -1, -1) for b in range(seqs)]
    nbuf = kvbuf.shape[0]

    def load(i):
        w, b = items[i]
        return pltpu.make_async_copy(kv_hbm.at[w, b], kvbuf.at[i % nbuf], kv_sem.at[i % nbuf])

    def start_load(i):
        if i < len(items):
            pl.when(r >= items[i][0])(lambda: load(i).start())

    for i in range(nbuf - 1):
        start_load(i)

    own_sem, give_send, give_recv = rs[:3]
    rs = rs[3:]
    gives, keeps = [], []
    for k, (src, dst) in enumerate(((g1_own, g1_ref), (out_own, out_ref))):
        for b in range(seqs):
            rows = pl.ds(pl.multiple_of(t * half, half), half)
            keeps.append(pltpu.make_async_copy(src.at[b], dst.at[b, rows], own_sem.at[k * seqs + b]))
            gives.append(
                remote(src.at[b], dst.at[b, rows], give_send.at[k * seqs + b], give_recv.at[k * seqs + b], {"tp": 1 - t})
            )
    for cp in keeps:
        cp.start()

    for b in range(seqs):
        split_pairs(qT_ref.at[b], qm.at[b], heads)
        split_pairs(doT_ref.at[b], dm.at[b], heads)
        for h in range(heads):
            hs = slice(h * HD, (h + 1) * HD)
            dd[b, h : h + 1, :] = col_sum(doT_ref[b, hs, :].astype(F32) * oT_ref[b, hs, :])
        dq_ref[b] = jnp.zeros((n, length), F32)

    steps = {}
    if fast:
        (s2, r2, w2, x2, y2, s1, r1, w1, y1, x1, so, ro, wo, yo, xo, vec_buf, rs_send, rs_recv, vec_send, vec_recv) = rs
        step = 512

        def product(g, rhs, core, dst):
            cols = rhs.shape[2]
            size = step if cols % step == 0 else cols // 2
            rows = pl.ds(pl.multiple_of(core * (lt_ref.shape[2] // 2), 64), lt_ref.shape[2] // 2)

            def body(j, carry):
                at = pl.ds(pl.multiple_of(j * size, size), size)
                acc = dot(lt_ref[0, g, rows, :], rhs[0, :, at])
                for b in range(1, seqs):
                    acc = acc + dot(lt_ref[b, g, rows, :], rhs[b, :, at])
                mid = acc.shape[0] // 2
                acc = acc.astype(BF)
                dst[0, :, at] = acc[:mid]
                dst[1, :, at] = acc[mid:]
                return carry

            lax.fori_loop(0, cols // size, body, 0)

        def add(dst, a, b):
            dst[...] = (a[...].astype(F32) + b[...].astype(F32)).astype(BF)

        live = {}

        def send(name, src, dst, i, device):
            live[name] = remote(src, dst, rs_send.at[i], rs_recv.at[i], device)
            live[name].start()

        def cols_of(ref, index):
            width = ref.shape[-1] // 2
            return pl.ds(pl.multiple_of(index * width, 128), width)

        def first(g, rhs, sbuf, rbuf, i):
            product(g, rhs, 1 - c, sbuf)
            send(("core", g), sbuf, rbuf, i, sib)

        def x_then_y(stage):
            if stage == 0:
                first(0, z_ref, s2, r2, 0)
            elif stage == 1:
                product(0, z_ref, c, w2)
            elif stage == 2:
                live[("core", 0)].wait_recv()
                add(w2.at[1 - s], w2.at[1 - s], r2.at[1 - s])
                send("x2", w2.at[1 - s], x2, 1, xpeer)
                add(w2.at[s], w2.at[s], r2.at[s])
            elif stage == 3:
                live["x2"].wait_recv()
                add(w2.at[s], w2.at[s], x2)
                send("y2", w2.at[s, :, cols_of(w2, 1 - t)], y2, 2, ypeer)
            elif stage == 4:
                live["y2"].wait_recv()
                add(part2_ref, w2.at[s, :, cols_of(w2, t)], y2)

        def y_then_x(stage, g, rhs, sb, rb, wb, yb, xb, part, i):
            if stage == 0:
                first(g, rhs, sb, rb, i)
            elif stage == 1:
                product(g, rhs, c, wb)
            elif stage == 2:
                live[("core", g)].wait_recv()
                for k in range(2):
                    add(wb.at[k], wb.at[k], rb.at[k])
                send(("y", g), wb.at[:, :, cols_of(wb, 1 - t)], yb, i + 1, ypeer)
            elif stage == 3:
                live[("y", g)].wait_recv()
                mine = cols_of(wb, t)
                add(wb.at[1 - s, :, mine], wb.at[1 - s, :, mine], yb.at[1 - s])
                send(("x", g), wb.at[1 - s, :, mine], xb, i + 2, xpeer)
                add(wb.at[s, :, mine], wb.at[s, :, mine], yb.at[s])
            elif stage == 4:
                live[("x", g)].wait_recv()
                add(part, wb.at[s, :, cols_of(wb, t)], xb)

        up = lambda stage: y_then_x(stage, 1, dh_ref, s1, r1, w1, y1, x1, part1_ref, 3)
        op = lambda stage: y_then_x(stage, 2, o_ref, so, ro, wo, yo, xo, parto_ref, 6)

        partners = [ypeer, xpeer, sib, {"ctx": r + 2 - 4 * z2}, {"ctx": r + 4 - 8 * hop4}]
        count = vec_buf.shape[0] - 1

        def vec(stage):
            if stage == 0:
                acc = sum_ref[0]
                for b in range(1, seqs):
                    acc = acc + sum_ref[b]
                total_ref[...] = acc
            else:
                live[("v", stage - 1)].wait()
                total_ref[...] = total_ref[...] + vec_buf[stage - 1]
            if stage < len(partners):
                vec_buf[count] = total_ref[...]
                live[("v", stage)] = remote(
                    vec_buf.at[count], vec_buf.at[stage], vec_send.at[stage], vec_recv.at[stage], partners[stage]
                )
                live[("v", stage)].start()

        plan = [
            [lambda: up(0), lambda: vec(0)],
            [lambda: up(1), lambda: x_then_y(0)],
            [lambda: up(2), lambda: x_then_y(1), lambda: vec(1)],
            [lambda: x_then_y(2), lambda: op(0), lambda: op(1), lambda: [cp.start() for cp in gives]],
            [lambda: op(2), lambda: vec(2)],
            [lambda: vec(3)],
            [lambda: up(3), lambda: vec(4)],
            [lambda: x_then_y(3), lambda: vec(5)],
            [lambda: op(3)],
            [lambda: up(4), lambda: op(4), lambda: x_then_y(4)],
        ]
        for i, what in enumerate(plan):
            steps.setdefault(min(i, len(items) - 1), []).extend(what)
        ends = lambda: [cp.wait_send() for key, cp in live.items() if not (isinstance(key, tuple) and key[0] == "v")]
    else:
        steps[0] = [lambda: [cp.start() for cp in gives]]
        ends = lambda: None

    sends = {}
    for i, (w, b) in enumerate(items):
        start_load(i + nbuf - 1)
        slot = slots.at[w, b]
        has = r >= w

        def work(i=i, w=w, b=b):
            load(i).wait()
            back_item(
                w, heads, length, bq, bk, kvbuf.at[i % nbuf], qT_ref.at[b], doT_ref.at[b], qm.at[b], dm.at[b], kT,
                lse_ref.at[b], dd.at[b], lo_ref[b] + (w - r) * length, bias, dq_ref.at[b], dk, dv,
            )

        pl.when(has)(work)
        dest = slots.at[w, b] if w else dkv_ref.at[b]
        if w < nw:
            arrived = remote(slots.at[w, b], slots.at[w, b], ring_send.at[w, b], ring_recv.at[w, b], left)

            def merge(w=w, b=b, dest=dest, arrived=arrived):
                arrived.wait_recv()
                dest[:n, :] = (dk[...] + slots[w, b, :n, :].astype(F32)).astype(BF)
                dest[n:, :] = (dv[...] + slots[w, b, n:, :].astype(F32)).astype(BF)

            pl.when(has & has_right)(merge)

        def plain(dest=dest):
            dest[:n, :] = dk[...].astype(BF)
            dest[n:, :] = dv[...].astype(BF)

        pl.when((has & jnp.logical_not(has_right)) if w < nw else has)(plain)
        if w:
            sends[w, b] = remote(slots.at[w, b], slots.at[w - 1, b], ring_send.at[w, b], ring_recv.at[w - 1, b], left)
            pl.when(has)(lambda cp=sends[w, b]: cp.start())
        for what in steps.get(i, []):
            what()
    for (w, b), cp in sends.items():
        pl.when(r >= w)(lambda cp=cp: cp.wait_send())
    ends()
    for cp in keeps:
        cp.wait()
    for cp in gives:
        cp.wait()


def back_call(fast, nw, nctx, qT, doT, oT, lse, lo, kv, lt, z, dh, o, out_own, g1_own, sums):
    seqs, n, length = qT.shape
    heads = n // HD
    width = g1_own.shape[-1]
    sds = jax.ShapeDtypeStruct
    ff = z.shape[-1]
    q4 = width // 4
    rows = q4 if fast else 8
    out_shape = [
        sds((seqs, n, length), F32),
        sds((seqs, 2 * n, length), BF),
        sds((rows, ff // 2), BF),
        sds((rows, ff // 2), BF),
        sds((rows, n), BF),
        sds(sums.shape[1:], F32),
        sds((seqs, length, width), BF),
        sds((seqs, length, width), BF),
    ]
    bq = min(256, length)
    dma = pltpu.SemaphoreType.DMA
    scratch = [
        pltpu.VMEM((nw + 1, seqs, 2 * n, length), BF),
        pltpu.VMEM((3, length, 2 * n), BF),
        pltpu.VMEM((seqs, heads, 128, length), BF),
        pltpu.VMEM((seqs, heads, 128, length), BF),
        pltpu.VMEM((n, length), BF),
        pltpu.VMEM((bq, bq), F32),
        pltpu.VMEM((n, length), F32),
        pltpu.VMEM((n, length), F32),
        pltpu.VMEM((seqs, 8, length), F32),
        dma((nw + 1, seqs)),
        dma((nw + 1, seqs)),
        dma((3,)),
        dma((2 * seqs,)),
        dma((2 * seqs,)),
        dma((2 * seqs,)),
    ]
    if fast:
        full = lambda cols: pltpu.VMEM((2, q4, cols), BF)
        scratch += [full(ff), full(ff), full(ff), pltpu.VMEM((q4, ff), BF), pltpu.VMEM((q4, ff // 2), BF)]
        for cols in (ff, 2 * n):
            scratch += [full(cols), full(cols), full(cols), full(cols // 2), pltpu.VMEM((q4, cols // 2), BF)]
        scratch += [pltpu.VMEM((6,) + sums.shape[1:], F32), dma((9,)), dma((9,)), dma((5,)), dma((5,))]
    return pl.pallas_call(
        functools.partial(back_kernel, fast, nw, nctx, heads, length),
        out_shape=tuple(out_shape),
        in_specs=[VMEM_SPEC] * 5 + [ANY_SPEC] + [VMEM_SPEC] * 4 + [ANY_SPEC] * 2 + [VMEM_SPEC],
        out_specs=tuple([VMEM_SPEC] * 6 + [ANY_SPEC] * 2),
        scratch_shapes=scratch,
        compiler_params=pltpu.CompilerParams(
            vmem_limit_bytes=62 * 1024 * 1024, collective_id=1, has_side_effects=True
        ),
        cost_estimate=pl.CostEstimate(
            flops=seqs * (nw + 1) * 10 * length * length * n, bytes_accessed=40 * 1024 * 1024, transcendentals=0
        ),
        name="attn_back",
    )(qT, doT, oT, lse, lo, kv, lt, z, dh, o, out_own, g1_own, sums)


def end_kernel(
    n, length,
    dq_ref, dkv_ref, w_ref, x_ref, g1_ref, aT_ref, gain_ref, p2_ref, p1_ref, po_ref,
    gt_ref, gq_ref, g2_ref, gu_ref, go_ref, total_ref,
    pT, pn, mine, peer, xh, rinv, sq, rq, wq, xq, zq, zq2, z2a, z2b, z1a, z1b, zoa, zob, vec_buf,
    da_send, da_recv, rs_send, rs_recv, vec_send, vec_recv,
):
    seqs = x_ref.shape[0]
    s, r, t = lax.axis_index("shard"), lax.axis_index("ctx"), lax.axis_index("tp")
    c, z = lax.rem(r, 2), r // 2
    lo_bit, hi_bit = lax.rem(z, 2), z // 2
    sib, ypeer, xpeer = {"ctx": r + 1 - 2 * c}, {"tp": 1 - t}, {"shard": 1 - s}
    zlo, zhi = {"ctx": r + 2 - 4 * lo_bit}, {"ctx": r + 4 - 8 * hi_bit}
    greet([(d, None) for d in (sib, ypeer, xpeer, zlo, zhi)])
    live = {}

    def send(name, src, dst, i, device):
        live[name] = remote(src, dst, rs_send.at[i], rs_recv.at[i], device)
        live[name].start()

    def add(dst, a, b):
        dst[...] = (a[...].astype(F32) + b[...].astype(F32)).astype(dst.dtype)

    groups = ((p2_ref, z2a, z2b, g2_ref), (p1_ref, z1a, z1b, gu_ref), (po_ref, zoa, zob, go_ref))
    for k, (part, za, zb, out) in enumerate(groups):
        send(("a", k), part.at[:, 1 - lo_bit], za, 2 * k, zlo)

    sums = [jnp.zeros((1, x_ref.shape[2]), F32) for _ in range(2)]
    bias = [jnp.zeros((1, n), F32) for _ in range(2)]
    exchange = []
    for b in range(seqs):
        pT[: n, :] = (dq_ref[b] * 0.125).astype(BF)
        pT[n:, :] = dkv_ref[b]
        for k in range(3 * n // 128):
            ks = slice(k * 128, (k + 1) * 128)
            pn[b, :, ks] = pT[ks, :].T
        da = dot_nt(pn[b, :, :n], w_ref[0])
        da = da + dot_nt(pn[b, :, n : 2 * n], w_ref[1])
        da = da + dot_nt(pn[b, :, 2 * n :], w_ref[2])
        mine[b] = da.astype(BF)
        exchange.append(remote(mine.at[b], peer.at[b], da_send.at[b], da_recv.at[b], ypeer))
        exchange[b].start()
        x = x_ref[b].astype(F32)
        cen = x - row_mean(x)
        inv = lax.rsqrt(row_mean(cen * cen) + EPS)
        rinv[b] = inv
        xh[b] = cen * inv
        sums[0] = sums[0] + col_sum(da * xh[b])
        sums[1] = sums[1] + col_sum(da)
        bias[0] = bias[0] + col_sum(pn[b, :, :n].astype(F32))
        bias[1] = bias[1] + col_sum(pn[b, :, 2 * n :].astype(F32))
    total_ref[...] = jnp.zeros_like(total_ref)
    total_ref[0:1, :] = sums[0]
    total_ref[1:2, :] = sums[1]
    total_ref[2:3, :n] = bias[0]
    total_ref[2:3, n:] = bias[1]
    partners = [sib, xpeer, zlo, zhi, ypeer]
    count = len(partners)

    def vec(stage):
        if stage:
            live[("v", stage - 1)].wait()
            if stage == count:
                total_ref[0:2, :] = total_ref[0:2, :] + vec_buf[stage - 1, 0:2, :]
            else:
                total_ref[...] = total_ref[...] + vec_buf[stage - 1]
        if stage < count:
            vec_buf[count] = total_ref[...]
            live[("v", stage)] = remote(
                vec_buf.at[count], vec_buf.at[stage], vec_send.at[stage], vec_recv.at[stage], partners[stage]
            )
            live[("v", stage)].start()

    vec(0)
    rows = aT_ref.shape[1] // 2

    def product(core, dst):
        at = pl.ds(pl.multiple_of(core * rows, 64), rows)
        for k in range(3):
            ks = slice(k * n, (k + 1) * n)
            acc = dot(aT_ref[0, at, :], pn[0, :, ks])
            for b in range(1, seqs):
                acc = acc + dot(aT_ref[b, at, :], pn[b, :, ks])
            acc = acc.astype(BF)
            for j in range(2):
                for i in range(4):
                    at_row = (j * 4 + i) * (rows // 8)
                    dst[j, i // 2, i % 2, :, ks] = acc[at_row : at_row + rows // 8]

    product(1 - c, sq)
    send("core", sq, rq, 6, sib)
    product(c, wq)
    vec(1)
    live["core"].wait_recv()
    add(wq.at[1 - s], wq.at[1 - s], rq.at[1 - s])
    send("x", wq.at[1 - s], xq, 7, xpeer)
    add(wq.at[s], wq.at[s], rq.at[s])
    for k, (part, za, zb, out) in enumerate(groups):
        live[("a", k)].wait_recv()
        add(za, part.at[:, lo_bit], za)
        send(("b", k), za.at[1 - hi_bit], zb, 2 * k + 1, zhi)
    vec(2)
    live["x"].wait_recv()
    add(wq.at[s], wq.at[s], xq)
    send("za", wq.at[s, :, 1 - lo_bit], zq, 8, zlo)
    vec(3)

    def finish(b):
        exchange[b].wait_recv()
        da = mine[b].astype(F32) + peer[b].astype(F32)
        e = da * gain_ref[...]
        h = xh[b]
        dx = rinv[b] * (e - row_mean(e) - h * row_mean(e * h))
        gt_ref[b] = (g1_ref[b].astype(F32) + dx).astype(BF)

    for b in range(seqs - 1):
        finish(b)
    live["za"].wait_recv()
    add(wq.at[s, :, lo_bit], wq.at[s, :, lo_bit], zq)
    send("zb", wq.at[s, 1 - hi_bit, lo_bit], zq2, 9, zhi)
    vec(4)
    for k, (part, za, zb, out) in enumerate(groups):
        live[("b", k)].wait_recv()
        add(out, za.at[hi_bit], zb)
    live["zb"].wait_recv()
    last = wq[s, hi_bit, lo_bit].astype(F32) + zq2[...].astype(F32)
    for k in range(3):
        gq_ref[k] = last[:, k * n : (k + 1) * n]
    vec(5)
    finish(seqs - 1)
    for key, cp in live.items():
        if not (isinstance(key, tuple) and key[0] == "v"):
            cp.wait_send()
    for cp in exchange:
        cp.wait_send()


def end_call(dq, dkv, w, x, g1, aT, gain, p2, p1, po):
    seqs, n, length = dq.shape
    width = x.shape[2]
    piece = width // 16
    sds = jax.ShapeDtypeStruct
    dma = pltpu.SemaphoreType.DMA
    c2, c1, co = p2.shape[-1], p1.shape[-1], po.shape[-1]
    return pl.pallas_call(
        functools.partial(end_kernel, n, length),
        out_shape=(
            sds((seqs, length, width), BF),
            sds((3, piece, n), F32),
            sds((piece, c2), F32),
            sds((piece, c1), F32),
            sds((piece, co), F32),
            sds((8, width), F32),
        ),
        in_specs=[VMEM_SPEC] * 10,
        out_specs=(VMEM_SPEC,) * 6,
        scratch_shapes=[
            pltpu.VMEM((3 * n, length), BF),
            pltpu.VMEM((seqs, length, 3 * n), BF),
            pltpu.VMEM((seqs, length, width), BF),
            pltpu.VMEM((seqs, length, width), BF),
            pltpu.VMEM((seqs, length, width), F32),
            pltpu.VMEM((seqs, length, 1), F32),
            pltpu.VMEM((2, 2, 2, piece, 3 * n), BF),
            pltpu.VMEM((2, 2, 2, piece, 3 * n), BF),
            pltpu.VMEM((2, 2, 2, piece, 3 * n), BF),
            pltpu.VMEM((2, 2, piece, 3 * n), BF),
            pltpu.VMEM((2, piece, 3 * n), BF),
            pltpu.VMEM((piece, 3 * n), BF),
            pltpu.VMEM((2, piece, c2), BF),
            pltpu.VMEM((piece, c2), BF),
            pltpu.VMEM((2, piece, c1), BF),
            pltpu.VMEM((piece, c1), BF),
            pltpu.VMEM((2, piece, co), BF),
            pltpu.VMEM((piece, co), BF),
            pltpu.VMEM((6, 8, width), F32),
            dma((seqs,)),
            dma((seqs,)),
            dma((10,)),
            dma((10,)),
            dma((5,)),
            dma((5,)),
        ],
        compiler_params=pltpu.CompilerParams(
            vmem_limit_bytes=56 * 1024 * 1024, collective_id=2, has_side_effects=True
        ),
        cost_estimate=pl.CostEstimate(
            flops=12 * seqs * length * width * n, bytes_accessed=16 * 1024 * 1024, transcendentals=0
        ),
        name="input_back",
    )(dq, dkv, w, x, g1, aT, gain, p2, p1, po)


def swap(value, axis):
    return lax.ppermute(value, axis, [(0, 1), (1, 0)])


def hop(value, bit):
    size = lax.axis_size("ctx")
    return lax.ppermute(value, "ctx", [(i, i ^ bit) for i in range(size)])


def shift(value, by):
    size = lax.axis_size("ctx")
    return lax.ppermute(value, "ctx", [(i, i + by) for i in range(size) if 0 <= i + by < size])


def ordered(own, peer, index, axis):
    first = jnp.where(index == 0, own, peer)
    second = jnp.where(index == 0, peer, own)
    return jnp.concatenate([first, second], axis)


def put(whole, piece, *start):
    return lax.dynamic_update_slice(whole, piece, start)


def gather_qkv(w, fast, s, c):
    if not fast:
        return lax.all_gather(w, "shard", axis=1, tiled=True)
    k, rows, cols = w.shape
    half = rows // 2
    mine = lax.dynamic_slice_in_dim(w, c * half, half, 1)
    far = swap(mine, "shard")
    rest = hop(far, 1)
    full = jnp.zeros((k, 2 * rows, cols), w.dtype)
    full = put(full, w, 0, s * rows, 0)
    full = put(full, far, 0, (1 - s) * rows + c * half, 0)
    return put(full, rest, 0, (1 - s) * rows + (1 - c) * half, 0)


def gather_ffn(w, fast, s, c, t):
    if not fast:
        w = lax.all_gather(w, "shard", axis=0, tiled=True)
        return lax.all_gather(w, "tp", axis=0)
    rows, cols = w.shape
    half = rows // 2
    mine = lax.dynamic_slice_in_dim(w, c * half, half, 0)
    near = swap(mine, "tp")
    far = swap(mine, "shard")
    both = swap(far, "tp")
    full = jnp.zeros((2, 2 * rows, cols), w.dtype)
    full = put(full, w[None], t, s * rows, 0)
    for piece, ti, si in ((far, t, 1 - s), (near, 1 - t, s), (both, 1 - t, 1 - s)):
        full = put(full, piece[None], ti, si * rows + c * half, 0)
        full = put(full, hop(piece, 1)[None], ti, si * rows + (1 - c) * half, 0)
    return full


def scatter_rows(grad, t=None):
    width, cols = grad.shape
    if t is not None:
        grad = lax.psum_scatter(grad.reshape(width, 2, cols // 2), "tp", scatter_dimension=1, tiled=False)
    return lax.psum_scatter(grad.astype(F32), ("shard", "ctx"), scatter_dimension=0, tiled=True)


def per_device(
    tokens,
    cotangent,
    segment_ids,
    w_qkv,
    w_out,
    w_fc1,
    w_fc2,
    norm_gain,
    norm_bias,
    head_gain,
    head_bias,
    ffn_gain,
    ffn_bias,
):
    seqs, length, width = tokens.shape
    n = w_qkv.shape[2]
    ff2 = w_fc1.shape[1]
    half = length // 2
    s, r, t = lax.axis_index("shard"), lax.axis_index("ctx"), lax.axis_index("tp")
    c = r % 2
    fast = lax.axis_size("shard") == 2 and lax.axis_size("ctx") == 8
    nw = min(-(-(MAXDOC - 1) // length), lax.axis_size("ctx") - 1)

    wqkv = gather_qkv(w_qkv.astype(BF), fast, s, c)
    small = jnp.concatenate([norm_gain, norm_bias]).astype(BF)
    if fast:
        small = ordered(small, swap(small, "shard"), s, 1)
    else:
        small = lax.all_gather(small, "shard", axis=1, tiled=True)
    small = small.astype(F32)
    gains, biases = small[:2], small[2:]
    vectors = jnp.concatenate([ffn_bias[0], ffn_gain, ffn_bias[1], head_gain, head_bias[2]])
    far = swap(vectors, "tp")
    v0, v1 = jnp.where(t == 0, vectors, far), jnp.where(t == 0, far, vectors)
    fvec = jnp.concatenate([v0[: 3 * ff2].reshape(3, ff2), v1[: 3 * ff2].reshape(3, ff2)], 1)
    hvec = jnp.concatenate([v0[3 * ff2 :].reshape(2, n), v1[3 * ff2 :].reshape(2, n)], 1)
    hg, hb = hvec[:1], hvec[1:]
    pack = jnp.concatenate([w_fc1.astype(BF), w_fc2.astype(BF).T, w_out.astype(BF).T], 1)
    fw = gather_ffn(pack, fast, s, c, t)
    vec = jnp.stack([gains[1], biases[1], biases[2], biases[3]])

    below = jnp.sum(segment_ids[:, None, :] < jnp.arange(1, 4, dtype=jnp.int32)[None, :, None], -1, dtype=jnp.int32)
    seg_q = lax.dynamic_slice_in_dim(segment_ids, r * length, length, 1)
    start = jnp.zeros_like(seg_q)
    for v in range(1, 4):
        start = jnp.where(seg_q == v, below[:, v - 1 : v], start)
    block = min(256, length)

    def bounds(b, w):
        lo = start[b] + (w - r) * length
        return jnp.concatenate([lo[::block], lo[block - 1 :: block]]), lo[None]

    acts, qTs, rings, states = [], [], [], []
    for b in range(seqs):
        a, qT, kv = qkv_call(fast, tokens[b], wqkv, gains[:1], biases[:1], head_bias[:1], head_bias[1:2])
        acts.append(a)
        qTs.append(qT)
        rings.append([kv])
        states.append(None)
    for w in range(nw):
        for b in range(seqs):
            rings[b].append(shift(rings[b][w], 1))
    for w in range(nw + 1):
        for b in range(seqs):
            sm, lo = bounds(b, w)
            states[b] = fwd_step(w, nw, sm, qTs[b], rings[b][w], lo, states[b])
    oT = jnp.stack([states[b][1] for b in range(seqs)])
    lse = jnp.stack([states[b][2] for b in range(seqs)])
    kv_all = jnp.stack([jnp.stack([rings[b][w] for b in range(seqs)]) for w in range(nw + 1)])
    qT_all = jnp.stack(qTs)

    def own_rows(value, index):
        return lax.dynamic_slice_in_dim(value, index * half, half, 0)

    doTs, mids = [], []
    for b in range(seqs):
        cen, _, _, mean = states[b]
        own, peer = own_rows(cen, t), swap(own_rows(cen, 1 - t), "tp")
        mrow = mean.reshape(length, 1)
        mown, mpeer = own_rows(mrow, t), swap(own_rows(mean[0], 1 - t), "tp").reshape(half, 1)
        first = t == 0
        c0, c1 = jnp.where(first, own, peer), jnp.where(first, peer, own)
        delta = jnp.where(first, mown - mpeer, mpeer - mown) * 0.5
        x, g = own_rows(tokens[b], t), own_rows(cotangent[b], t)
        mid = ffn_call(fast, c0, c1, delta, x, g, fw, hg, hb, vec, fvec)
        mids.append(mid + (g,))
        dat = mid[2]
        mine = lax.dynamic_slice_in_dim(dat, t * n, n, 1)
        theirs = lax.dynamic_slice_in_dim(dat, (1 - t) * n, n, 1)
        doTs.append(ordered(mine, swap(theirs, "tp"), t, 0).T)

    def stack(i):
        return jnp.stack([mids[b][i] for b in range(seqs)])

    out_own, g1_own, o, lt, z_act, dh = (stack(i) for i in (0, 1, 3, 4, 5, 6))
    sums = jnp.concatenate(
        [stack(7), stack(8), stack(9).reshape(seqs, -1, width), jnp.zeros((seqs, 6, width), F32)], 1
    )
    start3 = start[:, None, :]
    dq, dkv, part2, part1, parto, sums_all, out, g1 = back_call(
        fast, nw, lax.axis_size("ctx"), qT_all, jnp.stack(doTs), oT, lse, start3, kv_all,
        lt, z_act, dh, o, out_own, g1_own, sums,
    )

    def fold_rows(value):
        return value.reshape((-1,) + value.shape[2:])

    if fast:
        split = lambda part: part.reshape(2, 2, part.shape[0] // 4, part.shape[1])
        grad_tokens, grad_qkv, gd, gu, go, tails = end_call(
            dq, dkv, wqkv, tokens, g1, jnp.stack(acts), gains[:1], split(part2), split(part1), split(parto)
        )
        in_sums, bias_q, bias_v = tails[:2], tails[2, :n], tails[2, n:]
    else:
        outer = lambda left, right: lax.dot_general(
            fold_rows(left), fold_rows(right), (((0,), (0,)), ((), ())), preferred_element_type=F32
        ).astype(BF)
        g_own = stack(10)
        gd = scatter_rows(outer(g_own, z_act), t)
        gu = scatter_rows(outer(lt, dh), t)
        go = scatter_rows(outer(g1_own, o), t)
        sums_all = lax.psum(jnp.sum(sums, 0), ("shard", "ctx", "tp"))
        grad_tokens, in_sums, projs = [], 0.0, []
        for b in range(seqs):
            proj = jnp.concatenate([(dq[b].T * 0.125).astype(BF), dkv[b].T], 1)
            projs.append(proj)
            da = sum(dot_nt(proj[:, i * n : (i + 1) * n], wqkv[i]) for i in range(3)).astype(BF)
            gt, part = tail_call(da, swap(da, "tp"), tokens[b], g1[b], gains[:1])
            grad_tokens.append(gt)
            in_sums = in_sums + part
        grad_tokens = jnp.stack(grad_tokens)
        proj = jnp.concatenate(projs)
        grad_qkv = scatter_rows(outer(jnp.stack(acts), jnp.stack(projs))).reshape(-1, 3, n).transpose(1, 0, 2)
        tails = lax.psum(
            jnp.concatenate([in_sums.reshape(-1), jnp.sum(proj.astype(F32), 0)]), ("shard", "ctx")
        )
        in_sums, bias_q, bias_v = tails[: 2 * width].reshape(2, width), tails[2 * width :][:n], tails[-n:]

    hsum, dsum, fsum = sums_all[:2], sums_all[2:6], sums_all[6 : 6 + 6 * ff2 // width].reshape(3, 2 * ff2)
    piece = width // (lax.axis_size("shard") * lax.axis_size("ctx"))
    mine = (s * lax.axis_size("ctx") + r) * piece
    grad_gain = lax.dynamic_slice_in_dim(jnp.stack([in_sums[0], dsum[0]]), mine, piece, 1)
    grad_bias = lax.dynamic_slice_in_dim(jnp.stack([in_sums[1], dsum[1], dsum[2], dsum[3]]), mine, piece, 1)
    hsum = lax.dynamic_slice_in_dim(hsum, t * n, n, 1)
    fsum = lax.dynamic_slice_in_dim(fsum, t * ff2, ff2, 1)
    return (
        out,
        grad_tokens,
        grad_qkv,
        go.T,
        gu,
        gd.T,
        grad_gain,
        grad_bias,
        hsum[0],
        jnp.stack([bias_q, bias_v, hsum[1]]),
        fsum[1],
        jnp.stack([fsum[0], fsum[2]]),
    )


def solution(mesh):
    in_specs = (
        P("shard", "ctx", None),
        P("shard", "ctx", None),
        P("shard", None),
        P(None, "shard", "tp"),
        P("tp", "shard"),
        P("shard", "tp"),
        P("tp", "shard"),
        P(None, "shard"),
        P(None, "shard"),
        P("tp"),
        P(None, "tp"),
        P("tp"),
        P(None, "tp"),
    )
    out_specs = (
        P("shard", "ctx", None),
        P("shard", "ctx", None),
        P(None, ("shard", "ctx"), "tp"),
        P("tp", ("shard", "ctx")),
        P(("shard", "ctx"), "tp"),
        P("tp", ("shard", "ctx")),
        P(None, ("shard", "ctx")),
        P(None, ("shard", "ctx")),
        P("tp"),
        P(None, "tp"),
        P("tp"),
        P(None, "tp"),
    )
    return jax.shard_map(
        per_device, mesh=mesh, in_specs=in_specs, out_specs=out_specs, check_vma=False
    )
```

```python
import functools

import jax
import jax.numpy as jnp
from jax import lax
from jax.experimental import pallas as pl
from jax.experimental.pallas import tpu as pltpu
from jax.sharding import PartitionSpec as P

HD = 64
NEG = -1e30
VL = 48 * 1024 * 1024

EPS = 1e-05
MAXDOC = 1920
BF = jnp.bfloat16
F32 = jnp.float32
NT_DIMS = (((1,), (1,)), ((), ()))
VMEM_SPEC = pl.BlockSpec(memory_space=pltpu.VMEM)
ANY_SPEC = pl.BlockSpec(memory_space=pl.ANY)
GELU_C = 0.7978845608028654
GELU_A = 0.044715


def dot(left, right):
    return jnp.dot(left, right, preferred_element_type=F32)


def dot_nt(left, right):
    return lax.dot_general(left, right, NT_DIMS, preferred_element_type=F32)


def row_mean(values):
    return jnp.mean(values, -1, keepdims=True)


def col_sum(values):
    return jnp.sum(values, 0, keepdims=True)


def put_transposed(value, dst, tmp):
    width = value.shape[1]
    for k in range(width // 128):
        tmp[k * 128 : (k + 1) * 128, :] = value[:, k * 128 : (k + 1) * 128].T
    piece = width // 16
    for shard in range(2):
        for z in range(4):
            for core in range(2):
                to = core * (width // 2) + shard * (width // 4) + z * piece
                at = shard * (width // 2) + (z * 2 + core) * piece
                dst[to : to + piece, :] = tmp[at : at + piece, :]


def gelu_pair(h):
    inner = GELU_C * (h + GELU_A * h * h * h)
    t = jnp.tanh(inner)
    half = 0.5 * (1.0 + t)
    slope = half + 0.5 * h * (1.0 - t * t) * (GELU_C * (1.0 + (3.0 * GELU_A) * h * h))
    return h * half, slope


def tail_kernel(own_ref, peer_ref, x_ref, g1_ref, gain_ref, out_ref, sum_ref):
    da = own_ref[...].astype(F32) + peer_ref[...].astype(F32)
    x = x_ref[...].astype(F32)
    cen = x - row_mean(x)
    r = lax.rsqrt(row_mean(cen * cen) + EPS)
    xh = cen * r
    sum_ref[0:1, :] = col_sum(da * xh)
    sum_ref[1:2, :] = col_sum(da)
    e = da * gain_ref[...]
    dx = r * (e - row_mean(e) - xh * row_mean(e * xh))
    out_ref[...] = (g1_ref[...].astype(F32) + dx).astype(BF)


def tail_call(own, peer, x, g1, gain):
    rows, width = x.shape
    return pl.pallas_call(
        tail_kernel,
        out_shape=(jax.ShapeDtypeStruct((rows, width), BF), jax.ShapeDtypeStruct((2, width), F32)),
        in_specs=[VMEM_SPEC] * 5,
        out_specs=(VMEM_SPEC, VMEM_SPEC),
        compiler_params=pltpu.CompilerParams(vmem_limit_bytes=VL),
        cost_estimate=pl.CostEstimate(
            flops=20 * rows * width, bytes_accessed=10 * rows * width, transcendentals=rows
        ),
        name="tail",
    )(own, peer, x, g1, gain)


MESH_ID = pl.DeviceIdType.MESH


def remote(src, dst, send, recv, device):
    return pltpu.make_async_remote_copy(
        src_ref=src, dst_ref=dst, send_sem=send, recv_sem=recv, device_id=device, device_id_type=MESH_ID
    )


def greet(devices):
    sem = pltpu.get_barrier_semaphore()
    count = 0
    for device, cond in devices:
        def signal(device=device):
            pl.semaphore_signal(sem, inc=1, device_id=device, device_id_type=MESH_ID)
        if cond is None:
            signal()
            count = count + 1
        else:
            pl.when(cond)(signal)
            count = count + cond.astype(jnp.int32)
    pl.semaphore_wait(sem, count)


def chunk_blocks(w, length, bq, bk):
    found = []
    for kb in range(length // bk):
        for qb in range(length // bq):
            if w == 0 and kb * bk > qb * bq + bq - 1:
                continue
            if qb * bq + w * length - (MAXDOC - 1) > kb * bk + bk - 1:
                continue
            found.append((qb, kb))
    return found


def block_bias(w, lo, qb, kb, bq, bk):
    key = lax.broadcasted_iota(jnp.int32, (bk, bq), 0) + kb * bk
    seen = key >= lo[:, qb * bq : (qb + 1) * bq]
    if w == 0 and (kb + 1) * bk > qb * bq + 1:
        seen = seen & (key <= lax.broadcasted_iota(jnp.int32, (bk, bq), 1) + qb * bq)
    return jnp.where(seen, 0.0, NEG)


def split_pairs(src, dst, heads):
    row = lax.broadcasted_iota(jnp.int32, (2 * HD, src.shape[1]), 0)
    for p in range(heads // 2):
        block = src[p * 128 : (p + 1) * 128, :]
        dst[2 * p] = jnp.where(row < HD, block, jnp.zeros_like(block))
        dst[2 * p + 1] = jnp.where(row >= HD, block, jnp.zeros_like(block))


def back_item(w, heads, length, bq, bk, kv, qT, doT, qm, dm, kT, lse, dd, lo, bias, dq, dk, dv):
    n = heads * HD
    for p in range(heads // 2):
        ps = slice(p * 128, (p + 1) * 128)
        kT[ps, :] = kv[:, ps].T
    blocks = chunk_blocks(w, length, bq, bk)
    for kb in range(length // bk):
        ks = slice(kb * bk, (kb + 1) * bk)
        mine = [qb for qb, other in blocks if other == kb]
        if not mine:
            dk[:, ks] = jnp.zeros((n, bk), F32)
            dv[:, ks] = jnp.zeros((n, bk), F32)
        for turn, qb in enumerate(mine):
            qs = slice(qb * bq, (qb + 1) * bq)
            bias[...] = block_bias(w, lo, qb, kb, bq, bk)

            def scores(h):
                ps = slice((h // 2) * 128, (h // 2 + 1) * 128)
                pv = slice(n + (h // 2) * 128, n + (h // 2 + 1) * 128)
                return dot(kv[ks, ps], qm[h, :, qs]) + bias[...], dot(kv[ks, pv], dm[h, :, qs])

            ahead = scores(0)
            for h in range(heads):
                hs = slice(h * HD, (h + 1) * HD)
                s, dp = ahead
                ahead = scores(h + 1) if h + 1 < heads else None
                e = jnp.exp(s - lse[h : h + 1, qs])
                ds = (e * (dp - dd[h : h + 1, qs])).astype(BF)
                new_v = dot_nt(doT[hs, qs], e.astype(BF))
                new_k = dot_nt(qT[hs, qs], ds)
                if turn:
                    dv[hs, ks] += new_v
                    dk[hs, ks] += new_k
                else:
                    dv[hs, ks] = new_v
                    dk[hs, ks] = new_k
                dq[hs, qs] += dot(kT[hs, ks], ds)


def back_kernel(
    fast, nw, nctx, heads, length,
    qT_ref, doT_ref, oT_ref, lse_ref, lo_ref, kv_hbm, lt_ref, z_ref, dh_ref, o_ref, out_own, g1_own, sum_ref,
    dq_ref, dkv_ref, part2_ref, part1_ref, parto_ref, total_ref, out_ref, g1_ref,
    slots, kvbuf, qm, dm, kT, bias, dk, dv, dd,
    ring_send, ring_recv, kv_sem, *rs,
):
    n = heads * HD
    bq = bk = min(256, length)
    s, r, t = lax.axis_index("shard"), lax.axis_index("ctx"), lax.axis_index("tp")
    c = lax.rem(r, 2)
    sib = {"ctx": r + 1 - 2 * c}
    left, right = {"ctx": r - 1}, {"ctx": r + 1}
    has_left, has_right = r > 0, r < nctx - 1
    half = length // 2
    people = [(left, has_left), (right, has_right), ({"tp": 1 - t}, None)]
    if fast:
        ypeer, xpeer = {"tp": 1 - t}, {"shard": 1 - s}
        z2 = lax.rem(r // 2, 2)
        people += [(xpeer, None)]
        people += [({"ctx": r + 2 - 4 * z2}, None)]
        hop4 = lax.rem(r // 4, 2)
        people += [({"ctx": r + 4 - 8 * hop4}, None)]
    greet(people)

    seqs = qT_ref.shape[0]
    items = [(w, b) for w in range(nw, -1, -1) for b in range(seqs)]
    nbuf = kvbuf.shape[0]

    def load(i):
        w, b = items[i]
        return pltpu.make_async_copy(kv_hbm.at[w, b], kvbuf.at[i % nbuf], kv_sem.at[i % nbuf])

    def start_load(i):
        if i < len(items):
            pl.when(r >= items[i][0])(lambda: load(i).start())

    for i in range(nbuf - 1):
        start_load(i)

    own_sem, give_send, give_recv = rs[:3]
    rs = rs[3:]
    gives, keeps = [], []
    for k, (src, dst) in enumerate(((g1_own, g1_ref), (out_own, out_ref))):
        for b in range(seqs):
            rows = pl.ds(pl.multiple_of(t * half, half), half)
            keeps.append(pltpu.make_async_copy(src.at[b], dst.at[b, rows], own_sem.at[k * seqs + b]))
            gives.append(
                remote(src.at[b], dst.at[b, rows], give_send.at[k * seqs + b], give_recv.at[k * seqs + b], {"tp": 1 - t})
            )
    for cp in keeps:
        cp.start()

    for b in range(seqs):
        split_pairs(qT_ref.at[b], qm.at[b], heads)
        split_pairs(doT_ref.at[b], dm.at[b], heads)
        for h in range(heads):
            hs = slice(h * HD, (h + 1) * HD)
            dd[b, h : h + 1, :] = col_sum(doT_ref[b, hs, :].astype(F32) * oT_ref[b, hs, :])
        dq_ref[b] = jnp.zeros((n, length), F32)

    steps = {}
    if fast:
        (s2, r2, w2, x2, y2, s1, r1, w1, y1, x1, so, ro, wo, yo, xo, vec_buf, rs_send, rs_recv, vec_send, vec_recv) = rs
        step = 512

        def product(g, rhs, core, dst):
            cols = rhs.shape[2]
            size = step if cols % step == 0 else cols // 2
            rows = pl.ds(pl.multiple_of(core * (lt_ref.shape[2] // 2), 64), lt_ref.shape[2] // 2)

            def body(j, carry):
                at = pl.ds(pl.multiple_of(j * size, size), size)
                acc = dot(lt_ref[0, g, rows, :], rhs[0, :, at])
                for b in range(1, seqs):
                    acc = acc + dot(lt_ref[b, g, rows, :], rhs[b, :, at])
                mid = acc.shape[0] // 2
                acc = acc.astype(BF)
                dst[0, :, at] = acc[:mid]
                dst[1, :, at] = acc[mid:]
                return carry

            lax.fori_loop(0, cols // size, body, 0)

        def add(dst, a, b):
            dst[...] = (a[...].astype(F32) + b[...].astype(F32)).astype(BF)

        live = {}

        def send(name, src, dst, i, device):
            live[name] = remote(src, dst, rs_send.at[i], rs_recv.at[i], device)
            live[name].start()

        def cols_of(ref, index):
            width = ref.shape[-1] // 2
            return pl.ds(pl.multiple_of(index * width, 128), width)

        def first(g, rhs, sbuf, rbuf, i):
            product(g, rhs, 1 - c, sbuf)
            send(("core", g), sbuf, rbuf, i, sib)

        def x_then_y(stage):
            if stage == 0:
                first(0, z_ref, s2, r2, 0)
            elif stage == 1:
                product(0, z_ref, c, w2)
            elif stage == 2:
                live[("core", 0)].wait_recv()
                add(w2.at[1 - s], w2.at[1 - s], r2.at[1 - s])
                send("x2", w2.at[1 - s], x2, 1, xpeer)
                add(w2.at[s], w2.at[s], r2.at[s])
            elif stage == 3:
                live["x2"].wait_recv()
                add(w2.at[s], w2.at[s], x2)
                send("y2", w2.at[s, :, cols_of(w2, 1 - t)], y2, 2, ypeer)
            elif stage == 4:
                live["y2"].wait_recv()
                add(part2_ref, w2.at[s, :, cols_of(w2, t)], y2)

        def y_then_x(stage, g, rhs, sb, rb, wb, yb, xb, part, i):
            if stage == 0:
                first(g, rhs, sb, rb, i)
            elif stage == 1:
                product(g, rhs, c, wb)
            elif stage == 2:
                live[("core", g)].wait_recv()
                for k in range(2):
                    add(wb.at[k], wb.at[k], rb.at[k])
                send(("y", g), wb.at[:, :, cols_of(wb, 1 - t)], yb, i + 1, ypeer)
            elif stage == 3:
                live[("y", g)].wait_recv()
                mine = cols_of(wb, t)
                add(wb.at[1 - s, :, mine], wb.at[1 - s, :, mine], yb.at[1 - s])
                send(("x", g), wb.at[1 - s, :, mine], xb, i + 2, xpeer)
                add(wb.at[s, :, mine], wb.at[s, :, mine], yb.at[s])
            elif stage == 4:
                live[("x", g)].wait_recv()
                add(part, wb.at[s, :, cols_of(wb, t)], xb)

        up = lambda stage: y_then_x(stage, 1, dh_ref, s1, r1, w1, y1, x1, part1_ref, 3)
        op = lambda stage: y_then_x(stage, 2, o_ref, so, ro, wo, yo, xo, parto_ref, 6)

        partners = [ypeer, xpeer, sib, {"ctx": r + 2 - 4 * z2}, {"ctx": r + 4 - 8 * hop4}]
        count = vec_buf.shape[0] - 1

        def vec(stage):
            if stage == 0:
                acc = sum_ref[0]
                for b in range(1, sum_ref.shape[0]):
                    acc = acc + sum_ref[b]
                total_ref[...] = acc
            else:
                live[("v", stage - 1)].wait()
                total_ref[...] = total_ref[...] + vec_buf[stage - 1]
            if stage < len(partners):
                vec_buf[count] = total_ref[...]
                live[("v", stage)] = remote(
                    vec_buf.at[count], vec_buf.at[stage], vec_send.at[stage], vec_recv.at[stage], partners[stage]
                )
                live[("v", stage)].start()

        plan = [
            [lambda: up(0), lambda: vec(0)],
            [lambda: up(1), lambda: x_then_y(0)],
            [lambda: up(2), lambda: x_then_y(1), lambda: vec(1)],
            [lambda: x_then_y(2), lambda: op(0), lambda: op(1), lambda: [cp.start() for cp in gives]],
            [lambda: op(2), lambda: vec(2)],
            [lambda: vec(3)],
            [lambda: up(3), lambda: vec(4)],
            [lambda: x_then_y(3), lambda: vec(5)],
            [lambda: op(3)],
            [lambda: up(4), lambda: op(4), lambda: x_then_y(4)],
        ]
        for i, what in enumerate(plan):
            steps.setdefault(min(i, len(items) - 1), []).extend(what)
        ends = lambda: [cp.wait_send() for key, cp in live.items() if not (isinstance(key, tuple) and key[0] == "v")]
    else:
        steps[0] = [lambda: [cp.start() for cp in gives]]
        ends = lambda: None

    sends = {}
    for i, (w, b) in enumerate(items):
        start_load(i + nbuf - 1)
        slot = slots.at[w, b]
        has = r >= w

        def work(i=i, w=w, b=b):
            load(i).wait()
            back_item(
                w, heads, length, bq, bk, kvbuf.at[i % nbuf], qT_ref.at[b], doT_ref.at[b], qm.at[b], dm.at[b], kT,
                lse_ref.at[b], dd.at[b], lo_ref[b] + (w - r) * length, bias, dq_ref.at[b], dk, dv,
            )

        pl.when(has)(work)
        dest = slots.at[w, b] if w else dkv_ref.at[b]
        if w < nw:
            arrived = remote(slots.at[w, b], slots.at[w, b], ring_send.at[w, b], ring_recv.at[w, b], left)

            def merge(w=w, b=b, dest=dest, arrived=arrived):
                arrived.wait_recv()
                dest[:n, :] = (dk[...] + slots[w, b, :n, :].astype(F32)).astype(BF)
                dest[n:, :] = (dv[...] + slots[w, b, n:, :].astype(F32)).astype(BF)

            pl.when(has & has_right)(merge)

        def plain(dest=dest):
            dest[:n, :] = dk[...].astype(BF)
            dest[n:, :] = dv[...].astype(BF)

        pl.when((has & jnp.logical_not(has_right)) if w < nw else has)(plain)
        if w:
            sends[w, b] = remote(slots.at[w, b], slots.at[w - 1, b], ring_send.at[w, b], ring_recv.at[w - 1, b], left)
            pl.when(has)(lambda cp=sends[w, b]: cp.start())
        for what in steps.get(i, []):
            what()
    for (w, b), cp in sends.items():
        pl.when(r >= w)(lambda cp=cp: cp.wait_send())
    ends()
    for cp in keeps:
        cp.wait()
    for cp in gives:
        cp.wait()


def back_call(fast, nw, nctx, qT, doT, oT, lse, lo, kv, lt, z, dh, o, out_own, g1_own, sums):
    seqs, n, length = qT.shape
    heads = n // HD
    width = g1_own.shape[-1]
    sds = jax.ShapeDtypeStruct
    ff = z.shape[-1]
    q4 = width // 4
    rows = q4 if fast else 8
    out_shape = [
        sds((seqs, n, length), F32),
        sds((seqs, 2 * n, length), BF),
        sds((rows, ff // 2), BF),
        sds((rows, ff // 2), BF),
        sds((rows, n), BF),
        sds(sums.shape[1:], F32),
        sds((seqs, length, width), BF),
        sds((seqs, length, width), BF),
    ]
    bq = min(256, length)
    dma = pltpu.SemaphoreType.DMA
    scratch = [
        pltpu.VMEM((nw + 1, seqs, 2 * n, length), BF),
        pltpu.VMEM((3, length, 2 * n), BF),
        pltpu.VMEM((seqs, heads, 128, length), BF),
        pltpu.VMEM((seqs, heads, 128, length), BF),
        pltpu.VMEM((n, length), BF),
        pltpu.VMEM((bq, bq), F32),
        pltpu.VMEM((n, length), F32),
        pltpu.VMEM((n, length), F32),
        pltpu.VMEM((seqs, 8, length), F32),
        dma((nw + 1, seqs)),
        dma((nw + 1, seqs)),
        dma((3,)),
        dma((2 * seqs,)),
        dma((2 * seqs,)),
        dma((2 * seqs,)),
    ]
    if fast:
        full = lambda cols: pltpu.VMEM((2, q4, cols), BF)
        scratch += [full(ff), full(ff), full(ff), pltpu.VMEM((q4, ff), BF), pltpu.VMEM((q4, ff // 2), BF)]
        for cols in (ff, 2 * n):
            scratch += [full(cols), full(cols), full(cols), full(cols // 2), pltpu.VMEM((q4, cols // 2), BF)]
        scratch += [pltpu.VMEM((6,) + sums.shape[1:], F32), dma((9,)), dma((9,)), dma((5,)), dma((5,))]
    return pl.pallas_call(
        functools.partial(back_kernel, fast, nw, nctx, heads, length),
        out_shape=tuple(out_shape),
        in_specs=[VMEM_SPEC] * 5 + [ANY_SPEC] + [VMEM_SPEC] * 4 + [ANY_SPEC] * 2 + [VMEM_SPEC],
        out_specs=tuple([VMEM_SPEC] * 6 + [ANY_SPEC] * 2),
        scratch_shapes=scratch,
        compiler_params=pltpu.CompilerParams(
            vmem_limit_bytes=62 * 1024 * 1024, collective_id=1, has_side_effects=True
        ),
        cost_estimate=pl.CostEstimate(
            flops=seqs * (nw + 1) * 10 * length * length * n, bytes_accessed=40 * 1024 * 1024, transcendentals=0
        ),
        name="attn_back",
    )(qT, doT, oT, lse, lo, kv, lt, z, dh, o, out_own, g1_own, sums)


def forward_item(w, first, heads, length, bq, kv, qm, vT, lo, bias, m, l, acc):
    n = heads * HD
    for p in range(heads // 2):
        ps = slice(p * 128, (p + 1) * 128)
        vT[ps, :] = kv[:, n + p * 128 : n + (p + 1) * 128].T
    blocks = chunk_blocks(w, length, bq, min(256, length))
    size = min(256, length)
    for qb in range(length // bq):
        mine = [kb for q, kb in blocks if q == qb]
        if not mine:
            continue
        k0, k1 = min(mine) * size, (max(mine) + 1) * size
        qs, ks = slice(qb * bq, (qb + 1) * bq), slice(k0, k1)
        key = lax.broadcasted_iota(jnp.int32, (k1 - k0, bq), 0) + k0
        seen = key >= lo[:, qs]
        if w == 0:
            seen = seen & (key <= lax.broadcasted_iota(jnp.int32, (k1 - k0, bq), 1) + qb * bq)
        bias[: k1 - k0, :] = jnp.where(seen, 0.0, NEG)

        def scores(h):
            ps = slice((h // 2) * 128, (h // 2 + 1) * 128)
            return dot(kv[ks, ps], qm[h, :, qs]) + bias[: k1 - k0, :]

        ahead = scores(0)
        for h in range(heads):
            hs = slice(h * HD, (h + 1) * HD)
            s = ahead
            ahead = scores(h + 1) if h + 1 < heads else None
            if first:
                top = jnp.max(s, 0, keepdims=True)
                e = jnp.exp(s - top)
                l[h : h + 1, qs] = jnp.sum(e, 0, keepdims=True)
                acc[hs, qs] = dot(vT[hs, ks], e.astype(BF))
            else:
                old = m[h : h + 1, qs]
                top = jnp.maximum(old, jnp.max(s, 0, keepdims=True))
                e = jnp.exp(s - top)
                scale = jnp.exp(old - top)
                l[h : h + 1, qs] = l[h : h + 1, qs] * scale + jnp.sum(e, 0, keepdims=True)
                acc[hs, qs] = acc[hs, qs] * scale + dot(vT[hs, ks], e.astype(BF))
            m[h : h + 1, qs] = top


def front_kernel(
    fast, nw, nctx, heads, length,
    x_ref, wq_ref, small_ref, qb_ref, vb_ref, lo_ref, w1_hbm, w2_hbm, wo_hbm,
    aT_ref, qT_ref, oT_ref, lse_ref, cown_ref, cpeer_ref, mown_ref, mpeer_ref, wfull_ref, norms_ref, kv_hbm,
    f1_hbm, f2_hbm, fo_hbm,
    slots, kvbuf, qm, vT, bias, m, l, acc, cen, mean, tmp, norms,
    ring_send, ring_recv, side_send, side_recv, kv_sem, c_send, c_recv, *rs,
):
    n = heads * HD
    seqs, _, width = x_ref.shape
    half = length // 2
    bq = min(256, length)
    s, r, t = lax.axis_index("shard"), lax.axis_index("ctx"), lax.axis_index("tp")
    c = lax.rem(r, 2)
    even, odd = c == 0, c == 1
    left, right = {"ctx": r - 1}, {"ctx": r + 1}
    has_left, has_right = r > 0, r < nctx - 1
    ypeer, xpeer, sib = {"tp": 1 - t}, {"shard": 1 - s}, {"ctx": r + 1 - 2 * c}
    people = [(left, has_left), (right, has_right), (ypeer, None)]
    if fast:
        people.append((xpeer, None))
    greet(people)

    live = {}
    if fast:
        w_send, w_recv, f_send, f_recv, own_sem = rs
        rows = wq_ref.shape[1]
        part = rows // 2
        wcols = lambda shard, core: pl.ds(pl.multiple_of(shard * rows + core * part, 64), part)
        live["norms"] = remote(small_ref, norms.at[s], w_send.at[0], w_recv.at[0], xpeer)
        live["norms"].start()
        live["wq"] = remote(
            wq_ref.at[:, pl.ds(pl.multiple_of(c * part, 64), part)], wfull_ref.at[:, wcols(s, c)],
            w_send.at[1], w_recv.at[1], xpeer,
        )
        live["wq"].start()
        owns = [pltpu.make_async_copy(wq_ref, wfull_ref.at[:, pl.ds(pl.multiple_of(s * rows, 128), rows)], own_sem.at[0])]
        owns[0].start()
        norms[s] = small_ref[...]

        def region(k, tp, shard, core=None):
            if k == 1:
                size = w1_hbm.shape[0]
                at = pl.ds(pl.multiple_of(shard * size, 128), size)
                if core is not None:
                    at = pl.ds(pl.multiple_of(shard * size + core * (size // 2), 64), size // 2)
                return f1_hbm.at[tp, at]
            ref, src = ((fo_hbm, wo_hbm), None, (f2_hbm, w2_hbm))[k]
            size, cols = src.shape
            at = pl.ds(pl.multiple_of(shard * cols, 128), cols)
            if core is None:
                return ref.at[tp, :, at]
            return ref.at[tp, pl.ds(pl.multiple_of(core * (size // 2), 64), size // 2), at]

        sources = (wo_hbm, w1_hbm, w2_hbm)

        def half_of(k):
            size = sources[k].shape[0] // 2
            return sources[k].at[pl.ds(pl.multiple_of(c * size, 64), size)]

        def send(kind, k, src, tp, shard, device):
            live[kind, k] = remote(src, region(k, tp, shard, c), f_send.at[kind, k], f_recv.at[kind, k], device)
            live[kind, k].start()

        def weights_first():
            for k in range(3):
                send(0, k, half_of(k), t, s, ypeer)
                send(1, k, half_of(k), t, s, xpeer)
            for k in range(3):
                owns.append(pltpu.make_async_copy(sources[k], region(k, t, s), own_sem.at[1 + k]))
                owns[-1].start()

        def from_y(k):
            live[0, k].wait_recv()
            send(2, k, region(k, 1 - t, s, c), 1 - t, s, xpeer)
            send(3, k, region(k, 1 - t, s, c), 1 - t, s, sib)

        def from_x(k):
            live[1, k].wait_recv()
            send(4, k, region(k, t, 1 - s, c), t, 1 - s, sib)

        def from_diagonal(k):
            live[2, k].wait_recv()
            send(5, k, region(k, 1 - t, 1 - s, c), 1 - t, 1 - s, sib)

        live["norms"].wait_recv()
    else:
        norms[...] = small_ref[...]
        wfull_ref[...] = wq_ref[...]
    norms_ref[...] = jnp.concatenate([norms[0], norms[1]], 1)

    gain, shift = norms_ref[0:1, :].astype(F32), norms_ref[2:3, :].astype(F32)
    my_half = pl.ds(pl.multiple_of(t * half, 128), half)

    def pass_on(w, b):
        if w == nw:
            return []
        across = remote(
            slots.at[w, b, my_half], slots.at[w + 1, b, my_half], ring_send.at[w, b], ring_recv.at[w + 1, b], right
        )
        inside = remote(slots.at[w, b], slots.at[w + 1, b], ring_send.at[w, b], ring_recv.at[w + 1, b], right)
        has = r >= w
        cond = has & has_right
        pl.when(cond & odd)(lambda: across.start())
        pl.when(cond & even)(lambda: inside.start())
        return [(cond & odd, across), (cond & even, inside)]

    sent = []
    for b in range(seqs):
        x = x_ref[b].astype(F32)
        d = x - row_mean(x)
        a = (d * lax.rsqrt(row_mean(d * d) + EPS) * gain + shift).astype(BF)
        slots[0, b] = a
        sent += pass_on(0, b)
    if fast:
        weights_first()

    def side(w, b):
        return remote(slots.at[w, b, my_half], slots.at[w, b, my_half], side_send.at[w, b], side_recv.at[w, b], ypeer)

    def arrive(w):
        has = r >= w
        for b in range(seqs):
            def take(b=b):
                got = remote(
                    slots.at[w, b, my_half], slots.at[w, b, my_half], ring_send.at[w, b], ring_recv.at[w, b], left
                )
                got.wait_recv()
                side(w, b).start()

            pl.when(has & even)(take)
        for b in range(seqs):
            def whole(b=b):
                remote(slots.at[w, b], slots.at[w, b], ring_send.at[w, b], ring_recv.at[w, b], left).wait_recv()

            pl.when(has & even)(lambda b=b: side(w, b).wait_recv())
            pl.when(has & odd)(whole)
            sent.extend(pass_on(w, b))
            sent.append((has & even, side(w, b)))

    if nw >= 1:
        arrive(1)
    for b in range(seqs):
        put_transposed(slots[0, b], aT_ref.at[b], tmp) if fast else aT_ref.__setitem__(b, slots[0, b])
    if fast:
        live["wq"].wait_recv()
        far = wcols(1 - s, c)
        live["wsib"] = remote(wfull_ref.at[:, far], wfull_ref.at[:, far], w_send.at[2], w_recv.at[2], sib)
        live["wsib"].start()
        owns[0].wait()
        live["wsib"].wait_recv()

    plan = {}
    if fast:
        plan = {
            (0, seqs - 1): [lambda: from_y(0), lambda: from_y(1)],
            (1, 0): [lambda: from_y(2)],
            (1, seqs - 1): [lambda: from_x(0)],
            (2, 0): [lambda: from_x(1)],
            (2, seqs - 1): [lambda: from_x(2)],
            (3, seqs - 1): [lambda: from_diagonal(0)],
        }
    items = [(w, b) for w in range(nw + 1) for b in range(seqs)]
    nbuf = kvbuf.shape[0]

    def store(i):
        w, b = items[i]
        return pltpu.make_async_copy(kvbuf.at[i % nbuf], kv_hbm.at[w, b], kv_sem.at[i % nbuf])

    exchanges = []
    for i, (w, b) in enumerate(items):
        if b == 0 and 1 < w + 1 <= nw:
            arrive(w + 1)
        has = r >= w
        if i >= nbuf:
            pl.when(r >= items[i - nbuf][0])(lambda i=i: store(i - nbuf).wait())

        def work(i=i, w=w, b=b):
            a = slots[w, b]
            buf = kvbuf.at[i % nbuf]
            if w == 0:
                q = (dot(a, wfull_ref[0]) + qb_ref[...]).astype(BF).astype(F32) * 0.125
                for p in range(heads // 2):
                    ps = slice(p * 128, (p + 1) * 128)
                    qT_ref[b, ps, :] = q[:, ps].T.astype(BF)
                split_pairs(qT_ref.at[b], qm.at[b], heads)
            buf[:, :n] = dot(a, wfull_ref[1]).astype(BF)
            buf[:, n:] = (dot(a, wfull_ref[2]) + vb_ref[...]).astype(BF)
            store(i).start()
            forward_item(
                w, w == 0, heads, length, bq, buf, qm.at[b], vT, lo_ref[b] + (w - r) * length, bias,
                m.at[b], l.at[b], acc.at[b],
            )

        if w:
            pl.when(has)(work)
        else:
            work()
        for what in plan.get((w, b), []):
            what()
        if w == nw:
            tot = jnp.zeros((1, length), F32)
            for h in range(heads):
                hs = slice(h * HD, (h + 1) * HD)
                o = acc[b, hs, :] / l[b, h : h + 1, :]
                oT_ref[b, hs, :] = o
                tot = tot + col_sum(o)
            tot = tot / n
            mean[b] = tot
            lse_ref[b] = m[b] + jnp.log(l[b])
            for p in range(heads // 2):
                ps = slice(p * 128, (p + 1) * 128)
                cen[b, :, ps] = (oT_ref[b, ps, :] - tot).T.astype(BF)
            theirs = pl.ds(pl.multiple_of((1 - t) * half, 128), half)
            for k, (src, dst) in enumerate(
                ((cen.at[b, theirs], cpeer_ref.at[b]), (mean.at[b, :, theirs], mpeer_ref.at[b]))
            ):
                exchanges.append(remote(src, dst, c_send.at[b, k], c_recv.at[b, k], ypeer))
                exchanges[-1].start()
            cown_ref[b] = cen[b, my_half, :]
            mown_ref[b] = mean[b, :, my_half]
    for cond, cp in sent:
        pl.when(cond)(lambda cp=cp: cp.wait_send())
    for i in range(max(0, len(items) - nbuf), len(items)):
        pl.when(r >= items[i][0])(lambda i=i: store(i).wait())
    if fast:
        from_diagonal(1)
        from_diagonal(2)
        for k in range(3):
            for kind in (3, 4, 5):
                live[kind, k].wait_recv()
            for kind in range(6):
                live[kind, k].wait_send()
        for cp in owns[1:]:
            cp.wait()
        for key in ("norms", "wq", "wsib"):
            live[key].wait_send()
    for cp in exchanges:
        cp.wait()


def front_call(fast, nw, nctx, x, wq, small, qb, vb, lo, w1, w2, wo):
    seqs, length, width = x.shape
    n = qb.shape[1]
    heads = n // HD
    half = length // 2
    sds = jax.ShapeDtypeStruct
    dma = pltpu.SemaphoreType.DMA
    bq = min(256, length)
    full = lambda w, axes: sds((2,) + tuple(k * a for k, a in zip(w.shape, axes)), BF) if fast else sds((8, 128), BF)
    out_shape = (
        sds((seqs, width, length) if fast else (seqs, length, width), BF),
        sds((seqs, n, length), BF),
        sds((seqs, n, length), F32),
        sds((seqs, 8, length), F32),
        sds((seqs, half, n), BF),
        sds((seqs, half, n), BF),
        sds((seqs, 1, half), F32),
        sds((seqs, 1, half), F32),
        sds((3, width, n), BF),
        sds((16, width), BF),
        sds((nw + 1, seqs, length, 2 * n), BF),
        full(w1, (2, 1)),
        full(w2, (1, 2)),
        full(wo, (1, 2)),
    )
    scratch = [
        pltpu.VMEM((nw + 1, seqs, length, width), BF),
        pltpu.VMEM((3, length, 2 * n), BF),
        pltpu.VMEM((seqs, heads, 128, length), BF),
        pltpu.VMEM((n, length), BF),
        pltpu.VMEM((length, bq), F32),
        pltpu.VMEM((seqs, 8, length), F32),
        pltpu.VMEM((seqs, 8, length), F32),
        pltpu.VMEM((seqs, n, length), F32),
        pltpu.VMEM((seqs, length, n), BF),
        pltpu.VMEM((seqs, 1, length), F32),
        pltpu.VMEM((width, length), BF),
        pltpu.VMEM((2, 16, width // 2), BF),
        dma((nw + 1, seqs)),
        dma((nw + 1, seqs)),
        dma((nw + 1, seqs)),
        dma((nw + 1, seqs)),
        dma((3,)),
        dma((seqs, 2)),
        dma((seqs, 2)),
    ]
    if fast:
        scratch += [dma((3,)), dma((3,)), dma((6, 3)), dma((6, 3)), dma((4,))]
    return pl.pallas_call(
        functools.partial(front_kernel, fast, nw, nctx, heads, length),
        out_shape=out_shape,
        in_specs=[VMEM_SPEC] * 6 + [ANY_SPEC] * 3,
        out_specs=tuple([VMEM_SPEC] * 10 + [ANY_SPEC] * 4),
        scratch_shapes=scratch,
        compiler_params=pltpu.CompilerParams(
            vmem_limit_bytes=56 * 1024 * 1024, collective_id=3, has_side_effects=True
        ),
        cost_estimate=pl.CostEstimate(
            flops=seqs * (nw + 1) * length * n * (4 * length + 4 * width), bytes_accessed=32 * 1024 * 1024, transcendentals=0
        ),
        name="front",
    )(x, wq, small, qb, vb, lo, w1, w2, wo)


def middle_kernel(
    fast, n, half,
    cown_ref, cpeer_ref, mown_ref, mpeer_ref, norms_ref, hv_ref, fvec_ref, x_hbm, g_hbm, f1_hbm, f2_hbm, fo_hbm,
    out_ref, g1_ref, doT_ref, o_ref, f_ref, z_ref, dh_ref, sum_ref,
    x_s, g_s, f1, f2, fo, u_s, gp_s, e_s, dT, tmp, in_sem, w_sem, d_send, d_recv,
):
    seqs = cown_ref.shape[0]
    width = norms_ref.shape[1]
    step = width
    ff2 = f1.shape[2]
    ff = 2 * ff2
    t = lax.axis_index("tp")
    ypeer = {"tp": 1 - t}
    greet([(ypeer, None)])
    rows = pl.ds(pl.multiple_of(t * half, 128), half)
    loads = []
    for i, (src, dst) in enumerate(((x_hbm, x_s), (g_hbm, g_s))):
        for b in range(seqs):
            loads.append(pltpu.make_async_copy(src.at[b, rows], dst.at[b], in_sem.at[i, b]))
    weights = [pltpu.make_async_copy(src, dst, w_sem.at[i]) for i, (src, dst) in enumerate(((fo_hbm, fo), (f1_hbm, f1), (f2_hbm, f2)))]
    weights[0].start()
    for cp in loads:
        cp.start()
    weights[1].start()
    weights[2].start()
    vec = norms_ref[...].astype(F32)
    gain, shift, b_out, b_down = vec[1:2], vec[3:4], vec[4:5], vec[5:6]
    chunks = [(p, j) for p in range(2) for j in range(0, ff2, step)]
    first = t == 0

    def note(b, row, value):
        if b:
            sum_ref[row : row + 1, :] += value
        else:
            sum_ref[row : row + 1, :] = value

    sum_ref[...] = jnp.zeros_like(sum_ref)
    sends = []
    for b in range(seqs):
        gap = jnp.where(first, mown_ref[b] - mpeer_ref[b], mpeer_ref[b] - mown_ref[b]) * 0.5
        delta = jnp.broadcast_to(gap, (128, half)).T[:, :1]
        own, peer = cown_ref[b].astype(F32), cpeer_ref[b].astype(F32)
        n0 = jnp.where(first, own, peer) + delta
        n1 = jnp.where(first, peer, own) - delta
        var = (jnp.sum(n0 * n0, -1, keepdims=True) + jnp.sum(n1 * n1, -1, keepdims=True)) / (2 * n)
        rs = lax.rsqrt(var + EPS)
        nh = (n0 * rs, n1 * rs)
        os = []
        for p in range(2):
            cs = slice(p * n, (p + 1) * n)
            o = (nh[p] * hv_ref[0:1, cs] + hv_ref[1:2, cs]).astype(BF)
            o_ref[b, :, cs] = o
            os.append(o)
        if b == 0:
            weights[0].wait()
            for cp in loads:
                cp.wait()
        y1 = x_s[b].astype(F32) + b_out
        for p in range(2):
            y1 = y1 + dot(os[p], fo[p])
        cen = y1 - row_mean(y1)
        r2 = lax.rsqrt(row_mean(cen * cen) + EPS)
        yh = cen * r2
        f = (yh * gain + shift).astype(BF)
        g2 = g_s[b]
        if fast:
            put_transposed(g2, f_ref.at[b, 0], tmp)
            put_transposed(f, f_ref.at[b, 1], tmp)
        else:
            f_ref[b] = f
        if b == 0:
            weights[1].wait()
        usum = 0.0
        for p, j in chunks:
            cs = slice(p * ff2 + j, p * ff2 + j + step)
            h = dot(f, f1[p, :, j : j + step]) + fvec_ref[0:1, cs]
            u, slope = gelu_pair(h)
            u_s[:, cs] = u
            gp_s[:, cs] = slope
            usum = usum + jnp.sum(u, -1, keepdims=True)
        mu = usum / ff
        ssum = 0.0
        for p, j in chunks:
            cs = slice(p * ff2 + j, p * ff2 + j + step)
            d = u_s[:, cs] - mu
            ssum = ssum + jnp.sum(d * d, -1, keepdims=True)
        ru = lax.rsqrt(ssum / ff + EPS)
        if b == 0:
            weights[2].wait()
        y2 = y1 + b_down
        esum = 0.0
        ezsum = 0.0
        for i, (p, j) in enumerate(chunks):
            cs = slice(p * ff2 + j, p * ff2 + j + step)
            w2 = f2[p, j : j + step, :]
            zh = (u_s[:, cs] - mu) * ru
            u_s[:, cs] = zh
            z = (zh * fvec_ref[1:2, cs] + fvec_ref[2:3, cs]).astype(BF)
            z_ref[b, :, cs] = z
            y2 = y2 + dot(z, w2)
            dz = dot_nt(g2, w2)
            note(b, 6 + len(chunks) + i, col_sum(dz * zh))
            note(b, 6 + 2 * len(chunks) + i, col_sum(dz))
            e = dz * fvec_ref[1:2, cs]
            e_s[:, cs] = e
            esum = esum + jnp.sum(e, -1, keepdims=True)
            ezsum = ezsum + jnp.sum(e * zh, -1, keepdims=True)
        out_ref[b] = y2.astype(BF)
        em, ezm = esum / ff, ezsum / ff
        df = jnp.zeros_like(y1)
        for i, (p, j) in enumerate(chunks):
            cs = slice(p * ff2 + j, p * ff2 + j + step)
            du = ru * (e_s[:, cs] - em - u_s[:, cs] * ezm)
            dh = (du * gp_s[:, cs]).astype(BF)
            dh_ref[b, :, cs] = dh
            note(b, 6 + i, col_sum(dh.astype(F32)))
            df = df + dot_nt(dh, f1[p, :, j : j + step])
        note(b, 2, col_sum(df * yh))
        note(b, 3, col_sum(df))
        e2 = df * gain
        g = g2.astype(F32)
        dy1 = g + r2 * (e2 - row_mean(e2) - yh * row_mean(e2 * yh))
        g1 = dy1.astype(BF)
        g1_ref[b] = g1
        if fast:
            put_transposed(g1, f_ref.at[b, 2], tmp)
        note(b, 4, col_sum(g1.astype(F32)))
        note(b, 5, col_sum(g))
        es = []
        for p in range(2):
            cs = slice(p * n, (p + 1) * n)
            dsub = dot_nt(g1, fo[p])
            for k, value in enumerate((col_sum(dsub * nh[p]), col_sum(dsub))):
                if b:
                    sum_ref[k : k + 1, cs] += value
                else:
                    sum_ref[k : k + 1, cs] = value
            es.append(dsub * hv_ref[0:1, cs])
        em = sum(jnp.sum(e, -1, keepdims=True) for e in es) / (2 * n)
        ezm = sum(jnp.sum(e * h, -1, keepdims=True) for e, h in zip(es, nh)) / (2 * n)
        for p in range(2):
            dat = rs * (es[p] - em - nh[p] * ezm)
            for k in range(n // 128):
                ks = slice(k * 128, (k + 1) * 128)
                dT[b, p, ks, :] = dat[:, ks].T.astype(BF)
        sends.append(remote(dT.at[b, 1 - t], doT_ref.at[b, :, rows], d_send.at[b], d_recv.at[b], ypeer))
        sends[b].start()
        doT_ref[b, :, rows] = dT[b, t]
    for cp in sends:
        cp.wait()


def middle_call(fast, cown, cpeer, mown, mpeer, norms, hv, fvec, x, g, f1, f2, fo):
    seqs, half, n = cown.shape
    width = x.shape[2]
    ff = fvec.shape[1]
    sds = jax.ShapeDtypeStruct
    dma = pltpu.SemaphoreType.DMA
    return pl.pallas_call(
        functools.partial(middle_kernel, fast, n, half),
        out_shape=(
            sds((seqs, half, width), BF),
            sds((seqs, half, width), BF),
            sds((seqs, n, 2 * half), BF),
            sds((seqs, half, 2 * n), BF),
            sds((seqs, 3, width, half) if fast else (seqs, half, width), BF),
            sds((seqs, half, ff), BF),
            sds((seqs, half, ff), BF),
            sds((24, width), F32),
        ),
        in_specs=[VMEM_SPEC] * 7 + [ANY_SPEC] * 5,
        out_specs=(VMEM_SPEC,) * 8,
        scratch_shapes=[
            pltpu.VMEM((seqs, half, width), BF),
            pltpu.VMEM((seqs, half, width), BF),
            pltpu.VMEM(f1.shape, BF),
            pltpu.VMEM(f2.shape, BF),
            pltpu.VMEM(fo.shape, BF),
            pltpu.VMEM((half, ff), F32),
            pltpu.VMEM((half, ff), F32),
            pltpu.VMEM((half, ff), F32),
            pltpu.VMEM((seqs, 2, n, half), BF),
            pltpu.VMEM((width, half), BF),
            dma((2, seqs)),
            dma((3,)),
            dma((seqs,)),
            dma((seqs,)),
        ],
        compiler_params=pltpu.CompilerParams(
            vmem_limit_bytes=56 * 1024 * 1024, collective_id=4, has_side_effects=True
        ),
        cost_estimate=pl.CostEstimate(
            flops=4 * seqs * half * (f1.size + f2.size + fo.size), bytes_accessed=24 * 1024 * 1024, transcendentals=0
        ),
        name="middle",
    )(cown, cpeer, mown, mpeer, norms, hv, fvec, x, g, f1, f2, fo)


def end_kernel(
    n, length,
    dq_ref, dkv_ref, w_ref, x_ref, g1_ref, aT_ref, gain_ref, p2_ref, p1_ref, po_ref,
    gt_ref, gq_ref, g2_ref, gu_ref, go_ref, total_ref,
    pT, pn, mine, peer, xh, rinv, sq, rq, wq, xq, zq, zq2, z2a, z2b, z1a, z1b, zoa, zob, vec_buf,
    da_send, da_recv, rs_send, rs_recv, vec_send, vec_recv,
):
    seqs = x_ref.shape[0]
    s, r, t = lax.axis_index("shard"), lax.axis_index("ctx"), lax.axis_index("tp")
    c, z = lax.rem(r, 2), r // 2
    lo_bit, hi_bit = lax.rem(z, 2), z // 2
    sib, ypeer, xpeer = {"ctx": r + 1 - 2 * c}, {"tp": 1 - t}, {"shard": 1 - s}
    zlo, zhi = {"ctx": r + 2 - 4 * lo_bit}, {"ctx": r + 4 - 8 * hi_bit}
    greet([(d, None) for d in (sib, ypeer, xpeer, zlo, zhi)])
    live = {}

    def send(name, src, dst, i, device):
        live[name] = remote(src, dst, rs_send.at[i], rs_recv.at[i], device)
        live[name].start()

    def add(dst, a, b):
        dst[...] = (a[...].astype(F32) + b[...].astype(F32)).astype(dst.dtype)

    groups = ((p2_ref, z2a, z2b, g2_ref), (p1_ref, z1a, z1b, gu_ref), (po_ref, zoa, zob, go_ref))
    for k, (part, za, zb, out) in enumerate(groups):
        send(("a", k), part.at[:, 1 - lo_bit], za, 2 * k, zlo)

    sums = [jnp.zeros((1, x_ref.shape[2]), F32) for _ in range(2)]
    bias = [jnp.zeros((1, n), F32) for _ in range(2)]
    exchange = []
    for b in range(seqs):
        pT[: n, :] = (dq_ref[b] * 0.125).astype(BF)
        pT[n:, :] = dkv_ref[b]
        for k in range(3 * n // 128):
            ks = slice(k * 128, (k + 1) * 128)
            pn[b, :, ks] = pT[ks, :].T
        da = dot_nt(pn[b, :, :n], w_ref[0])
        da = da + dot_nt(pn[b, :, n : 2 * n], w_ref[1])
        da = da + dot_nt(pn[b, :, 2 * n :], w_ref[2])
        mine[b] = da.astype(BF)
        exchange.append(remote(mine.at[b], peer.at[b], da_send.at[b], da_recv.at[b], ypeer))
        exchange[b].start()
        x = x_ref[b].astype(F32)
        cen = x - row_mean(x)
        inv = lax.rsqrt(row_mean(cen * cen) + EPS)
        rinv[b] = inv
        xh[b] = cen * inv
        sums[0] = sums[0] + col_sum(da * xh[b])
        sums[1] = sums[1] + col_sum(da)
        bias[0] = bias[0] + col_sum(pn[b, :, :n].astype(F32))
        bias[1] = bias[1] + col_sum(pn[b, :, 2 * n :].astype(F32))
    total_ref[...] = jnp.zeros_like(total_ref)
    total_ref[0:1, :] = sums[0]
    total_ref[1:2, :] = sums[1]
    total_ref[2:3, :n] = bias[0]
    total_ref[2:3, n:] = bias[1]
    partners = [sib, xpeer, zlo, zhi, ypeer]
    count = len(partners)

    def vec(stage):
        if stage:
            live[("v", stage - 1)].wait()
            if stage == count:
                total_ref[0:2, :] = total_ref[0:2, :] + vec_buf[stage - 1, 0:2, :]
            else:
                total_ref[...] = total_ref[...] + vec_buf[stage - 1]
        if stage < count:
            vec_buf[count] = total_ref[...]
            live[("v", stage)] = remote(
                vec_buf.at[count], vec_buf.at[stage], vec_send.at[stage], vec_recv.at[stage], partners[stage]
            )
            live[("v", stage)].start()

    vec(0)
    rows = aT_ref.shape[1] // 2

    def product(core, dst):
        at = pl.ds(pl.multiple_of(core * rows, 64), rows)
        for k in range(3):
            ks = slice(k * n, (k + 1) * n)
            acc = dot(aT_ref[0, at, :], pn[0, :, ks])
            for b in range(1, seqs):
                acc = acc + dot(aT_ref[b, at, :], pn[b, :, ks])
            acc = acc.astype(BF)
            for j in range(2):
                for i in range(4):
                    at_row = (j * 4 + i) * (rows // 8)
                    dst[j, i // 2, i % 2, :, ks] = acc[at_row : at_row + rows // 8]

    product(1 - c, sq)
    send("core", sq, rq, 6, sib)
    product(c, wq)
    vec(1)
    live["core"].wait_recv()
    add(wq.at[1 - s], wq.at[1 - s], rq.at[1 - s])
    send("x", wq.at[1 - s], xq, 7, xpeer)
    add(wq.at[s], wq.at[s], rq.at[s])
    for k, (part, za, zb, out) in enumerate(groups):
        live[("a", k)].wait_recv()
        add(za, part.at[:, lo_bit], za)
        send(("b", k), za.at[1 - hi_bit], zb, 2 * k + 1, zhi)
    vec(2)
    live["x"].wait_recv()
    add(wq.at[s], wq.at[s], xq)
    send("za", wq.at[s, :, 1 - lo_bit], zq, 8, zlo)
    vec(3)

    def finish(b):
        exchange[b].wait_recv()
        da = mine[b].astype(F32) + peer[b].astype(F32)
        e = da * gain_ref[...]
        h = xh[b]
        dx = rinv[b] * (e - row_mean(e) - h * row_mean(e * h))
        gt_ref[b] = (g1_ref[b].astype(F32) + dx).astype(BF)

    for b in range(seqs - 1):
        finish(b)
    live["za"].wait_recv()
    add(wq.at[s, :, lo_bit], wq.at[s, :, lo_bit], zq)
    send("zb", wq.at[s, 1 - hi_bit, lo_bit], zq2, 9, zhi)
    vec(4)
    for k, (part, za, zb, out) in enumerate(groups):
        live[("b", k)].wait_recv()
        add(out, za.at[hi_bit], zb)
    live["zb"].wait_recv()
    last = wq[s, hi_bit, lo_bit].astype(F32) + zq2[...].astype(F32)
    for k in range(3):
        gq_ref[k] = last[:, k * n : (k + 1) * n]
    vec(5)
    finish(seqs - 1)
    for key, cp in live.items():
        if not (isinstance(key, tuple) and key[0] == "v"):
            cp.wait_send()
    for cp in exchange:
        cp.wait_send()


def end_call(dq, dkv, w, x, g1, aT, gain, p2, p1, po):
    seqs, n, length = dq.shape
    width = x.shape[2]
    piece = width // 16
    sds = jax.ShapeDtypeStruct
    dma = pltpu.SemaphoreType.DMA
    c2, c1, co = p2.shape[-1], p1.shape[-1], po.shape[-1]
    return pl.pallas_call(
        functools.partial(end_kernel, n, length),
        out_shape=(
            sds((seqs, length, width), BF),
            sds((3, piece, n), F32),
            sds((piece, c2), F32),
            sds((piece, c1), F32),
            sds((piece, co), F32),
            sds((8, width), F32),
        ),
        in_specs=[VMEM_SPEC] * 10,
        out_specs=(VMEM_SPEC,) * 6,
        scratch_shapes=[
            pltpu.VMEM((3 * n, length), BF),
            pltpu.VMEM((seqs, length, 3 * n), BF),
            pltpu.VMEM((seqs, length, width), BF),
            pltpu.VMEM((seqs, length, width), BF),
            pltpu.VMEM((seqs, length, width), F32),
            pltpu.VMEM((seqs, length, 1), F32),
            pltpu.VMEM((2, 2, 2, piece, 3 * n), BF),
            pltpu.VMEM((2, 2, 2, piece, 3 * n), BF),
            pltpu.VMEM((2, 2, 2, piece, 3 * n), BF),
            pltpu.VMEM((2, 2, piece, 3 * n), BF),
            pltpu.VMEM((2, piece, 3 * n), BF),
            pltpu.VMEM((piece, 3 * n), BF),
            pltpu.VMEM((2, piece, c2), BF),
            pltpu.VMEM((piece, c2), BF),
            pltpu.VMEM((2, piece, c1), BF),
            pltpu.VMEM((piece, c1), BF),
            pltpu.VMEM((2, piece, co), BF),
            pltpu.VMEM((piece, co), BF),
            pltpu.VMEM((6, 8, width), F32),
            dma((seqs,)),
            dma((seqs,)),
            dma((10,)),
            dma((10,)),
            dma((5,)),
            dma((5,)),
        ],
        compiler_params=pltpu.CompilerParams(
            vmem_limit_bytes=56 * 1024 * 1024, collective_id=2, has_side_effects=True
        ),
        cost_estimate=pl.CostEstimate(
            flops=12 * seqs * length * width * n, bytes_accessed=16 * 1024 * 1024, transcendentals=0
        ),
        name="input_back",
    )(dq, dkv, w, x, g1, aT, gain, p2, p1, po)


def swap(value, axis):
    return lax.ppermute(value, axis, [(0, 1), (1, 0)])


def scatter_rows(grad, t=None):
    width, cols = grad.shape
    if t is not None:
        grad = lax.psum_scatter(grad.reshape(width, 2, cols // 2), "tp", scatter_dimension=1, tiled=False)
    return lax.psum_scatter(grad.astype(F32), ("shard", "ctx"), scatter_dimension=0, tiled=True)


def per_device(
    tokens,
    cotangent,
    segment_ids,
    w_qkv,
    w_out,
    w_fc1,
    w_fc2,
    norm_gain,
    norm_bias,
    head_gain,
    head_bias,
    ffn_gain,
    ffn_bias,
):
    seqs, length, width = tokens.shape
    n = w_qkv.shape[2]
    ff2 = w_fc1.shape[1]
    s, r, t = lax.axis_index("shard"), lax.axis_index("ctx"), lax.axis_index("tp")
    nctx = lax.axis_size("ctx")
    fast = lax.axis_size("shard") == 2 and nctx == 8
    nw = min(-(-(MAXDOC - 1) // length), nctx - 1)

    wq, w1, w2, wo = (w.astype(BF) for w in (w_qkv, w_fc1, w_fc2, w_out))
    small = jnp.concatenate([norm_gain, norm_bias, jnp.zeros((10, norm_gain.shape[1]), F32)]).astype(BF)
    if not fast:
        wq = lax.all_gather(wq, "shard", axis=1, tiled=True)
        small = lax.all_gather(small, "shard", axis=1, tiled=True)
        small = small.reshape(16, 2, width // 2).transpose(1, 0, 2)
        full = [lax.all_gather(w, "shard", axis=a, tiled=True) for w, a in ((w1, 0), (w2, 1), (wo, 1))]
        full = [lax.all_gather(w, "tp", axis=0) for w in full]
    vectors = jnp.concatenate([ffn_bias[0], ffn_gain, ffn_bias[1], head_gain, head_bias[2]])
    far = swap(vectors, "tp")
    v0, v1 = jnp.where(t == 0, vectors, far), jnp.where(t == 0, far, vectors)
    fvec = jnp.concatenate([v0[: 3 * ff2].reshape(3, ff2), v1[: 3 * ff2].reshape(3, ff2)], 1)
    hvec = jnp.concatenate([v0[3 * ff2 :].reshape(2, n), v1[3 * ff2 :].reshape(2, n)], 1)

    below = jnp.sum(segment_ids[:, None, :] < jnp.arange(1, 4, dtype=jnp.int32)[None, :, None], -1, dtype=jnp.int32)
    seg_q = lax.dynamic_slice_in_dim(segment_ids, r * length, length, 1)
    start = jnp.zeros_like(seg_q)
    for v in range(1, 4):
        start = jnp.where(seg_q == v, below[:, v - 1 : v], start)
    start = start[:, None, :]

    acts, qT, oT, lse, cown, cpeer, mown, mpeer, wfull, norms, kv, f1, f2, fo = front_call(
        fast, nw, nctx, tokens, wq, small, head_bias[:1], head_bias[1:2], start, w1, w2, wo
    )
    if not fast:
        f1, f2, fo = full
    out_own, g1_own, doT, o, lt, z_act, dh, sums = middle_call(
        fast, cown, cpeer, mown, mpeer, norms, hvec, fvec, tokens, cotangent, f1, f2, fo
    )
    dq, dkv, part2, part1, parto, sums_all, out, g1 = back_call(
        fast, nw, nctx, qT, doT, oT, lse, start, kv, lt, z_act, dh, o, out_own, g1_own, sums[None]
    )
    gains = norms[:1].astype(F32)

    def fold_rows(value):
        return value.reshape((-1,) + value.shape[2:])

    if fast:
        split = lambda part: part.reshape(2, 2, part.shape[0] // 4, part.shape[1])
        grad_tokens, grad_qkv, gd, gu, go, tails = end_call(
            dq, dkv, wfull, tokens, g1, acts, gains, split(part2), split(part1), split(parto)
        )
        in_sums, bias_q, bias_v = tails[:2], tails[2, :n], tails[2, n:]
    else:
        outer = lambda left, right: lax.dot_general(
            fold_rows(left), fold_rows(right), (((0,), (0,)), ((), ())), preferred_element_type=F32
        ).astype(BF)
        g_own = lax.dynamic_slice_in_dim(cotangent, t * (length // 2), length // 2, 1)
        gd = scatter_rows(outer(g_own, z_act), t)
        gu = scatter_rows(outer(lt, dh), t)
        go = scatter_rows(outer(g1_own, o), t)
        sums_all = lax.psum(sums, ("shard", "ctx", "tp"))
        grad_tokens, in_sums, projs = [], 0.0, []
        for b in range(seqs):
            proj = jnp.concatenate([(dq[b].T * 0.125).astype(BF), dkv[b].T], 1)
            projs.append(proj)
            da = sum(dot_nt(proj[:, i * n : (i + 1) * n], wfull[i]) for i in range(3)).astype(BF)
            gt, part = tail_call(da, swap(da, "tp"), tokens[b], g1[b], gains)
            grad_tokens.append(gt)
            in_sums = in_sums + part
        grad_tokens = jnp.stack(grad_tokens)
        grad_qkv = scatter_rows(outer(acts, jnp.stack(projs))).reshape(-1, 3, n).transpose(1, 0, 2)
        tails = lax.psum(
            jnp.concatenate([in_sums.reshape(-1), jnp.sum(jnp.concatenate(projs).astype(F32), 0)]), ("shard", "ctx")
        )
        in_sums, bias_q, bias_v = tails[: 2 * width].reshape(2, width), tails[2 * width :][:n], tails[-n:]

    hsum, dsum, fsum = sums_all[:2], sums_all[2:6], sums_all[6 : 6 + 6 * ff2 // width].reshape(3, 2 * ff2)
    piece = width // (lax.axis_size("shard") * lax.axis_size("ctx"))
    mine = (s * lax.axis_size("ctx") + r) * piece
    grad_gain = lax.dynamic_slice_in_dim(jnp.stack([in_sums[0], dsum[0]]), mine, piece, 1)
    grad_bias = lax.dynamic_slice_in_dim(jnp.stack([in_sums[1], dsum[1], dsum[2], dsum[3]]), mine, piece, 1)
    hsum = lax.dynamic_slice_in_dim(hsum, t * n, n, 1)
    fsum = lax.dynamic_slice_in_dim(fsum, t * ff2, ff2, 1)
    return (
        out,
        grad_tokens,
        grad_qkv,
        go.T,
        gu,
        gd.T,
        grad_gain,
        grad_bias,
        hsum[0],
        jnp.stack([bias_q, bias_v, hsum[1]]),
        fsum[1],
        jnp.stack([fsum[0], fsum[2]]),
    )


def solution(mesh):
    in_specs = (
        P("shard", "ctx", None),
        P("shard", "ctx", None),
        P("shard", None),
        P(None, "shard", "tp"),
        P("tp", "shard"),
        P("shard", "tp"),
        P("tp", "shard"),
        P(None, "shard"),
        P(None, "shard"),
        P("tp"),
        P(None, "tp"),
        P("tp"),
        P(None, "tp"),
    )
    out_specs = (
        P("shard", "ctx", None),
        P("shard", "ctx", None),
        P(None, ("shard", "ctx"), "tp"),
        P("tp", ("shard", "ctx")),
        P(("shard", "ctx"), "tp"),
        P("tp", ("shard", "ctx")),
        P(None, ("shard", "ctx")),
        P(None, ("shard", "ctx")),
        P("tp"),
        P(None, "tp"),
        P("tp"),
        P(None, "tp"),
    )
    return jax.shard_map(
        per_device, mesh=mesh, in_specs=in_specs, out_specs=out_specs, check_vma=False
    )
```

```python
import functools

import jax
import jax.numpy as jnp
from jax import lax
from jax.experimental import pallas as pl
from jax.experimental.pallas import tpu as pltpu
from jax.sharding import PartitionSpec as P

HD = 64
NEG = -1e30
VL = 48 * 1024 * 1024

EPS = 1e-05
MAXDOC = 1920
BF = jnp.bfloat16
F32 = jnp.float32
NT_DIMS = (((1,), (1,)), ((), ()))
VMEM_SPEC = pl.BlockSpec(memory_space=pltpu.VMEM)
ANY_SPEC = pl.BlockSpec(memory_space=pl.ANY)
GELU_C = 0.7978845608028654
GELU_A = 0.044715


def dot(left, right):
    return jnp.dot(left, right, preferred_element_type=F32)


def dot_nt(left, right):
    return lax.dot_general(left, right, NT_DIMS, preferred_element_type=F32)


def row_mean(values):
    return jnp.mean(values, -1, keepdims=True)


def col_sum(values):
    return jnp.sum(values, 0, keepdims=True)


def put_transposed(value, dst, tmp):
    width = value.shape[1]
    for k in range(width // 128):
        tmp[k * 128 : (k + 1) * 128, :] = value[:, k * 128 : (k + 1) * 128].T
    piece = width // 16
    for shard in range(2):
        for z in range(4):
            for core in range(2):
                to = core * (width // 2) + shard * (width // 4) + z * piece
                at = shard * (width // 2) + (z * 2 + core) * piece
                dst[to : to + piece, :] = tmp[at : at + piece, :]


def gelu_pair(h):
    inner = GELU_C * (h + GELU_A * h * h * h)
    t = jnp.tanh(inner)
    half = 0.5 * (1.0 + t)
    slope = half + 0.5 * h * (1.0 - t * t) * (GELU_C * (1.0 + (3.0 * GELU_A) * h * h))
    return h * half, slope


def tail_kernel(own_ref, peer_ref, x_ref, g1_ref, gain_ref, out_ref, sum_ref):
    da = own_ref[...].astype(F32) + peer_ref[...].astype(F32)
    x = x_ref[...].astype(F32)
    cen = x - row_mean(x)
    r = lax.rsqrt(row_mean(cen * cen) + EPS)
    xh = cen * r
    sum_ref[0:1, :] = col_sum(da * xh)
    sum_ref[1:2, :] = col_sum(da)
    e = da * gain_ref[...]
    dx = r * (e - row_mean(e) - xh * row_mean(e * xh))
    out_ref[...] = (g1_ref[...].astype(F32) + dx).astype(BF)


def tail_call(own, peer, x, g1, gain):
    rows, width = x.shape
    return pl.pallas_call(
        tail_kernel,
        out_shape=(jax.ShapeDtypeStruct((rows, width), BF), jax.ShapeDtypeStruct((2, width), F32)),
        in_specs=[VMEM_SPEC] * 5,
        out_specs=(VMEM_SPEC, VMEM_SPEC),
        compiler_params=pltpu.CompilerParams(vmem_limit_bytes=VL),
        cost_estimate=pl.CostEstimate(
            flops=20 * rows * width, bytes_accessed=10 * rows * width, transcendentals=rows
        ),
        name="tail",
    )(own, peer, x, g1, gain)


MESH_ID = pl.DeviceIdType.MESH


def remote(src, dst, send, recv, device):
    return pltpu.make_async_remote_copy(
        src_ref=src, dst_ref=dst, send_sem=send, recv_sem=recv, device_id=device, device_id_type=MESH_ID
    )


def greet(devices):
    sem = pltpu.get_barrier_semaphore()
    count = 0
    for device, cond in devices:
        def signal(device=device):
            pl.semaphore_signal(sem, inc=1, device_id=device, device_id_type=MESH_ID)
        if cond is None:
            signal()
            count = count + 1
        else:
            pl.when(cond)(signal)
            count = count + cond.astype(jnp.int32)
    pl.semaphore_wait(sem, count)


def chunk_blocks(w, length, bq, bk):
    found = []
    for kb in range(length // bk):
        for qb in range(length // bq):
            if w == 0 and kb * bk > qb * bq + bq - 1:
                continue
            if qb * bq + w * length - (MAXDOC - 1) > kb * bk + bk - 1:
                continue
            found.append((qb, kb))
    return found


def block_bias(w, lo, qb, kb, bq, bk):
    key = lax.broadcasted_iota(jnp.int32, (bk, bq), 0) + kb * bk
    seen = key >= lo[:, qb * bq : (qb + 1) * bq]
    if w == 0 and (kb + 1) * bk > qb * bq + 1:
        seen = seen & (key <= lax.broadcasted_iota(jnp.int32, (bk, bq), 1) + qb * bq)
    return jnp.where(seen, 0.0, NEG)


def split_pairs(src, dst, heads):
    row = lax.broadcasted_iota(jnp.int32, (2 * HD, src.shape[1]), 0)
    for p in range(heads // 2):
        block = src[p * 128 : (p + 1) * 128, :]
        dst[2 * p] = jnp.where(row < HD, block, jnp.zeros_like(block))
        dst[2 * p + 1] = jnp.where(row >= HD, block, jnp.zeros_like(block))


def back_item(w, heads, length, bq, bk, kv, qT, doT, qm, dm, kT, lse, dd, lo, bias, dq, dk, dv):
    n = heads * HD
    for p in range(heads // 2):
        ps = slice(p * 128, (p + 1) * 128)
        kT[ps, :] = kv[:, ps].T
    blocks = chunk_blocks(w, length, bq, bk)
    for kb in range(length // bk):
        ks = slice(kb * bk, (kb + 1) * bk)
        mine = [qb for qb, other in blocks if other == kb]
        if not mine:
            dk[:, ks] = jnp.zeros((n, bk), F32)
            dv[:, ks] = jnp.zeros((n, bk), F32)
        for turn, qb in enumerate(mine):
            qs = slice(qb * bq, (qb + 1) * bq)
            bias[...] = block_bias(w, lo, qb, kb, bq, bk)

            def scores(h):
                ps = slice((h // 2) * 128, (h // 2 + 1) * 128)
                pv = slice(n + (h // 2) * 128, n + (h // 2 + 1) * 128)
                return dot(kv[ks, ps], qm[h, :, qs]) + bias[...], dot(kv[ks, pv], dm[h, :, qs])

            ahead = scores(0)
            for h in range(heads):
                hs = slice(h * HD, (h + 1) * HD)
                s, dp = ahead
                ahead = scores(h + 1) if h + 1 < heads else None
                e = jnp.exp(s - lse[h : h + 1, qs])
                ds = (e * (dp - dd[h : h + 1, qs])).astype(BF)
                new_v = dot_nt(doT[hs, qs], e.astype(BF))
                new_k = dot_nt(qT[hs, qs], ds)
                if turn:
                    dv[hs, ks] += new_v
                    dk[hs, ks] += new_k
                else:
                    dv[hs, ks] = new_v
                    dk[hs, ks] = new_k
                dq[hs, qs] += dot(kT[hs, ks], ds)


def back_kernel(
    fast, nw, nctx, heads, length,
    qT_ref, doT_ref, dlast_ref, oT_ref, lse_ref, lo_ref, wfull_ref, sum_ref,
    kv_hbm, lt_hbm, z_hbm, dh_hbm, o_hbm, g1_own, out_own,
    pn_ref, mine_ref, peer_ref, part2_ref, part1_ref, parto_ref, total_ref, g1_ref, out_ref,
    slots, kvbuf, qm, dm, kT, bias, dk, dv, dd, dq, dlast,
    ring_send, ring_recv, kv_sem, da_send, da_recv, last_send, last_recv, own_sem, give_send, give_recv, *rs,
):
    n = heads * HD
    bq = bk = min(256, length)
    s, r, t = lax.axis_index("shard"), lax.axis_index("ctx"), lax.axis_index("tp")
    c = lax.rem(r, 2)
    sib, ypeer = {"ctx": r + 1 - 2 * c}, {"tp": 1 - t}
    left, right = {"ctx": r - 1}, {"ctx": r + 1}
    has_left, has_right = r > 0, r < nctx - 1
    half = length // 2
    seqs = qT_ref.shape[0]
    last = seqs - 1
    order = [(w, b) for b in range(last) for w in range(nw, -1, -1)]
    tail = [(w, last) for w in range(nw, -1, -1)]
    items = order[:-1] + tail[:1] + order[-1:] + tail[1:]
    nbuf = kvbuf.shape[0]

    def load(i):
        w, b = items[i]
        return pltpu.make_async_copy(kv_hbm.at[w, b], kvbuf.at[i % nbuf], kv_sem.at[i % nbuf])

    def start_load(i):
        if i < len(items):
            pl.when(r >= items[i][0])(lambda: load(i).start())

    for i in range(nbuf - 1):
        start_load(i)
    people = [(left, has_left), (right, has_right), (ypeer, None)]
    if fast:
        (lt_ref, z_ref, dh_ref, o_ref, mid_sem) = rs[:5]
        rs = rs[5:]
        mids = [
            pltpu.make_async_copy(src, dst, mid_sem.at[i])
            for i, (src, dst) in enumerate(((lt_hbm, lt_ref), (z_hbm, z_ref), (dh_hbm, dh_ref), (o_hbm, o_ref)))
        ]
        for cp in mids:
            cp.start()
        xpeer = {"shard": 1 - s}
        z2 = lax.rem(r // 2, 2)
        hop4 = lax.rem(r // 4, 2)
        people += [(xpeer, None), ({"ctx": r + 2 - 4 * z2}, None), ({"ctx": r + 4 - 8 * hop4}, None)]
    greet(people)

    rows = pl.ds(pl.multiple_of(t * half, 128), half)
    share = remote(dlast_ref.at[1], dlast.at[:, rows], last_send, last_recv, ypeer)
    share.start()
    dlast[:, rows] = dlast_ref[0]

    keeps, gives = [], []
    for i, (src, dst) in enumerate([(g1_own, g1_ref)] + [(out_own.at[b], out_ref.at[b]) for b in range(last)]):
        keeps.append(pltpu.make_async_copy(src, dst.at[rows], own_sem.at[i]))
        gives.append(remote(src, dst.at[rows], give_send.at[i], give_recv.at[i], ypeer))
        keeps[i].start()
        gives[i].start()

    def grads_of(b):
        return dlast if b == last else doT_ref.at[b]

    def prepare(b):
        src = grads_of(b)
        split_pairs(qT_ref.at[b], qm.at[b], heads)
        split_pairs(src, dm.at[b], heads)
        for h in range(heads):
            hs = slice(h * HD, (h + 1) * HD)
            dd[b, h : h + 1, :] = col_sum(src[hs, :].astype(F32) * oT_ref[b, hs, :])
        dq[b] = jnp.zeros((n, length), F32)

    for b in range(last):
        prepare(b)

    steps = {}
    if fast:
        (s2, r2, w2, x2, y2, s1, r1, w1, y1, x1, so, ro, wo, yo, xo, vec_buf, rs_send, rs_recv, vec_send, vec_recv) = rs
        step = 512

        def product(g, rhs, core, dst, plus=None):
            cols = rhs.shape[2]
            size = step if cols % step == 0 else cols // 2
            rows = pl.ds(pl.multiple_of(core * (lt_ref.shape[2] // 2), 64), lt_ref.shape[2] // 2)

            def body(j, carry):
                at = pl.ds(pl.multiple_of(j * size, size), size)
                acc = dot(lt_ref[0, g, rows, :], rhs[0, :, at])
                for b in range(1, seqs):
                    acc = acc + dot(lt_ref[b, g, rows, :], rhs[b, :, at])
                mid = acc.shape[0] // 2
                for k in range(2):
                    value = acc[k * mid : (k + 1) * mid]
                    if plus is not None:
                        value = value + plus[k, :, at].astype(F32)
                    dst[k, :, at] = value.astype(BF)
                return carry

            lax.fori_loop(0, cols // size, body, 0)

        def add(dst, a, b):
            dst[...] = (a[...].astype(F32) + b[...].astype(F32)).astype(BF)

        live = {}

        def send(name, src, dst, i, device):
            live[name] = remote(src, dst, rs_send.at[i], rs_recv.at[i], device)
            live[name].start()

        def cols_of(ref, index):
            width = ref.shape[-1] // 2
            return pl.ds(pl.multiple_of(index * width, 128), width)

        def first(g, rhs, sbuf, rbuf, i):
            mids[1 + g].wait()
            product(g, rhs, 1 - c, sbuf)
            send(("core", g), sbuf, rbuf, i, sib)

        def x_then_y(stage):
            if stage == 0:
                first(0, z_ref, s2, r2, 0)
            elif stage == 2:
                live[("core", 0)].wait_recv()
                product(0, z_ref, c, w2, r2)
                send("x2", w2.at[1 - s], x2, 1, xpeer)
            elif stage == 3:
                live["x2"].wait_recv()
                add(w2.at[s], w2.at[s], x2)
                send("y2", w2.at[s, :, cols_of(w2, 1 - t)], y2, 2, ypeer)
            elif stage == 4:
                live["y2"].wait_recv()
                add(part2_ref, w2.at[s, :, cols_of(w2, t)], y2)

        def y_then_x(stage, g, rhs, sb, rb, wb, yb, xb, part, i):
            if stage == 0:
                first(g, rhs, sb, rb, i)
            elif stage == 2:
                live[("core", g)].wait_recv()
                product(g, rhs, c, wb, rb)
                send(("y", g), wb.at[:, :, cols_of(wb, 1 - t)], yb, i + 1, ypeer)
            elif stage == 3:
                live[("y", g)].wait_recv()
                mine = cols_of(wb, t)
                add(wb.at[1 - s, :, mine], wb.at[1 - s, :, mine], yb.at[1 - s])
                send(("x", g), wb.at[1 - s, :, mine], xb, i + 2, xpeer)
                add(wb.at[s, :, mine], wb.at[s, :, mine], yb.at[s])
            elif stage == 4:
                live[("x", g)].wait_recv()
                add(part, wb.at[s, :, cols_of(wb, t)], xb)

        up = lambda stage: y_then_x(stage, 1, dh_ref, s1, r1, w1, y1, x1, part1_ref, 3)
        op = lambda stage: y_then_x(stage, 2, o_ref, so, ro, wo, yo, xo, parto_ref, 6)

        partners = [ypeer, xpeer, sib, {"ctx": r + 2 - 4 * z2}, {"ctx": r + 4 - 8 * hop4}]
        count = vec_buf.shape[0] - 1

        def vec(stage):
            if stage == 0:
                acc = sum_ref[0]
                for b in range(1, sum_ref.shape[0]):
                    acc = acc + sum_ref[b]
                total_ref[...] = acc
            else:
                live[("v", stage - 1)].wait()
                total_ref[...] = total_ref[...] + vec_buf[stage - 1]
            if stage < len(partners):
                vec_buf[count] = total_ref[...]
                live[("v", stage)] = remote(
                    vec_buf.at[count], vec_buf.at[stage], vec_send.at[stage], vec_recv.at[stage], partners[stage]
                )
                live[("v", stage)].start()

        plan = [
            [],
            [lambda: mids[0].wait(), lambda: up(0), lambda: x_then_y(0)],
            [lambda: up(2)],
            [lambda: x_then_y(2)],
            [lambda: op(0)],
            [lambda: op(2), lambda: vec(0)],
            [lambda: up(3), lambda: vec(1)],
            [lambda: x_then_y(3), lambda: vec(2)],
            [lambda: op(3), lambda: vec(3)],
            [lambda: vec(4)],
            [lambda: vec(5), lambda: op(4), lambda: up(4), lambda: x_then_y(4)],
        ]
        for i, what in enumerate(plan):
            steps[i] = what
        ends = lambda: [cp.wait_send() for key, cp in live.items() if not (isinstance(key, tuple) and key[0] == "v")]
    else:
        ends = lambda: None

    def project(b):
        for k in range(n // 128):
            ks = slice(k * 128, (k + 1) * 128)
            pn_ref[b, :, ks] = (dq[b, ks, :] * 0.125).T.astype(BF)
        for k in range(2 * n // 128):
            pn_ref[b, :, n + k * 128 : n + (k + 1) * 128] = slots[0, b, k * 128 : (k + 1) * 128, :].T

    unseen = max(0, nw * length - (MAXDOC - 1)) // 128 * 128
    sends = []
    shares = []
    for i, (w, b) in enumerate(items):
        start_load(i + nbuf - 1)
        has = r >= w
        if b == last and w == nw:
            share.wait_recv()
            prepare(b)

        def work(i=i, w=w, b=b):
            load(i).wait()
            back_item(
                w, heads, length, bq, bk, kvbuf.at[i % nbuf], qT_ref.at[b], grads_of(b), qm.at[b], dm.at[b], kT,
                lse_ref.at[b], dd.at[b], lo_ref[b] + (w - r) * length, bias, dq.at[b], dk, dv,
            )

        pl.when(has)(work)
        if w < nw:
            for what in steps.get(i, []):
                what()
        dest = slots.at[w, b]
        if w < nw:
            far = unseen if w == nw - 1 else 0
            keys = slice(far, length)

            def merge(w=w, b=b, dest=dest, far=far, keys=keys):
                place = slots.at[w, b, :, keys]
                remote(place, place, ring_send.at[w, b], ring_recv.at[w, b], left).wait_recv()
                dest[:n, keys] = (dk[:, keys] + slots[w, b, :n, keys].astype(F32)).astype(BF)
                dest[n:, keys] = (dv[:, keys] + slots[w, b, n:, keys].astype(F32)).astype(BF)
                if far:
                    dest[:n, :far] = dk[:, :far].astype(BF)
                    dest[n:, :far] = dv[:, :far].astype(BF)

            pl.when(has & has_right)(merge)

        def plain(dest=dest):
            dest[:n, :] = dk[...].astype(BF)
            dest[n:, :] = dv[...].astype(BF)

        pl.when((has & jnp.logical_not(has_right)) if w < nw else has)(plain)
        if w:
            keys = slice(unseen if w == nw else 0, length)
            cp = remote(
                slots.at[w, b, :, keys], slots.at[w - 1, b, :, keys], ring_send.at[w, b], ring_recv.at[w - 1, b], left
            )
            pl.when(has)(lambda cp=cp: cp.start())
            sends.append((has, cp))
            if w == nw:
                for what in steps.get(i, []):
                    what()
        else:
            project(b)
            if b < last:
                da = dot_nt(pn_ref[b, :, :n], wfull_ref[0])
                da = da + dot_nt(pn_ref[b, :, n : 2 * n], wfull_ref[1])
                da = da + dot_nt(pn_ref[b, :, 2 * n :], wfull_ref[2])
                mine_ref[b] = da.astype(BF)
                shares.append(remote(mine_ref.at[b], peer_ref.at[b], da_send.at[b], da_recv.at[b], ypeer))
                shares[-1].start()
    for what in steps.get(len(items), []):
        what()
    for has, cp in sends:
        pl.when(has)(lambda cp=cp: cp.wait_send())
    ends()
    for cp in keeps + gives + shares:
        cp.wait()
    share.wait_send()


def back_call(fast, nw, nctx, qT, doT, dlast, oT, lse, lo, wfull, sums, kv, lt, z, dh, o, g1_own, out_own):
    seqs, n, length = qT.shape
    heads = n // HD
    width = g1_own.shape[-1]
    sds = jax.ShapeDtypeStruct
    ff = z.shape[-1]
    q4 = width // 4
    rows = q4 if fast else 8
    out_shape = [
        sds((seqs, length, 3 * n), BF),
        sds((seqs - 1, length, width), BF),
        sds((seqs - 1, length, width), BF),
        sds((rows, ff // 2), BF),
        sds((rows, ff // 2), BF),
        sds((rows, n), BF),
        sds(sums.shape[1:], F32),
        sds((length, width), BF),
        sds((seqs - 1, length, width), BF),
    ]
    bq = min(256, length)
    dma = pltpu.SemaphoreType.DMA
    scratch = [
        pltpu.VMEM((nw + 1, seqs, 2 * n, length), BF),
        pltpu.VMEM((3, length, 2 * n), BF),
        pltpu.VMEM((seqs, heads, 128, length), BF),
        pltpu.VMEM((seqs, heads, 128, length), BF),
        pltpu.VMEM((n, length), BF),
        pltpu.VMEM((bq, bq), F32),
        pltpu.VMEM((n, length), F32),
        pltpu.VMEM((n, length), F32),
        pltpu.VMEM((seqs, 8, length), F32),
        pltpu.VMEM((seqs, n, length), F32),
        pltpu.VMEM((n, length), BF),
        dma((nw + 1, seqs)),
        dma((nw + 1, seqs)),
        dma((3,)),
        dma((seqs,)),
        dma((seqs,)),
        dma,
        dma,
        dma((seqs,)),
        dma((seqs,)),
        dma((seqs,)),
    ]
    if fast:
        scratch += [pltpu.VMEM(v.shape, BF) for v in (lt, z, dh, o)] + [dma((4,))]
        full = lambda cols: pltpu.VMEM((2, q4, cols), BF)
        scratch += [full(ff), full(ff), full(ff), pltpu.VMEM((q4, ff), BF), pltpu.VMEM((q4, ff // 2), BF)]
        for cols in (ff, 2 * n):
            scratch += [full(cols), full(cols), full(cols), full(cols // 2), pltpu.VMEM((q4, cols // 2), BF)]
        scratch += [pltpu.VMEM((6,) + sums.shape[1:], F32), dma((9,)), dma((9,)), dma((5,)), dma((5,))]
    return pl.pallas_call(
        functools.partial(back_kernel, fast, nw, nctx, heads, length),
        out_shape=tuple(out_shape),
        in_specs=[VMEM_SPEC] * 8 + [ANY_SPEC] * 7,
        out_specs=tuple([VMEM_SPEC] * 7 + [ANY_SPEC] * 2),
        scratch_shapes=scratch,
        compiler_params=pltpu.CompilerParams(
            vmem_limit_bytes=63 * 1024 * 1024, collective_id=1, has_side_effects=True
        ),
        cost_estimate=pl.CostEstimate(
            flops=seqs * (nw + 1) * 10 * length * length * n, bytes_accessed=40 * 1024 * 1024, transcendentals=0
        ),
        name="attn_back",
    )(qT, doT, dlast, oT, lse, lo, wfull, sums, kv, lt, z, dh, o, g1_own, out_own)


def forward_item(w, first, heads, length, bq, kv, qm, vT, lo, bias, m, l, acc):
    n = heads * HD
    for p in range(heads // 2):
        ps = slice(p * 128, (p + 1) * 128)
        vT[ps, :] = kv[:, n + p * 128 : n + (p + 1) * 128].T
    blocks = chunk_blocks(w, length, bq, min(256, length))
    size = min(256, length)
    for qb in range(length // bq):
        mine = [kb for q, kb in blocks if q == qb]
        if not mine:
            continue
        k0, k1 = min(mine) * size, (max(mine) + 1) * size
        qs, ks = slice(qb * bq, (qb + 1) * bq), slice(k0, k1)
        key = lax.broadcasted_iota(jnp.int32, (k1 - k0, bq), 0) + k0
        seen = key >= lo[:, qs]
        if w == 0:
            seen = seen & (key <= lax.broadcasted_iota(jnp.int32, (k1 - k0, bq), 1) + qb * bq)
        bias[: k1 - k0, :] = jnp.where(seen, 0.0, NEG)

        def scores(h):
            ps = slice((h // 2) * 128, (h // 2 + 1) * 128)
            return dot(kv[ks, ps], qm[h, :, qs]) + bias[: k1 - k0, :]

        ahead = scores(0)
        for h in range(heads):
            hs = slice(h * HD, (h + 1) * HD)
            s = ahead
            ahead = scores(h + 1) if h + 1 < heads else None
            if first:
                top = jnp.max(s, 0, keepdims=True)
                e = jnp.exp(s - top)
                l[h : h + 1, qs] = jnp.sum(e, 0, keepdims=True)
                acc[hs, qs] = dot(vT[hs, ks], e.astype(BF))
            else:
                old = m[h : h + 1, qs]
                top = jnp.maximum(old, jnp.max(s, 0, keepdims=True))
                e = jnp.exp(s - top)
                scale = jnp.exp(old - top)
                l[h : h + 1, qs] = l[h : h + 1, qs] * scale + jnp.sum(e, 0, keepdims=True)
                acc[hs, qs] = acc[hs, qs] * scale + dot(vT[hs, ks], e.astype(BF))
            m[h : h + 1, qs] = top


def front_kernel(
    fast, nw, nctx, heads, length,
    x_ref, wq_ref, ng_ref, nb_ref, hb_ref, fg_ref, fb_ref, hg_ref, seg_ref, w1_hbm, w2_hbm, wo_hbm,
    aT_ref, qT_ref, oT_ref, lse_ref, cown_ref, cpeer_ref, mown_ref, mpeer_ref, wfull_ref, norms_ref, start_ref,
    fgs_ref, fbs_ref, hgs_ref, hbs_ref, kv_hbm, f1_hbm, f2_hbm, fo_hbm,
    slots, kvbuf, qm, vT, bias, m, l, acc, cen, mean, tmp, ngs, nbs,
    ring_send, ring_recv, side_send, side_recv, kv_sem, c_send, c_recv, v_send, v_recv, *rs,
):
    n = heads * HD
    seqs, _, width = x_ref.shape
    half = length // 2
    bq = min(256, length)
    s, r, t = lax.axis_index("shard"), lax.axis_index("ctx"), lax.axis_index("tp")
    c = lax.rem(r, 2)
    even, odd = c == 0, c == 1
    left, right = {"ctx": r - 1}, {"ctx": r + 1}
    has_left, has_right = r > 0, r < nctx - 1
    ypeer, xpeer, sib = {"tp": 1 - t}, {"shard": 1 - s}, {"ctx": r + 1 - 2 * c}
    people = [(left, has_left), (right, has_right), (ypeer, None)]
    if fast:
        zl = lax.rem(r // 2, 2)
        zpeer = {"ctx": r + 2 - 4 * zl}
        people += [(xpeer, None), (zpeer, None)]
        w_send, w_recv, f_send, f_recv, own_sem, load_sem, wq16, w1f, w2f, wof, w1b, w2b, wob = rs
        loads = [
            pltpu.make_async_copy(src, dst, load_sem.at[i])
            for i, (src, dst) in enumerate(((wo_hbm, wof), (w1_hbm, w1f), (w2_hbm, w2f)))
        ]
        for cp in loads:
            cp.start()
    greet(people)

    live = {}
    if fast:
        rows = wq_ref.shape[1]
        part = rows // 2
        wcols = lambda shard, core: pl.ds(pl.multiple_of(shard * rows + core * part, 64), part)
        for i, (src, dst) in enumerate(((ng_ref, ngs), (nb_ref, nbs))):
            live["norms", i] = remote(src, dst.at[s], w_send.at[i], w_recv.at[i], xpeer)
            live["norms", i].start()
            dst[s] = src[...]
        wq16[...] = wq_ref[...].astype(BF)
        live["wq"] = remote(
            wq16.at[:, pl.ds(pl.multiple_of(c * part, 64), part)], wfull_ref.at[:, wcols(s, c)],
            w_send.at[2], w_recv.at[2], xpeer,
        )
        live["wq"].start()
        wfull_ref[:, pl.ds(pl.multiple_of(s * rows, 128), rows), :] = wq16[...]
        owns = []

        def piece_of(size, core, part):
            if core is None:
                return 0, size
            if part is None:
                return core * (size // 2), size // 2
            return core * (size // 2) + part * (size // 4), size // 4

        def region(k, tp, shard, core=None, part=None):
            if k == 1:
                size = w1_hbm.shape[0]
                at, count = piece_of(size, core, part)
                return f1_hbm.at[tp, pl.ds(pl.multiple_of(shard * size + at, 32), count)]
            ref, src = ((fo_hbm, wo_hbm), None, (f2_hbm, w2_hbm))[k]
            size, cols = src.shape
            at, count = piece_of(size, core, part)
            return ref.at[tp, pl.ds(pl.multiple_of(at, 32), count), pl.ds(pl.multiple_of(shard * cols, 128), cols)]

        wide, narrow = (wof, w1f, w2f), (wob, w1b, w2b)

        def own_rows(k, part=None):
            at, count = piece_of(narrow[k].shape[0], c, part)
            return narrow[k].at[pl.ds(pl.multiple_of(at, 32), count)]

        def send(kind, k, src, dst, device):
            live[kind, k] = remote(src, dst, f_send.at[kind, k], f_recv.at[kind, k], device)
            live[kind, k].start()

        def forward(kind, k, place, device):
            send(kind, k, place, place, device)

        def round_weight(k):
            loads[k].wait()
            narrow[k][...] = wide[k][...].astype(BF)
            owns.append(pltpu.make_async_copy(narrow[k], region(k, t, s), own_sem.at[k]))
            owns[-1].start()

        def to_y(k):
            send(0, k, own_rows(k, zl), region(k, t, s, c, zl), ypeer)

        def to_x(k):
            send(1, k, own_rows(k), region(k, t, s, c), xpeer)

        def from_y(k):
            live[0, k].wait_recv()
            forward(2, k, region(k, 1 - t, s, c, zl), xpeer)
            forward(3, k, region(k, 1 - t, s, c, zl), zpeer)

        def from_x(k):
            live[1, k].wait_recv()
            forward(5, k, region(k, t, 1 - s, c), sib)

        def from_z(k):
            live[3, k].wait_recv()
            forward(6, k, region(k, 1 - t, s, c), sib)
            forward(4, k, region(k, 1 - t, s, c, 1 - zl), xpeer)

        def complete(k):
            live[2, k].wait_recv()
            live[4, k].wait_recv()
            forward(7, k, region(k, 1 - t, 1 - s, c), sib)
    else:
        ngs[...] = ng_ref[...]
        nbs[...] = nb_ref[...]
        wfull_ref[...] = wq_ref[...]

    my_half = pl.ds(pl.multiple_of(t * half, 128), half)
    sent = []

    def pass_on(w, b, parity):
        if w == nw:
            return
        if parity:
            cp = remote(
                slots.at[w, b, my_half], slots.at[w + 1, b, my_half], ring_send.at[w, b], ring_recv.at[w + 1, b], right
            )
        else:
            cp = remote(slots.at[w, b], slots.at[w + 1, b], ring_send.at[w, b], ring_recv.at[w + 1, b], right)
        cond = (r >= w) & has_right & (c == parity)
        pl.when(cond)(lambda: cp.start())
        sent.append((cond, cp))

    def side(w, b):
        return remote(slots.at[w, b, my_half], slots.at[w, b, my_half], side_send.at[w, b], side_recv.at[w, b], ypeer)

    def take(w, b):
        if w > nw:
            return

        def go():
            remote(
                slots.at[w, b, my_half], slots.at[w, b, my_half], ring_send.at[w, b], ring_recv.at[w, b], left
            ).wait_recv()
            side(w, b).start()

        pl.when((r >= w) & even)(go)
        sent.append(((r >= w) & even, side(w, b)))

    def whole(w, b, parity):
        if w > nw:
            return

        def go():
            if parity:
                remote(slots.at[w, b], slots.at[w, b], ring_send.at[w, b], ring_recv.at[w, b], left).wait_recv()
            else:
                side(w, b).wait_recv()

        pl.when((r >= w) & (c == parity))(go)
        pass_on(w, b, parity)

    if fast:
        for k in range(3):
            round_weight(k)
            to_y(k)
        to_x(0)
        to_x(1)
    for b in range(seqs):
        x = x_ref[b].astype(F32)
        d = x - row_mean(x)
        acc_n = d * lax.rsqrt(row_mean(d * d) + EPS)
        if b == 0:
            if fast:
                for i in range(2):
                    live["norms", i].wait_recv()
            norms_ref[...] = jnp.zeros_like(norms_ref)
            norms_ref[0:2, :] = jnp.concatenate([ngs[0], ngs[1]], 1).astype(BF).astype(F32)
            norms_ref[2:6, :] = jnp.concatenate([nbs[0], nbs[1]], 1).astype(BF).astype(F32)
        slots[0, b] = (acc_n * norms_ref[0:1, :] + norms_ref[2:3, :]).astype(BF)
        for parity in range(2):
            pass_on(0, b, parity)
    small = []
    for i, (src, dst) in enumerate(((fg_ref, fgs_ref), (fb_ref, fbs_ref), (hg_ref, hgs_ref), (hb_ref, hbs_ref))):
        small.append(remote(src, dst.at[t], v_send.at[i], v_recv.at[i], ypeer))
        small[-1].start()
        dst[t] = src[...]

    for b in range(seqs):
        seg = seg_ref[b : b + 1, :]
        mine = seg_ref[b : b + 1, pl.ds(pl.multiple_of(r * length, 128), length)]
        first = jnp.zeros_like(mine)
        for v in range(1, 4):
            below = jnp.sum(jnp.where(seg < v, 1.0, 0.0), -1, keepdims=True).astype(jnp.int32)
            first = jnp.where(mine == v, below, first)
        start_ref[b] = first

    for b in range(seqs):
        take(1, b)
    for b in range(seqs):
        whole(1, b, 1)
    for b in range(seqs):
        if fast:
            put_transposed(slots[0, b], aT_ref.at[b], tmp)
        else:
            aT_ref[b] = slots[0, b]
    if fast:
        live["wq"].wait_recv()
        far = wcols(1 - s, c)
        live["wsib"] = remote(wfull_ref.at[:, far], wfull_ref.at[:, far], w_send.at[3], w_recv.at[3], sib)
        live["wsib"].start()
        live["wsib"].wait_recv()

    plan = {}
    if fast:
        last = seqs - 1
        plan = {
            (0, 0): [lambda: from_y(0)],
            (0, last): [lambda: from_y(1)],
            (1, 0): [lambda: from_y(2), lambda: to_x(2)],
            (1, last): [lambda: from_x(0)],
            (2, 0): [lambda: from_z(0), lambda: from_x(1)],
            (2, last): [lambda: from_z(1)],
            (3, 0): [lambda: from_z(2)],
        }
    items = [(w, b) for w in range(nw + 1) for b in range(seqs)]
    nbuf = kvbuf.shape[0]

    def store(i):
        w, b = items[i]
        return pltpu.make_async_copy(kvbuf.at[i % nbuf], kv_hbm.at[w, b], kv_sem.at[i % nbuf])

    exchanges = []
    qb, vb = hb_ref[0:1, :], hb_ref[1:2, :]
    for i, (w, b) in enumerate(items):
        has = r >= w
        if i >= nbuf:
            pl.when(r >= items[i - nbuf][0])(lambda i=i: store(i - nbuf).wait())

        def work(i=i, w=w, b=b):
            a = slots[w, b]
            buf = kvbuf.at[i % nbuf]
            if w == 0:
                q = (dot(a, wfull_ref[0]) + qb).astype(BF).astype(F32) * 0.125
                for p in range(heads // 2):
                    ps = slice(p * 128, (p + 1) * 128)
                    qT_ref[b, ps, :] = q[:, ps].T.astype(BF)
                split_pairs(qT_ref.at[b], qm.at[b], heads)
            buf[:, :n] = dot(a, wfull_ref[1]).astype(BF)
            buf[:, n:] = (dot(a, wfull_ref[2]) + vb).astype(BF)
            store(i).start()
            forward_item(
                w, w == 0, heads, length, bq, buf, qm.at[b], vT, start_ref[b] + (w - r) * length, bias,
                m.at[b], l.at[b], acc.at[b],
            )

        if w:
            pl.when(has)(work)
        else:
            work()
        whole(w + 1, b, 0)
        take(w + 2, b)
        whole(w + 2, b, 1)
        for what in plan.get((w, b), []):
            what()
        if w == nw:
            tot = jnp.zeros((1, length), F32)
            for h in range(heads):
                hs = slice(h * HD, (h + 1) * HD)
                o = acc[b, hs, :] / l[b, h : h + 1, :]
                oT_ref[b, hs, :] = o
                tot = tot + col_sum(o)
            tot = tot / n
            mean[b] = tot
            lse_ref[b] = m[b] + jnp.log(l[b])
            for p in range(heads // 2):
                ps = slice(p * 128, (p + 1) * 128)
                cen[b, :, ps] = (oT_ref[b, ps, :] - tot).T.astype(BF)
            theirs = pl.ds(pl.multiple_of((1 - t) * half, 128), half)
            cown_ref[b] = cen[b, my_half, :]
            mown_ref[b] = mean[b, :, my_half]
            if b == seqs - 1:
                cpeer_ref[b] = cen[b, theirs, :]
                mpeer_ref[b] = mean[b, :, theirs]
            else:
                for k, (src, dst) in enumerate(
                    ((cen.at[b, theirs], cpeer_ref.at[b]), (mean.at[b, :, theirs], mpeer_ref.at[b]))
                ):
                    exchanges.append(remote(src, dst, c_send.at[b, k], c_recv.at[b, k], ypeer))
                    exchanges[-1].start()
    for cond, cp in sent:
        pl.when(cond)(lambda cp=cp: cp.wait_send())
    for i in range(max(0, len(items) - nbuf), len(items)):
        pl.when(r >= items[i][0])(lambda i=i: store(i).wait())
    if fast:
        from_x(2)
        for k in range(3):
            complete(k)
        for k in range(3):
            for kind in (5, 6, 7):
                live[kind, k].wait_recv()
            for kind in range(8):
                live[kind, k].wait_send()
        for cp in owns:
            cp.wait()
        for key in (("norms", 0), ("norms", 1), "wq", "wsib"):
            live[key].wait_send()
    for cp in exchanges + small:
        cp.wait()


def front_call(fast, nw, nctx, x, wq, ng, nb, hb, fg, fb, hg, seg, w1, w2, wo):
    seqs, length, width = x.shape
    n = hb.shape[1]
    heads = n // HD
    half = length // 2
    sds = jax.ShapeDtypeStruct
    dma = pltpu.SemaphoreType.DMA
    bq = min(256, length)
    full = lambda w, axes: sds((2,) + tuple(k * a for k, a in zip(w.shape, axes)), BF) if fast else sds((8, 128), BF)
    out_shape = (
        sds((seqs, width, length) if fast else (seqs, length, width), BF),
        sds((seqs, n, length), BF),
        sds((seqs, n, length), F32),
        sds((seqs, 8, length), F32),
        sds((seqs, half, n), BF),
        sds((seqs, half, n), BF),
        sds((seqs, 1, half), F32),
        sds((seqs, 1, half), F32),
        sds((3, width, n), BF),
        sds((8, width), F32),
        sds((seqs, 1, length), jnp.int32),
        sds((2,) + fg.shape, F32),
        sds((2,) + fb.shape, F32),
        sds((2,) + hg.shape, F32),
        sds((2,) + hb.shape, F32),
        sds((nw + 1, seqs, length, 2 * n), BF),
        full(w1, (2, 1)),
        full(w2, (1, 2)),
        full(wo, (1, 2)),
    )
    scratch = [
        pltpu.VMEM((nw + 1, seqs, length, width), BF),
        pltpu.VMEM((3, length, 2 * n), BF),
        pltpu.VMEM((seqs, heads, 128, length), BF),
        pltpu.VMEM((n, length), BF),
        pltpu.VMEM((length, bq), F32),
        pltpu.VMEM((seqs, 8, length), F32),
        pltpu.VMEM((seqs, 8, length), F32),
        pltpu.VMEM((seqs, n, length), F32),
        pltpu.VMEM((seqs, length, n), BF),
        pltpu.VMEM((seqs, 1, length), F32),
        pltpu.VMEM((width, length), BF),
        pltpu.VMEM((2, 2, width // 2), F32),
        pltpu.VMEM((2, 4, width // 2), F32),
        dma((nw + 1, seqs)),
        dma((nw + 1, seqs)),
        dma((nw + 1, seqs)),
        dma((nw + 1, seqs)),
        dma((3,)),
        dma((seqs, 2)),
        dma((seqs, 2)),
        dma((4,)),
        dma((4,)),
    ]
    if fast:
        scratch += [dma((4,)), dma((4,)), dma((8, 3)), dma((8, 3)), dma((3,)), dma((3,)), pltpu.VMEM(wq.shape, BF)]
        scratch += [pltpu.VMEM(w.shape, F32) for w in (w1, w2, wo)]
        scratch += [pltpu.VMEM(w.shape, BF) for w in (w1, w2, wo)]
    return pl.pallas_call(
        functools.partial(front_kernel, fast, nw, nctx, heads, length),
        out_shape=out_shape,
        in_specs=[VMEM_SPEC] * 9 + [ANY_SPEC] * 3,
        out_specs=tuple([VMEM_SPEC] * 15 + [ANY_SPEC] * 4),
        scratch_shapes=scratch,
        compiler_params=pltpu.CompilerParams(
            vmem_limit_bytes=58 * 1024 * 1024, collective_id=3, has_side_effects=True
        ),
        cost_estimate=pl.CostEstimate(
            flops=seqs * (nw + 1) * length * n * (4 * length + 4 * width), bytes_accessed=32 * 1024 * 1024, transcendentals=0
        ),
        name="front",
    )(x, wq, ng, nb, hb, fg, fb, hg, seg, w1, w2, wo)


def middle_kernel(
    fast, n, half,
    cown_ref, cpeer_ref, mown_ref, mpeer_ref, norms_ref, fgs_ref, fbs_ref, hgs_ref, hbs_ref,
    x_hbm, g_hbm, f1_hbm, f2_hbm, fo_hbm,
    out_ref, g1_ref, g1s_ref, doT_ref, dlast_ref, o_ref, f_ref, z_ref, dh_ref, sum_ref,
    x_s, g_s, f1, f2, fo, u_s, gp_s, e_s, dT, tmp, clast, mlast, in_sem, w_sem, d_send, d_recv, c_send, c_recv, g_send, g_recv,
):
    seqs = cown_ref.shape[0]
    width = norms_ref.shape[1]
    step = width
    ff2 = f1.shape[2]
    ff = 2 * ff2
    t = lax.axis_index("tp")
    ypeer = {"tp": 1 - t}
    last = seqs - 1
    rows = pl.ds(pl.multiple_of(t * half, 128), half)
    loads = []
    for i, (src, dst) in enumerate(((x_hbm, x_s), (g_hbm, g_s))):
        for b in range(seqs):
            loads.append(pltpu.make_async_copy(src.at[b, rows], dst.at[b], in_sem.at[i, b]))
    weights = [pltpu.make_async_copy(src, dst, w_sem.at[i]) for i, (src, dst) in enumerate(((fo_hbm, fo), (f1_hbm, f1), (f2_hbm, f2)))]
    weights[0].start()
    for cp in loads:
        cp.start()
    weights[1].start()
    weights[2].start()
    greet([(ypeer, None)])
    sends = []
    for k, (src, dst) in enumerate(((cpeer_ref.at[last], clast), (mpeer_ref.at[last], mlast))):
        sends.append(remote(src, dst, c_send.at[k], c_recv.at[k], ypeer))
        sends[-1].start()
    vec = norms_ref[...]
    gain, shift, b_out, b_down = vec[1:2], vec[3:4], vec[4:5], vec[5:6]
    chunks = [(p, j) for p in range(2) for j in range(0, ff2, step)]
    first = t == 0

    def note(b, row, value):
        if b:
            sum_ref[row : row + 1, :] += value
        else:
            sum_ref[row : row + 1, :] = value

    def give(b, ref, value):
        ref[b, rows] = value
        sends.append(remote(ref.at[b, rows], ref.at[b, rows], g_send.at[b], g_recv.at[b], ypeer))
        sends[-1].start()

    sum_ref[...] = jnp.zeros_like(sum_ref)
    for b in range(seqs):
        if b == last:
            for cp in sends[:2]:
                cp.wait()
        mine, far = mown_ref[b], mlast[...] if b == last else mpeer_ref[b]
        gap = jnp.where(first, mine - far, far - mine) * 0.5
        delta = jnp.broadcast_to(gap, (128, half)).T[:, :1]
        own, peer = cown_ref[b].astype(F32), (clast[...] if b == last else cpeer_ref[b]).astype(F32)
        n0 = jnp.where(first, own, peer) + delta
        n1 = jnp.where(first, peer, own) - delta
        var = (jnp.sum(n0 * n0, -1, keepdims=True) + jnp.sum(n1 * n1, -1, keepdims=True)) / (2 * n)
        rs = lax.rsqrt(var + EPS)
        nh = (n0 * rs, n1 * rs)
        os = []
        for p in range(2):
            cs = slice(p * n, (p + 1) * n)
            o = (nh[p] * hgs_ref[p] + hbs_ref[p, 2:3, :]).astype(BF)
            o_ref[b, :, cs] = o
            os.append(o)
        if b == 0:
            weights[0].wait()
            for cp in loads:
                cp.wait()
        y1 = x_s[b].astype(F32) + b_out
        for p in range(2):
            y1 = y1 + dot(os[p], fo[p])
        cen = y1 - row_mean(y1)
        r2 = lax.rsqrt(row_mean(cen * cen) + EPS)
        yh = cen * r2
        f = (yh * gain + shift).astype(BF)
        g2 = g_s[b]
        if fast:
            put_transposed(g2, f_ref.at[b, 0], tmp)
            put_transposed(f, f_ref.at[b, 1], tmp)
        else:
            f_ref[b] = f
        if b == 0:
            weights[1].wait()
        usum = 0.0
        for p, j in chunks:
            cs = slice(p * ff2 + j, p * ff2 + j + step)
            h = dot(f, f1[p, :, j : j + step]) + fbs_ref[p, 0:1, j : j + step]
            u, slope = gelu_pair(h)
            u_s[:, cs] = u
            gp_s[:, cs] = slope
            usum = usum + jnp.sum(u, -1, keepdims=True)
        mu = usum / ff
        ssum = 0.0
        for p, j in chunks:
            cs = slice(p * ff2 + j, p * ff2 + j + step)
            d = u_s[:, cs] - mu
            ssum = ssum + jnp.sum(d * d, -1, keepdims=True)
        ru = lax.rsqrt(ssum / ff + EPS)
        if b == 0:
            weights[2].wait()
        y2 = y1 + b_down
        esum = 0.0
        ezsum = 0.0
        for i, (p, j) in enumerate(chunks):
            cs = slice(p * ff2 + j, p * ff2 + j + step)
            w2 = f2[p, j : j + step, :]
            zh = (u_s[:, cs] - mu) * ru
            u_s[:, cs] = zh
            fg = fgs_ref[p, :, j : j + step]
            z = (zh * fg + fbs_ref[p, 1:2, j : j + step]).astype(BF)
            z_ref[b, :, cs] = z
            y2 = y2 + dot(z, w2)
            dz = dot_nt(g2, w2)
            note(b, 6 + len(chunks) + i, col_sum(dz * zh))
            note(b, 6 + 2 * len(chunks) + i, col_sum(dz))
            e = dz * fg
            e_s[:, cs] = e
            esum = esum + jnp.sum(e, -1, keepdims=True)
            ezsum = ezsum + jnp.sum(e * zh, -1, keepdims=True)
        out_ref[b] = y2.astype(BF)
        em, ezm = esum / ff, ezsum / ff
        df = jnp.zeros_like(y1)
        for i, (p, j) in enumerate(chunks):
            cs = slice(p * ff2 + j, p * ff2 + j + step)
            du = ru * (e_s[:, cs] - em - u_s[:, cs] * ezm)
            dh = (du * gp_s[:, cs]).astype(BF)
            dh_ref[b, :, cs] = dh
            note(b, 6 + i, col_sum(dh.astype(F32)))
            df = df + dot_nt(dh, f1[p, :, j : j + step])
        note(b, 2, col_sum(df * yh))
        note(b, 3, col_sum(df))
        e2 = df * gain
        g = g2.astype(F32)
        dy1 = g + r2 * (e2 - row_mean(e2) - yh * row_mean(e2 * yh))
        g1 = dy1.astype(BF)
        if b == last:
            g1_ref[...] = g1
        else:
            give(b, g1s_ref, g1)
        if fast:
            put_transposed(g1, f_ref.at[b, 2], tmp)
        note(b, 4, col_sum(g1.astype(F32)))
        note(b, 5, col_sum(g))
        es = []
        for p in range(2):
            cs = slice(p * n, (p + 1) * n)
            dsub = dot_nt(g1, fo[p])
            for k, value in enumerate((col_sum(dsub * nh[p]), col_sum(dsub))):
                if b:
                    sum_ref[k : k + 1, cs] += value
                else:
                    sum_ref[k : k + 1, cs] = value
            es.append(dsub * hgs_ref[p])
        em = sum(jnp.sum(e, -1, keepdims=True) for e in es) / (2 * n)
        ezm = sum(jnp.sum(e * h, -1, keepdims=True) for e, h in zip(es, nh)) / (2 * n)
        for p in range(2):
            dat = rs * (es[p] - em - nh[p] * ezm)
            for k in range(n // 128):
                ks = slice(k * 128, (k + 1) * 128)
                dT[b, p, ks, :] = dat[:, ks].T.astype(BF)
        if b == last:
            dlast_ref[0] = dT[b, t]
            dlast_ref[1] = dT[b, 1 - t]
        else:
            sends.append(remote(dT.at[b, 1 - t], doT_ref.at[b, :, rows], d_send.at[b], d_recv.at[b], ypeer))
            sends[-1].start()
            doT_ref[b, :, rows] = dT[b, t]
    for cp in sends[2:]:
        cp.wait()


def middle_call(fast, cown, cpeer, mown, mpeer, norms, fgs, fbs, hgs, hbs, x, g, f1, f2, fo):
    seqs, half, n = cown.shape
    width = x.shape[2]
    ff = 2 * fgs.shape[2]
    sds = jax.ShapeDtypeStruct
    dma = pltpu.SemaphoreType.DMA
    return pl.pallas_call(
        functools.partial(middle_kernel, fast, n, half),
        out_shape=(
            sds((seqs, half, width), BF),
            sds((half, width), BF),
            sds((seqs - 1, 2 * half, width), BF),
            sds((seqs - 1, n, 2 * half), BF),
            sds((2, n, half), BF),
            sds((seqs, half, 2 * n), BF),
            sds((seqs, 3, width, half) if fast else (seqs, half, width), BF),
            sds((seqs, half, ff), BF),
            sds((seqs, half, ff), BF),
            sds((24, width), F32),
        ),
        in_specs=[VMEM_SPEC] * 9 + [ANY_SPEC] * 5,
        out_specs=(VMEM_SPEC,) * 10,
        scratch_shapes=[
            pltpu.VMEM((seqs, half, width), BF),
            pltpu.VMEM((seqs, half, width), BF),
            pltpu.VMEM(f1.shape, BF),
            pltpu.VMEM(f2.shape, BF),
            pltpu.VMEM(fo.shape, BF),
            pltpu.VMEM((half, ff), F32),
            pltpu.VMEM((half, ff), F32),
            pltpu.VMEM((half, ff), F32),
            pltpu.VMEM((seqs, 2, n, half), BF),
            pltpu.VMEM((width, half), BF),
            pltpu.VMEM((half, n), BF),
            pltpu.VMEM((1, half), F32),
            dma((2, seqs)),
            dma((3,)),
            dma((seqs,)),
            dma((seqs,)),
            dma((2,)),
            dma((2,)),
            dma((seqs - 1,)),
            dma((seqs - 1,)),
        ],
        compiler_params=pltpu.CompilerParams(
            vmem_limit_bytes=56 * 1024 * 1024, collective_id=4, has_side_effects=True
        ),
        cost_estimate=pl.CostEstimate(
            flops=4 * seqs * half * (f1.size + f2.size + fo.size), bytes_accessed=24 * 1024 * 1024, transcendentals=0
        ),
        name="middle",
    )(cown, cpeer, mown, mpeer, norms, fgs, fbs, hgs, hbs, x, g, f1, f2, fo)


def end_kernel(
    n, length,
    pn, mine0, peer0, w_ref, x_ref, g10_ref, g1_ref, aT_ref, gain_ref, p2_ref, p1_ref, po_ref, out_own,
    gt_ref, gq_ref, g2_ref, gu_ref, go_ref, total_ref, out_ref,
    mine, peer, xh, rinv, sq, rq, wq, xq, zq, zq2, z2a, z2b, z1a, z1b, zoa, zob, vec_buf,
    da_send, da_recv, out_send, out_recv, rs_send, rs_recv, vec_send, vec_recv,
):
    seqs = x_ref.shape[0]
    s, r, t = lax.axis_index("shard"), lax.axis_index("ctx"), lax.axis_index("tp")
    c, z = lax.rem(r, 2), r // 2
    lo_bit, hi_bit = lax.rem(z, 2), z // 2
    sib, ypeer, xpeer = {"ctx": r + 1 - 2 * c}, {"tp": 1 - t}, {"shard": 1 - s}
    zlo, zhi = {"ctx": r + 2 - 4 * lo_bit}, {"ctx": r + 4 - 8 * hi_bit}
    greet([(d, None) for d in (sib, ypeer, xpeer, zlo, zhi)])
    live = {}

    def send(name, src, dst, i, device):
        live[name] = remote(src, dst, rs_send.at[i], rs_recv.at[i], device)
        live[name].start()

    def add(dst, a, b):
        dst[...] = (a[...].astype(F32) + b[...].astype(F32)).astype(dst.dtype)

    groups = ((p2_ref, z2a, z2b, g2_ref), (p1_ref, z1a, z1b, gu_ref), (po_ref, zoa, zob, go_ref))
    for k, (part, za, zb, out) in enumerate(groups):
        send(("a", k), part.at[:, 1 - lo_bit], za, 2 * k, zlo)

    last = seqs - 1
    da = dot_nt(pn[last, :, :n], w_ref[0])
    da = da + dot_nt(pn[last, :, n : 2 * n], w_ref[1])
    da = da + dot_nt(pn[last, :, 2 * n :], w_ref[2])
    mine[...] = da.astype(BF)
    exchange = remote(mine, peer, da_send, da_recv, ypeer)
    exchange.start()
    half = length // 2
    my_rows = pl.ds(pl.multiple_of(t * half, 128), half)
    out_ref[my_rows, :] = out_own[...]
    give = remote(out_own, out_ref.at[my_rows], out_send, out_recv, ypeer)
    give.start()
    rows = aT_ref.shape[1] // 2

    def product(core, dst):
        at = pl.ds(pl.multiple_of(core * rows, 64), rows)
        for k in range(3):
            ks = slice(k * n, (k + 1) * n)
            acc = dot(aT_ref[0, at, :], pn[0, :, ks])
            for b in range(1, seqs):
                acc = acc + dot(aT_ref[b, at, :], pn[b, :, ks])
            acc = acc.astype(BF)
            for j in range(2):
                for i in range(4):
                    at_row = (j * 4 + i) * (rows // 8)
                    dst[j, i // 2, i % 2, :, ks] = acc[at_row : at_row + rows // 8]

    product(1 - c, sq)
    send("core", sq, rq, 6, sib)
    product(c, wq)
    sums = [jnp.zeros((1, x_ref.shape[2]), F32) for _ in range(2)]
    bias = [jnp.zeros((1, n), F32) for _ in range(2)]
    live["core"].wait_recv()
    add(wq.at[1 - s], wq.at[1 - s], rq.at[1 - s])
    send("x", wq.at[1 - s], xq, 7, xpeer)
    add(wq.at[s], wq.at[s], rq.at[s])
    for b in range(seqs):
        share = mine[...].astype(F32) if b == last else mine0[b].astype(F32)
        x = x_ref[b].astype(F32)
        cen = x - row_mean(x)
        inv = lax.rsqrt(row_mean(cen * cen) + EPS)
        rinv[b] = inv
        xh[b] = cen * inv
        sums[0] = sums[0] + col_sum(share * xh[b])
        sums[1] = sums[1] + col_sum(share)
        bias[0] = bias[0] + col_sum(pn[b, :, :n].astype(F32))
        bias[1] = bias[1] + col_sum(pn[b, :, 2 * n :].astype(F32))
    total_ref[...] = jnp.zeros_like(total_ref)
    total_ref[0:1, :] = sums[0]
    total_ref[1:2, :] = sums[1]
    total_ref[2:3, :n] = bias[0]
    total_ref[2:3, n:] = bias[1]
    partners = [sib, xpeer, zlo, zhi, ypeer]
    count = len(partners)

    def vec(stage):
        if stage:
            live[("v", stage - 1)].wait()
            if stage == count:
                total_ref[0:2, :] = total_ref[0:2, :] + vec_buf[stage - 1, 0:2, :]
            else:
                total_ref[...] = total_ref[...] + vec_buf[stage - 1]
        if stage < count:
            vec_buf[count] = total_ref[...]
            live[("v", stage)] = remote(
                vec_buf.at[count], vec_buf.at[stage], vec_send.at[stage], vec_recv.at[stage], partners[stage]
            )
            live[("v", stage)].start()

    vec(0)
    vec(1)
    for k, (part, za, zb, out) in enumerate(groups):
        live[("a", k)].wait_recv()
        add(za, part.at[:, lo_bit], za)
        send(("b", k), za.at[1 - hi_bit], zb, 2 * k + 1, zhi)
    vec(2)
    live["x"].wait_recv()
    add(wq.at[s], wq.at[s], xq)
    send("za", wq.at[s, :, 1 - lo_bit], zq, 8, zlo)
    vec(3)

    def finish(b):
        own, far = (mine[...], peer[...]) if b == last else (mine0[b], peer0[b])
        e = (own.astype(F32) + far.astype(F32)) * gain_ref[...]
        h = xh[b]
        dx = rinv[b] * (e - row_mean(e) - h * row_mean(e * h))
        g1 = g1_ref[...] if b == last else g10_ref[b]
        gt_ref[b] = (g1.astype(F32) + dx).astype(BF)

    for b in range(last):
        finish(b)
    live["za"].wait_recv()
    add(wq.at[s, :, lo_bit], wq.at[s, :, lo_bit], zq)
    send("zb", wq.at[s, 1 - hi_bit, lo_bit], zq2, 9, zhi)
    vec(4)
    for k, (part, za, zb, out) in enumerate(groups):
        live[("b", k)].wait_recv()
        add(out, za.at[hi_bit], zb)
    exchange.wait()
    finish(last)
    live["zb"].wait_recv()
    total = wq[s, hi_bit, lo_bit].astype(F32) + zq2[...].astype(F32)
    for k in range(3):
        gq_ref[k] = total[:, k * n : (k + 1) * n]
    vec(5)
    for key, cp in live.items():
        if not (isinstance(key, tuple) and key[0] == "v"):
            cp.wait_send()
    give.wait()


def end_call(pn, mine0, peer0, w, x, g10, g1, aT, gain, p2, p1, po, out_own):
    seqs, length, width = x.shape
    n = pn.shape[2] // 3
    piece = width // 16
    sds = jax.ShapeDtypeStruct
    dma = pltpu.SemaphoreType.DMA
    c2, c1, co = p2.shape[-1], p1.shape[-1], po.shape[-1]
    return pl.pallas_call(
        functools.partial(end_kernel, n, length),
        out_shape=(
            sds((seqs, length, width), BF),
            sds((3, piece, n), F32),
            sds((piece, c2), F32),
            sds((piece, c1), F32),
            sds((piece, co), F32),
            sds((8, width), F32),
            sds((length, width), BF),
        ),
        in_specs=[VMEM_SPEC] * 13,
        out_specs=(VMEM_SPEC,) * 7,
        scratch_shapes=[
            pltpu.VMEM((length, width), BF),
            pltpu.VMEM((length, width), BF),
            pltpu.VMEM((seqs, length, width), F32),
            pltpu.VMEM((seqs, length, 1), F32),
            pltpu.VMEM((2, 2, 2, piece, 3 * n), BF),
            pltpu.VMEM((2, 2, 2, piece, 3 * n), BF),
            pltpu.VMEM((2, 2, 2, piece, 3 * n), BF),
            pltpu.VMEM((2, 2, piece, 3 * n), BF),
            pltpu.VMEM((2, piece, 3 * n), BF),
            pltpu.VMEM((piece, 3 * n), BF),
            pltpu.VMEM((2, piece, c2), BF),
            pltpu.VMEM((piece, c2), BF),
            pltpu.VMEM((2, piece, c1), BF),
            pltpu.VMEM((piece, c1), BF),
            pltpu.VMEM((2, piece, co), BF),
            pltpu.VMEM((piece, co), BF),
            pltpu.VMEM((6, 8, width), F32),
            dma,
            dma,
            dma,
            dma,
            dma((10,)),
            dma((10,)),
            dma((5,)),
            dma((5,)),
        ],
        compiler_params=pltpu.CompilerParams(
            vmem_limit_bytes=56 * 1024 * 1024, collective_id=2, has_side_effects=True
        ),
        cost_estimate=pl.CostEstimate(
            flops=12 * seqs * length * width * n, bytes_accessed=16 * 1024 * 1024, transcendentals=0
        ),
        name="input_back",
    )(pn, mine0, peer0, w, x, g10, g1, aT, gain, p2, p1, po, out_own)


def swap(value, axis):
    return lax.ppermute(value, axis, [(0, 1), (1, 0)])


def scatter_rows(grad, t=None):
    width, cols = grad.shape
    if t is not None:
        grad = lax.psum_scatter(grad.reshape(width, 2, cols // 2), "tp", scatter_dimension=1, tiled=False)
    return lax.psum_scatter(grad.astype(F32), ("shard", "ctx"), scatter_dimension=0, tiled=True)


def per_device(
    tokens,
    cotangent,
    segment_ids,
    w_qkv,
    w_out,
    w_fc1,
    w_fc2,
    norm_gain,
    norm_bias,
    head_gain,
    head_bias,
    ffn_gain,
    ffn_bias,
):
    seqs, length, width = tokens.shape
    n = w_qkv.shape[2]
    ff2 = w_fc1.shape[1]
    s, r, t = lax.axis_index("shard"), lax.axis_index("ctx"), lax.axis_index("tp")
    nctx = lax.axis_size("ctx")
    fast = lax.axis_size("shard") == 2 and nctx == 8
    nw = min(-(-(MAXDOC - 1) // length), nctx - 1)

    wq, w1, w2, wo, ng, nb = w_qkv, w_fc1, w_fc2, w_out, norm_gain, norm_bias
    if not fast:
        wq = lax.all_gather(wq.astype(BF), "shard", axis=1, tiled=True)
        ng, nb = (
            lax.all_gather(v, "shard", axis=1, tiled=True).reshape(-1, 2, width // 2).transpose(1, 0, 2) for v in (ng, nb)
        )
        full = [lax.all_gather(w.astype(BF), "shard", axis=a, tiled=True) for w, a in ((w1, 0), (w2, 1), (wo, 1))]
        full = [lax.all_gather(w, "tp", axis=0) for w in full]

    (acts, qT, oT, lse, cown, cpeer, mown, mpeer, wfull, norms, start, fgs, fbs, hgs, hbs, kv, f1, f2, fo) = front_call(
        fast, nw, nctx, tokens, wq, ng, nb, head_bias, ffn_gain[None], ffn_bias, head_gain[None], segment_ids, w1, w2, wo
    )
    if not fast:
        f1, f2, fo = full
    out_own, g1_own, g10, doT, dlast, o, lt, z_act, dh, sums = middle_call(
        fast, cown, cpeer, mown, mpeer, norms, fgs, fbs, hgs, hbs, tokens, cotangent, f1, f2, fo
    )
    pn, mine0, peer0, part2, part1, parto, sums_all, g1, out0 = back_call(
        fast, nw, nctx, qT, doT, dlast, oT, lse, start, wfull, sums[None], kv, lt, z_act, dh, o, g1_own, out_own
    )
    gains = norms[:1]

    def fold_rows(value):
        return value.reshape((-1,) + value.shape[2:])

    if fast:
        split = lambda part: part.reshape(2, 2, part.shape[0] // 4, part.shape[1])
        grad_tokens, grad_qkv, gd, gu, go, tails, out1 = end_call(
            pn, mine0, peer0, wfull, tokens, g10, g1, acts, gains, split(part2), split(part1), split(parto), out_own[seqs - 1]
        )
        in_sums, bias_q, bias_v = tails[:2], tails[2, :n], tails[2, n:]
    else:
        outer = lambda left, right: lax.dot_general(
            fold_rows(left), fold_rows(right), (((0,), (0,)), ((), ())), preferred_element_type=F32
        ).astype(BF)
        g_all = jnp.concatenate([g10, g1[None]])
        g1_rows = lax.dynamic_slice_in_dim(g_all, t * (length // 2), length // 2, 1)
        both = lax.all_gather(out_own[seqs - 1], "tp", axis=0, tiled=True)
        out1 = both
        g_own = lax.dynamic_slice_in_dim(cotangent, t * (length // 2), length // 2, 1)
        gd = scatter_rows(outer(g_own, z_act), t)
        gu = scatter_rows(outer(lt, dh), t)
        go = scatter_rows(outer(g1_rows, o), t)
        sums_all = lax.psum(sums, ("shard", "ctx", "tp"))
        grad_tokens, in_sums = [], 0.0
        for b in range(seqs):
            da = sum(dot_nt(pn[b, :, i * n : (i + 1) * n], wfull[i]) for i in range(3)).astype(BF)
            gt, part = tail_call(da, swap(da, "tp"), tokens[b], g_all[b], gains)
            grad_tokens.append(gt)
            in_sums = in_sums + part
        grad_tokens = jnp.stack(grad_tokens)
        grad_qkv = scatter_rows(outer(acts, pn)).reshape(-1, 3, n).transpose(1, 0, 2)
        tails = lax.psum(
            jnp.concatenate([in_sums.reshape(-1), jnp.sum(pn.astype(F32), (0, 1))]), ("shard", "ctx")
        )
        in_sums, bias_q, bias_v = tails[: 2 * width].reshape(2, width), tails[2 * width :][:n], tails[-n:]

    hsum, dsum, fsum = sums_all[:2], sums_all[2:6], sums_all[6 : 6 + 6 * ff2 // width].reshape(3, 2 * ff2)
    piece = width // (lax.axis_size("shard") * lax.axis_size("ctx"))
    mine = (s * lax.axis_size("ctx") + r) * piece
    grad_gain = lax.dynamic_slice_in_dim(jnp.stack([in_sums[0], dsum[0]]), mine, piece, 1)
    grad_bias = lax.dynamic_slice_in_dim(jnp.stack([in_sums[1], dsum[1], dsum[2], dsum[3]]), mine, piece, 1)
    hsum = lax.dynamic_slice_in_dim(hsum, t * n, n, 1)
    fsum = lax.dynamic_slice_in_dim(fsum, t * ff2, ff2, 1)
    return (
        jnp.concatenate([out0, out1[None]]),
        grad_tokens,
        grad_qkv,
        go.T,
        gu,
        gd.T,
        grad_gain,
        grad_bias,
        hsum[0],
        jnp.stack([bias_q, bias_v, hsum[1]]),
        fsum[1],
        jnp.stack([fsum[0], fsum[2]]),
    )


def solution(mesh):
    in_specs = (
        P("shard", "ctx", None),
        P("shard", "ctx", None),
        P("shard", None),
        P(None, "shard", "tp"),
        P("tp", "shard"),
        P("shard", "tp"),
        P("tp", "shard"),
        P(None, "shard"),
        P(None, "shard"),
        P("tp"),
        P(None, "tp"),
        P("tp"),
        P(None, "tp"),
    )
    out_specs = (
        P("shard", "ctx", None),
        P("shard", "ctx", None),
        P(None, ("shard", "ctx"), "tp"),
        P("tp", ("shard", "ctx")),
        P(("shard", "ctx"), "tp"),
        P("tp", ("shard", "ctx")),
        P(None, ("shard", "ctx")),
        P(None, ("shard", "ctx")),
        P("tp"),
        P(None, "tp"),
        P("tp"),
        P(None, "tp"),
    )
    return jax.shard_map(
        per_device, mesh=mesh, in_specs=in_specs, out_specs=out_specs, check_vma=False
    )
```

```python
import functools

import jax
import jax.numpy as jnp
from jax import lax
from jax.experimental import pallas as pl
from jax.experimental.pallas import tpu as pltpu
from jax.sharding import PartitionSpec as P

HD = 64
NEG = -1e30
VL = 48 * 1024 * 1024

EPS = 1e-05
MAXDOC = 1920
BF = jnp.bfloat16
F32 = jnp.float32
NT_DIMS = (((1,), (1,)), ((), ()))
VMEM_SPEC = pl.BlockSpec(memory_space=pltpu.VMEM)
ANY_SPEC = pl.BlockSpec(memory_space=pl.ANY)
GELU_C = 0.7978845608028654
GELU_A = 0.044715


def dot(left, right):
    return jnp.dot(left, right, preferred_element_type=F32)


def dot_nt(left, right):
    return lax.dot_general(left, right, NT_DIMS, preferred_element_type=F32)


def row_mean(values):
    return jnp.mean(values, -1, keepdims=True)


def col_sum(values):
    return jnp.sum(values, 0, keepdims=True)


def put_transposed(value, dst, tmp):
    width = value.shape[1]
    for k in range(width // 128):
        tmp[k * 128 : (k + 1) * 128, :] = value[:, k * 128 : (k + 1) * 128].T
    piece = width // 16
    for shard in range(2):
        for z in range(4):
            for core in range(2):
                to = core * (width // 2) + shard * (width // 4) + z * piece
                at = shard * (width // 2) + (z * 2 + core) * piece
                dst[to : to + piece, :] = tmp[at : at + piece, :]


def gelu_pair(h):
    inner = GELU_C * (h + GELU_A * h * h * h)
    t = jnp.tanh(inner)
    half = 0.5 * (1.0 + t)
    slope = half + 0.5 * h * (1.0 - t * t) * (GELU_C * (1.0 + (3.0 * GELU_A) * h * h))
    return h * half, slope


def tail_kernel(own_ref, peer_ref, x_ref, g1_ref, gain_ref, out_ref, sum_ref):
    da = own_ref[...].astype(F32) + peer_ref[...].astype(F32)
    x = x_ref[...].astype(F32)
    cen = x - row_mean(x)
    r = lax.rsqrt(row_mean(cen * cen) + EPS)
    xh = cen * r
    sum_ref[0:1, :] = col_sum(da * xh)
    sum_ref[1:2, :] = col_sum(da)
    e = da * gain_ref[...]
    dx = r * (e - row_mean(e) - xh * row_mean(e * xh))
    out_ref[...] = (g1_ref[...].astype(F32) + dx).astype(BF)


def tail_call(own, peer, x, g1, gain):
    rows, width = x.shape
    return pl.pallas_call(
        tail_kernel,
        out_shape=(jax.ShapeDtypeStruct((rows, width), BF), jax.ShapeDtypeStruct((2, width), F32)),
        in_specs=[VMEM_SPEC] * 5,
        out_specs=(VMEM_SPEC, VMEM_SPEC),
        compiler_params=pltpu.CompilerParams(vmem_limit_bytes=VL),
        cost_estimate=pl.CostEstimate(
            flops=20 * rows * width, bytes_accessed=10 * rows * width, transcendentals=rows
        ),
        name="tail",
    )(own, peer, x, g1, gain)


MESH_ID = pl.DeviceIdType.MESH


def remote(src, dst, send, recv, device):
    return pltpu.make_async_remote_copy(
        src_ref=src, dst_ref=dst, send_sem=send, recv_sem=recv, device_id=device, device_id_type=MESH_ID
    )


def greet(devices):
    sem = pltpu.get_barrier_semaphore()
    count = 0
    for device, cond in devices:
        def signal(device=device):
            pl.semaphore_signal(sem, inc=1, device_id=device, device_id_type=MESH_ID)
        if cond is None:
            signal()
            count = count + 1
        else:
            pl.when(cond)(signal)
            count = count + cond.astype(jnp.int32)
    pl.semaphore_wait(sem, count)


def chunk_blocks(w, length, bq, bk):
    found = []
    for kb in range(length // bk):
        for qb in range(length // bq):
            if w == 0 and kb * bk > qb * bq + bq - 1:
                continue
            if qb * bq + w * length - (MAXDOC - 1) > kb * bk + bk - 1:
                continue
            found.append((qb, kb))
    return found


def block_bias(w, lo, qb, kb, bq, bk):
    key = lax.broadcasted_iota(jnp.int32, (bk, bq), 0) + kb * bk
    seen = key >= lo[:, qb * bq : (qb + 1) * bq]
    if w == 0 and (kb + 1) * bk > qb * bq + 1:
        seen = seen & (key <= lax.broadcasted_iota(jnp.int32, (bk, bq), 1) + qb * bq)
    return jnp.where(seen, 0.0, NEG)


def split_pairs(src, dst, heads):
    row = lax.broadcasted_iota(jnp.int32, (2 * HD, src.shape[1]), 0)
    for p in range(heads // 2):
        block = src[p * 128 : (p + 1) * 128, :]
        dst[2 * p] = jnp.where(row < HD, block, jnp.zeros_like(block))
        dst[2 * p + 1] = jnp.where(row >= HD, block, jnp.zeros_like(block))


def back_item(w, heads, length, bq, bk, kv, qT, doT, qm, dm, kT, lse, dd, lo, bias, dq, dk, dv):
    n = heads * HD
    for p in range(heads // 2):
        ps = slice(p * 128, (p + 1) * 128)
        kT[ps, :] = kv[:, ps].T
    blocks = chunk_blocks(w, length, bq, bk)
    for kb in range(length // bk):
        ks = slice(kb * bk, (kb + 1) * bk)
        mine = [qb for qb, other in blocks if other == kb]
        if not mine:
            dk[:, ks] = jnp.zeros((n, bk), F32)
            dv[:, ks] = jnp.zeros((n, bk), F32)
        for turn, qb in enumerate(mine):
            qs = slice(qb * bq, (qb + 1) * bq)
            bias[...] = block_bias(w, lo, qb, kb, bq, bk)

            def scores(h):
                ps = slice((h // 2) * 128, (h // 2 + 1) * 128)
                pv = slice(n + (h // 2) * 128, n + (h // 2 + 1) * 128)
                return dot(kv[ks, ps], qm[h, :, qs]) + bias[...], dot(kv[ks, pv], dm[h, :, qs])

            ahead = scores(0)
            for h in range(heads):
                hs = slice(h * HD, (h + 1) * HD)
                s, dp = ahead
                ahead = scores(h + 1) if h + 1 < heads else None
                e = jnp.exp(s - lse[h : h + 1, qs])
                ds = (e * (dp - dd[h : h + 1, qs])).astype(BF)
                new_v = dot_nt(doT[hs, qs], e.astype(BF))
                new_k = dot_nt(qT[hs, qs], ds)
                if turn:
                    dv[hs, ks] += new_v
                    dk[hs, ks] += new_k
                else:
                    dv[hs, ks] = new_v
                    dk[hs, ks] = new_k
                dq[hs, qs] += dot(kT[hs, ks], ds)


def back_kernel(
    fast, nw, nctx, heads, length,
    qT_ref, doT_ref, dlast_ref, oT_ref, lse_ref, lo_ref, wfull_ref, sum_ref,
    kv_hbm, lt_hbm, z_hbm, dh_hbm, o_hbm, g1_own,
    pn_ref, mine_ref, peer_ref, part2_ref, part1_ref, parto_ref, total_ref, g1_ref,
    slots, kvbuf, qm, dm, kT, bias, dk, dv, dd, dq, dlast,
    ring_send, ring_recv, kv_sem, da_send, da_recv, last_send, last_recv, own_sem, give_send, give_recv, *rs,
):
    n = heads * HD
    bq = bk = min(256, length)
    s, r, t = lax.axis_index("shard"), lax.axis_index("ctx"), lax.axis_index("tp")
    c = lax.rem(r, 2)
    sib, ypeer = {"ctx": r + 1 - 2 * c}, {"tp": 1 - t}
    left, right = {"ctx": r - 1}, {"ctx": r + 1}
    has_left, has_right = r > 0, r < nctx - 1
    half = length // 2
    seqs = qT_ref.shape[0]
    last = seqs - 1
    order = [(w, b) for b in range(last) for w in range(nw, -1, -1)]
    tail = [(w, last) for w in range(nw, -1, -1)]
    items = order[:-1] + tail[:1] + order[-1:] + tail[1:]
    nbuf = kvbuf.shape[0]

    def load(i):
        w, b = items[i]
        return pltpu.make_async_copy(kv_hbm.at[w, b], kvbuf.at[i % nbuf], kv_sem.at[i % nbuf])

    def start_load(i):
        if i < len(items):
            pl.when(r >= items[i][0])(lambda: load(i).start())

    for i in range(nbuf - 1):
        start_load(i)
    people = [(left, has_left), (right, has_right), (ypeer, None)]
    if fast:
        (lt_ref, z_ref, dh_ref, o_ref, mid_sem) = rs[:5]
        rs = rs[5:]
        mids = [
            pltpu.make_async_copy(src, dst, mid_sem.at[i])
            for i, (src, dst) in enumerate(((lt_hbm, lt_ref), (z_hbm, z_ref), (dh_hbm, dh_ref), (o_hbm, o_ref)))
        ]
        for cp in mids:
            cp.start()
        xpeer = {"shard": 1 - s}
        z2 = lax.rem(r // 2, 2)
        hop4 = lax.rem(r // 4, 2)
        people += [(xpeer, None), ({"ctx": r + 2 - 4 * z2}, None), ({"ctx": r + 4 - 8 * hop4}, None)]
    greet(people)

    rows = pl.ds(pl.multiple_of(t * half, 128), half)
    share = remote(dlast_ref.at[1], dlast.at[:, rows], last_send, last_recv, ypeer)
    share.start()
    dlast[:, rows] = dlast_ref[0]

    keeps, gives = [], []
    for i, (src, dst) in enumerate([(g1_own, g1_ref)]):
        keeps.append(pltpu.make_async_copy(src, dst.at[rows], own_sem.at[i]))
        gives.append(remote(src, dst.at[rows], give_send.at[i], give_recv.at[i], ypeer))
        keeps[i].start()
        gives[i].start()

    def grads_of(b):
        return dlast if b == last else doT_ref.at[b]

    def prepare(b):
        src = grads_of(b)
        split_pairs(qT_ref.at[b], qm.at[b], heads)
        split_pairs(src, dm.at[b], heads)
        for h in range(heads):
            hs = slice(h * HD, (h + 1) * HD)
            dd[b, h : h + 1, :] = col_sum(src[hs, :].astype(F32) * oT_ref[b, hs, :])
        dq[b] = jnp.zeros((n, length), F32)

    for b in range(last):
        prepare(b)

    steps = {}
    if fast:
        (s2, r2, w2, x2, y2, s1, r1, w1, y1, x1, so, ro, wo, yo, xo, vec_buf, rs_send, rs_recv, vec_send, vec_recv) = rs
        step = 512

        def product(g, rhs, core, dst, plus=None):
            cols = rhs.shape[2]
            size = step if cols % step == 0 else cols // 2
            rows = pl.ds(pl.multiple_of(core * (lt_ref.shape[2] // 2), 64), lt_ref.shape[2] // 2)

            def body(j, carry):
                at = pl.ds(pl.multiple_of(j * size, size), size)
                acc = dot(lt_ref[0, g, rows, :], rhs[0, :, at])
                for b in range(1, seqs):
                    acc = acc + dot(lt_ref[b, g, rows, :], rhs[b, :, at])
                mid = acc.shape[0] // 2
                for k in range(2):
                    value = acc[k * mid : (k + 1) * mid]
                    if plus is not None:
                        value = value + plus[k, :, at].astype(F32)
                    dst[k, :, at] = value.astype(BF)
                return carry

            lax.fori_loop(0, cols // size, body, 0)

        def add(dst, a, b):
            dst[...] = (a[...].astype(F32) + b[...].astype(F32)).astype(BF)

        live = {}

        def send(name, src, dst, i, device):
            live[name] = remote(src, dst, rs_send.at[i], rs_recv.at[i], device)
            live[name].start()

        def cols_of(ref, index):
            width = ref.shape[-1] // 2
            return pl.ds(pl.multiple_of(index * width, 128), width)

        def first(g, rhs, sbuf, rbuf, i):
            mids[1 + g].wait()
            product(g, rhs, 1 - c, sbuf)
            send(("core", g), sbuf, rbuf, i, sib)

        def x_then_y(stage):
            if stage == 0:
                first(0, z_ref, s2, r2, 0)
            elif stage == 2:
                live[("core", 0)].wait_recv()
                product(0, z_ref, c, w2, r2)
                send("x2", w2.at[1 - s], x2, 1, xpeer)
            elif stage == 3:
                live["x2"].wait_recv()
                add(w2.at[s], w2.at[s], x2)
                send("y2", w2.at[s, :, cols_of(w2, 1 - t)], y2, 2, ypeer)
            elif stage == 4:
                live["y2"].wait_recv()
                add(part2_ref, w2.at[s, :, cols_of(w2, t)], y2)

        def y_then_x(stage, g, rhs, sb, rb, wb, yb, xb, part, i):
            if stage == 0:
                first(g, rhs, sb, rb, i)
            elif stage == 2:
                live[("core", g)].wait_recv()
                product(g, rhs, c, wb, rb)
                send(("y", g), wb.at[:, :, cols_of(wb, 1 - t)], yb, i + 1, ypeer)
            elif stage == 3:
                live[("y", g)].wait_recv()
                mine = cols_of(wb, t)
                add(wb.at[1 - s, :, mine], wb.at[1 - s, :, mine], yb.at[1 - s])
                send(("x", g), wb.at[1 - s, :, mine], xb, i + 2, xpeer)
                add(wb.at[s, :, mine], wb.at[s, :, mine], yb.at[s])
            elif stage == 4:
                live[("x", g)].wait_recv()
                add(part, wb.at[s, :, cols_of(wb, t)], xb)

        up = lambda stage: y_then_x(stage, 1, dh_ref, s1, r1, w1, y1, x1, part1_ref, 3)
        op = lambda stage: y_then_x(stage, 2, o_ref, so, ro, wo, yo, xo, parto_ref, 6)

        partners = [ypeer, xpeer, sib, {"ctx": r + 2 - 4 * z2}, {"ctx": r + 4 - 8 * hop4}]
        count = vec_buf.shape[0] - 1

        def vec(stage):
            if stage == 0:
                acc = sum_ref[0]
                for b in range(1, sum_ref.shape[0]):
                    acc = acc + sum_ref[b]
                total_ref[...] = acc
            else:
                live[("v", stage - 1)].wait()
                total_ref[...] = total_ref[...] + vec_buf[stage - 1]
            if stage < len(partners):
                vec_buf[count] = total_ref[...]
                live[("v", stage)] = remote(
                    vec_buf.at[count], vec_buf.at[stage], vec_send.at[stage], vec_recv.at[stage], partners[stage]
                )
                live[("v", stage)].start()

        plan = [
            [],
            [lambda: mids[0].wait(), lambda: up(0), lambda: x_then_y(0)],
            [lambda: up(2)],
            [lambda: x_then_y(2)],
            [lambda: op(0)],
            [lambda: op(2), lambda: vec(0)],
            [lambda: up(3), lambda: vec(1)],
            [lambda: op(3), lambda: vec(2)],
            [lambda: x_then_y(3), lambda: vec(3)],
            [lambda: vec(4)],
            [lambda: vec(5), lambda: op(4), lambda: up(4), lambda: x_then_y(4)],
        ]
        for i, what in enumerate(plan):
            steps[i] = what
        ends = lambda: [cp.wait_send() for key, cp in live.items() if not (isinstance(key, tuple) and key[0] == "v")]
    else:
        ends = lambda: None

    def project(b):
        for k in range(n // 128):
            ks = slice(k * 128, (k + 1) * 128)
            pn_ref[b, :, ks] = (dq[b, ks, :] * 0.125).T.astype(BF)
        for k in range(2 * n // 128):
            pn_ref[b, :, n + k * 128 : n + (k + 1) * 128] = slots[0, b, k * 128 : (k + 1) * 128, :].T

    unseen = max(0, nw * length - (MAXDOC - 1)) // 128 * 128
    sends = []
    shares = []
    for i, (w, b) in enumerate(items):
        start_load(i + nbuf - 1)
        has = r >= w
        if b == last and w == nw:
            share.wait_recv()
            prepare(b)

        def work(i=i, w=w, b=b):
            load(i).wait()
            back_item(
                w, heads, length, bq, bk, kvbuf.at[i % nbuf], qT_ref.at[b], grads_of(b), qm.at[b], dm.at[b], kT,
                lse_ref.at[b], dd.at[b], lo_ref[b] + (w - r) * length, bias, dq.at[b], dk, dv,
            )

        pl.when(has)(work)
        if w < nw:
            for what in steps.get(i, []):
                what()
        dest = slots.at[w, b]
        if w < nw:
            far = unseen if w == nw - 1 else 0
            keys = slice(far, length)

            def merge(w=w, b=b, dest=dest, far=far, keys=keys):
                place = slots.at[w, b, :, keys]
                remote(place, place, ring_send.at[w, b], ring_recv.at[w, b], left).wait_recv()
                dest[:n, keys] = (dk[:, keys] + slots[w, b, :n, keys].astype(F32)).astype(BF)
                dest[n:, keys] = (dv[:, keys] + slots[w, b, n:, keys].astype(F32)).astype(BF)
                if far:
                    dest[:n, :far] = dk[:, :far].astype(BF)
                    dest[n:, :far] = dv[:, :far].astype(BF)

            pl.when(has & has_right)(merge)

        def plain(dest=dest):
            dest[:n, :] = dk[...].astype(BF)
            dest[n:, :] = dv[...].astype(BF)

        pl.when((has & jnp.logical_not(has_right)) if w < nw else has)(plain)
        if w:
            keys = slice(unseen if w == nw else 0, length)
            cp = remote(
                slots.at[w, b, :, keys], slots.at[w - 1, b, :, keys], ring_send.at[w, b], ring_recv.at[w - 1, b], left
            )
            pl.when(has)(lambda cp=cp: cp.start())
            sends.append((has, cp))
            if w == nw:
                for what in steps.get(i, []):
                    what()
        else:
            project(b)
            if b < last:
                da = dot_nt(pn_ref[b, :, :n], wfull_ref[0])
                da = da + dot_nt(pn_ref[b, :, n : 2 * n], wfull_ref[1])
                da = da + dot_nt(pn_ref[b, :, 2 * n :], wfull_ref[2])
                mine_ref[b] = da.astype(BF)
                shares.append(remote(mine_ref.at[b], peer_ref.at[b], da_send.at[b], da_recv.at[b], ypeer))
                shares[-1].start()
    for what in steps.get(len(items), []):
        what()
    for has, cp in sends:
        pl.when(has)(lambda cp=cp: cp.wait_send())
    ends()
    for cp in keeps + gives + shares:
        cp.wait()
    share.wait_send()


def back_call(fast, nw, nctx, qT, doT, dlast, oT, lse, lo, wfull, sums, kv, lt, z, dh, o, g1_own):
    seqs, n, length = qT.shape
    heads = n // HD
    width = g1_own.shape[-1]
    sds = jax.ShapeDtypeStruct
    ff = z.shape[-1]
    q4 = width // 4
    rows = q4 if fast else 8
    out_shape = [
        sds((seqs, length, 3 * n), BF),
        sds((seqs - 1, length, width), BF),
        sds((seqs - 1, length, width), BF),
        sds((rows, ff // 2), BF),
        sds((rows, ff // 2), BF),
        sds((rows, n), BF),
        sds(sums.shape[1:], F32),
        sds((length, width), BF),
    ]
    bq = min(256, length)
    dma = pltpu.SemaphoreType.DMA
    scratch = [
        pltpu.VMEM((nw + 1, seqs, 2 * n, length), BF),
        pltpu.VMEM((3, length, 2 * n), BF),
        pltpu.VMEM((seqs, heads, 128, length), BF),
        pltpu.VMEM((seqs, heads, 128, length), BF),
        pltpu.VMEM((n, length), BF),
        pltpu.VMEM((bq, bq), F32),
        pltpu.VMEM((n, length), F32),
        pltpu.VMEM((n, length), F32),
        pltpu.VMEM((seqs, 8, length), F32),
        pltpu.VMEM((seqs, n, length), F32),
        pltpu.VMEM((n, length), BF),
        dma((nw + 1, seqs)),
        dma((nw + 1, seqs)),
        dma((3,)),
        dma((seqs,)),
        dma((seqs,)),
        dma,
        dma,
        dma((seqs,)),
        dma((seqs,)),
        dma((seqs,)),
    ]
    if fast:
        scratch += [pltpu.VMEM(v.shape, BF) for v in (lt, z, dh, o)] + [dma((4,))]
        full = lambda cols: pltpu.VMEM((2, q4, cols), BF)
        scratch += [full(ff), full(ff), full(ff), pltpu.VMEM((q4, ff), BF), pltpu.VMEM((q4, ff // 2), BF)]
        for cols in (ff, 2 * n):
            scratch += [full(cols), full(cols), full(cols), full(cols // 2), pltpu.VMEM((q4, cols // 2), BF)]
        scratch += [pltpu.VMEM((6,) + sums.shape[1:], F32), dma((9,)), dma((9,)), dma((5,)), dma((5,))]
    return pl.pallas_call(
        functools.partial(back_kernel, fast, nw, nctx, heads, length),
        out_shape=tuple(out_shape),
        in_specs=[VMEM_SPEC] * 8 + [ANY_SPEC] * 6,
        out_specs=tuple([VMEM_SPEC] * 7 + [ANY_SPEC]),
        scratch_shapes=scratch,
        compiler_params=pltpu.CompilerParams(
            vmem_limit_bytes=63 * 1024 * 1024, collective_id=1, has_side_effects=True
        ),
        cost_estimate=pl.CostEstimate(
            flops=seqs * (nw + 1) * 10 * length * length * n, bytes_accessed=40 * 1024 * 1024, transcendentals=0
        ),
        name="attn_back",
    )(qT, doT, dlast, oT, lse, lo, wfull, sums, kv, lt, z, dh, o, g1_own)


def forward_item(w, first, heads, length, bq, kv, qm, vT, lo, bias, m, l, acc):
    n = heads * HD
    for p in range(heads // 2):
        ps = slice(p * 128, (p + 1) * 128)
        vT[ps, :] = kv[:, n + p * 128 : n + (p + 1) * 128].T
    blocks = chunk_blocks(w, length, bq, min(256, length))
    size = min(256, length)
    for qb in range(length // bq):
        mine = [kb for q, kb in blocks if q == qb]
        if not mine:
            continue
        k0, k1 = min(mine) * size, (max(mine) + 1) * size
        qs, ks = slice(qb * bq, (qb + 1) * bq), slice(k0, k1)
        key = lax.broadcasted_iota(jnp.int32, (k1 - k0, bq), 0) + k0
        seen = key >= lo[:, qs]
        if w == 0:
            seen = seen & (key <= lax.broadcasted_iota(jnp.int32, (k1 - k0, bq), 1) + qb * bq)
        bias[: k1 - k0, :] = jnp.where(seen, 0.0, NEG)

        def scores(h):
            ps = slice((h // 2) * 128, (h // 2 + 1) * 128)
            return dot(kv[ks, ps], qm[h, :, qs]) + bias[: k1 - k0, :]

        ahead = scores(0)
        for h in range(heads):
            hs = slice(h * HD, (h + 1) * HD)
            s = ahead
            ahead = scores(h + 1) if h + 1 < heads else None
            if first:
                top = jnp.max(s, 0, keepdims=True)
                e = jnp.exp(s - top)
                l[h : h + 1, qs] = jnp.sum(e, 0, keepdims=True)
                acc[hs, qs] = dot(vT[hs, ks], e.astype(BF))
            else:
                old = m[h : h + 1, qs]
                top = jnp.maximum(old, jnp.max(s, 0, keepdims=True))
                e = jnp.exp(s - top)
                scale = jnp.exp(old - top)
                l[h : h + 1, qs] = l[h : h + 1, qs] * scale + jnp.sum(e, 0, keepdims=True)
                acc[hs, qs] = acc[hs, qs] * scale + dot(vT[hs, ks], e.astype(BF))
            m[h : h + 1, qs] = top


def front_kernel(
    fast, nw, nctx, heads, length,
    x_ref, wq_ref, ng_ref, nb_ref, hb_ref, fg_ref, fb_ref, hg_ref, seg_ref, w1_hbm, w2_hbm, wo_hbm,
    aT_ref, qT_ref, oT_ref, lse_ref, cown_ref, cpeer_ref, mown_ref, mpeer_ref, wfull_ref, norms_ref, start_ref,
    fgs_ref, fbs_ref, hgs_ref, hbs_ref, kv_hbm, f1_hbm, f2_hbm, fo_hbm,
    slots, kvbuf, qm, vT, bias, m, l, acc, cen, mean, tmp, ngs, nbs,
    ring_send, ring_recv, side_send, side_recv, kv_sem, c_send, c_recv, v_send, v_recv, *rs,
):
    n = heads * HD
    seqs, _, width = x_ref.shape
    half = length // 2
    bq = min(256, length)
    s, r, t = lax.axis_index("shard"), lax.axis_index("ctx"), lax.axis_index("tp")
    c = lax.rem(r, 2)
    even, odd = c == 0, c == 1
    left, right = {"ctx": r - 1}, {"ctx": r + 1}
    has_left, has_right = r > 0, r < nctx - 1
    ypeer, xpeer, sib = {"tp": 1 - t}, {"shard": 1 - s}, {"ctx": r + 1 - 2 * c}
    people = [(left, has_left), (right, has_right), (ypeer, None)]
    if fast:
        zl = lax.rem(r // 2, 2)
        zpeer = {"ctx": r + 2 - 4 * zl}
        people += [(xpeer, None), (zpeer, None)]
        w_send, w_recv, f_send, f_recv, own_sem, load_sem, wq16, w1f, w2f, wof, w1b, w2b, wob = rs
        loads = [
            pltpu.make_async_copy(src, dst, load_sem.at[i])
            for i, (src, dst) in enumerate(((wo_hbm, wof), (w1_hbm, w1f), (w2_hbm, w2f)))
        ]
        for cp in loads:
            cp.start()
    greet(people)

    live = {}
    if fast:
        rows = wq_ref.shape[1]
        part = rows // 2
        wcols = lambda shard, core: pl.ds(pl.multiple_of(shard * rows + core * part, 64), part)
        for i, (src, dst) in enumerate(((ng_ref, ngs), (nb_ref, nbs))):
            live["norms", i] = remote(src, dst.at[s], w_send.at[i], w_recv.at[i], xpeer)
            live["norms", i].start()
            dst[s] = src[...]
        wq16[...] = wq_ref[...].astype(BF)
        live["wq"] = remote(
            wq16.at[:, pl.ds(pl.multiple_of(c * part, 64), part)], wfull_ref.at[:, wcols(s, c)],
            w_send.at[2], w_recv.at[2], xpeer,
        )
        live["wq"].start()
        wfull_ref[:, pl.ds(pl.multiple_of(s * rows, 128), rows), :] = wq16[...]
        owns = []

        def piece_of(size, core, part):
            if core is None:
                return 0, size
            if part is None:
                return core * (size // 2), size // 2
            return core * (size // 2) + part * (size // 4), size // 4

        def region(k, tp, shard, core=None, part=None):
            if k == 1:
                size = w1_hbm.shape[0]
                at, count = piece_of(size, core, part)
                return f1_hbm.at[tp, pl.ds(pl.multiple_of(shard * size + at, 32), count)]
            ref, src = ((fo_hbm, wo_hbm), None, (f2_hbm, w2_hbm))[k]
            size, cols = src.shape
            at, count = piece_of(size, core, part)
            return ref.at[tp, pl.ds(pl.multiple_of(at, 32), count), pl.ds(pl.multiple_of(shard * cols, 128), cols)]

        wide, narrow = (wof, w1f, w2f), (wob, w1b, w2b)

        def own_rows(k, part=None):
            at, count = piece_of(narrow[k].shape[0], c, part)
            return narrow[k].at[pl.ds(pl.multiple_of(at, 32), count)]

        def send(kind, k, src, dst, device):
            live[kind, k] = remote(src, dst, f_send.at[kind, k], f_recv.at[kind, k], device)
            live[kind, k].start()

        def forward(kind, k, place, device):
            send(kind, k, place, place, device)

        def round_weight(k):
            loads[k].wait()
            narrow[k][...] = wide[k][...].astype(BF)
            owns.append(pltpu.make_async_copy(narrow[k], region(k, t, s), own_sem.at[k]))
            owns[-1].start()

        def to_y(k):
            send(0, k, own_rows(k, zl), region(k, t, s, c, zl), ypeer)

        def to_x(k):
            send(1, k, own_rows(k), region(k, t, s, c), xpeer)

        def from_y(k):
            live[0, k].wait_recv()
            forward(2, k, region(k, 1 - t, s, c, zl), xpeer)
            forward(3, k, region(k, 1 - t, s, c, zl), zpeer)

        def from_x(k):
            live[1, k].wait_recv()
            forward(5, k, region(k, t, 1 - s, c), sib)

        def from_z(k):
            live[3, k].wait_recv()
            forward(6, k, region(k, 1 - t, s, c), sib)
            forward(4, k, region(k, 1 - t, s, c, 1 - zl), xpeer)

        def complete(k):
            live[2, k].wait_recv()
            live[4, k].wait_recv()
            forward(7, k, region(k, 1 - t, 1 - s, c), sib)
    else:
        ngs[...] = ng_ref[...]
        nbs[...] = nb_ref[...]
        wfull_ref[...] = wq_ref[...]

    my_half = pl.ds(pl.multiple_of(t * half, 128), half)
    sent = []

    def pass_on(w, b, parity):
        if w == nw:
            return
        if parity:
            cp = remote(
                slots.at[w, b, my_half], slots.at[w + 1, b, my_half], ring_send.at[w, b], ring_recv.at[w + 1, b], right
            )
        else:
            cp = remote(slots.at[w, b], slots.at[w + 1, b], ring_send.at[w, b], ring_recv.at[w + 1, b], right)
        cond = (r >= w) & has_right & (c == parity)
        pl.when(cond)(lambda: cp.start())
        sent.append((cond, cp))

    def side(w, b):
        return remote(slots.at[w, b, my_half], slots.at[w, b, my_half], side_send.at[w, b], side_recv.at[w, b], ypeer)

    def take(w, b):
        if w > nw:
            return

        def go():
            remote(
                slots.at[w, b, my_half], slots.at[w, b, my_half], ring_send.at[w, b], ring_recv.at[w, b], left
            ).wait_recv()
            side(w, b).start()

        pl.when((r >= w) & even)(go)
        sent.append(((r >= w) & even, side(w, b)))

    def whole(w, b, parity):
        if w > nw:
            return

        def go():
            if parity:
                remote(slots.at[w, b], slots.at[w, b], ring_send.at[w, b], ring_recv.at[w, b], left).wait_recv()
            else:
                side(w, b).wait_recv()

        pl.when((r >= w) & (c == parity))(go)
        pass_on(w, b, parity)

    if fast:
        for k in range(3):
            round_weight(k)
            to_y(k)
        to_x(0)
        to_x(1)
    for b in range(seqs):
        x = x_ref[b].astype(F32)
        d = x - row_mean(x)
        acc_n = d * lax.rsqrt(row_mean(d * d) + EPS)
        if b == 0:
            if fast:
                for i in range(2):
                    live["norms", i].wait_recv()
            norms_ref[...] = jnp.zeros_like(norms_ref)
            norms_ref[0:2, :] = jnp.concatenate([ngs[0], ngs[1]], 1).astype(BF).astype(F32)
            norms_ref[2:6, :] = jnp.concatenate([nbs[0], nbs[1]], 1).astype(BF).astype(F32)
        slots[0, b] = (acc_n * norms_ref[0:1, :] + norms_ref[2:3, :]).astype(BF)
        for parity in range(2):
            pass_on(0, b, parity)
    small = []
    for i, (src, dst) in enumerate(((fg_ref, fgs_ref), (fb_ref, fbs_ref), (hg_ref, hgs_ref), (hb_ref, hbs_ref))):
        small.append(remote(src, dst.at[t], v_send.at[i], v_recv.at[i], ypeer))
        small[-1].start()
        dst[t] = src[...]

    for b in range(seqs):
        seg = seg_ref[b : b + 1, :]
        mine = seg_ref[b : b + 1, pl.ds(pl.multiple_of(r * length, 128), length)]
        first = jnp.zeros_like(mine)
        for v in range(1, 4):
            below = jnp.sum(jnp.where(seg < v, 1.0, 0.0), -1, keepdims=True).astype(jnp.int32)
            first = jnp.where(mine == v, below, first)
        start_ref[b] = first

    for b in range(seqs):
        take(1, b)
    for b in range(seqs):
        whole(1, b, 1)
    for b in range(seqs):
        if fast:
            put_transposed(slots[0, b], aT_ref.at[b], tmp)
        else:
            aT_ref[b] = slots[0, b]
    if fast:
        live["wq"].wait_recv()
        far = wcols(1 - s, c)
        live["wsib"] = remote(wfull_ref.at[:, far], wfull_ref.at[:, far], w_send.at[3], w_recv.at[3], sib)
        live["wsib"].start()
        live["wsib"].wait_recv()

    plan = {}
    if fast:
        last = seqs - 1
        plan = {
            (0, 0): [lambda: from_y(0)],
            (0, last): [lambda: from_y(1)],
            (1, 0): [lambda: from_y(2), lambda: to_x(2)],
            (1, last): [lambda: from_x(0)],
            (2, 0): [lambda: from_z(0), lambda: from_x(1)],
            (2, last): [lambda: from_z(1)],
            (3, 0): [lambda: from_z(2)],
        }
    items = [(w, b) for w in range(nw + 1) for b in range(seqs)]
    nbuf = kvbuf.shape[0]

    def store(i):
        w, b = items[i]
        return pltpu.make_async_copy(kvbuf.at[i % nbuf], kv_hbm.at[w, b], kv_sem.at[i % nbuf])

    exchanges = []
    qb, vb = hb_ref[0:1, :], hb_ref[1:2, :]
    for i, (w, b) in enumerate(items):
        has = r >= w
        if i >= nbuf:
            pl.when(r >= items[i - nbuf][0])(lambda i=i: store(i - nbuf).wait())

        def work(i=i, w=w, b=b):
            a = slots[w, b]
            buf = kvbuf.at[i % nbuf]
            if w == 0:
                q = (dot(a, wfull_ref[0]) + qb).astype(BF).astype(F32) * 0.125
                for p in range(heads // 2):
                    ps = slice(p * 128, (p + 1) * 128)
                    qT_ref[b, ps, :] = q[:, ps].T.astype(BF)
                split_pairs(qT_ref.at[b], qm.at[b], heads)
            buf[:, :n] = dot(a, wfull_ref[1]).astype(BF)
            buf[:, n:] = (dot(a, wfull_ref[2]) + vb).astype(BF)
            store(i).start()
            forward_item(
                w, w == 0, heads, length, bq, buf, qm.at[b], vT, start_ref[b] + (w - r) * length, bias,
                m.at[b], l.at[b], acc.at[b],
            )

        if w:
            pl.when(has)(work)
        else:
            work()
        whole(w + 1, b, 0)
        take(w + 2, b)
        whole(w + 2, b, 1)
        for what in plan.get((w, b), []):
            what()
        if w == nw:
            tot = jnp.zeros((1, length), F32)
            for h in range(heads):
                hs = slice(h * HD, (h + 1) * HD)
                o = acc[b, hs, :] / l[b, h : h + 1, :]
                oT_ref[b, hs, :] = o
                tot = tot + col_sum(o)
            tot = tot / n
            mean[b] = tot
            lse_ref[b] = m[b] + jnp.log(l[b])
            for p in range(heads // 2):
                ps = slice(p * 128, (p + 1) * 128)
                cen[b, :, ps] = (oT_ref[b, ps, :] - tot).T.astype(BF)
            theirs = pl.ds(pl.multiple_of((1 - t) * half, 128), half)
            cown_ref[b] = cen[b, my_half, :]
            mown_ref[b] = mean[b, :, my_half]
            if b == seqs - 1:
                cpeer_ref[b] = cen[b, theirs, :]
                mpeer_ref[b] = mean[b, :, theirs]
            else:
                for k, (src, dst) in enumerate(
                    ((cen.at[b, theirs], cpeer_ref.at[b]), (mean.at[b, :, theirs], mpeer_ref.at[b]))
                ):
                    exchanges.append(remote(src, dst, c_send.at[b, k], c_recv.at[b, k], ypeer))
                    exchanges[-1].start()
    for cond, cp in sent:
        pl.when(cond)(lambda cp=cp: cp.wait_send())
    for i in range(max(0, len(items) - nbuf), len(items)):
        pl.when(r >= items[i][0])(lambda i=i: store(i).wait())
    if fast:
        from_x(2)
        for k in range(3):
            complete(k)
        for k in range(3):
            for kind in (5, 6, 7):
                live[kind, k].wait_recv()
            for kind in range(8):
                live[kind, k].wait_send()
        for cp in owns:
            cp.wait()
        for key in (("norms", 0), ("norms", 1), "wq", "wsib"):
            live[key].wait_send()
    for cp in exchanges + small:
        cp.wait()


def front_call(fast, nw, nctx, x, wq, ng, nb, hb, fg, fb, hg, seg, w1, w2, wo):
    seqs, length, width = x.shape
    n = hb.shape[1]
    heads = n // HD
    half = length // 2
    sds = jax.ShapeDtypeStruct
    dma = pltpu.SemaphoreType.DMA
    bq = min(256, length)
    full = lambda w, axes: sds((2,) + tuple(k * a for k, a in zip(w.shape, axes)), BF) if fast else sds((8, 128), BF)
    out_shape = (
        sds((seqs, width, length) if fast else (seqs, length, width), BF),
        sds((seqs, n, length), BF),
        sds((seqs, n, length), F32),
        sds((seqs, 8, length), F32),
        sds((seqs, half, n), BF),
        sds((seqs, half, n), BF),
        sds((seqs, 1, half), F32),
        sds((seqs, 1, half), F32),
        sds((3, width, n), BF),
        sds((8, width), F32),
        sds((seqs, 1, length), jnp.int32),
        sds((2,) + fg.shape, F32),
        sds((2,) + fb.shape, F32),
        sds((2,) + hg.shape, F32),
        sds((2,) + hb.shape, F32),
        sds((nw + 1, seqs, length, 2 * n), BF),
        full(w1, (2, 1)),
        full(w2, (1, 2)),
        full(wo, (1, 2)),
    )
    scratch = [
        pltpu.VMEM((nw + 1, seqs, length, width), BF),
        pltpu.VMEM((3, length, 2 * n), BF),
        pltpu.VMEM((seqs, heads, 128, length), BF),
        pltpu.VMEM((n, length), BF),
        pltpu.VMEM((length, bq), F32),
        pltpu.VMEM((seqs, 8, length), F32),
        pltpu.VMEM((seqs, 8, length), F32),
        pltpu.VMEM((seqs, n, length), F32),
        pltpu.VMEM((seqs, length, n), BF),
        pltpu.VMEM((seqs, 1, length), F32),
        pltpu.VMEM((width, length), BF),
        pltpu.VMEM((2, 2, width // 2), F32),
        pltpu.VMEM((2, 4, width // 2), F32),
        dma((nw + 1, seqs)),
        dma((nw + 1, seqs)),
        dma((nw + 1, seqs)),
        dma((nw + 1, seqs)),
        dma((3,)),
        dma((seqs, 2)),
        dma((seqs, 2)),
        dma((4,)),
        dma((4,)),
    ]
    if fast:
        scratch += [dma((4,)), dma((4,)), dma((8, 3)), dma((8, 3)), dma((3,)), dma((3,)), pltpu.VMEM(wq.shape, BF)]
        scratch += [pltpu.VMEM(w.shape, F32) for w in (w1, w2, wo)]
        scratch += [pltpu.VMEM(w.shape, BF) for w in (w1, w2, wo)]
    return pl.pallas_call(
        functools.partial(front_kernel, fast, nw, nctx, heads, length),
        out_shape=out_shape,
        in_specs=[VMEM_SPEC] * 9 + [ANY_SPEC] * 3,
        out_specs=tuple([VMEM_SPEC] * 15 + [ANY_SPEC] * 4),
        scratch_shapes=scratch,
        compiler_params=pltpu.CompilerParams(
            vmem_limit_bytes=58 * 1024 * 1024, collective_id=3, has_side_effects=True
        ),
        cost_estimate=pl.CostEstimate(
            flops=seqs * (nw + 1) * length * n * (4 * length + 4 * width), bytes_accessed=32 * 1024 * 1024, transcendentals=0
        ),
        name="front",
    )(x, wq, ng, nb, hb, fg, fb, hg, seg, w1, w2, wo)


def middle_kernel(
    fast, n, half,
    cown_ref, cpeer_ref, mown_ref, mpeer_ref, norms_ref, fgs_ref, fbs_ref, hgs_ref, hbs_ref,
    x_hbm, g_hbm, f1_hbm, f2_hbm, fo_hbm,
    out_ref, g1_ref, g1s_ref, doT_ref, dlast_ref, o_ref, f_ref, z_ref, dh_ref, sum_ref,
    x_s, g_s, f1, f2, fo, u_s, gp_s, e_s, dT, tmp, clast, mlast, in_sem, w_sem, d_send, d_recv, c_send, c_recv, g_send, g_recv,
):
    seqs = cown_ref.shape[0]
    width = norms_ref.shape[1]
    step = width
    ff2 = f1.shape[2]
    ff = 2 * ff2
    t = lax.axis_index("tp")
    ypeer = {"tp": 1 - t}
    last = seqs - 1
    rows = pl.ds(pl.multiple_of(t * half, 128), half)
    loads = []
    for i, (src, dst) in enumerate(((x_hbm, x_s), (g_hbm, g_s))):
        for b in range(seqs):
            loads.append(pltpu.make_async_copy(src.at[b, rows], dst.at[b], in_sem.at[i, b]))
    weights = [pltpu.make_async_copy(src, dst, w_sem.at[i]) for i, (src, dst) in enumerate(((fo_hbm, fo), (f1_hbm, f1), (f2_hbm, f2)))]
    weights[0].start()
    for cp in loads:
        cp.start()
    weights[1].start()
    weights[2].start()
    greet([(ypeer, None)])
    sends = []
    for k, (src, dst) in enumerate(((cpeer_ref.at[last], clast), (mpeer_ref.at[last], mlast))):
        sends.append(remote(src, dst, c_send.at[k], c_recv.at[k], ypeer))
        sends[-1].start()
    vec = norms_ref[...]
    gain, shift, b_out, b_down = vec[1:2], vec[3:4], vec[4:5], vec[5:6]
    chunks = [(p, j) for p in range(2) for j in range(0, ff2, step)]
    first = t == 0

    def note(b, row, value):
        if b:
            sum_ref[row : row + 1, :] += value
        else:
            sum_ref[row : row + 1, :] = value

    def give(b, ref, value):
        ref[b, rows] = value
        sends.append(remote(ref.at[b, rows], ref.at[b, rows], g_send.at[b], g_recv.at[b], ypeer))
        sends[-1].start()

    sum_ref[...] = jnp.zeros_like(sum_ref)
    for b in range(seqs):
        if b == last:
            for cp in sends[:2]:
                cp.wait()
        mine, far = mown_ref[b], mlast[...] if b == last else mpeer_ref[b]
        gap = jnp.where(first, mine - far, far - mine) * 0.5
        delta = jnp.broadcast_to(gap, (128, half)).T[:, :1]
        own, peer = cown_ref[b].astype(F32), (clast[...] if b == last else cpeer_ref[b]).astype(F32)
        n0 = jnp.where(first, own, peer) + delta
        n1 = jnp.where(first, peer, own) - delta
        var = (jnp.sum(n0 * n0, -1, keepdims=True) + jnp.sum(n1 * n1, -1, keepdims=True)) / (2 * n)
        rs = lax.rsqrt(var + EPS)
        nh = (n0 * rs, n1 * rs)
        os = []
        for p in range(2):
            cs = slice(p * n, (p + 1) * n)
            o = (nh[p] * hgs_ref[p] + hbs_ref[p, 2:3, :]).astype(BF)
            o_ref[b, :, cs] = o
            os.append(o)
        if b == 0:
            weights[0].wait()
            for cp in loads:
                cp.wait()
        y1 = x_s[b].astype(F32) + b_out
        for p in range(2):
            y1 = y1 + dot(os[p], fo[p])
        cen = y1 - row_mean(y1)
        r2 = lax.rsqrt(row_mean(cen * cen) + EPS)
        yh = cen * r2
        f = (yh * gain + shift).astype(BF)
        g2 = g_s[b]
        if fast:
            put_transposed(g2, f_ref.at[b, 0], tmp)
            put_transposed(f, f_ref.at[b, 1], tmp)
        else:
            f_ref[b] = f
        if b == 0:
            weights[1].wait()
        usum = 0.0
        for p, j in chunks:
            cs = slice(p * ff2 + j, p * ff2 + j + step)
            h = dot(f, f1[p, :, j : j + step]) + fbs_ref[p, 0:1, j : j + step]
            u, slope = gelu_pair(h)
            u_s[:, cs] = u
            gp_s[:, cs] = slope
            usum = usum + jnp.sum(u, -1, keepdims=True)
        mu = usum / ff
        ssum = 0.0
        for p, j in chunks:
            cs = slice(p * ff2 + j, p * ff2 + j + step)
            d = u_s[:, cs] - mu
            ssum = ssum + jnp.sum(d * d, -1, keepdims=True)
        ru = lax.rsqrt(ssum / ff + EPS)
        if b == 0:
            weights[2].wait()
        y2 = y1 + b_down
        esum = 0.0
        ezsum = 0.0
        for i, (p, j) in enumerate(chunks):
            cs = slice(p * ff2 + j, p * ff2 + j + step)
            w2 = f2[p, j : j + step, :]
            zh = (u_s[:, cs] - mu) * ru
            u_s[:, cs] = zh
            fg = fgs_ref[p, :, j : j + step]
            z = (zh * fg + fbs_ref[p, 1:2, j : j + step]).astype(BF)
            z_ref[b, :, cs] = z
            y2 = y2 + dot(z, w2)
            dz = dot_nt(g2, w2)
            note(b, 6 + len(chunks) + i, col_sum(dz * zh))
            note(b, 6 + 2 * len(chunks) + i, col_sum(dz))
            e = dz * fg
            e_s[:, cs] = e
            esum = esum + jnp.sum(e, -1, keepdims=True)
            ezsum = ezsum + jnp.sum(e * zh, -1, keepdims=True)
        out_ref[b] = y2.astype(BF)
        em, ezm = esum / ff, ezsum / ff
        df = jnp.zeros_like(y1)
        for i, (p, j) in enumerate(chunks):
            cs = slice(p * ff2 + j, p * ff2 + j + step)
            du = ru * (e_s[:, cs] - em - u_s[:, cs] * ezm)
            dh = (du * gp_s[:, cs]).astype(BF)
            dh_ref[b, :, cs] = dh
            note(b, 6 + i, col_sum(dh.astype(F32)))
            df = df + dot_nt(dh, f1[p, :, j : j + step])
        note(b, 2, col_sum(df * yh))
        note(b, 3, col_sum(df))
        e2 = df * gain
        g = g2.astype(F32)
        dy1 = g + r2 * (e2 - row_mean(e2) - yh * row_mean(e2 * yh))
        g1 = dy1.astype(BF)
        if b == last:
            g1_ref[...] = g1
        else:
            give(b, g1s_ref, g1)
        if fast:
            put_transposed(g1, f_ref.at[b, 2], tmp)
        note(b, 4, col_sum(g1.astype(F32)))
        note(b, 5, col_sum(g))
        es = []
        for p in range(2):
            cs = slice(p * n, (p + 1) * n)
            dsub = dot_nt(g1, fo[p])
            for k, value in enumerate((col_sum(dsub * nh[p]), col_sum(dsub))):
                if b:
                    sum_ref[k : k + 1, cs] += value
                else:
                    sum_ref[k : k + 1, cs] = value
            es.append(dsub * hgs_ref[p])
        em = sum(jnp.sum(e, -1, keepdims=True) for e in es) / (2 * n)
        ezm = sum(jnp.sum(e * h, -1, keepdims=True) for e, h in zip(es, nh)) / (2 * n)
        for p in range(2):
            dat = rs * (es[p] - em - nh[p] * ezm)
            for k in range(n // 128):
                ks = slice(k * 128, (k + 1) * 128)
                dT[b, p, ks, :] = dat[:, ks].T.astype(BF)
        if b == last:
            dlast_ref[0] = dT[b, t]
            dlast_ref[1] = dT[b, 1 - t]
        else:
            sends.append(remote(dT.at[b, 1 - t], doT_ref.at[b, :, rows], d_send.at[b], d_recv.at[b], ypeer))
            sends[-1].start()
            doT_ref[b, :, rows] = dT[b, t]
    for cp in sends[2:]:
        cp.wait()


def middle_call(fast, cown, cpeer, mown, mpeer, norms, fgs, fbs, hgs, hbs, x, g, f1, f2, fo):
    seqs, half, n = cown.shape
    width = x.shape[2]
    ff = 2 * fgs.shape[2]
    sds = jax.ShapeDtypeStruct
    dma = pltpu.SemaphoreType.DMA
    return pl.pallas_call(
        functools.partial(middle_kernel, fast, n, half),
        out_shape=(
            sds((seqs, half, width), BF),
            sds((half, width), BF),
            sds((seqs - 1, 2 * half, width), BF),
            sds((seqs - 1, n, 2 * half), BF),
            sds((2, n, half), BF),
            sds((seqs, half, 2 * n), BF),
            sds((seqs, 3, width, half) if fast else (seqs, half, width), BF),
            sds((seqs, half, ff), BF),
            sds((seqs, half, ff), BF),
            sds((24, width), F32),
        ),
        in_specs=[VMEM_SPEC] * 9 + [ANY_SPEC] * 5,
        out_specs=(VMEM_SPEC,) * 10,
        scratch_shapes=[
            pltpu.VMEM((seqs, half, width), BF),
            pltpu.VMEM((seqs, half, width), BF),
            pltpu.VMEM(f1.shape, BF),
            pltpu.VMEM(f2.shape, BF),
            pltpu.VMEM(fo.shape, BF),
            pltpu.VMEM((half, ff), F32),
            pltpu.VMEM((half, ff), F32),
            pltpu.VMEM((half, ff), F32),
            pltpu.VMEM((seqs, 2, n, half), BF),
            pltpu.VMEM((width, half), BF),
            pltpu.VMEM((half, n), BF),
            pltpu.VMEM((1, half), F32),
            dma((2, seqs)),
            dma((3,)),
            dma((seqs,)),
            dma((seqs,)),
            dma((2,)),
            dma((2,)),
            dma((seqs - 1,)),
            dma((seqs - 1,)),
        ],
        compiler_params=pltpu.CompilerParams(
            vmem_limit_bytes=56 * 1024 * 1024, collective_id=4, has_side_effects=True
        ),
        cost_estimate=pl.CostEstimate(
            flops=4 * seqs * half * (f1.size + f2.size + fo.size), bytes_accessed=24 * 1024 * 1024, transcendentals=0
        ),
        name="middle",
    )(cown, cpeer, mown, mpeer, norms, fgs, fbs, hgs, hbs, x, g, f1, f2, fo)


def end_kernel(
    n, length,
    pn, mine0, peer0, w_ref, x_ref, g10_ref, g1_ref, aT_ref, gain_ref, p2_ref, p1_ref, po_ref, out_own,
    gt_ref, gq_ref, g2_ref, gu_ref, go_ref, total_ref, out_ref,
    mine, peer, xh, rinv, sq, rq, wq, xq, zq, zq2, z2a, z2b, z1a, z1b, zoa, zob, vec_buf,
    da_send, da_recv, out_send, out_recv, rs_send, rs_recv, vec_send, vec_recv,
):
    seqs = x_ref.shape[0]
    s, r, t = lax.axis_index("shard"), lax.axis_index("ctx"), lax.axis_index("tp")
    c, z = lax.rem(r, 2), r // 2
    lo_bit, hi_bit = lax.rem(z, 2), z // 2
    sib, ypeer, xpeer = {"ctx": r + 1 - 2 * c}, {"tp": 1 - t}, {"shard": 1 - s}
    zlo, zhi = {"ctx": r + 2 - 4 * lo_bit}, {"ctx": r + 4 - 8 * hi_bit}
    greet([(d, None) for d in (sib, ypeer, xpeer, zlo, zhi)])
    live = {}

    def send(name, src, dst, i, device):
        live[name] = remote(src, dst, rs_send.at[i], rs_recv.at[i], device)
        live[name].start()

    def add(dst, a, b):
        dst[...] = (a[...].astype(F32) + b[...].astype(F32)).astype(dst.dtype)

    groups = ((p2_ref, z2a, z2b, g2_ref), (p1_ref, z1a, z1b, gu_ref), (po_ref, zoa, zob, go_ref))
    for k, (part, za, zb, out) in enumerate(groups):
        send(("a", k), part.at[:, 1 - lo_bit], za, 2 * k, zlo)

    last = seqs - 1
    da = dot_nt(pn[last, :, :n], w_ref[0])
    da = da + dot_nt(pn[last, :, n : 2 * n], w_ref[1])
    da = da + dot_nt(pn[last, :, 2 * n :], w_ref[2])
    mine[...] = da.astype(BF)
    exchange = remote(mine, peer, da_send, da_recv, ypeer)
    exchange.start()
    half = length // 2
    my_rows = pl.ds(pl.multiple_of(t * half, 128), half)
    gives = []
    for b in range(seqs):
        out_ref[b, my_rows, :] = out_own[b]
        gives.append(remote(out_own.at[b], out_ref.at[b, my_rows], out_send.at[b], out_recv.at[b], ypeer))
        gives[b].start()
    rows = aT_ref.shape[1] // 2

    def product(core, dst):
        at = pl.ds(pl.multiple_of(core * rows, 64), rows)
        for k in range(3):
            ks = slice(k * n, (k + 1) * n)
            acc = dot(aT_ref[0, at, :], pn[0, :, ks])
            for b in range(1, seqs):
                acc = acc + dot(aT_ref[b, at, :], pn[b, :, ks])
            acc = acc.astype(BF)
            for j in range(2):
                for i in range(4):
                    at_row = (j * 4 + i) * (rows // 8)
                    dst[j, i // 2, i % 2, :, ks] = acc[at_row : at_row + rows // 8]

    product(1 - c, sq)
    send("core", sq, rq, 6, sib)
    product(c, wq)
    sums = [jnp.zeros((1, x_ref.shape[2]), F32) for _ in range(2)]
    bias = [jnp.zeros((1, n), F32) for _ in range(2)]
    live["core"].wait_recv()
    add(wq.at[1 - s], wq.at[1 - s], rq.at[1 - s])
    send("x", wq.at[1 - s], xq, 7, xpeer)
    add(wq.at[s], wq.at[s], rq.at[s])
    for b in range(seqs):
        share = mine[...].astype(F32) if b == last else mine0[b].astype(F32)
        x = x_ref[b].astype(F32)
        cen = x - row_mean(x)
        inv = lax.rsqrt(row_mean(cen * cen) + EPS)
        rinv[b] = inv
        xh[b] = cen * inv
        sums[0] = sums[0] + col_sum(share * xh[b])
        sums[1] = sums[1] + col_sum(share)
        bias[0] = bias[0] + col_sum(pn[b, :, :n].astype(F32))
        bias[1] = bias[1] + col_sum(pn[b, :, 2 * n :].astype(F32))
    total_ref[...] = jnp.zeros_like(total_ref)
    total_ref[0:1, :] = sums[0]
    total_ref[1:2, :] = sums[1]
    total_ref[2:3, :n] = bias[0]
    total_ref[2:3, n:] = bias[1]
    partners = [sib, xpeer, zlo, zhi, ypeer]
    count = len(partners)

    def vec(stage):
        if stage:
            live[("v", stage - 1)].wait()
            if stage == count:
                total_ref[0:2, :] = total_ref[0:2, :] + vec_buf[stage - 1, 0:2, :]
            else:
                total_ref[...] = total_ref[...] + vec_buf[stage - 1]
        if stage < count:
            vec_buf[count] = total_ref[...]
            live[("v", stage)] = remote(
                vec_buf.at[count], vec_buf.at[stage], vec_send.at[stage], vec_recv.at[stage], partners[stage]
            )
            live[("v", stage)].start()

    vec(0)
    vec(1)
    for k, (part, za, zb, out) in enumerate(groups):
        live[("a", k)].wait_recv()
        add(za, part.at[:, lo_bit], za)
        send(("b", k), za.at[1 - hi_bit], zb, 2 * k + 1, zhi)
    vec(2)
    live["x"].wait_recv()
    add(wq.at[s], wq.at[s], xq)
    send("za", wq.at[s, :, 1 - lo_bit], zq, 8, zlo)
    vec(3)

    def finish(b):
        own, far = (mine[...], peer[...]) if b == last else (mine0[b], peer0[b])
        e = (own.astype(F32) + far.astype(F32)) * gain_ref[0:1, :]
        h = xh[b]
        dx = rinv[b] * (e - row_mean(e) - h * row_mean(e * h))
        g1 = g1_ref[...] if b == last else g10_ref[b]
        gt_ref[b] = (g1.astype(F32) + dx).astype(BF)

    for b in range(last):
        finish(b)
    live["za"].wait_recv()
    add(wq.at[s, :, lo_bit], wq.at[s, :, lo_bit], zq)
    send("zb", wq.at[s, 1 - hi_bit, lo_bit], zq2, 9, zhi)
    vec(4)
    for k, (part, za, zb, out) in enumerate(groups):
        live[("b", k)].wait_recv()
        add(out, za.at[hi_bit], zb)
    exchange.wait()
    finish(last)
    live["zb"].wait_recv()
    total = wq[s, hi_bit, lo_bit].astype(F32) + zq2[...].astype(F32)
    for k in range(3):
        gq_ref[k] = total[:, k * n : (k + 1) * n]
    vec(5)
    for key, cp in live.items():
        if not (isinstance(key, tuple) and key[0] == "v"):
            cp.wait_send()
    for cp in gives:
        cp.wait()


def end_call(pn, mine0, peer0, w, x, g10, g1, aT, gain, p2, p1, po, out_own):
    seqs, length, width = x.shape
    n = pn.shape[2] // 3
    piece = width // 16
    sds = jax.ShapeDtypeStruct
    dma = pltpu.SemaphoreType.DMA
    c2, c1, co = p2.shape[-1], p1.shape[-1], po.shape[-1]
    return pl.pallas_call(
        functools.partial(end_kernel, n, length),
        out_shape=(
            sds((seqs, length, width), BF),
            sds((3, piece, n), F32),
            sds((piece, c2), F32),
            sds((piece, c1), F32),
            sds((piece, co), F32),
            sds((8, width), F32),
            sds((seqs, length, width), BF),
        ),
        in_specs=[VMEM_SPEC] * 13,
        out_specs=(VMEM_SPEC,) * 7,
        scratch_shapes=[
            pltpu.VMEM((length, width), BF),
            pltpu.VMEM((length, width), BF),
            pltpu.VMEM((seqs, length, width), F32),
            pltpu.VMEM((seqs, length, 1), F32),
            pltpu.VMEM((2, 2, 2, piece, 3 * n), BF),
            pltpu.VMEM((2, 2, 2, piece, 3 * n), BF),
            pltpu.VMEM((2, 2, 2, piece, 3 * n), BF),
            pltpu.VMEM((2, 2, piece, 3 * n), BF),
            pltpu.VMEM((2, piece, 3 * n), BF),
            pltpu.VMEM((piece, 3 * n), BF),
            pltpu.VMEM((2, piece, c2), BF),
            pltpu.VMEM((piece, c2), BF),
            pltpu.VMEM((2, piece, c1), BF),
            pltpu.VMEM((piece, c1), BF),
            pltpu.VMEM((2, piece, co), BF),
            pltpu.VMEM((piece, co), BF),
            pltpu.VMEM((6, 8, width), F32),
            dma,
            dma,
            dma((seqs,)),
            dma((seqs,)),
            dma((10,)),
            dma((10,)),
            dma((5,)),
            dma((5,)),
        ],
        compiler_params=pltpu.CompilerParams(
            vmem_limit_bytes=56 * 1024 * 1024, collective_id=2, has_side_effects=True
        ),
        cost_estimate=pl.CostEstimate(
            flops=12 * seqs * length * width * n, bytes_accessed=16 * 1024 * 1024, transcendentals=0
        ),
        name="input_back",
    )(pn, mine0, peer0, w, x, g10, g1, aT, gain, p2, p1, po, out_own)


def pack_kernel(n, gd_ref, gu_ref, go_ref, gq_ref, tail_ref, sum_ref, down_ref, up_ref, out_ref, qkv_ref, ng_ref, nb_ref, hg_ref, hb_ref, fg_ref, fb_ref):
    s, r, t = lax.axis_index("shard"), lax.axis_index("ctx"), lax.axis_index("tp")
    width = tail_ref.shape[1]
    piece = gd_ref.shape[0]
    down_ref[...] = gd_ref[...].T
    out_ref[...] = go_ref[...].T
    up_ref[...] = gu_ref[...]
    qkv_ref[...] = gq_ref[...]
    mine = lax.rem(width - (s * 8 + r) * piece, width)
    ends = pltpu.roll(tail_ref[...], mine, 1)[:, :piece]
    mids = pltpu.roll(sum_ref[0:8, :], mine, 1)[:, :piece]
    ng_ref[0:1, :] = ends[0:1]
    ng_ref[1:2, :] = mids[2:3]
    nb_ref[0:1, :] = ends[1:2]
    nb_ref[1:4, :] = mids[3:6]
    heads = pl.ds(pl.multiple_of(t * n, 128), n)
    hg_ref[...] = sum_ref[0:1, heads]
    hb_ref[0:1, :] = tail_ref[2:3, :n]
    hb_ref[1:2, :] = tail_ref[2:3, n:]
    hb_ref[2:3, :] = sum_ref[1:2, heads]
    for k, (dst, row) in enumerate(((fb_ref, 0), (fg_ref, 0), (fb_ref, 1))):
        for j in range(2):
            dst[row : row + 1, j * width : (j + 1) * width] = sum_ref[pl.ds(6 + 4 * k + 2 * t + j, 1), :]


def pack_call(gd, gu, go, gq, tails, sums):
    piece, ff2 = gd.shape
    n = go.shape[1]
    sds = jax.ShapeDtypeStruct
    return pl.pallas_call(
        functools.partial(pack_kernel, n),
        out_shape=(
            sds((ff2, piece), F32),
            sds((piece, ff2), F32),
            sds((n, piece), F32),
            sds(gq.shape, F32),
            sds((2, piece), F32),
            sds((4, piece), F32),
            sds((1, n), F32),
            sds((3, n), F32),
            sds((1, ff2), F32),
            sds((2, ff2), F32),
        ),
        in_specs=[VMEM_SPEC] * 6,
        out_specs=(VMEM_SPEC,) * 10,
        compiler_params=pltpu.CompilerParams(vmem_limit_bytes=62 * 1024 * 1024),
        name="pack",
    )(gd, gu, go, gq, tails, sums)


def swap(value, axis):
    return lax.ppermute(value, axis, [(0, 1), (1, 0)])


def scatter_rows(grad, t=None):
    width, cols = grad.shape
    if t is not None:
        grad = lax.psum_scatter(grad.reshape(width, 2, cols // 2), "tp", scatter_dimension=1, tiled=False)
    return lax.psum_scatter(grad.astype(F32), ("shard", "ctx"), scatter_dimension=0, tiled=True)


def per_device(
    tokens,
    cotangent,
    segment_ids,
    w_qkv,
    w_out,
    w_fc1,
    w_fc2,
    norm_gain,
    norm_bias,
    head_gain,
    head_bias,
    ffn_gain,
    ffn_bias,
):
    seqs, length, width = tokens.shape
    n = w_qkv.shape[2]
    ff2 = w_fc1.shape[1]
    s, r, t = lax.axis_index("shard"), lax.axis_index("ctx"), lax.axis_index("tp")
    nctx = lax.axis_size("ctx")
    fast = lax.axis_size("shard") == 2 and nctx == 8
    nw = min(-(-(MAXDOC - 1) // length), nctx - 1)

    wq, w1, w2, wo, ng, nb = w_qkv, w_fc1, w_fc2, w_out, norm_gain, norm_bias
    if not fast:
        wq = lax.all_gather(wq.astype(BF), "shard", axis=1, tiled=True)
        ng, nb = (
            lax.all_gather(v, "shard", axis=1, tiled=True).reshape(-1, 2, width // 2).transpose(1, 0, 2) for v in (ng, nb)
        )
        full = [lax.all_gather(w.astype(BF), "shard", axis=a, tiled=True) for w, a in ((w1, 0), (w2, 1), (wo, 1))]
        full = [lax.all_gather(w, "tp", axis=0) for w in full]

    (acts, qT, oT, lse, cown, cpeer, mown, mpeer, wfull, norms, start, fgs, fbs, hgs, hbs, kv, f1, f2, fo) = front_call(
        fast, nw, nctx, tokens, wq, ng, nb, head_bias, ffn_gain[None], ffn_bias, head_gain[None], segment_ids, w1, w2, wo
    )
    if not fast:
        f1, f2, fo = full
    out_own, g1_own, g10, doT, dlast, o, lt, z_act, dh, sums = middle_call(
        fast, cown, cpeer, mown, mpeer, norms, fgs, fbs, hgs, hbs, tokens, cotangent, f1, f2, fo
    )
    pn, mine0, peer0, part2, part1, parto, sums_all, g1 = back_call(
        fast, nw, nctx, qT, doT, dlast, oT, lse, start, wfull, sums[None], kv, lt, z_act, dh, o, g1_own
    )
    gains = norms[:1]

    def fold_rows(value):
        return value.reshape((-1,) + value.shape[2:])

    if fast:
        split = lambda part: part.reshape(2, 2, part.shape[0] // 4, part.shape[1])
        grad_tokens, grad_qkv, gd, gu, go, tails, out = end_call(
            pn, mine0, peer0, wfull, tokens, g10, g1, acts, norms, split(part2), split(part1), split(parto), out_own
        )
        down, up, wout, qkv, ng, nb, hg, hb, fg, fb = pack_call(gd, gu, go, grad_qkv, tails, sums_all)
        return out, grad_tokens, qkv, wout, up, down, ng, nb, hg.reshape(-1), hb, fg.reshape(-1), fb
    else:
        outer = lambda left, right: lax.dot_general(
            fold_rows(left), fold_rows(right), (((0,), (0,)), ((), ())), preferred_element_type=F32
        ).astype(BF)
        g_all = jnp.concatenate([g10, g1[None]])
        g1_rows = lax.dynamic_slice_in_dim(g_all, t * (length // 2), length // 2, 1)
        out = lax.all_gather(out_own, "tp", axis=1, tiled=True)
        g_own = lax.dynamic_slice_in_dim(cotangent, t * (length // 2), length // 2, 1)
        gd = scatter_rows(outer(g_own, z_act), t)
        gu = scatter_rows(outer(lt, dh), t)
        go = scatter_rows(outer(g1_rows, o), t)
        sums_all = lax.psum(sums, ("shard", "ctx", "tp"))
        grad_tokens, in_sums = [], 0.0
        for b in range(seqs):
            da = sum(dot_nt(pn[b, :, i * n : (i + 1) * n], wfull[i]) for i in range(3)).astype(BF)
            gt, part = tail_call(da, swap(da, "tp"), tokens[b], g_all[b], gains)
            grad_tokens.append(gt)
            in_sums = in_sums + part
        grad_tokens = jnp.stack(grad_tokens)
        grad_qkv = scatter_rows(outer(acts, pn)).reshape(-1, 3, n).transpose(1, 0, 2)
        tails = lax.psum(
            jnp.concatenate([in_sums.reshape(-1), jnp.sum(pn.astype(F32), (0, 1))]), ("shard", "ctx")
        )
        in_sums, bias_q, bias_v = tails[: 2 * width].reshape(2, width), tails[2 * width :][:n], tails[-n:]

    hsum, dsum, fsum = sums_all[:2], sums_all[2:6], sums_all[6 : 6 + 6 * ff2 // width].reshape(3, 2 * ff2)
    piece = width // (lax.axis_size("shard") * lax.axis_size("ctx"))
    mine = (s * lax.axis_size("ctx") + r) * piece
    grad_gain = lax.dynamic_slice_in_dim(jnp.stack([in_sums[0], dsum[0]]), mine, piece, 1)
    grad_bias = lax.dynamic_slice_in_dim(jnp.stack([in_sums[1], dsum[1], dsum[2], dsum[3]]), mine, piece, 1)
    hsum = lax.dynamic_slice_in_dim(hsum, t * n, n, 1)
    fsum = lax.dynamic_slice_in_dim(fsum, t * ff2, ff2, 1)
    return (
        out,
        grad_tokens,
        grad_qkv,
        go.T,
        gu,
        gd.T,
        grad_gain,
        grad_bias,
        hsum[0],
        jnp.stack([bias_q, bias_v, hsum[1]]),
        fsum[1],
        jnp.stack([fsum[0], fsum[2]]),
    )


def solution(mesh):
    in_specs = (
        P("shard", "ctx", None),
        P("shard", "ctx", None),
        P("shard", None),
        P(None, "shard", "tp"),
        P("tp", "shard"),
        P("shard", "tp"),
        P("tp", "shard"),
        P(None, "shard"),
        P(None, "shard"),
        P("tp"),
        P(None, "tp"),
        P("tp"),
        P(None, "tp"),
    )
    out_specs = (
        P("shard", "ctx", None),
        P("shard", "ctx", None),
        P(None, ("shard", "ctx"), "tp"),
        P("tp", ("shard", "ctx")),
        P(("shard", "ctx"), "tp"),
        P("tp", ("shard", "ctx")),
        P(None, ("shard", "ctx")),
        P(None, ("shard", "ctx")),
        P("tp"),
        P(None, "tp"),
        P("tp"),
        P(None, "tp"),
    )
    return jax.shard_map(
        per_device, mesh=mesh, in_specs=in_specs, out_specs=out_specs, check_vma=False
    )
```

```python
import functools

import jax
import jax.numpy as jnp
from jax import lax
from jax.experimental import pallas as pl
from jax.experimental.pallas import tpu as pltpu
from jax.sharding import PartitionSpec as P

HD = 64
NEG = -1e30
VL = 48 * 1024 * 1024

EPS = 1e-05
MAXDOC = 1920
BF = jnp.bfloat16
F32 = jnp.float32
NT_DIMS = (((1,), (1,)), ((), ()))
VMEM_SPEC = pl.BlockSpec(memory_space=pltpu.VMEM)
ANY_SPEC = pl.BlockSpec(memory_space=pl.ANY)
GELU_C = 0.7978845608028654
GELU_A = 0.044715


def dot(left, right):
    return jnp.dot(left, right, preferred_element_type=F32)


def dot_nt(left, right):
    return lax.dot_general(left, right, NT_DIMS, preferred_element_type=F32)


def row_mean(values):
    return jnp.mean(values, -1, keepdims=True)


def col_sum(values):
    return jnp.sum(values, 0, keepdims=True)


def put_transposed(value, dst, tmp):
    width = value.shape[1]
    for k in range(width // 128):
        tmp[k * 128 : (k + 1) * 128, :] = value[:, k * 128 : (k + 1) * 128].T
    piece = width // 16
    for shard in range(2):
        for z in range(4):
            for core in range(2):
                to = core * (width // 2) + shard * (width // 4) + z * piece
                at = shard * (width // 2) + (z * 2 + core) * piece
                dst[to : to + piece, :] = tmp[at : at + piece, :]


def gelu_pair(h):
    inner = GELU_C * (h + GELU_A * h * h * h)
    t = jnp.tanh(inner)
    half = 0.5 * (1.0 + t)
    slope = half + 0.5 * h * (1.0 - t * t) * (GELU_C * (1.0 + (3.0 * GELU_A) * h * h))
    return h * half, slope


def tail_kernel(own_ref, peer_ref, x_ref, g1_ref, gain_ref, out_ref, sum_ref):
    da = own_ref[...].astype(F32) + peer_ref[...].astype(F32)
    x = x_ref[...].astype(F32)
    cen = x - row_mean(x)
    r = lax.rsqrt(row_mean(cen * cen) + EPS)
    xh = cen * r
    sum_ref[0:1, :] = col_sum(da * xh)
    sum_ref[1:2, :] = col_sum(da)
    e = da * gain_ref[...]
    dx = r * (e - row_mean(e) - xh * row_mean(e * xh))
    out_ref[...] = (g1_ref[...].astype(F32) + dx).astype(BF)


def tail_call(own, peer, x, g1, gain):
    rows, width = x.shape
    return pl.pallas_call(
        tail_kernel,
        out_shape=(jax.ShapeDtypeStruct((rows, width), BF), jax.ShapeDtypeStruct((2, width), F32)),
        in_specs=[VMEM_SPEC] * 5,
        out_specs=(VMEM_SPEC, VMEM_SPEC),
        compiler_params=pltpu.CompilerParams(vmem_limit_bytes=VL),
        cost_estimate=pl.CostEstimate(
            flops=20 * rows * width, bytes_accessed=10 * rows * width, transcendentals=rows
        ),
        name="tail",
    )(own, peer, x, g1, gain)


MESH_ID = pl.DeviceIdType.MESH


def remote(src, dst, send, recv, device):
    return pltpu.make_async_remote_copy(
        src_ref=src, dst_ref=dst, send_sem=send, recv_sem=recv, device_id=device, device_id_type=MESH_ID
    )


def greet(devices):
    sem = pltpu.get_barrier_semaphore()
    count = 0
    for device, cond in devices:
        def signal(device=device):
            pl.semaphore_signal(sem, inc=1, device_id=device, device_id_type=MESH_ID)
        if cond is None:
            signal()
            count = count + 1
        else:
            pl.when(cond)(signal)
            count = count + cond.astype(jnp.int32)
    pl.semaphore_wait(sem, count)


def chunk_blocks(w, length, bq, bk):
    found = []
    for kb in range(length // bk):
        for qb in range(length // bq):
            if w == 0 and kb * bk > qb * bq + bq - 1:
                continue
            if qb * bq + w * length - (MAXDOC - 1) > kb * bk + bk - 1:
                continue
            found.append((qb, kb))
    return found


def block_bias(w, lo, qb, kb, bq, bk):
    key = lax.broadcasted_iota(jnp.int32, (bk, bq), 0) + kb * bk
    seen = key >= lo[:, qb * bq : (qb + 1) * bq]
    if w == 0 and (kb + 1) * bk > qb * bq + 1:
        seen = seen & (key <= lax.broadcasted_iota(jnp.int32, (bk, bq), 1) + qb * bq)
    return jnp.where(seen, 0.0, NEG)


def split_pairs(src, dst, heads):
    row = lax.broadcasted_iota(jnp.int32, (2 * HD, src.shape[1]), 0)
    for p in range(heads // 2):
        block = src[p * 128 : (p + 1) * 128, :]
        dst[2 * p] = jnp.where(row < HD, block, jnp.zeros_like(block))
        dst[2 * p + 1] = jnp.where(row >= HD, block, jnp.zeros_like(block))


def back_item(w, heads, length, bq, bk, kv, qT, doT, qm, dm, kT, lse, dd, lo, bias, dq, dk, dv):
    n = heads * HD
    for p in range(heads // 2):
        ps = slice(p * 128, (p + 1) * 128)
        kT[ps, :] = kv[:, ps].T
    blocks = chunk_blocks(w, length, bq, bk)
    for kb in range(length // bk):
        ks = slice(kb * bk, (kb + 1) * bk)
        mine = [qb for qb, other in blocks if other == kb]
        if not mine:
            dk[:, ks] = jnp.zeros((n, bk), F32)
            dv[:, ks] = jnp.zeros((n, bk), F32)
        for turn, qb in enumerate(mine):
            qs = slice(qb * bq, (qb + 1) * bq)
            bias[...] = block_bias(w, lo, qb, kb, bq, bk)

            def scores(h):
                ps = slice((h // 2) * 128, (h // 2 + 1) * 128)
                pv = slice(n + (h // 2) * 128, n + (h // 2 + 1) * 128)
                return dot(kv[ks, ps], qm[h, :, qs]) + bias[...], dot(kv[ks, pv], dm[h, :, qs])

            ahead = scores(0)
            for h in range(heads):
                hs = slice(h * HD, (h + 1) * HD)
                s, dp = ahead
                ahead = scores(h + 1) if h + 1 < heads else None
                e = jnp.exp(s - lse[h : h + 1, qs])
                ds = (e * (dp - dd[h : h + 1, qs])).astype(BF)
                new_v = dot_nt(doT[hs, qs], e.astype(BF))
                new_k = dot_nt(qT[hs, qs], ds)
                if turn:
                    dv[hs, ks] += new_v
                    dk[hs, ks] += new_k
                else:
                    dv[hs, ks] = new_v
                    dk[hs, ks] = new_k
                dq[hs, qs] += dot(kT[hs, ks], ds)


def back_kernel(
    fast, nw, nctx, heads, length,
    qT_ref, doT_ref, dlast_ref, oT_ref, lse_ref, lo_ref, wfull_ref, sum_ref,
    kv_hbm, lt_hbm, z_hbm, dh_hbm, o_hbm, g1_own,
    pn_ref, mine_ref, peer_ref, part2_ref, part1_ref, parto_ref, total_ref, g1_ref,
    slots, kvbuf, qm, dm, kT, bias, dk, dv, dd, dq, dlast,
    ring_send, ring_recv, kv_sem, da_send, da_recv, last_send, last_recv, own_sem, give_send, give_recv, *rs,
):
    n = heads * HD
    bq = bk = min(256, length)
    s, r, t = lax.axis_index("shard"), lax.axis_index("ctx"), lax.axis_index("tp")
    c = lax.rem(r, 2)
    sib, ypeer = {"ctx": r + 1 - 2 * c}, {"tp": 1 - t}
    left, right = {"ctx": r - 1}, {"ctx": r + 1}
    has_left, has_right = r > 0, r < nctx - 1
    half = length // 2
    seqs = qT_ref.shape[0]
    last = seqs - 1
    order = [(w, b) for b in range(last) for w in range(nw, -1, -1)]
    tail = [(w, last) for w in range(nw, -1, -1)]
    lead = order[:1]
    for k in range(nw):
        lead += [order[k + 1], tail[k]]
    items = lead + tail[nw:]
    nbuf = kvbuf.shape[0]

    def load(i):
        w, b = items[i]
        return pltpu.make_async_copy(kv_hbm.at[w, b], kvbuf.at[i % nbuf], kv_sem.at[i % nbuf])

    def start_load(i):
        if i < len(items):
            pl.when(r >= items[i][0])(lambda: load(i).start())

    for i in range(nbuf - 1):
        start_load(i)
    people = [(left, has_left), (right, has_right), (ypeer, None)]
    if fast:
        (lt_ref, z_ref, dh_ref, o_ref, mid_sem) = rs[:5]
        rs = rs[5:]
        mids = [
            pltpu.make_async_copy(src, dst, mid_sem.at[i])
            for i, (src, dst) in enumerate(((lt_hbm, lt_ref), (z_hbm, z_ref), (dh_hbm, dh_ref), (o_hbm, o_ref)))
        ]
        for cp in mids:
            cp.start()
        xpeer = {"shard": 1 - s}
        z2 = lax.rem(r // 2, 2)
        hop4 = lax.rem(r // 4, 2)
        people += [(xpeer, None), ({"ctx": r + 2 - 4 * z2}, None), ({"ctx": r + 4 - 8 * hop4}, None)]
    greet(people)

    rows = pl.ds(pl.multiple_of(t * half, 128), half)
    share = remote(dlast_ref.at[1], dlast.at[:, rows], last_send, last_recv, ypeer)
    share.start()
    dlast[:, rows] = dlast_ref[0]

    keeps, gives = [], []
    for i, (src, dst) in enumerate([(g1_own, g1_ref)]):
        keeps.append(pltpu.make_async_copy(src, dst.at[rows], own_sem.at[i]))
        gives.append(remote(src, dst.at[rows], give_send.at[i], give_recv.at[i], ypeer))
        keeps[i].start()
        gives[i].start()

    def grads_of(b):
        return dlast if b == last else doT_ref.at[b]

    def prepare(b):
        src = grads_of(b)
        split_pairs(qT_ref.at[b], qm.at[b], heads)
        split_pairs(src, dm.at[b], heads)
        for h in range(heads):
            hs = slice(h * HD, (h + 1) * HD)
            dd[b, h : h + 1, :] = col_sum(src[hs, :].astype(F32) * oT_ref[b, hs, :])
        dq[b] = jnp.zeros((n, length), F32)

    for b in range(last):
        prepare(b)

    steps = {}
    if fast:
        (s2, r2, w2, x2, y2, s1, r1, w1, y1, x1, so, ro, wo, yo, xo, vec_buf, rs_send, rs_recv, vec_send, vec_recv) = rs
        step = 512

        def product(g, rhs, core, dst, plus=None):
            cols = rhs.shape[2]
            size = step if cols % step == 0 else cols // 2
            rows = pl.ds(pl.multiple_of(core * (lt_ref.shape[2] // 2), 64), lt_ref.shape[2] // 2)

            def body(j, carry):
                at = pl.ds(pl.multiple_of(j * size, size), size)
                acc = dot(lt_ref[0, g, rows, :], rhs[0, :, at])
                for b in range(1, seqs):
                    acc = acc + dot(lt_ref[b, g, rows, :], rhs[b, :, at])
                mid = acc.shape[0] // 2
                for k in range(2):
                    value = acc[k * mid : (k + 1) * mid]
                    if plus is not None:
                        value = value + plus[k, :, at].astype(F32)
                    dst[k, :, at] = value.astype(BF)
                return carry

            lax.fori_loop(0, cols // size, body, 0)

        def add(dst, a, b):
            dst[...] = (a[...].astype(F32) + b[...].astype(F32)).astype(BF)

        live = {}

        def send(name, src, dst, i, device):
            live[name] = remote(src, dst, rs_send.at[i], rs_recv.at[i], device)
            live[name].start()

        def cols_of(ref, index):
            width = ref.shape[-1] // 2
            return pl.ds(pl.multiple_of(index * width, 128), width)

        def first(g, rhs, sbuf, rbuf, i):
            mids[1 + g].wait()
            product(g, rhs, 1 - c, sbuf)
            send(("core", g), sbuf, rbuf, i, sib)

        def x_then_y(stage):
            if stage == 0:
                first(0, z_ref, s2, r2, 0)
            elif stage == 2:
                live[("core", 0)].wait_recv()
                product(0, z_ref, c, w2, r2)
                send("x2", w2.at[1 - s], x2, 1, xpeer)
            elif stage == 3:
                live["x2"].wait_recv()
                add(w2.at[s], w2.at[s], x2)
                send("y2", w2.at[s, :, cols_of(w2, 1 - t)], y2, 2, ypeer)
            elif stage == 4:
                live["y2"].wait_recv()
                add(part2_ref, w2.at[s, :, cols_of(w2, t)], y2)

        def y_then_x(stage, g, rhs, sb, rb, wb, yb, xb, part, i):
            if stage == 0:
                first(g, rhs, sb, rb, i)
            elif stage == 2:
                live[("core", g)].wait_recv()
                product(g, rhs, c, wb, rb)
                send(("y", g), wb.at[:, :, cols_of(wb, 1 - t)], yb, i + 1, ypeer)
            elif stage == 3:
                live[("y", g)].wait_recv()
                mine = cols_of(wb, t)
                add(wb.at[1 - s, :, mine], wb.at[1 - s, :, mine], yb.at[1 - s])
                send(("x", g), wb.at[1 - s, :, mine], xb, i + 2, xpeer)
                add(wb.at[s, :, mine], wb.at[s, :, mine], yb.at[s])
            elif stage == 4:
                live[("x", g)].wait_recv()
                add(part, wb.at[s, :, cols_of(wb, t)], xb)

        up = lambda stage: y_then_x(stage, 1, dh_ref, s1, r1, w1, y1, x1, part1_ref, 3)
        op = lambda stage: y_then_x(stage, 2, o_ref, so, ro, wo, yo, xo, parto_ref, 6)

        partners = [ypeer, xpeer, sib, {"ctx": r + 2 - 4 * z2}, {"ctx": r + 4 - 8 * hop4}]
        count = vec_buf.shape[0] - 1

        def vec(stage):
            if stage == 0:
                acc = sum_ref[0]
                for b in range(1, sum_ref.shape[0]):
                    acc = acc + sum_ref[b]
                total_ref[...] = acc
            else:
                live[("v", stage - 1)].wait()
                total_ref[...] = total_ref[...] + vec_buf[stage - 1]
            if stage < len(partners):
                vec_buf[count] = total_ref[...]
                live[("v", stage)] = remote(
                    vec_buf.at[count], vec_buf.at[stage], vec_send.at[stage], vec_recv.at[stage], partners[stage]
                )
                live[("v", stage)].start()

        plan = [[],[lambda: mids[0].wait(), lambda: up(0), lambda: x_then_y(0)],[lambda: up(2)],[],[lambda: x_then_y(2)],[lambda: op(0)],[lambda: op(2), lambda: vec(0)],[lambda: up(3), lambda: vec(1)],[lambda: x_then_y(3), lambda: vec(2)],[lambda: op(3), lambda: vec(3), lambda: vec(4)],[lambda: vec(5), lambda: op(4), lambda: up(4), lambda: x_then_y(4)]]
        for i, what in enumerate(plan):
            steps[i] = what
        ends = lambda: [cp.wait_send() for key, cp in live.items() if not (isinstance(key, tuple) and key[0] == "v")]
    else:
        ends = lambda: None

    def project(b):
        for k in range(n // 128):
            ks = slice(k * 128, (k + 1) * 128)
            pn_ref[b, :, ks] = (dq[b, ks, :] * 0.125).T.astype(BF)
        for k in range(2 * n // 128):
            pn_ref[b, :, n + k * 128 : n + (k + 1) * 128] = slots[0, b, k * 128 : (k + 1) * 128, :].T

    unseen = max(0, nw * length - (MAXDOC - 1)) // 128 * 128
    sends = []
    shares = []
    for i, (w, b) in enumerate(items):
        start_load(i + nbuf - 1)
        has = r >= w
        if b == last and w == nw:
            share.wait_recv()
            prepare(b)

        def work(i=i, w=w, b=b):
            load(i).wait()
            back_item(
                w, heads, length, bq, bk, kvbuf.at[i % nbuf], qT_ref.at[b], grads_of(b), qm.at[b], dm.at[b], kT,
                lse_ref.at[b], dd.at[b], lo_ref[b] + (w - r) * length, bias, dq.at[b], dk, dv,
            )

        pl.when(has)(work)
        if w < nw:
            for what in steps.get(i, []):
                what()
        dest = slots.at[w, b]
        if w < nw:
            far = unseen if w == nw - 1 else 0
            keys = slice(far, length)

            def merge(w=w, b=b, dest=dest, far=far, keys=keys):
                place = slots.at[w, b, :, keys]
                remote(place, place, ring_send.at[w, b], ring_recv.at[w, b], left).wait_recv()
                dest[:n, keys] = (dk[:, keys] + slots[w, b, :n, keys].astype(F32)).astype(BF)
                dest[n:, keys] = (dv[:, keys] + slots[w, b, n:, keys].astype(F32)).astype(BF)
                if far:
                    dest[:n, :far] = dk[:, :far].astype(BF)
                    dest[n:, :far] = dv[:, :far].astype(BF)

            pl.when(has & has_right)(merge)

        def plain(dest=dest):
            dest[:n, :] = dk[...].astype(BF)
            dest[n:, :] = dv[...].astype(BF)

        pl.when((has & jnp.logical_not(has_right)) if w < nw else has)(plain)
        if w:
            keys = slice(unseen if w == nw else 0, length)
            cp = remote(
                slots.at[w, b, :, keys], slots.at[w - 1, b, :, keys], ring_send.at[w, b], ring_recv.at[w - 1, b], left
            )
            pl.when(has)(lambda cp=cp: cp.start())
            sends.append((has, cp))
            if w == nw:
                for what in steps.get(i, []):
                    what()
        else:
            project(b)
            if b < last:
                da = dot_nt(pn_ref[b, :, :n], wfull_ref[0])
                da = da + dot_nt(pn_ref[b, :, n : 2 * n], wfull_ref[1])
                da = da + dot_nt(pn_ref[b, :, 2 * n :], wfull_ref[2])
                mine_ref[b] = da.astype(BF)
                shares.append(remote(mine_ref.at[b], peer_ref.at[b], da_send.at[b], da_recv.at[b], ypeer))
                shares[-1].start()
    for what in steps.get(len(items), []):
        what()
    for has, cp in sends:
        pl.when(has)(lambda cp=cp: cp.wait_send())
    ends()
    for cp in keeps + gives + shares:
        cp.wait()
    share.wait_send()


def back_call(fast, nw, nctx, qT, doT, dlast, oT, lse, lo, wfull, sums, kv, lt, z, dh, o, g1_own):
    seqs, n, length = qT.shape
    heads = n // HD
    width = g1_own.shape[-1]
    sds = jax.ShapeDtypeStruct
    ff = z.shape[-1]
    q4 = width // 4
    rows = q4 if fast else 8
    out_shape = [
        sds((seqs, length, 3 * n), BF),
        sds((seqs - 1, length, width), BF),
        sds((seqs - 1, length, width), BF),
        sds((rows, ff // 2), BF),
        sds((rows, ff // 2), BF),
        sds((rows, n), BF),
        sds(sums.shape[1:], F32),
        sds((length, width), BF),
    ]
    bq = min(256, length)
    dma = pltpu.SemaphoreType.DMA
    scratch = [
        pltpu.VMEM((nw + 1, seqs, 2 * n, length), BF),
        pltpu.VMEM((3, length, 2 * n), BF),
        pltpu.VMEM((seqs, heads, 128, length), BF),
        pltpu.VMEM((seqs, heads, 128, length), BF),
        pltpu.VMEM((n, length), BF),
        pltpu.VMEM((bq, bq), F32),
        pltpu.VMEM((n, length), F32),
        pltpu.VMEM((n, length), F32),
        pltpu.VMEM((seqs, 8, length), F32),
        pltpu.VMEM((seqs, n, length), F32),
        pltpu.VMEM((n, length), BF),
        dma((nw + 1, seqs)),
        dma((nw + 1, seqs)),
        dma((3,)),
        dma((seqs,)),
        dma((seqs,)),
        dma,
        dma,
        dma((seqs,)),
        dma((seqs,)),
        dma((seqs,)),
    ]
    if fast:
        scratch += [pltpu.VMEM(v.shape, BF) for v in (lt, z, dh, o)] + [dma((4,))]
        full = lambda cols: pltpu.VMEM((2, q4, cols), BF)
        scratch += [full(ff), full(ff), full(ff), pltpu.VMEM((q4, ff), BF), pltpu.VMEM((q4, ff // 2), BF)]
        for cols in (ff, 2 * n):
            scratch += [full(cols), full(cols), full(cols), full(cols // 2), pltpu.VMEM((q4, cols // 2), BF)]
        scratch += [pltpu.VMEM((6,) + sums.shape[1:], F32), dma((9,)), dma((9,)), dma((5,)), dma((5,))]
    return pl.pallas_call(
        functools.partial(back_kernel, fast, nw, nctx, heads, length),
        out_shape=tuple(out_shape),
        in_specs=[VMEM_SPEC] * 8 + [ANY_SPEC] * 6,
        out_specs=tuple([VMEM_SPEC] * 7 + [ANY_SPEC]),
        scratch_shapes=scratch,
        compiler_params=pltpu.CompilerParams(
            vmem_limit_bytes=63 * 1024 * 1024, collective_id=1, has_side_effects=True
        ),
        cost_estimate=pl.CostEstimate(
            flops=seqs * (nw + 1) * 10 * length * length * n, bytes_accessed=40 * 1024 * 1024, transcendentals=0
        ),
        name="attn_back",
    )(qT, doT, dlast, oT, lse, lo, wfull, sums, kv, lt, z, dh, o, g1_own)


def forward_item(w, first, heads, length, bq, kv, qm, vT, lo, bias, m, l, acc):
    n = heads * HD
    for p in range(heads // 2):
        ps = slice(p * 128, (p + 1) * 128)
        vT[ps, :] = kv[:, n + p * 128 : n + (p + 1) * 128].T
    blocks = chunk_blocks(w, length, bq, min(256, length))
    size = min(256, length)
    for qb in range(length // bq):
        mine = [kb for q, kb in blocks if q == qb]
        if not mine:
            continue
        k0, k1 = min(mine) * size, (max(mine) + 1) * size
        qs, ks = slice(qb * bq, (qb + 1) * bq), slice(k0, k1)
        key = lax.broadcasted_iota(jnp.int32, (k1 - k0, bq), 0) + k0
        seen = key >= lo[:, qs]
        if w == 0:
            seen = seen & (key <= lax.broadcasted_iota(jnp.int32, (k1 - k0, bq), 1) + qb * bq)
        bias[: k1 - k0, :] = jnp.where(seen, 0.0, NEG)

        def scores(h):
            ps = slice((h // 2) * 128, (h // 2 + 1) * 128)
            return dot(kv[ks, ps], qm[h, :, qs]) + bias[: k1 - k0, :]

        ahead = scores(0)
        for h in range(heads):
            hs = slice(h * HD, (h + 1) * HD)
            s = ahead
            ahead = scores(h + 1) if h + 1 < heads else None
            if first:
                top = jnp.max(s, 0, keepdims=True)
                e = jnp.exp(s - top)
                l[h : h + 1, qs] = jnp.sum(e, 0, keepdims=True)
                acc[hs, qs] = dot(vT[hs, ks], e.astype(BF))
            else:
                old = m[h : h + 1, qs]
                top = jnp.maximum(old, jnp.max(s, 0, keepdims=True))
                e = jnp.exp(s - top)
                scale = jnp.exp(old - top)
                l[h : h + 1, qs] = l[h : h + 1, qs] * scale + jnp.sum(e, 0, keepdims=True)
                acc[hs, qs] = acc[hs, qs] * scale + dot(vT[hs, ks], e.astype(BF))
            m[h : h + 1, qs] = top


def front_kernel(
    fast, nw, nctx, heads, length,
    x_ref, wq_ref, ng_ref, nb_ref, hb_ref, fg_ref, fb_ref, hg_ref, seg_ref, w1_hbm, w2_hbm, wo_hbm,
    aT_ref, qT_ref, oT_ref, lse_ref, cown_ref, cpeer_ref, mown_ref, mpeer_ref, wfull_ref, norms_ref, start_ref,
    fgs_ref, fbs_ref, hgs_ref, hbs_ref, kv_hbm, f1_hbm, f2_hbm, fo_hbm,
    slots, kvbuf, qm, vT, bias, m, l, acc, cen, mean, tmp, ngs, nbs,
    ring_send, ring_recv, side_send, side_recv, kv_sem, c_send, c_recv, v_send, v_recv, *rs,
):
    n = heads * HD
    seqs, _, width = x_ref.shape
    half = length // 2
    bq = min(256, length)
    s, r, t = lax.axis_index("shard"), lax.axis_index("ctx"), lax.axis_index("tp")
    c = lax.rem(r, 2)
    even, odd = c == 0, c == 1
    left, right = {"ctx": r - 1}, {"ctx": r + 1}
    has_left, has_right = r > 0, r < nctx - 1
    ypeer, xpeer, sib = {"tp": 1 - t}, {"shard": 1 - s}, {"ctx": r + 1 - 2 * c}
    people = [(left, has_left), (right, has_right), (ypeer, None)]
    if fast:
        zl = lax.rem(r // 2, 2)
        zpeer = {"ctx": r + 2 - 4 * zl}
        people += [(xpeer, None), (zpeer, None)]
        w_send, w_recv, f_send, f_recv, own_sem, load_sem, wq16, w1f, w2f, wof, w1b, w2b, wob = rs
        loads = [
            pltpu.make_async_copy(src, dst, load_sem.at[i])
            for i, (src, dst) in enumerate(((wo_hbm, wof), (w1_hbm, w1f), (w2_hbm, w2f)))
        ]
        for cp in loads:
            cp.start()
    greet(people)

    live = {}
    if fast:
        rows = wq_ref.shape[1]
        part = rows // 2
        wcols = lambda shard, core: pl.ds(pl.multiple_of(shard * rows + core * part, 64), part)
        for i, (src, dst) in enumerate(((ng_ref, ngs), (nb_ref, nbs))):
            live["norms", i] = remote(src, dst.at[s], w_send.at[i], w_recv.at[i], xpeer)
            live["norms", i].start()
            dst[s] = src[...]
        wq16[...] = wq_ref[...].astype(BF)
        live["wq"] = remote(
            wq16.at[:, pl.ds(pl.multiple_of(c * part, 64), part)], wfull_ref.at[:, wcols(s, c)],
            w_send.at[2], w_recv.at[2], xpeer,
        )
        live["wq"].start()
        wfull_ref[:, pl.ds(pl.multiple_of(s * rows, 128), rows), :] = wq16[...]
        owns = []

        def piece_of(size, core, part):
            if core is None:
                return 0, size
            if part is None:
                return core * (size // 2), size // 2
            return core * (size // 2) + part * (size // 4), size // 4

        def region(k, tp, shard, core=None, part=None):
            if k == 1:
                size = w1_hbm.shape[0]
                at, count = piece_of(size, core, part)
                return f1_hbm.at[tp, pl.ds(pl.multiple_of(shard * size + at, 32), count)]
            ref, src = ((fo_hbm, wo_hbm), None, (f2_hbm, w2_hbm))[k]
            size, cols = src.shape
            at, count = piece_of(size, core, part)
            return ref.at[tp, pl.ds(pl.multiple_of(at, 32), count), pl.ds(pl.multiple_of(shard * cols, 128), cols)]

        wide, narrow = (wof, w1f, w2f), (wob, w1b, w2b)

        def own_rows(k, part=None):
            at, count = piece_of(narrow[k].shape[0], c, part)
            return narrow[k].at[pl.ds(pl.multiple_of(at, 32), count)]

        def send(kind, k, src, dst, device):
            live[kind, k] = remote(src, dst, f_send.at[kind, k], f_recv.at[kind, k], device)
            live[kind, k].start()

        def forward(kind, k, place, device):
            send(kind, k, place, place, device)

        def round_weight(k):
            loads[k].wait()
            narrow[k][...] = wide[k][...].astype(BF)
            owns.append(pltpu.make_async_copy(narrow[k], region(k, t, s), own_sem.at[k]))
            owns[-1].start()

        def to_y(k):
            send(0, k, own_rows(k, zl), region(k, t, s, c, zl), ypeer)

        def to_x(k):
            send(1, k, own_rows(k), region(k, t, s, c), xpeer)

        def from_y(k):
            live[0, k].wait_recv()
            forward(2, k, region(k, 1 - t, s, c, zl), xpeer)
            forward(3, k, region(k, 1 - t, s, c, zl), zpeer)

        def from_x(k):
            live[1, k].wait_recv()
            forward(5, k, region(k, t, 1 - s, c), sib)

        def from_z(k):
            live[3, k].wait_recv()
            forward(6, k, region(k, 1 - t, s, c), sib)
            forward(4, k, region(k, 1 - t, s, c, 1 - zl), xpeer)

        def complete(k):
            live[2, k].wait_recv()
            live[4, k].wait_recv()
            forward(7, k, region(k, 1 - t, 1 - s, c), sib)
    else:
        ngs[...] = ng_ref[...]
        nbs[...] = nb_ref[...]
        wfull_ref[...] = wq_ref[...]

    my_half = pl.ds(pl.multiple_of(t * half, 128), half)
    sent = []

    def pass_on(w, b, parity):
        if w == nw:
            return
        if parity:
            cp = remote(
                slots.at[w, b, my_half], slots.at[w + 1, b, my_half], ring_send.at[w, b], ring_recv.at[w + 1, b], right
            )
        else:
            cp = remote(slots.at[w, b], slots.at[w + 1, b], ring_send.at[w, b], ring_recv.at[w + 1, b], right)
        cond = (r >= w) & has_right & (c == parity)
        pl.when(cond)(lambda: cp.start())
        sent.append((cond, cp))

    def side(w, b):
        return remote(slots.at[w, b, my_half], slots.at[w, b, my_half], side_send.at[w, b], side_recv.at[w, b], ypeer)

    def take(w, b):
        if w > nw:
            return

        def go():
            remote(
                slots.at[w, b, my_half], slots.at[w, b, my_half], ring_send.at[w, b], ring_recv.at[w, b], left
            ).wait_recv()
            side(w, b).start()

        pl.when((r >= w) & even)(go)
        sent.append(((r >= w) & even, side(w, b)))

    def whole(w, b, parity):
        if w > nw:
            return

        def go():
            if parity:
                remote(slots.at[w, b], slots.at[w, b], ring_send.at[w, b], ring_recv.at[w, b], left).wait_recv()
            else:
                side(w, b).wait_recv()

        pl.when((r >= w) & (c == parity))(go)
        pass_on(w, b, parity)

    if fast:
        for k in range(3):
            round_weight(k)
            to_y(k)
        to_x(0)
        to_x(1)
    for b in range(seqs):
        x = x_ref[b].astype(F32)
        d = x - row_mean(x)
        acc_n = d * lax.rsqrt(row_mean(d * d) + EPS)
        if b == 0:
            if fast:
                for i in range(2):
                    live["norms", i].wait_recv()
            norms_ref[...] = jnp.zeros_like(norms_ref)
            norms_ref[0:2, :] = jnp.concatenate([ngs[0], ngs[1]], 1).astype(BF).astype(F32)
            norms_ref[2:6, :] = jnp.concatenate([nbs[0], nbs[1]], 1).astype(BF).astype(F32)
        slots[0, b] = (acc_n * norms_ref[0:1, :] + norms_ref[2:3, :]).astype(BF)
        for parity in range(2):
            pass_on(0, b, parity)
    small = []
    for i, (src, dst) in enumerate(((fg_ref, fgs_ref), (fb_ref, fbs_ref), (hg_ref, hgs_ref), (hb_ref, hbs_ref))):
        small.append(remote(src, dst.at[t], v_send.at[i], v_recv.at[i], ypeer))
        small[-1].start()
        dst[t] = src[...]

    for b in range(seqs):
        seg = seg_ref[b : b + 1, :]
        mine = seg_ref[b : b + 1, pl.ds(pl.multiple_of(r * length, 128), length)]
        first = jnp.zeros_like(mine)
        for v in range(1, 4):
            below = jnp.sum(jnp.where(seg < v, 1.0, 0.0), -1, keepdims=True).astype(jnp.int32)
            first = jnp.where(mine == v, below, first)
        start_ref[b] = first

    for b in range(seqs):
        take(1, b)
    for b in range(seqs):
        whole(1, b, 1)
    for b in range(seqs):
        if fast:
            put_transposed(slots[0, b], aT_ref.at[b], tmp)
        else:
            aT_ref[b] = slots[0, b]
    if fast:
        live["wq"].wait_recv()
        far = wcols(1 - s, c)
        live["wsib"] = remote(wfull_ref.at[:, far], wfull_ref.at[:, far], w_send.at[3], w_recv.at[3], sib)
        live["wsib"].start()
        live["wsib"].wait_recv()

    plan = {}
    if fast:
        last = seqs - 1
        plan = {
            (0, 0): [lambda: from_y(0)],
            (0, last): [lambda: from_y(1)],
            (1, 0): [lambda: from_y(2), lambda: to_x(2)],
            (1, last): [lambda: from_x(0)],
            (2, 0): [lambda: from_z(0), lambda: from_x(1)],
            (2, last): [lambda: from_z(1)],
            (3, 0): [lambda: from_z(2)],
        }
    items = [(w, b) for w in range(nw + 1) for b in range(seqs)]
    nbuf = kvbuf.shape[0]

    def store(i):
        w, b = items[i]
        return pltpu.make_async_copy(kvbuf.at[i % nbuf], kv_hbm.at[w, b], kv_sem.at[i % nbuf])

    exchanges = []
    qb, vb = hb_ref[0:1, :], hb_ref[1:2, :]
    for i, (w, b) in enumerate(items):
        has = r >= w
        if i >= nbuf:
            pl.when(r >= items[i - nbuf][0])(lambda i=i: store(i - nbuf).wait())

        def work(i=i, w=w, b=b):
            a = slots[w, b]
            buf = kvbuf.at[i % nbuf]
            if w == 0:
                q = (dot(a, wfull_ref[0]) + qb).astype(BF).astype(F32) * 0.125
                for p in range(heads // 2):
                    ps = slice(p * 128, (p + 1) * 128)
                    qT_ref[b, ps, :] = q[:, ps].T.astype(BF)
                split_pairs(qT_ref.at[b], qm.at[b], heads)
            buf[:, :n] = dot(a, wfull_ref[1]).astype(BF)
            buf[:, n:] = (dot(a, wfull_ref[2]) + vb).astype(BF)
            store(i).start()
            forward_item(
                w, w == 0, heads, length, bq, buf, qm.at[b], vT, start_ref[b] + (w - r) * length, bias,
                m.at[b], l.at[b], acc.at[b],
            )

        if w:
            pl.when(has)(work)
        else:
            work()
        whole(w + 1, b, 0)
        take(w + 2, b)
        whole(w + 2, b, 1)
        for what in plan.get((w, b), []):
            what()
        if w == nw:
            tot = jnp.zeros((1, length), F32)
            for h in range(heads):
                hs = slice(h * HD, (h + 1) * HD)
                o = acc[b, hs, :] / l[b, h : h + 1, :]
                oT_ref[b, hs, :] = o
                tot = tot + col_sum(o)
            tot = tot / n
            mean[b] = tot
            lse_ref[b] = m[b] + jnp.log(l[b])
            for p in range(heads // 2):
                ps = slice(p * 128, (p + 1) * 128)
                cen[b, :, ps] = (oT_ref[b, ps, :] - tot).T.astype(BF)
            theirs = pl.ds(pl.multiple_of((1 - t) * half, 128), half)
            cown_ref[b] = cen[b, my_half, :]
            mown_ref[b] = mean[b, :, my_half]
            if b == seqs - 1:
                cpeer_ref[b] = cen[b, theirs, :]
                mpeer_ref[b] = mean[b, :, theirs]
            else:
                for k, (src, dst) in enumerate(
                    ((cen.at[b, theirs], cpeer_ref.at[b]), (mean.at[b, :, theirs], mpeer_ref.at[b]))
                ):
                    exchanges.append(remote(src, dst, c_send.at[b, k], c_recv.at[b, k], ypeer))
                    exchanges[-1].start()
    for cond, cp in sent:
        pl.when(cond)(lambda cp=cp: cp.wait_send())
    for i in range(max(0, len(items) - nbuf), len(items)):
        pl.when(r >= items[i][0])(lambda i=i: store(i).wait())
    if fast:
        from_x(2)
        for k in range(3):
            complete(k)
        for k in range(3):
            for kind in (5, 6, 7):
                live[kind, k].wait_recv()
            for kind in range(8):
                live[kind, k].wait_send()
        for cp in owns:
            cp.wait()
        for key in (("norms", 0), ("norms", 1), "wq", "wsib"):
            live[key].wait_send()
    for cp in exchanges + small:
        cp.wait()


def front_call(fast, nw, nctx, x, wq, ng, nb, hb, fg, fb, hg, seg, w1, w2, wo):
    seqs, length, width = x.shape
    n = hb.shape[1]
    heads = n // HD
    half = length // 2
    sds = jax.ShapeDtypeStruct
    dma = pltpu.SemaphoreType.DMA
    bq = min(256, length)
    full = lambda w, axes: sds((2,) + tuple(k * a for k, a in zip(w.shape, axes)), BF) if fast else sds((8, 128), BF)
    out_shape = (
        sds((seqs, width, length) if fast else (seqs, length, width), BF),
        sds((seqs, n, length), BF),
        sds((seqs, n, length), F32),
        sds((seqs, 8, length), F32),
        sds((seqs, half, n), BF),
        sds((seqs, half, n), BF),
        sds((seqs, 1, half), F32),
        sds((seqs, 1, half), F32),
        sds((3, width, n), BF),
        sds((8, width), F32),
        sds((seqs, 1, length), jnp.int32),
        sds((2,) + fg.shape, F32),
        sds((2,) + fb.shape, F32),
        sds((2,) + hg.shape, F32),
        sds((2,) + hb.shape, F32),
        sds((nw + 1, seqs, length, 2 * n), BF),
        full(w1, (2, 1)),
        full(w2, (1, 2)),
        full(wo, (1, 2)),
    )
    scratch = [
        pltpu.VMEM((nw + 1, seqs, length, width), BF),
        pltpu.VMEM((3, length, 2 * n), BF),
        pltpu.VMEM((seqs, heads, 128, length), BF),
        pltpu.VMEM((n, length), BF),
        pltpu.VMEM((length, bq), F32),
        pltpu.VMEM((seqs, 8, length), F32),
        pltpu.VMEM((seqs, 8, length), F32),
        pltpu.VMEM((seqs, n, length), F32),
        pltpu.VMEM((seqs, length, n), BF),
        pltpu.VMEM((seqs, 1, length), F32),
        pltpu.VMEM((width, length), BF),
        pltpu.VMEM((2, 2, width // 2), F32),
        pltpu.VMEM((2, 4, width // 2), F32),
        dma((nw + 1, seqs)),
        dma((nw + 1, seqs)),
        dma((nw + 1, seqs)),
        dma((nw + 1, seqs)),
        dma((3,)),
        dma((seqs, 2)),
        dma((seqs, 2)),
        dma((4,)),
        dma((4,)),
    ]
    if fast:
        scratch += [dma((4,)), dma((4,)), dma((8, 3)), dma((8, 3)), dma((3,)), dma((3,)), pltpu.VMEM(wq.shape, BF)]
        scratch += [pltpu.VMEM(w.shape, F32) for w in (w1, w2, wo)]
        scratch += [pltpu.VMEM(w.shape, BF) for w in (w1, w2, wo)]
    return pl.pallas_call(
        functools.partial(front_kernel, fast, nw, nctx, heads, length),
        out_shape=out_shape,
        in_specs=[VMEM_SPEC] * 9 + [ANY_SPEC] * 3,
        out_specs=tuple([VMEM_SPEC] * 15 + [ANY_SPEC] * 4),
        scratch_shapes=scratch,
        compiler_params=pltpu.CompilerParams(
            vmem_limit_bytes=58 * 1024 * 1024, collective_id=3, has_side_effects=True
        ),
        cost_estimate=pl.CostEstimate(
            flops=seqs * (nw + 1) * length * n * (4 * length + 4 * width), bytes_accessed=32 * 1024 * 1024, transcendentals=0
        ),
        name="front",
    )(x, wq, ng, nb, hb, fg, fb, hg, seg, w1, w2, wo)


def middle_kernel(
    fast, n, half,
    cown_ref, cpeer_ref, mown_ref, mpeer_ref, norms_ref, fgs_ref, fbs_ref, hgs_ref, hbs_ref,
    x_hbm, g_hbm, f1_hbm, f2_hbm, fo_hbm,
    out_ref, g1_ref, g1s_ref, doT_ref, dlast_ref, o_ref, f_ref, z_ref, dh_ref, sum_ref,
    x_s, g_s, f1, f2, fo, u_s, gp_s, e_s, dT, tmp, clast, mlast, in_sem, w_sem, d_send, d_recv, c_send, c_recv, g_send, g_recv,
):
    seqs = cown_ref.shape[0]
    width = norms_ref.shape[1]
    step = width
    ff2 = f1.shape[2]
    ff = 2 * ff2
    t = lax.axis_index("tp")
    ypeer = {"tp": 1 - t}
    last = seqs - 1
    rows = pl.ds(pl.multiple_of(t * half, 128), half)
    loads = []
    for i, (src, dst) in enumerate(((x_hbm, x_s), (g_hbm, g_s))):
        for b in range(seqs):
            loads.append(pltpu.make_async_copy(src.at[b, rows], dst.at[b], in_sem.at[i, b]))
    weights = [pltpu.make_async_copy(src, dst, w_sem.at[i]) for i, (src, dst) in enumerate(((fo_hbm, fo), (f1_hbm, f1), (f2_hbm, f2)))]
    weights[0].start()
    for cp in loads:
        cp.start()
    weights[1].start()
    weights[2].start()
    greet([(ypeer, None)])
    sends = []
    for k, (src, dst) in enumerate(((cpeer_ref.at[last], clast), (mpeer_ref.at[last], mlast))):
        sends.append(remote(src, dst, c_send.at[k], c_recv.at[k], ypeer))
        sends[-1].start()
    vec = norms_ref[...]
    gain, shift, b_out, b_down = vec[1:2], vec[3:4], vec[4:5], vec[5:6]
    chunks = [(p, j) for p in range(2) for j in range(0, ff2, step)]
    first = t == 0

    def note(b, row, value):
        if b:
            sum_ref[row : row + 1, :] += value
        else:
            sum_ref[row : row + 1, :] = value

    def give(b, ref, value):
        ref[b, rows] = value
        sends.append(remote(ref.at[b, rows], ref.at[b, rows], g_send.at[b], g_recv.at[b], ypeer))
        sends[-1].start()

    sum_ref[...] = jnp.zeros_like(sum_ref)
    for b in range(seqs):
        if b == last:
            for cp in sends[:2]:
                cp.wait()
        mine, far = mown_ref[b], mlast[...] if b == last else mpeer_ref[b]
        gap = jnp.where(first, mine - far, far - mine) * 0.5
        delta = jnp.broadcast_to(gap, (128, half)).T[:, :1]
        own, peer = cown_ref[b].astype(F32), (clast[...] if b == last else cpeer_ref[b]).astype(F32)
        n0 = jnp.where(first, own, peer) + delta
        n1 = jnp.where(first, peer, own) - delta
        var = (jnp.sum(n0 * n0, -1, keepdims=True) + jnp.sum(n1 * n1, -1, keepdims=True)) / (2 * n)
        rs = lax.rsqrt(var + EPS)
        nh = (n0 * rs, n1 * rs)
        os = []
        for p in range(2):
            cs = slice(p * n, (p + 1) * n)
            o = (nh[p] * hgs_ref[p] + hbs_ref[p, 2:3, :]).astype(BF)
            o_ref[b, :, cs] = o
            os.append(o)
        if b == 0:
            weights[0].wait()
            for cp in loads:
                cp.wait()
        y1 = x_s[b].astype(F32) + b_out
        for p in range(2):
            y1 = y1 + dot(os[p], fo[p])
        cen = y1 - row_mean(y1)
        r2 = lax.rsqrt(row_mean(cen * cen) + EPS)
        yh = cen * r2
        f = (yh * gain + shift).astype(BF)
        g2 = g_s[b]
        if fast:
            put_transposed(g2, f_ref.at[b, 0], tmp)
            put_transposed(f, f_ref.at[b, 1], tmp)
        else:
            f_ref[b] = f
        if b == 0:
            weights[1].wait()
        usum = 0.0
        for p, j in chunks:
            cs = slice(p * ff2 + j, p * ff2 + j + step)
            h = dot(f, f1[p, :, j : j + step]) + fbs_ref[p, 0:1, j : j + step]
            u, slope = gelu_pair(h)
            u_s[:, cs] = u
            gp_s[:, cs] = slope
            usum = usum + jnp.sum(u, -1, keepdims=True)
        mu = usum / ff
        ssum = 0.0
        for p, j in chunks:
            cs = slice(p * ff2 + j, p * ff2 + j + step)
            d = u_s[:, cs] - mu
            ssum = ssum + jnp.sum(d * d, -1, keepdims=True)
        ru = lax.rsqrt(ssum / ff + EPS)
        if b == 0:
            weights[2].wait()
        y2 = y1 + b_down
        esum = 0.0
        ezsum = 0.0
        for i, (p, j) in enumerate(chunks):
            cs = slice(p * ff2 + j, p * ff2 + j + step)
            w2 = f2[p, j : j + step, :]
            zh = (u_s[:, cs] - mu) * ru
            u_s[:, cs] = zh
            fg = fgs_ref[p, :, j : j + step]
            z = (zh * fg + fbs_ref[p, 1:2, j : j + step]).astype(BF)
            z_ref[b, :, cs] = z
            y2 = y2 + dot(z, w2)
            dz = dot_nt(g2, w2)
            note(b, 6 + len(chunks) + i, col_sum(dz * zh))
            note(b, 6 + 2 * len(chunks) + i, col_sum(dz))
            e = dz * fg
            e_s[:, cs] = e
            esum = esum + jnp.sum(e, -1, keepdims=True)
            ezsum = ezsum + jnp.sum(e * zh, -1, keepdims=True)
        out_ref[b] = y2.astype(BF)
        em, ezm = esum / ff, ezsum / ff
        df = jnp.zeros_like(y1)
        for i, (p, j) in enumerate(chunks):
            cs = slice(p * ff2 + j, p * ff2 + j + step)
            du = ru * (e_s[:, cs] - em - u_s[:, cs] * ezm)
            dh = (du * gp_s[:, cs]).astype(BF)
            dh_ref[b, :, cs] = dh
            note(b, 6 + i, col_sum(dh.astype(F32)))
            df = df + dot_nt(dh, f1[p, :, j : j + step])
        note(b, 2, col_sum(df * yh))
        note(b, 3, col_sum(df))
        e2 = df * gain
        g = g2.astype(F32)
        dy1 = g + r2 * (e2 - row_mean(e2) - yh * row_mean(e2 * yh))
        g1 = dy1.astype(BF)
        if b == last:
            g1_ref[...] = g1
        else:
            give(b, g1s_ref, g1)
        if fast:
            put_transposed(g1, f_ref.at[b, 2], tmp)
        note(b, 4, col_sum(g1.astype(F32)))
        note(b, 5, col_sum(g))
        es = []
        for p in range(2):
            cs = slice(p * n, (p + 1) * n)
            dsub = dot_nt(g1, fo[p])
            for k, value in enumerate((col_sum(dsub * nh[p]), col_sum(dsub))):
                if b:
                    sum_ref[k : k + 1, cs] += value
                else:
                    sum_ref[k : k + 1, cs] = value
            es.append(dsub * hgs_ref[p])
        em = sum(jnp.sum(e, -1, keepdims=True) for e in es) / (2 * n)
        ezm = sum(jnp.sum(e * h, -1, keepdims=True) for e, h in zip(es, nh)) / (2 * n)
        for p in range(2):
            dat = rs * (es[p] - em - nh[p] * ezm)
            for k in range(n // 128):
                ks = slice(k * 128, (k + 1) * 128)
                dT[b, p, ks, :] = dat[:, ks].T.astype(BF)
        if b == last:
            dlast_ref[0] = dT[b, t]
            dlast_ref[1] = dT[b, 1 - t]
        else:
            sends.append(remote(dT.at[b, 1 - t], doT_ref.at[b, :, rows], d_send.at[b], d_recv.at[b], ypeer))
            sends[-1].start()
            doT_ref[b, :, rows] = dT[b, t]
    for cp in sends[2:]:
        cp.wait()


def middle_call(fast, cown, cpeer, mown, mpeer, norms, fgs, fbs, hgs, hbs, x, g, f1, f2, fo):
    seqs, half, n = cown.shape
    width = x.shape[2]
    ff = 2 * fgs.shape[2]
    sds = jax.ShapeDtypeStruct
    dma = pltpu.SemaphoreType.DMA
    return pl.pallas_call(
        functools.partial(middle_kernel, fast, n, half),
        out_shape=(
            sds((seqs, half, width), BF),
            sds((half, width), BF),
            sds((seqs - 1, 2 * half, width), BF),
            sds((seqs - 1, n, 2 * half), BF),
            sds((2, n, half), BF),
            sds((seqs, half, 2 * n), BF),
            sds((seqs, 3, width, half) if fast else (seqs, half, width), BF),
            sds((seqs, half, ff), BF),
            sds((seqs, half, ff), BF),
            sds((24, width), F32),
        ),
        in_specs=[VMEM_SPEC] * 9 + [ANY_SPEC] * 5,
        out_specs=(VMEM_SPEC,) * 10,
        scratch_shapes=[
            pltpu.VMEM((seqs, half, width), BF),
            pltpu.VMEM((seqs, half, width), BF),
            pltpu.VMEM(f1.shape, BF),
            pltpu.VMEM(f2.shape, BF),
            pltpu.VMEM(fo.shape, BF),
            pltpu.VMEM((half, ff), F32),
            pltpu.VMEM((half, ff), F32),
            pltpu.VMEM((half, ff), F32),
            pltpu.VMEM((seqs, 2, n, half), BF),
            pltpu.VMEM((width, half), BF),
            pltpu.VMEM((half, n), BF),
            pltpu.VMEM((1, half), F32),
            dma((2, seqs)),
            dma((3,)),
            dma((seqs,)),
            dma((seqs,)),
            dma((2,)),
            dma((2,)),
            dma((seqs - 1,)),
            dma((seqs - 1,)),
        ],
        compiler_params=pltpu.CompilerParams(
            vmem_limit_bytes=56 * 1024 * 1024, collective_id=4, has_side_effects=True
        ),
        cost_estimate=pl.CostEstimate(
            flops=4 * seqs * half * (f1.size + f2.size + fo.size), bytes_accessed=24 * 1024 * 1024, transcendentals=0
        ),
        name="middle",
    )(cown, cpeer, mown, mpeer, norms, fgs, fbs, hgs, hbs, x, g, f1, f2, fo)


def end_kernel(
    n, length,
    pn, mine0, peer0, w_ref, x_ref, g10_ref, g1_ref, aT_ref, gain_ref, p2_ref, p1_ref, po_ref, out_own,
    gt_ref, gq_ref, g2_ref, gu_ref, go_ref, total_ref, out_ref,
    mine, peer, xh, rinv, sq, rq, wq, xq, zq, zq2, z2a, z2b, z1a, z1b, zoa, zob, vec_buf,
    da_send, da_recv, out_send, out_recv, rs_send, rs_recv, vec_send, vec_recv,
):
    seqs = x_ref.shape[0]
    s, r, t = lax.axis_index("shard"), lax.axis_index("ctx"), lax.axis_index("tp")
    c, z = lax.rem(r, 2), r // 2
    lo_bit, hi_bit = lax.rem(z, 2), z // 2
    sib, ypeer, xpeer = {"ctx": r + 1 - 2 * c}, {"tp": 1 - t}, {"shard": 1 - s}
    zlo, zhi = {"ctx": r + 2 - 4 * lo_bit}, {"ctx": r + 4 - 8 * hi_bit}
    greet([(d, None) for d in (sib, ypeer, xpeer, zlo, zhi)])
    live = {}

    def send(name, src, dst, i, device):
        live[name] = remote(src, dst, rs_send.at[i], rs_recv.at[i], device)
        live[name].start()

    def add(dst, a, b):
        dst[...] = (a[...].astype(F32) + b[...].astype(F32)).astype(dst.dtype)

    groups = ((p2_ref, z2a, z2b, g2_ref), (p1_ref, z1a, z1b, gu_ref), (po_ref, zoa, zob, go_ref))
    for k, (part, za, zb, out) in enumerate(groups):
        send(("a", k), part.at[:, 1 - lo_bit], za, 2 * k, zlo)

    last = seqs - 1
    da = dot_nt(pn[last, :, :n], w_ref[0])
    da = da + dot_nt(pn[last, :, n : 2 * n], w_ref[1])
    da = da + dot_nt(pn[last, :, 2 * n :], w_ref[2])
    mine[...] = da.astype(BF)
    exchange = remote(mine, peer, da_send, da_recv, ypeer)
    exchange.start()
    half = length // 2
    my_rows = pl.ds(pl.multiple_of(t * half, 128), half)
    gives = []
    for b in range(seqs):
        out_ref[b, my_rows, :] = out_own[b]
        gives.append(remote(out_own.at[b], out_ref.at[b, my_rows], out_send.at[b], out_recv.at[b], ypeer))
        gives[b].start()
    rows = aT_ref.shape[1] // 2

    def product(core, dst):
        at = pl.ds(pl.multiple_of(core * rows, 64), rows)
        for k in range(3):
            ks = slice(k * n, (k + 1) * n)
            acc = dot(aT_ref[0, at, :], pn[0, :, ks])
            for b in range(1, seqs):
                acc = acc + dot(aT_ref[b, at, :], pn[b, :, ks])
            acc = acc.astype(BF)
            for j in range(2):
                for i in range(4):
                    at_row = (j * 4 + i) * (rows // 8)
                    dst[j, i // 2, i % 2, :, ks] = acc[at_row : at_row + rows // 8]

    product(1 - c, sq)
    send("core", sq, rq, 6, sib)
    product(c, wq)
    sums = [jnp.zeros((1, x_ref.shape[2]), F32) for _ in range(2)]
    bias = [jnp.zeros((1, n), F32) for _ in range(2)]
    live["core"].wait_recv()
    add(wq.at[1 - s], wq.at[1 - s], rq.at[1 - s])
    send("x", wq.at[1 - s], xq, 7, xpeer)
    add(wq.at[s], wq.at[s], rq.at[s])
    for b in range(seqs):
        share = mine[...].astype(F32) if b == last else mine0[b].astype(F32)
        x = x_ref[b].astype(F32)
        cen = x - row_mean(x)
        inv = lax.rsqrt(row_mean(cen * cen) + EPS)
        rinv[b] = inv
        xh[b] = cen * inv
        sums[0] = sums[0] + col_sum(share * xh[b])
        sums[1] = sums[1] + col_sum(share)
        bias[0] = bias[0] + col_sum(pn[b, :, :n].astype(F32))
        bias[1] = bias[1] + col_sum(pn[b, :, 2 * n :].astype(F32))
    total_ref[...] = jnp.zeros_like(total_ref)
    total_ref[0:1, :] = sums[0]
    total_ref[1:2, :] = sums[1]
    total_ref[2:3, :n] = bias[0]
    total_ref[2:3, n:] = bias[1]
    partners = [sib, xpeer, zlo, zhi, ypeer]
    count = len(partners)

    def vec(stage):
        if stage:
            live[("v", stage - 1)].wait()
            if stage == count:
                total_ref[0:2, :] = total_ref[0:2, :] + vec_buf[stage - 1, 0:2, :]
            else:
                total_ref[...] = total_ref[...] + vec_buf[stage - 1]
        if stage < count:
            vec_buf[count] = total_ref[...]
            live[("v", stage)] = remote(
                vec_buf.at[count], vec_buf.at[stage], vec_send.at[stage], vec_recv.at[stage], partners[stage]
            )
            live[("v", stage)].start()

    vec(0)
    vec(1)
    for k, (part, za, zb, out) in enumerate(groups):
        live[("a", k)].wait_recv()
        add(za, part.at[:, lo_bit], za)
        send(("b", k), za.at[1 - hi_bit], zb, 2 * k + 1, zhi)
    vec(2)
    live["x"].wait_recv()
    add(wq.at[s], wq.at[s], xq)
    send("za", wq.at[s, :, 1 - lo_bit], zq, 8, zlo)
    vec(3)

    def finish(b):
        own, far = (mine[...], peer[...]) if b == last else (mine0[b], peer0[b])
        e = (own.astype(F32) + far.astype(F32)) * gain_ref[0:1, :]
        h = xh[b]
        dx = rinv[b] * (e - row_mean(e) - h * row_mean(e * h))
        g1 = g1_ref[...] if b == last else g10_ref[b]
        gt_ref[b] = (g1.astype(F32) + dx).astype(BF)

    for b in range(last):
        finish(b)
    live["za"].wait_recv()
    add(wq.at[s, :, lo_bit], wq.at[s, :, lo_bit], zq)
    send("zb", wq.at[s, 1 - hi_bit, lo_bit], zq2, 9, zhi)
    vec(4)
    for k, (part, za, zb, out) in enumerate(groups):
        live[("b", k)].wait_recv()
        add(out, za.at[hi_bit], zb)
    exchange.wait()
    finish(last)
    live["zb"].wait_recv()
    total = wq[s, hi_bit, lo_bit].astype(F32) + zq2[...].astype(F32)
    for k in range(3):
        gq_ref[k] = total[:, k * n : (k + 1) * n]
    vec(5)
    for key, cp in live.items():
        if not (isinstance(key, tuple) and key[0] == "v"):
            cp.wait_send()
    for cp in gives:
        cp.wait()


def end_call(pn, mine0, peer0, w, x, g10, g1, aT, gain, p2, p1, po, out_own):
    seqs, length, width = x.shape
    n = pn.shape[2] // 3
    piece = width // 16
    sds = jax.ShapeDtypeStruct
    dma = pltpu.SemaphoreType.DMA
    c2, c1, co = p2.shape[-1], p1.shape[-1], po.shape[-1]
    return pl.pallas_call(
        functools.partial(end_kernel, n, length),
        out_shape=(
            sds((seqs, length, width), BF),
            sds((3, piece, n), F32),
            sds((piece, c2), F32),
            sds((piece, c1), F32),
            sds((piece, co), F32),
            sds((8, width), F32),
            sds((seqs, length, width), BF),
        ),
        in_specs=[VMEM_SPEC] * 13,
        out_specs=(VMEM_SPEC,) * 7,
        scratch_shapes=[
            pltpu.VMEM((length, width), BF),
            pltpu.VMEM((length, width), BF),
            pltpu.VMEM((seqs, length, width), F32),
            pltpu.VMEM((seqs, length, 1), F32),
            pltpu.VMEM((2, 2, 2, piece, 3 * n), BF),
            pltpu.VMEM((2, 2, 2, piece, 3 * n), BF),
            pltpu.VMEM((2, 2, 2, piece, 3 * n), BF),
            pltpu.VMEM((2, 2, piece, 3 * n), BF),
            pltpu.VMEM((2, piece, 3 * n), BF),
            pltpu.VMEM((piece, 3 * n), BF),
            pltpu.VMEM((2, piece, c2), BF),
            pltpu.VMEM((piece, c2), BF),
            pltpu.VMEM((2, piece, c1), BF),
            pltpu.VMEM((piece, c1), BF),
            pltpu.VMEM((2, piece, co), BF),
            pltpu.VMEM((piece, co), BF),
            pltpu.VMEM((6, 8, width), F32),
            dma,
            dma,
            dma((seqs,)),
            dma((seqs,)),
            dma((10,)),
            dma((10,)),
            dma((5,)),
            dma((5,)),
        ],
        compiler_params=pltpu.CompilerParams(
            vmem_limit_bytes=56 * 1024 * 1024, collective_id=2, has_side_effects=True
        ),
        cost_estimate=pl.CostEstimate(
            flops=12 * seqs * length * width * n, bytes_accessed=16 * 1024 * 1024, transcendentals=0
        ),
        name="input_back",
    )(pn, mine0, peer0, w, x, g10, g1, aT, gain, p2, p1, po, out_own)


def pack_kernel(n, gd_ref, gu_ref, go_ref, gq_ref, tail_ref, sum_ref, down_ref, up_ref, out_ref, qkv_ref, ng_ref, nb_ref, hg_ref, hb_ref, fg_ref, fb_ref):
    s, r, t = lax.axis_index("shard"), lax.axis_index("ctx"), lax.axis_index("tp")
    width = tail_ref.shape[1]
    piece = gd_ref.shape[0]
    down_ref[...] = gd_ref[...].T
    out_ref[...] = go_ref[...].T
    up_ref[...] = gu_ref[...]
    qkv_ref[...] = gq_ref[...]
    mine = lax.rem(width - (s * 8 + r) * piece, width)
    ends = pltpu.roll(tail_ref[...], mine, 1)[:, :piece]
    mids = pltpu.roll(sum_ref[0:8, :], mine, 1)[:, :piece]
    ng_ref[0:1, :] = ends[0:1]
    ng_ref[1:2, :] = mids[2:3]
    nb_ref[0:1, :] = ends[1:2]
    nb_ref[1:4, :] = mids[3:6]
    heads = pl.ds(pl.multiple_of(t * n, 128), n)
    hg_ref[...] = sum_ref[0:1, heads]
    hb_ref[0:1, :] = tail_ref[2:3, :n]
    hb_ref[1:2, :] = tail_ref[2:3, n:]
    hb_ref[2:3, :] = sum_ref[1:2, heads]
    for k, (dst, row) in enumerate(((fb_ref, 0), (fg_ref, 0), (fb_ref, 1))):
        for j in range(2):
            dst[row : row + 1, j * width : (j + 1) * width] = sum_ref[pl.ds(6 + 4 * k + 2 * t + j, 1), :]


def pack_call(gd, gu, go, gq, tails, sums):
    piece, ff2 = gd.shape
    n = go.shape[1]
    sds = jax.ShapeDtypeStruct
    return pl.pallas_call(
        functools.partial(pack_kernel, n),
        out_shape=(
            sds((ff2, piece), F32),
            sds((piece, ff2), F32),
            sds((n, piece), F32),
            sds(gq.shape, F32),
            sds((2, piece), F32),
            sds((4, piece), F32),
            sds((1, n), F32),
            sds((3, n), F32),
            sds((1, ff2), F32),
            sds((2, ff2), F32),
        ),
        in_specs=[VMEM_SPEC] * 6,
        out_specs=(VMEM_SPEC,) * 10,
        compiler_params=pltpu.CompilerParams(vmem_limit_bytes=62 * 1024 * 1024),
        name="pack",
    )(gd, gu, go, gq, tails, sums)


def swap(value, axis):
    return lax.ppermute(value, axis, [(0, 1), (1, 0)])


def scatter_rows(grad, t=None):
    width, cols = grad.shape
    if t is not None:
        grad = lax.psum_scatter(grad.reshape(width, 2, cols // 2), "tp", scatter_dimension=1, tiled=False)
    return lax.psum_scatter(grad.astype(F32), ("shard", "ctx"), scatter_dimension=0, tiled=True)


def per_device(
    tokens,
    cotangent,
    segment_ids,
    w_qkv,
    w_out,
    w_fc1,
    w_fc2,
    norm_gain,
    norm_bias,
    head_gain,
    head_bias,
    ffn_gain,
    ffn_bias,
):
    seqs, length, width = tokens.shape
    n = w_qkv.shape[2]
    ff2 = w_fc1.shape[1]
    s, r, t = lax.axis_index("shard"), lax.axis_index("ctx"), lax.axis_index("tp")
    nctx = lax.axis_size("ctx")
    fast = lax.axis_size("shard") == 2 and nctx == 8
    nw = min(-(-(MAXDOC - 1) // length), nctx - 1)

    wq, w1, w2, wo, ng, nb = w_qkv, w_fc1, w_fc2, w_out, norm_gain, norm_bias
    if not fast:
        wq = lax.all_gather(wq.astype(BF), "shard", axis=1, tiled=True)
        ng, nb = (
            lax.all_gather(v, "shard", axis=1, tiled=True).reshape(-1, 2, width // 2).transpose(1, 0, 2) for v in (ng, nb)
        )
        full = [lax.all_gather(w.astype(BF), "shard", axis=a, tiled=True) for w, a in ((w1, 0), (w2, 1), (wo, 1))]
        full = [lax.all_gather(w, "tp", axis=0) for w in full]

    (acts, qT, oT, lse, cown, cpeer, mown, mpeer, wfull, norms, start, fgs, fbs, hgs, hbs, kv, f1, f2, fo) = front_call(
        fast, nw, nctx, tokens, wq, ng, nb, head_bias, ffn_gain[None], ffn_bias, head_gain[None], segment_ids, w1, w2, wo
    )
    if not fast:
        f1, f2, fo = full
    out_own, g1_own, g10, doT, dlast, o, lt, z_act, dh, sums = middle_call(
        fast, cown, cpeer, mown, mpeer, norms, fgs, fbs, hgs, hbs, tokens, cotangent, f1, f2, fo
    )
    pn, mine0, peer0, part2, part1, parto, sums_all, g1 = back_call(
        fast, nw, nctx, qT, doT, dlast, oT, lse, start, wfull, sums[None], kv, lt, z_act, dh, o, g1_own
    )
    gains = norms[:1]

    def fold_rows(value):
        return value.reshape((-1,) + value.shape[2:])

    if fast:
        split = lambda part: part.reshape(2, 2, part.shape[0] // 4, part.shape[1])
        grad_tokens, grad_qkv, gd, gu, go, tails, out = end_call(
            pn, mine0, peer0, wfull, tokens, g10, g1, acts, norms, split(part2), split(part1), split(parto), out_own
        )
        down, up, wout, qkv, ng, nb, hg, hb, fg, fb = pack_call(gd, gu, go, grad_qkv, tails, sums_all)
        return out, grad_tokens, qkv, wout, up, down, ng, nb, hg.reshape(-1), hb, fg.reshape(-1), fb
    else:
        outer = lambda left, right: lax.dot_general(
            fold_rows(left), fold_rows(right), (((0,), (0,)), ((), ())), preferred_element_type=F32
        ).astype(BF)
        g_all = jnp.concatenate([g10, g1[None]])
        g1_rows = lax.dynamic_slice_in_dim(g_all, t * (length // 2), length // 2, 1)
        out = lax.all_gather(out_own, "tp", axis=1, tiled=True)
        g_own = lax.dynamic_slice_in_dim(cotangent, t * (length // 2), length // 2, 1)
        gd = scatter_rows(outer(g_own, z_act), t)
        gu = scatter_rows(outer(lt, dh), t)
        go = scatter_rows(outer(g1_rows, o), t)
        sums_all = lax.psum(sums, ("shard", "ctx", "tp"))
        grad_tokens, in_sums = [], 0.0
        for b in range(seqs):
            da = sum(dot_nt(pn[b, :, i * n : (i + 1) * n], wfull[i]) for i in range(3)).astype(BF)
            gt, part = tail_call(da, swap(da, "tp"), tokens[b], g_all[b], gains)
            grad_tokens.append(gt)
            in_sums = in_sums + part
        grad_tokens = jnp.stack(grad_tokens)
        grad_qkv = scatter_rows(outer(acts, pn)).reshape(-1, 3, n).transpose(1, 0, 2)
        tails = lax.psum(
            jnp.concatenate([in_sums.reshape(-1), jnp.sum(pn.astype(F32), (0, 1))]), ("shard", "ctx")
        )
        in_sums, bias_q, bias_v = tails[: 2 * width].reshape(2, width), tails[2 * width :][:n], tails[-n:]

    hsum, dsum, fsum = sums_all[:2], sums_all[2:6], sums_all[6 : 6 + 6 * ff2 // width].reshape(3, 2 * ff2)
    piece = width // (lax.axis_size("shard") * lax.axis_size("ctx"))
    mine = (s * lax.axis_size("ctx") + r) * piece
    grad_gain = lax.dynamic_slice_in_dim(jnp.stack([in_sums[0], dsum[0]]), mine, piece, 1)
    grad_bias = lax.dynamic_slice_in_dim(jnp.stack([in_sums[1], dsum[1], dsum[2], dsum[3]]), mine, piece, 1)
    hsum = lax.dynamic_slice_in_dim(hsum, t * n, n, 1)
    fsum = lax.dynamic_slice_in_dim(fsum, t * ff2, ff2, 1)
    return (
        out,
        grad_tokens,
        grad_qkv,
        go.T,
        gu,
        gd.T,
        grad_gain,
        grad_bias,
        hsum[0],
        jnp.stack([bias_q, bias_v, hsum[1]]),
        fsum[1],
        jnp.stack([fsum[0], fsum[2]]),
    )


def solution(mesh):
    in_specs = (
        P("shard", "ctx", None),
        P("shard", "ctx", None),
        P("shard", None),
        P(None, "shard", "tp"),
        P("tp", "shard"),
        P("shard", "tp"),
        P("tp", "shard"),
        P(None, "shard"),
        P(None, "shard"),
        P("tp"),
        P(None, "tp"),
        P("tp"),
        P(None, "tp"),
    )
    out_specs = (
        P("shard", "ctx", None),
        P("shard", "ctx", None),
        P(None, ("shard", "ctx"), "tp"),
        P("tp", ("shard", "ctx")),
        P(("shard", "ctx"), "tp"),
        P("tp", ("shard", "ctx")),
        P(None, ("shard", "ctx")),
        P(None, ("shard", "ctx")),
        P("tp"),
        P(None, "tp"),
        P("tp"),
        P(None, "tp"),
    )
    return jax.shard_map(
        per_device, mesh=mesh, in_specs=in_specs, out_specs=out_specs, check_vma=False
    )
```
